128 devices in a mesh: row: 8 (over y_hi, x), col: 16 (over y_lo, z, core).
Axes of the slice: x: 4, y: 4 (y_hi: 2, y_lo: 2; y = y_hi * 2 + y_lo), z: 4, core: 2. Of those that a mesh axis runs over, the one named last changes fastest.
Arguments:
- field_real: float32 [4096, 4096], P('row', 'col'), may hold values from -6 to 6
- field_imag: float32 [4096, 4096], P('row', 'col'), may hold values from -6 to 6
Outputs:
- slm_real: float32 [4096, 4096], P('row', 'col')
- slm_imag: float32 [4096, 4096], P('row', 'col')
The draws below stay inside these ranges and needn't reach their ends.
All inputs are finite; a program needn't handle non-finite values.
Results may differ from the reference program's by a relative error of at most 0.0003.
Values sent between devices are 32-bit elements; how exact they have to be, the bound alone decides.
A program may use at most 128 MiB of HBM per device.

```python
import math
import jax
import jax.numpy as jnp
from jax import lax

N = 4096


def block_levels(stream_key, shape, split, low, high):
    level = 1.0
    for dim, blocks in split:
        draws = jax.random.uniform(jax.random.fold_in(jax.random.fold_in(stream_key, 6), dim), (blocks,), jnp.float32, low / len(split), high / len(split))
        level = level * jnp.repeat(jnp.exp(draws), shape[dim] // blocks).reshape((-1,) + (1,) * (len(shape) - 1 - dim))
    return level


def normal_values(key, dims, deviation, bound, shards=(), kind=jnp.bfloat16):
    drawn = deviation * jax.random.normal(key, dims, jnp.float32)
    if shards:
        drawn = drawn * block_levels(key, dims, shards, -0.22, 0.18)
    return jnp.clip(drawn, -bound, bound).astype(kind)


def setup_inputs(seed: int = 0) -> dict:
    streams_of = jax.random.split(jax.random.key(seed), 3)
    return {
        "field_real": normal_values(streams_of[0], (N, N), 1.0, 6.0, ((0, 8), (1, 16)), jnp.float32),
        "field_imag": normal_values(streams_of[1], (N, N), 1.0, 6.0, ((0, 8), (1, 16)), jnp.float32),
    }


wavelength = 5.2e-07
distance = 0.2

def optics(padded_side):
    pitch = 2e-06 * math.sqrt(8192.0 / padded_side)
    extent = padded_side * pitch
    ratio_sq = (wavelength / extent) ** 2
    band_limit = extent / (wavelength * math.sqrt((2.0 * distance / extent) ** 2 + 1.0))
    return (ratio_sq, band_limit)

def signed_index(index_ids, modulus):
    return jnp.where(index_ids >= modulus // 2, index_ids - modulus, index_ids)

def transfer(row_signed, col_signed, ratio_sq, band_limit):
    square = row_signed[:, None] * row_signed[:, None] + col_signed[None, :] * col_signed[None, :]
    scaled = ratio_sq * square
    phase_angle = -2.0 * math.pi * distance / wavelength * scaled / (1.0 + jnp.sqrt(1.0 - scaled))
    gauss_gain = jnp.exp(square * (-2.0 / (band_limit * band_limit)))
    inside = (jnp.abs(row_signed)[:, None] < band_limit) & (jnp.abs(col_signed)[None, :] < band_limit)
    total_gain = jnp.where(inside, gauss_gain, 0.0)
    return (total_gain * jnp.cos(phase_angle), total_gain * jnp.sin(phase_angle))

def encode(near_real, near_imag, amplitude, peak, even_cell):
    amp_level = 0.8 * amplitude / peak
    amp_floor = jnp.maximum(amplitude, 0.05 * peak)
    unit_real = near_real / amp_floor
    unit_imag = near_imag / amp_floor
    lift_part = jnp.sqrt(1.0 - amp_level * amp_level)
    cell_sign = jnp.where(even_cell, 1.0, -1.0)
    out_real = unit_real * amp_level + cell_sign * unit_imag * lift_part
    out_imag = unit_imag * amp_level - cell_sign * unit_real * lift_part
    return (out_real, out_imag)

def reference(field_real, field_imag):
    padded_side = 2 * N
    quarter = padded_side // 4
    complex_field = lax.complex(field_real, field_imag)
    padded = jnp.pad(complex_field, ((quarter, quarter), (quarter, quarter)))
    spectrum = jnp.fft.fft2(padded)
    ratio_sq, band_limit = optics(padded_side)
    col_signed = signed_index(jnp.arange(padded_side, dtype=jnp.int32), padded_side).astype(jnp.float32)
    blocks = spectrum.reshape(padded_side // 512, 512, padded_side)
    starts = jnp.arange(padded_side // 512, dtype=jnp.int32) * 512

    def filter_block(block_pair):
        row_block, row_start = block_pair
        row_ids = row_start + jnp.arange(512, dtype=jnp.int32)
        row_signed = signed_index(row_ids, padded_side).astype(jnp.float32)
        gain_real, gain_imag = transfer(row_signed, col_signed, ratio_sq, band_limit)
        return row_block * lax.complex(gain_real, gain_imag)
    filtered = lax.map(filter_block, (blocks, starts)).reshape(padded_side, padded_side)
    row_part = jnp.fft.ifft(filtered, axis=0)[quarter:quarter + N]
    propagated = jnp.fft.ifft(row_part, axis=1)[:, quarter:quarter + N]
    sum_scale = float(padded_side) * float(padded_side)
    near_real = jnp.real(propagated) * sum_scale
    near_imag = jnp.imag(propagated) * sum_scale
    amplitude = jnp.sqrt(near_real * near_real + near_imag * near_imag)
    peak = jnp.max(amplitude)
    row_ids = jnp.arange(N, dtype=jnp.int32)
    even_cell = (row_ids[:, None] + row_ids[None, :]) % 2 == 0
    slm_real, slm_imag = encode(near_real, near_imag, amplitude, peak, even_cell)
    return (slm_real.astype(jnp.float32), slm_imag.astype(jnp.float32))
```

```python
from functools import partial
import math

import jax
import jax.numpy as jnp
from jax import lax
from jax.sharding import PartitionSpec as P
from jax.experimental import pallas as pl
from jax.experimental.pallas import tpu as pltpu
import functools

N = 4096


wavelength = 5.2e-07
distance = 0.2


def optics(padded_side):
    pitch = 2e-06 * math.sqrt(8192.0 / padded_side)
    extent = padded_side * pitch
    ratio_sq = (wavelength / extent) ** 2
    band_limit = extent / (wavelength * math.sqrt((2.0 * distance / extent) ** 2 + 1.0))
    return (ratio_sq, band_limit)


def factor_pair(length):
    bit_count = length.bit_length() - 1
    inner_size = 2 ** ((bit_count + 1) // 2)
    return (length // inner_size, inner_size)


def signed_index(index_ids, modulus):
    return jnp.where(index_ids >= modulus // 2, index_ids - modulus, index_ids)


def transfer(row_signed, col_signed, ratio_sq, band_limit):
    square = row_signed[:, None] * row_signed[:, None] + col_signed[None, :] * col_signed[None, :]
    scaled = ratio_sq * square
    phase_angle = -2.0 * math.pi * distance / wavelength * scaled / (1.0 + jnp.sqrt(1.0 - scaled))
    gauss_gain = jnp.exp(square * (-2.0 / (band_limit * band_limit)))
    inside = (jnp.abs(row_signed)[:, None] < band_limit) & (
        jnp.abs(col_signed)[None, :] < band_limit
    )
    total_gain = jnp.where(inside, gauss_gain, 0.0)
    return (total_gain * jnp.cos(phase_angle), total_gain * jnp.sin(phase_angle))


def encode(near_real, near_imag, amplitude, peak, even_cell):
    amp_level = 0.8 * amplitude / peak
    amp_floor = jnp.maximum(amplitude, 0.05 * peak)
    unit_real = near_real / amp_floor
    unit_imag = near_imag / amp_floor
    lift_part = jnp.sqrt(1.0 - amp_level * amp_level)
    cell_sign = jnp.where(even_cell, 1.0, -1.0)
    out_real = unit_real * amp_level + cell_sign * unit_imag * lift_part
    out_imag = unit_imag * amp_level - cell_sign * unit_real * lift_part
    return (out_real, out_imag)


def index_range(range_start, id_count):
    return jnp.arange(id_count, dtype=jnp.int32) + range_start


def phase_table(first_ids, second_ids, modulus, exponent_sign):
    product = first_ids[:, None] * second_ids[None, :] % modulus
    phase_arg = exponent_sign * 2.0 * math.pi / modulus * product.astype(jnp.float32)
    return (jnp.cos(phase_arg), jnp.sin(phase_arg))


def complex_einsum(form, left_real, left_imag, right_real, right_imag):
    real_dot = partial(jnp.einsum, form, precision=lax.Precision.HIGHEST)
    out_real = real_dot(left_real, right_real) - real_dot(left_imag, right_imag)
    out_imag = real_dot(left_real, right_imag) + real_dot(left_imag, right_real)
    return (out_real, out_imag)


def transform_last(values_real, values_imag, exponent_sign, in_start, out_start, out_count, length):
    outer_size, inner_size = factor_pair(length)
    row_count = values_real.shape[0]
    blocks_in = values_real.shape[1] // inner_size
    first_block = in_start // inner_size
    cube_real = values_real.reshape(row_count, blocks_in, inner_size)
    cube_imag = values_imag.reshape(row_count, blocks_in, inner_size)
    step_real, step_imag = phase_table(
        index_range(first_block, blocks_in), index_range(0, outer_size), outer_size, exponent_sign
    )
    mid_real, mid_imag = complex_einsum("rnq,nk->rkq", cube_real, cube_imag, step_real, step_imag)
    twist_real, twist_imag = phase_table(
        index_range(0, outer_size), index_range(0, inner_size), length, exponent_sign
    )
    mid_real, mid_imag = (
        mid_real * twist_real - mid_imag * twist_imag,
        mid_real * twist_imag + mid_imag * twist_real,
    )
    blocks_out = out_count // outer_size
    second_block = out_start // outer_size
    last_real, last_imag = phase_table(
        index_range(0, inner_size), index_range(second_block, blocks_out), inner_size, exponent_sign
    )
    done_real, done_imag = complex_einsum("rkq,qj->rjk", mid_real, mid_imag, last_real, last_imag)
    return (
        done_real.reshape(row_count, blocks_out * outer_size),
        done_imag.reshape(row_count, blocks_out * outer_size),
    )


def _allmax_kernel(nr, nc, x_ref, o_ref, buf_c, buf_r, part, ssem_c, rsem_c, ssem_r, rsem_r):
    me_r = lax.axis_index("row")
    me_c = lax.axis_index("col")
    mesh_t = pl.DeviceIdType.MESH
    barrier = pltpu.get_barrier_semaphore()
    for k in range(1, nc):
        pl.semaphore_signal(barrier, inc=1, device_id=(me_r, lax.rem(me_c + k, nc)), device_id_type=mesh_t)
    for k in range(1, nr):
        pl.semaphore_signal(barrier, inc=1, device_id=(lax.rem(me_r + k, nr), me_c), device_id_type=mesh_t)
    pl.semaphore_wait(barrier, (nc - 1) + (nr - 1))

    def col_copy(dst_c, slot):
        return pltpu.make_async_remote_copy(
            src_ref=x_ref, dst_ref=buf_c.at[slot], send_sem=ssem_c.at[dst_c],
            recv_sem=rsem_c.at[slot], device_id=(me_r, dst_c), device_id_type=mesh_t)
    sends = []
    for k in range(1, nc):
        cp = col_copy(lax.rem(me_c + k, nc), me_c)
        cp.start()
        sends.append(cp)
    acc = x_ref[...]
    for k in range(1, nc):
        src = lax.rem(me_c + nc - k, nc)
        col_copy(src, src).wait_recv()
        acc = jnp.maximum(acc, buf_c[src])
    for cp in sends:
        cp.wait_send()
    part[...] = acc

    def row_copy(dst_r, slot):
        return pltpu.make_async_remote_copy(
            src_ref=part, dst_ref=buf_r.at[slot], send_sem=ssem_r.at[dst_r],
            recv_sem=rsem_r.at[slot], device_id=(dst_r, me_c), device_id_type=mesh_t)
    sends = []
    for k in range(1, nr):
        cp = row_copy(lax.rem(me_r + k, nr), me_r)
        cp.start()
        sends.append(cp)
    for k in range(1, nr):
        src = lax.rem(me_r + nr - k, nr)
        row_copy(src, src).wait_recv()
        acc = jnp.maximum(acc, buf_r[src])
    for cp in sends:
        cp.wait_send()
    o_ref[...] = acc


def global_max(tile, nr, nc):
    return pl.pallas_call(
        functools.partial(_allmax_kernel, nr, nc),
        out_shape=jax.ShapeDtypeStruct(tile.shape, tile.dtype),
        in_specs=[pl.BlockSpec(memory_space=pltpu.VMEM)],
        out_specs=pl.BlockSpec(memory_space=pltpu.VMEM),
        scratch_shapes=[
            pltpu.VMEM((nc,) + tile.shape, tile.dtype),
            pltpu.VMEM((nr,) + tile.shape, tile.dtype),
            pltpu.VMEM(tile.shape, tile.dtype),
            pltpu.SemaphoreType.DMA((nc,)),
            pltpu.SemaphoreType.DMA((nc,)),
            pltpu.SemaphoreType.DMA((nr,)),
            pltpu.SemaphoreType.DMA((nr,)),
        ],
        compiler_params=pltpu.CompilerParams(collective_id=0, has_side_effects=True),
    )(tile)


def body(field_real, field_imag):
    padded = 2 * N
    quarter = padded // 4
    col_total = lax.axis_size("col")
    device = lax.axis_index("row") * col_total + lax.axis_index("col")
    strip_real, strip_imag = (
        lax.all_to_all(field_real, "col", split_axis=0, concat_axis=1, tiled=True),
        lax.all_to_all(field_imag, "col", split_axis=0, concat_axis=1, tiled=True),
    )
    wide_real, wide_imag = transform_last(strip_real, strip_imag, -1.0, quarter, 0, padded, padded)
    ratio_sq, band_limit = optics(padded)
    pick_real, pick_imag = (wide_real, wide_imag)
    freq_start = 0
    column_real, column_imag = (
        lax.all_to_all(pick_real, ("row", "col"), split_axis=1, concat_axis=0, tiled=True),
        lax.all_to_all(pick_imag, ("row", "col"), split_axis=1, concat_axis=0, tiled=True),
    )
    col_width = column_real.shape[1]
    turned_real = column_real.T
    turned_imag = column_imag.T
    spec_real, spec_imag = transform_last(
        turned_real, turned_imag, -1.0, quarter, freq_start, padded, padded
    )
    freq_ids = index_range(freq_start, padded)
    freq_signed = signed_index(freq_ids, padded).astype(jnp.float32)
    col_ids = device * col_width + jnp.arange(col_width, dtype=jnp.int32)
    col_signed = signed_index(col_ids, padded).astype(jnp.float32)
    gain_real, gain_imag = transfer(col_signed, freq_signed, ratio_sq, band_limit)
    mixed_real = spec_real * gain_real - spec_imag * gain_imag
    mixed_imag = spec_real * gain_imag + spec_imag * gain_real
    inv_real, inv_imag = transform_last(mixed_real, mixed_imag, 1.0, freq_start, quarter, N, padded)
    back_real = inv_real.T
    back_imag = inv_imag.T
    line_real, line_imag = (
        lax.all_to_all(back_real, ("row", "col"), split_axis=0, concat_axis=1, tiled=True),
        lax.all_to_all(back_imag, ("row", "col"), split_axis=0, concat_axis=1, tiled=True),
    )
    line_rows = line_real.shape[0]
    full_real, full_imag = (line_real, line_imag)
    near_real, near_imag = transform_last(full_real, full_imag, 1.0, 0, quarter, N, padded)
    amplitude = jnp.sqrt(near_real * near_real + near_imag * near_imag)
    row_total = lax.axis_size("row")
    peak_tile = jnp.full((8, 128), jnp.max(amplitude), jnp.float32)
    peak = global_max(peak_tile, row_total, col_total)[0, 0]
    row_ids = device * line_rows + jnp.arange(line_rows, dtype=jnp.int32)
    col_all = jnp.arange(N, dtype=jnp.int32)
    even_cell = (row_ids[:, None] + col_all[None, :]) % 2 == 0
    slm_real, slm_imag = encode(near_real, near_imag, amplitude, peak, even_cell)
    tile_real, tile_imag = (
        lax.all_to_all(slm_real, "col", split_axis=1, concat_axis=0, tiled=True),
        lax.all_to_all(slm_imag, "col", split_axis=1, concat_axis=0, tiled=True),
    )
    return (tile_real, tile_imag)


def solution(mesh):
    in_specs = (P("row", "col"), P("row", "col"))
    out_specs = (P("row", "col"), P("row", "col"))
    return jax.shard_map(body, mesh=mesh, in_specs=in_specs, out_specs=out_specs, check_vma=False)
```

```python
from functools import partial
import math

import jax
import jax.numpy as jnp
from jax import lax
from jax.sharding import PartitionSpec as P
from jax.experimental import pallas as pl
from jax.experimental.pallas import tpu as pltpu
import functools

N = 4096


wavelength = 5.2e-07
distance = 0.2


def optics(padded_side):
    pitch = 2e-06 * math.sqrt(8192.0 / padded_side)
    extent = padded_side * pitch
    ratio_sq = (wavelength / extent) ** 2
    band_limit = extent / (wavelength * math.sqrt((2.0 * distance / extent) ** 2 + 1.0))
    return (ratio_sq, band_limit)


def factor_pair(length):
    bit_count = length.bit_length() - 1
    inner_size = 2 ** ((bit_count + 1) // 2)
    return (length // inner_size, inner_size)


def signed_index(index_ids, modulus):
    return jnp.where(index_ids >= modulus // 2, index_ids - modulus, index_ids)


def transfer(row_signed, col_signed, ratio_sq, band_limit):
    square = row_signed[:, None] * row_signed[:, None] + col_signed[None, :] * col_signed[None, :]
    scaled = ratio_sq * square
    phase_angle = -2.0 * math.pi * distance / wavelength * scaled / (1.0 + jnp.sqrt(1.0 - scaled))
    gauss_gain = jnp.exp(square * (-2.0 / (band_limit * band_limit)))
    inside = (jnp.abs(row_signed)[:, None] < band_limit) & (
        jnp.abs(col_signed)[None, :] < band_limit
    )
    total_gain = jnp.where(inside, gauss_gain, 0.0)
    return (total_gain * jnp.cos(phase_angle), total_gain * jnp.sin(phase_angle))


def encode(near_real, near_imag, amplitude, peak, even_cell):
    amp_level = 0.8 * amplitude / peak
    amp_floor = jnp.maximum(amplitude, 0.05 * peak)
    unit_real = near_real / amp_floor
    unit_imag = near_imag / amp_floor
    lift_part = jnp.sqrt(1.0 - amp_level * amp_level)
    cell_sign = jnp.where(even_cell, 1.0, -1.0)
    out_real = unit_real * amp_level + cell_sign * unit_imag * lift_part
    out_imag = unit_imag * amp_level - cell_sign * unit_real * lift_part
    return (out_real, out_imag)


def index_range(range_start, id_count):
    return jnp.arange(id_count, dtype=jnp.int32) + range_start


def phase_table(first_ids, second_ids, modulus, exponent_sign):
    product = first_ids[:, None] * second_ids[None, :] % modulus
    phase_arg = exponent_sign * 2.0 * math.pi / modulus * product.astype(jnp.float32)
    return (jnp.cos(phase_arg), jnp.sin(phase_arg))


def complex_einsum(form, left_real, left_imag, right_real, right_imag):
    real_dot = partial(jnp.einsum, form, precision=lax.Precision.HIGHEST)
    out_real = real_dot(left_real, right_real) - real_dot(left_imag, right_imag)
    out_imag = real_dot(left_real, right_imag) + real_dot(left_imag, right_real)
    return (out_real, out_imag)


def transform_last(values_real, values_imag, exponent_sign, in_start, out_start, out_count, length):
    outer_size, inner_size = factor_pair(length)
    row_count = values_real.shape[0]
    blocks_in = values_real.shape[1] // inner_size
    first_block = in_start // inner_size
    cube_real = values_real.reshape(row_count, blocks_in, inner_size)
    cube_imag = values_imag.reshape(row_count, blocks_in, inner_size)
    step_real, step_imag = phase_table(
        index_range(first_block, blocks_in), index_range(0, outer_size), outer_size, exponent_sign
    )
    mid_real, mid_imag = complex_einsum("rnq,nk->rkq", cube_real, cube_imag, step_real, step_imag)
    twist_real, twist_imag = phase_table(
        index_range(0, outer_size), index_range(0, inner_size), length, exponent_sign
    )
    mid_real, mid_imag = (
        mid_real * twist_real - mid_imag * twist_imag,
        mid_real * twist_imag + mid_imag * twist_real,
    )
    blocks_out = out_count // outer_size
    second_block = out_start // outer_size
    last_real, last_imag = phase_table(
        index_range(0, inner_size), index_range(second_block, blocks_out), inner_size, exponent_sign
    )
    done_real, done_imag = complex_einsum("rkq,qj->rjk", mid_real, mid_imag, last_real, last_imag)
    return (
        done_real.reshape(row_count, blocks_out * outer_size),
        done_imag.reshape(row_count, blocks_out * outer_size),
    )


def _allmax_kernel(nr, nc, x_ref, o_ref, buf_c, buf_r, part, ssem_c, rsem_c, ssem_r, rsem_r):
    me_r = lax.axis_index("row")
    me_c = lax.axis_index("col")
    mesh_t = pl.DeviceIdType.MESH
    barrier = pltpu.get_barrier_semaphore()
    for k in range(1, nc):
        pl.semaphore_signal(barrier, inc=1, device_id=(me_r, lax.rem(me_c + k, nc)), device_id_type=mesh_t)
    for k in range(1, nr):
        pl.semaphore_signal(barrier, inc=1, device_id=(lax.rem(me_r + k, nr), me_c), device_id_type=mesh_t)
    pl.semaphore_wait(barrier, (nc - 1) + (nr - 1))

    def col_copy(dst_c, slot):
        return pltpu.make_async_remote_copy(
            src_ref=x_ref, dst_ref=buf_c.at[slot], send_sem=ssem_c.at[dst_c],
            recv_sem=rsem_c.at[slot], device_id=(me_r, dst_c), device_id_type=mesh_t)
    sends = []
    for k in range(1, nc):
        cp = col_copy(lax.rem(me_c + k, nc), me_c)
        cp.start()
        sends.append(cp)
    acc = x_ref[...]
    for k in range(1, nc):
        src = lax.rem(me_c + nc - k, nc)
        col_copy(src, src).wait_recv()
        acc = jnp.maximum(acc, buf_c[src])
    for cp in sends:
        cp.wait_send()
    part[...] = acc

    def row_copy(dst_r, slot):
        return pltpu.make_async_remote_copy(
            src_ref=part, dst_ref=buf_r.at[slot], send_sem=ssem_r.at[dst_r],
            recv_sem=rsem_r.at[slot], device_id=(dst_r, me_c), device_id_type=mesh_t)
    sends = []
    for k in range(1, nr):
        cp = row_copy(lax.rem(me_r + k, nr), me_r)
        cp.start()
        sends.append(cp)
    for k in range(1, nr):
        src = lax.rem(me_r + nr - k, nr)
        row_copy(src, src).wait_recv()
        acc = jnp.maximum(acc, buf_r[src])
    for cp in sends:
        cp.wait_send()
    o_ref[...] = acc


def global_max(tile, nr, nc):
    return pl.pallas_call(
        functools.partial(_allmax_kernel, nr, nc),
        out_shape=jax.ShapeDtypeStruct(tile.shape, tile.dtype),
        in_specs=[pl.BlockSpec(memory_space=pltpu.VMEM)],
        out_specs=pl.BlockSpec(memory_space=pltpu.VMEM),
        scratch_shapes=[
            pltpu.VMEM((nc,) + tile.shape, tile.dtype),
            pltpu.VMEM((nr,) + tile.shape, tile.dtype),
            pltpu.VMEM(tile.shape, tile.dtype),
            pltpu.SemaphoreType.DMA((nc,)),
            pltpu.SemaphoreType.DMA((nc,)),
            pltpu.SemaphoreType.DMA((nr,)),
            pltpu.SemaphoreType.DMA((nr,)),
        ],
        compiler_params=pltpu.CompilerParams(collective_id=0, has_side_effects=True),
    )(tile)


def body(field_real, field_imag):
    padded = 2 * N
    quarter = padded // 4
    col_total = lax.axis_size("col")
    device = lax.axis_index("row") * col_total + lax.axis_index("col")
    strip = lax.all_to_all(
        jnp.stack([field_real, field_imag]), "col", split_axis=1, concat_axis=2, tiled=True
    )
    strip_real, strip_imag = strip[0], strip[1]
    wide_real, wide_imag = transform_last(strip_real, strip_imag, -1.0, quarter, 0, padded, padded)
    ratio_sq, band_limit = optics(padded)
    pick_real, pick_imag = (wide_real, wide_imag)
    freq_start = 0
    column = lax.all_to_all(
        jnp.stack([pick_real, pick_imag]), ("row", "col"), split_axis=2, concat_axis=1, tiled=True
    )
    column_real, column_imag = column[0], column[1]
    col_width = column_real.shape[1]
    turned_real = column_real.T
    turned_imag = column_imag.T
    spec_real, spec_imag = transform_last(
        turned_real, turned_imag, -1.0, quarter, freq_start, padded, padded
    )
    freq_ids = index_range(freq_start, padded)
    freq_signed = signed_index(freq_ids, padded).astype(jnp.float32)
    col_ids = device * col_width + jnp.arange(col_width, dtype=jnp.int32)
    col_signed = signed_index(col_ids, padded).astype(jnp.float32)
    gain_real, gain_imag = transfer(col_signed, freq_signed, ratio_sq, band_limit)
    mixed_real = spec_real * gain_real - spec_imag * gain_imag
    mixed_imag = spec_real * gain_imag + spec_imag * gain_real
    inv_real, inv_imag = transform_last(mixed_real, mixed_imag, 1.0, freq_start, quarter, N, padded)
    back_real = inv_real.T
    back_imag = inv_imag.T
    line = lax.all_to_all(
        jnp.stack([back_real, back_imag]), ("row", "col"), split_axis=1, concat_axis=2, tiled=True
    )
    line_real, line_imag = line[0], line[1]
    line_rows = line_real.shape[0]
    full_real, full_imag = (line_real, line_imag)
    near_real, near_imag = transform_last(full_real, full_imag, 1.0, 0, quarter, N, padded)
    amplitude = jnp.sqrt(near_real * near_real + near_imag * near_imag)
    row_total = lax.axis_size("row")
    peak_tile = jnp.full((8, 128), jnp.max(amplitude), jnp.float32)
    peak = global_max(peak_tile, row_total, col_total)[0, 0]
    row_ids = device * line_rows + jnp.arange(line_rows, dtype=jnp.int32)
    col_all = jnp.arange(N, dtype=jnp.int32)
    even_cell = (row_ids[:, None] + col_all[None, :]) % 2 == 0
    slm_real, slm_imag = encode(near_real, near_imag, amplitude, peak, even_cell)
    tile = lax.all_to_all(
        jnp.stack([slm_real, slm_imag]), "col", split_axis=2, concat_axis=1, tiled=True
    )
    tile_real, tile_imag = tile[0], tile[1]
    return (tile_real, tile_imag)


def solution(mesh):
    in_specs = (P("row", "col"), P("row", "col"))
    out_specs = (P("row", "col"), P("row", "col"))
    return jax.shard_map(body, mesh=mesh, in_specs=in_specs, out_specs=out_specs, check_vma=False)
```

```python
from functools import partial
import math

import jax
import jax.numpy as jnp
from jax import lax
from jax.sharding import PartitionSpec as P
from jax.experimental import pallas as pl
from jax.experimental.pallas import tpu as pltpu
import functools

N = 4096


wavelength = 5.2e-07
distance = 0.2


def optics(padded_side):
    pitch = 2e-06 * math.sqrt(8192.0 / padded_side)
    extent = padded_side * pitch
    ratio_sq = (wavelength / extent) ** 2
    band_limit = extent / (wavelength * math.sqrt((2.0 * distance / extent) ** 2 + 1.0))
    return (ratio_sq, band_limit)


def factor_pair(length):
    bit_count = length.bit_length() - 1
    inner_size = 2 ** ((bit_count + 1) // 2)
    return (length // inner_size, inner_size)


def signed_index(index_ids, modulus):
    return jnp.where(index_ids >= modulus // 2, index_ids - modulus, index_ids)


def transfer(row_signed, col_signed, ratio_sq, band_limit):
    square = row_signed[:, None] * row_signed[:, None] + col_signed[None, :] * col_signed[None, :]
    scaled = ratio_sq * square
    phase_angle = -2.0 * math.pi * distance / wavelength * scaled / (1.0 + jnp.sqrt(1.0 - scaled))
    gauss_gain = jnp.exp(square * (-2.0 / (band_limit * band_limit)))
    inside = (jnp.abs(row_signed)[:, None] < band_limit) & (
        jnp.abs(col_signed)[None, :] < band_limit
    )
    total_gain = jnp.where(inside, gauss_gain, 0.0)
    return (total_gain * jnp.cos(phase_angle), total_gain * jnp.sin(phase_angle))


def encode(near_real, near_imag, amplitude, peak, even_cell):
    amp_level = 0.8 * amplitude / peak
    amp_floor = jnp.maximum(amplitude, 0.05 * peak)
    unit_real = near_real / amp_floor
    unit_imag = near_imag / amp_floor
    lift_part = jnp.sqrt(1.0 - amp_level * amp_level)
    cell_sign = jnp.where(even_cell, 1.0, -1.0)
    out_real = unit_real * amp_level + cell_sign * unit_imag * lift_part
    out_imag = unit_imag * amp_level - cell_sign * unit_real * lift_part
    return (out_real, out_imag)


def index_range(range_start, id_count):
    return jnp.arange(id_count, dtype=jnp.int32) + range_start


def phase_table(first_ids, second_ids, modulus, exponent_sign):
    product = first_ids[:, None] * second_ids[None, :] % modulus
    phase_arg = exponent_sign * 2.0 * math.pi / modulus * product.astype(jnp.float32)
    return (jnp.cos(phase_arg), jnp.sin(phase_arg))


def complex_einsum(form, left_real, left_imag, right_real, right_imag):
    real_dot = partial(jnp.einsum, form, precision=lax.Precision.HIGHEST)
    out_real = real_dot(left_real, right_real) - real_dot(left_imag, right_imag)
    out_imag = real_dot(left_real, right_imag) + real_dot(left_imag, right_real)
    return (out_real, out_imag)


def transform_last(values_real, values_imag, exponent_sign, in_start, out_start, out_count, length):
    outer_size, inner_size = factor_pair(length)
    row_count = values_real.shape[0]
    blocks_in = values_real.shape[1] // inner_size
    first_block = in_start // inner_size
    cube_real = values_real.reshape(row_count, blocks_in, inner_size)
    cube_imag = values_imag.reshape(row_count, blocks_in, inner_size)
    step_real, step_imag = phase_table(
        index_range(first_block, blocks_in), index_range(0, outer_size), outer_size, exponent_sign
    )
    mid_real, mid_imag = complex_einsum("rnq,nk->rkq", cube_real, cube_imag, step_real, step_imag)
    twist_real, twist_imag = phase_table(
        index_range(0, outer_size), index_range(0, inner_size), length, exponent_sign
    )
    mid_real, mid_imag = (
        mid_real * twist_real - mid_imag * twist_imag,
        mid_real * twist_imag + mid_imag * twist_real,
    )
    blocks_out = out_count // outer_size
    second_block = out_start // outer_size
    last_real, last_imag = phase_table(
        index_range(0, inner_size), index_range(second_block, blocks_out), inner_size, exponent_sign
    )
    done_real, done_imag = complex_einsum("rkq,qj->rjk", mid_real, mid_imag, last_real, last_imag)
    return (
        done_real.reshape(row_count, blocks_out * outer_size),
        done_imag.reshape(row_count, blocks_out * outer_size),
    )


def _allmax_kernel(nr, nc, x_ref, o_ref, buf_c, buf_r, part, ssem_c, rsem_c, ssem_r, rsem_r):
    me_r = lax.axis_index("row")
    me_c = lax.axis_index("col")
    mesh_t = pl.DeviceIdType.MESH
    barrier = pltpu.get_barrier_semaphore()
    for k in range(1, nc):
        pl.semaphore_signal(barrier, inc=1, device_id=(me_r, lax.rem(me_c + k, nc)), device_id_type=mesh_t)
    for k in range(1, nr):
        pl.semaphore_signal(barrier, inc=1, device_id=(lax.rem(me_r + k, nr), me_c), device_id_type=mesh_t)
    pl.semaphore_wait(barrier, (nc - 1) + (nr - 1))

    def col_copy(dst_c, slot):
        return pltpu.make_async_remote_copy(
            src_ref=x_ref, dst_ref=buf_c.at[slot], send_sem=ssem_c.at[dst_c],
            recv_sem=rsem_c.at[slot], device_id=(me_r, dst_c), device_id_type=mesh_t)
    sends = []
    for k in range(1, nc):
        cp = col_copy(lax.rem(me_c + k, nc), me_c)
        cp.start()
        sends.append(cp)
    acc = x_ref[...]
    for k in range(1, nc):
        src = lax.rem(me_c + nc - k, nc)
        col_copy(src, src).wait_recv()
        acc = jnp.maximum(acc, buf_c[src])
    for cp in sends:
        cp.wait_send()
    part[...] = acc

    def row_copy(dst_r, slot):
        return pltpu.make_async_remote_copy(
            src_ref=part, dst_ref=buf_r.at[slot], send_sem=ssem_r.at[dst_r],
            recv_sem=rsem_r.at[slot], device_id=(dst_r, me_c), device_id_type=mesh_t)
    sends = []
    for k in range(1, nr):
        cp = row_copy(lax.rem(me_r + k, nr), me_r)
        cp.start()
        sends.append(cp)
    for k in range(1, nr):
        src = lax.rem(me_r + nr - k, nr)
        row_copy(src, src).wait_recv()
        acc = jnp.maximum(acc, buf_r[src])
    for cp in sends:
        cp.wait_send()
    o_ref[...] = acc


def global_max(tile, nr, nc):
    return pl.pallas_call(
        functools.partial(_allmax_kernel, nr, nc),
        out_shape=jax.ShapeDtypeStruct(tile.shape, tile.dtype),
        in_specs=[pl.BlockSpec(memory_space=pltpu.VMEM)],
        out_specs=pl.BlockSpec(memory_space=pltpu.VMEM),
        scratch_shapes=[
            pltpu.VMEM((nc,) + tile.shape, tile.dtype),
            pltpu.VMEM((nr,) + tile.shape, tile.dtype),
            pltpu.VMEM(tile.shape, tile.dtype),
            pltpu.SemaphoreType.DMA((nc,)),
            pltpu.SemaphoreType.DMA((nc,)),
            pltpu.SemaphoreType.DMA((nr,)),
            pltpu.SemaphoreType.DMA((nr,)),
        ],
        compiler_params=pltpu.CompilerParams(collective_id=0, has_side_effects=True),
    )(tile)


def _col_exchange_kernel(nc, piece, place, re_ref, im_ref, re_out, im_out, send_sem, recv_sem, own_sem):
    me_r = lax.axis_index("row")
    me = lax.axis_index("col")
    mesh_t = pl.DeviceIdType.MESH
    barrier = pltpu.get_barrier_semaphore()
    for k in range(1, nc):
        pl.semaphore_signal(barrier, inc=1, device_id=(me_r, lax.rem(me + k, nc)), device_id_type=mesh_t)
    pl.semaphore_wait(barrier, nc - 1)
    srcs = (re_ref, im_ref)
    dsts = (re_out, im_out)

    def remote(peer, slot, part):
        return pltpu.make_async_remote_copy(
            src_ref=piece(srcs[part], peer), dst_ref=place(dsts[part], slot),
            send_sem=send_sem.at[peer, part], recv_sem=recv_sem.at[slot, part],
            device_id=(me_r, peer), device_id_type=mesh_t)

    sends = []
    for k in range(1, nc):
        peer = lax.rem(me + k, nc)
        for part in range(2):
            cp = remote(peer, me, part)
            cp.start()
            sends.append(cp)
    owns = []
    for part in range(2):
        cp = pltpu.make_async_copy(piece(srcs[part], me), place(dsts[part], me), own_sem.at[part])
        cp.start()
        owns.append(cp)
    for cp in owns:
        cp.wait()
    for k in range(1, nc):
        src = lax.rem(me + nc - k, nc)
        for part in range(2):
            remote(src, src, part).wait_recv()
    for cp in sends:
        cp.wait_send()


def col_exchange(re, im, out_rows, out_cols, piece, place, nc, cid):
    out = jax.ShapeDtypeStruct((out_rows, out_cols), re.dtype)
    return pl.pallas_call(
        functools.partial(_col_exchange_kernel, nc, piece, place),
        out_shape=(out, out),
        in_specs=[pl.BlockSpec(memory_space=pl.ANY)] * 2,
        out_specs=(pl.BlockSpec(memory_space=pl.ANY),) * 2,
        scratch_shapes=[
            pltpu.SemaphoreType.DMA((nc, 2)),
            pltpu.SemaphoreType.DMA((nc, 2)),
            pltpu.SemaphoreType.DMA((2,)),
        ],
        compiler_params=pltpu.CompilerParams(collective_id=cid, has_side_effects=True),
    )(re, im)


def rows_to_strip(re, im, nc, cid):
    rows, cols = re.shape
    band = rows // nc
    piece = lambda ref, p: ref.at[pl.ds(p * band, band), :]
    place = lambda ref, s: ref.at[:, pl.ds(s * cols, cols)]
    return col_exchange(re, im, band, cols * nc, piece, place, nc, cid)


def strip_to_rows(re, im, nc, cid):
    rows, cols = re.shape
    width = cols // nc
    piece = lambda ref, p: ref.at[:, pl.ds(p * width, width)]
    place = lambda ref, s: ref.at[pl.ds(s * rows, rows), :]
    return col_exchange(re, im, rows * nc, width, piece, place, nc, cid)


def body(field_real, field_imag):
    padded = 2 * N
    quarter = padded // 4
    col_total = lax.axis_size("col")
    device = lax.axis_index("row") * col_total + lax.axis_index("col")
    strip_real, strip_imag = rows_to_strip(field_real, field_imag, col_total, 1)
    wide_real, wide_imag = transform_last(strip_real, strip_imag, -1.0, quarter, 0, padded, padded)
    ratio_sq, band_limit = optics(padded)
    pick_real, pick_imag = (wide_real, wide_imag)
    freq_start = 0
    column_real, column_imag = (
        lax.all_to_all(pick_real, ("row", "col"), split_axis=1, concat_axis=0, tiled=True),
        lax.all_to_all(pick_imag, ("row", "col"), split_axis=1, concat_axis=0, tiled=True),
    )
    col_width = column_real.shape[1]
    turned_real = column_real.T
    turned_imag = column_imag.T
    spec_real, spec_imag = transform_last(
        turned_real, turned_imag, -1.0, quarter, freq_start, padded, padded
    )
    freq_ids = index_range(freq_start, padded)
    freq_signed = signed_index(freq_ids, padded).astype(jnp.float32)
    col_ids = device * col_width + jnp.arange(col_width, dtype=jnp.int32)
    col_signed = signed_index(col_ids, padded).astype(jnp.float32)
    gain_real, gain_imag = transfer(col_signed, freq_signed, ratio_sq, band_limit)
    mixed_real = spec_real * gain_real - spec_imag * gain_imag
    mixed_imag = spec_real * gain_imag + spec_imag * gain_real
    inv_real, inv_imag = transform_last(mixed_real, mixed_imag, 1.0, freq_start, quarter, N, padded)
    back_real = inv_real.T
    back_imag = inv_imag.T
    line_real, line_imag = (
        lax.all_to_all(back_real, ("row", "col"), split_axis=0, concat_axis=1, tiled=True),
        lax.all_to_all(back_imag, ("row", "col"), split_axis=0, concat_axis=1, tiled=True),
    )
    line_rows = line_real.shape[0]
    full_real, full_imag = (line_real, line_imag)
    near_real, near_imag = transform_last(full_real, full_imag, 1.0, 0, quarter, N, padded)
    amplitude = jnp.sqrt(near_real * near_real + near_imag * near_imag)
    row_total = lax.axis_size("row")
    peak_tile = jnp.full((8, 128), jnp.max(amplitude), jnp.float32)
    peak = global_max(peak_tile, row_total, col_total)[0, 0]
    row_ids = device * line_rows + jnp.arange(line_rows, dtype=jnp.int32)
    col_all = jnp.arange(N, dtype=jnp.int32)
    even_cell = (row_ids[:, None] + col_all[None, :]) % 2 == 0
    slm_real, slm_imag = encode(near_real, near_imag, amplitude, peak, even_cell)
    tile_real, tile_imag = strip_to_rows(slm_real, slm_imag, col_total, 2)
    return (tile_real, tile_imag)


def solution(mesh):
    in_specs = (P("row", "col"), P("row", "col"))
    out_specs = (P("row", "col"), P("row", "col"))
    return jax.shard_map(body, mesh=mesh, in_specs=in_specs, out_specs=out_specs, check_vma=False)
```

```python
from functools import partial
import math

import jax
import jax.numpy as jnp
from jax import lax
from jax.sharding import PartitionSpec as P
from jax.experimental import pallas as pl
from jax.experimental.pallas import tpu as pltpu
import functools

N = 4096


wavelength = 5.2e-07
distance = 0.2


def optics(padded_side):
    pitch = 2e-06 * math.sqrt(8192.0 / padded_side)
    extent = padded_side * pitch
    ratio_sq = (wavelength / extent) ** 2
    band_limit = extent / (wavelength * math.sqrt((2.0 * distance / extent) ** 2 + 1.0))
    return (ratio_sq, band_limit)


def factor_pair(length):
    bit_count = length.bit_length() - 1
    inner_size = 2 ** ((bit_count + 1) // 2)
    return (length // inner_size, inner_size)


def signed_index(index_ids, modulus):
    return jnp.where(index_ids >= modulus // 2, index_ids - modulus, index_ids)


def transfer(row_signed, col_signed, ratio_sq, band_limit):
    square = row_signed[:, None] * row_signed[:, None] + col_signed[None, :] * col_signed[None, :]
    scaled = ratio_sq * square
    phase_angle = -2.0 * math.pi * distance / wavelength * scaled / (1.0 + jnp.sqrt(1.0 - scaled))
    gauss_gain = jnp.exp(square * (-2.0 / (band_limit * band_limit)))
    inside = (jnp.abs(row_signed)[:, None] < band_limit) & (
        jnp.abs(col_signed)[None, :] < band_limit
    )
    total_gain = jnp.where(inside, gauss_gain, 0.0)
    return (total_gain * jnp.cos(phase_angle), total_gain * jnp.sin(phase_angle))


def encode(near_real, near_imag, amplitude, peak, even_cell):
    amp_level = 0.8 * amplitude / peak
    amp_floor = jnp.maximum(amplitude, 0.05 * peak)
    unit_real = near_real / amp_floor
    unit_imag = near_imag / amp_floor
    lift_part = jnp.sqrt(1.0 - amp_level * amp_level)
    cell_sign = jnp.where(even_cell, 1.0, -1.0)
    out_real = unit_real * amp_level + cell_sign * unit_imag * lift_part
    out_imag = unit_imag * amp_level - cell_sign * unit_real * lift_part
    return (out_real, out_imag)


def index_range(range_start, id_count):
    return jnp.arange(id_count, dtype=jnp.int32) + range_start


def phase_table(first_ids, second_ids, modulus, exponent_sign):
    product = first_ids[:, None] * second_ids[None, :] % modulus
    phase_arg = exponent_sign * 2.0 * math.pi / modulus * product.astype(jnp.float32)
    return (jnp.cos(phase_arg), jnp.sin(phase_arg))


def complex_einsum(form, left_real, left_imag, right_real, right_imag):
    real_dot = partial(jnp.einsum, form, precision=lax.Precision.HIGHEST)
    out_real = real_dot(left_real, right_real) - real_dot(left_imag, right_imag)
    out_imag = real_dot(left_real, right_imag) + real_dot(left_imag, right_real)
    return (out_real, out_imag)


def transform_last(values_real, values_imag, exponent_sign, in_start, out_start, out_count, length):
    outer_size, inner_size = factor_pair(length)
    row_count = values_real.shape[0]
    blocks_in = values_real.shape[1] // inner_size
    first_block = in_start // inner_size
    cube_real = values_real.reshape(row_count, blocks_in, inner_size)
    cube_imag = values_imag.reshape(row_count, blocks_in, inner_size)
    step_real, step_imag = phase_table(
        index_range(first_block, blocks_in), index_range(0, outer_size), outer_size, exponent_sign
    )
    mid_real, mid_imag = complex_einsum("rnq,nk->rkq", cube_real, cube_imag, step_real, step_imag)
    twist_real, twist_imag = phase_table(
        index_range(0, outer_size), index_range(0, inner_size), length, exponent_sign
    )
    mid_real, mid_imag = (
        mid_real * twist_real - mid_imag * twist_imag,
        mid_real * twist_imag + mid_imag * twist_real,
    )
    blocks_out = out_count // outer_size
    second_block = out_start // outer_size
    last_real, last_imag = phase_table(
        index_range(0, inner_size), index_range(second_block, blocks_out), inner_size, exponent_sign
    )
    done_real, done_imag = complex_einsum("rkq,qj->rjk", mid_real, mid_imag, last_real, last_imag)
    return (
        done_real.reshape(row_count, blocks_out * outer_size),
        done_imag.reshape(row_count, blocks_out * outer_size),
    )


def _allmax_kernel(nr, nc, x_ref, o_ref, buf_c, buf_r, part, ssem_c, rsem_c, ssem_r, rsem_r):
    me_r = lax.axis_index("row")
    me_c = lax.axis_index("col")
    mesh_t = pl.DeviceIdType.MESH
    barrier = pltpu.get_barrier_semaphore()
    for k in range(1, nc):
        pl.semaphore_signal(barrier, inc=1, device_id=(me_r, lax.rem(me_c + k, nc)), device_id_type=mesh_t)
    for k in range(1, nr):
        pl.semaphore_signal(barrier, inc=1, device_id=(lax.rem(me_r + k, nr), me_c), device_id_type=mesh_t)
    pl.semaphore_wait(barrier, (nc - 1) + (nr - 1))

    def col_copy(dst_c, slot):
        return pltpu.make_async_remote_copy(
            src_ref=x_ref, dst_ref=buf_c.at[slot], send_sem=ssem_c.at[dst_c],
            recv_sem=rsem_c.at[slot], device_id=(me_r, dst_c), device_id_type=mesh_t)
    sends = []
    for k in range(1, nc):
        cp = col_copy(lax.rem(me_c + k, nc), me_c)
        cp.start()
        sends.append(cp)
    acc = x_ref[...]
    for k in range(1, nc):
        src = lax.rem(me_c + nc - k, nc)
        col_copy(src, src).wait_recv()
        acc = jnp.maximum(acc, buf_c[src])
    for cp in sends:
        cp.wait_send()
    part[...] = acc

    def row_copy(dst_r, slot):
        return pltpu.make_async_remote_copy(
            src_ref=part, dst_ref=buf_r.at[slot], send_sem=ssem_r.at[dst_r],
            recv_sem=rsem_r.at[slot], device_id=(dst_r, me_c), device_id_type=mesh_t)
    sends = []
    for k in range(1, nr):
        cp = row_copy(lax.rem(me_r + k, nr), me_r)
        cp.start()
        sends.append(cp)
    for k in range(1, nr):
        src = lax.rem(me_r + nr - k, nr)
        row_copy(src, src).wait_recv()
        acc = jnp.maximum(acc, buf_r[src])
    for cp in sends:
        cp.wait_send()
    o_ref[...] = acc


def global_max(tile, nr, nc):
    return pl.pallas_call(
        functools.partial(_allmax_kernel, nr, nc),
        out_shape=jax.ShapeDtypeStruct(tile.shape, tile.dtype),
        in_specs=[pl.BlockSpec(memory_space=pltpu.VMEM)],
        out_specs=pl.BlockSpec(memory_space=pltpu.VMEM),
        scratch_shapes=[
            pltpu.VMEM((nc,) + tile.shape, tile.dtype),
            pltpu.VMEM((nr,) + tile.shape, tile.dtype),
            pltpu.VMEM(tile.shape, tile.dtype),
            pltpu.SemaphoreType.DMA((nc,)),
            pltpu.SemaphoreType.DMA((nc,)),
            pltpu.SemaphoreType.DMA((nr,)),
            pltpu.SemaphoreType.DMA((nr,)),
        ],
        compiler_params=pltpu.CompilerParams(collective_id=0, has_side_effects=True),
    )(tile)


def _col_exchange_kernel(nc, piece, place, re_ref, im_ref, re_out, im_out, send_sem, recv_sem, own_sem):
    me_r = lax.axis_index("row")
    me = lax.axis_index("col")
    mesh_t = pl.DeviceIdType.MESH
    barrier = pltpu.get_barrier_semaphore()
    for k in range(1, nc):
        pl.semaphore_signal(barrier, inc=1, device_id=(me_r, lax.rem(me + k, nc)), device_id_type=mesh_t)
    pl.semaphore_wait(barrier, nc - 1)
    srcs = (re_ref, im_ref)
    dsts = (re_out, im_out)

    def remote(peer, slot, part):
        return pltpu.make_async_remote_copy(
            src_ref=piece(srcs[part], peer), dst_ref=place(dsts[part], slot),
            send_sem=send_sem.at[peer, part], recv_sem=recv_sem.at[slot, part],
            device_id=(me_r, peer), device_id_type=mesh_t)

    sends = []
    for k in range(1, nc):
        peer = lax.rem(me + k, nc)
        for part in range(2):
            cp = remote(peer, me, part)
            cp.start()
            sends.append(cp)
    owns = []
    for part in range(2):
        cp = pltpu.make_async_copy(piece(srcs[part], me), place(dsts[part], me), own_sem.at[part])
        cp.start()
        owns.append(cp)
    for cp in owns:
        cp.wait()
    for k in range(1, nc):
        src = lax.rem(me + nc - k, nc)
        for part in range(2):
            remote(src, src, part).wait_recv()
    for cp in sends:
        cp.wait_send()


def col_exchange(re, im, out_rows, out_cols, piece, place, nc, cid):
    out = jax.ShapeDtypeStruct((out_rows, out_cols), re.dtype)
    return pl.pallas_call(
        functools.partial(_col_exchange_kernel, nc, piece, place),
        out_shape=(out, out),
        in_specs=[pl.BlockSpec(memory_space=pl.ANY)] * 2,
        out_specs=(pl.BlockSpec(memory_space=pl.ANY),) * 2,
        scratch_shapes=[
            pltpu.SemaphoreType.DMA((nc, 2)),
            pltpu.SemaphoreType.DMA((nc, 2)),
            pltpu.SemaphoreType.DMA((2,)),
        ],
        compiler_params=pltpu.CompilerParams(collective_id=cid, has_side_effects=True),
    )(re, im)


def rows_to_strip(re, im, nc, cid):
    rows, cols = re.shape
    band = rows // nc
    piece = lambda ref, p: ref.at[pl.ds(p * band, band), :]
    place = lambda ref, s: ref.at[:, pl.ds(s * cols, cols)]
    return col_exchange(re, im, band, cols * nc, piece, place, nc, cid)


def strip_to_rows(re, im, nc, cid):
    rows, cols = re.shape
    width = cols // nc
    piece = lambda ref, p: ref.at[:, pl.ds(p * width, width)]
    place = lambda ref, s: ref.at[pl.ds(s * rows, rows), :]
    return col_exchange(re, im, rows * nc, width, piece, place, nc, cid)


def transform_blocks(values_real, values_imag, exponent_sign, length, outer_size, in_blocks, out_blocks):
    inner_size = length // outer_size
    row_count = values_real.shape[0]
    cube_real = values_real.reshape(row_count, len(in_blocks), inner_size)
    cube_imag = values_imag.reshape(row_count, len(in_blocks), inner_size)
    step_real, step_imag = phase_table(
        jnp.asarray(in_blocks, jnp.int32), index_range(0, outer_size), outer_size, exponent_sign
    )
    mid_real, mid_imag = complex_einsum("rnq,nk->rkq", cube_real, cube_imag, step_real, step_imag)
    twist_real, twist_imag = phase_table(
        index_range(0, outer_size), index_range(0, inner_size), length, exponent_sign
    )
    mid_real, mid_imag = (
        mid_real * twist_real - mid_imag * twist_imag,
        mid_real * twist_imag + mid_imag * twist_real,
    )
    last_real, last_imag = phase_table(
        index_range(0, inner_size), jnp.asarray(out_blocks, jnp.int32), inner_size, exponent_sign
    )
    done_real, done_imag = complex_einsum("rkq,qj->rjk", mid_real, mid_imag, last_real, last_imag)
    return (
        done_real.reshape(row_count, len(out_blocks) * outer_size),
        done_imag.reshape(row_count, len(out_blocks) * outer_size),
    )


def band_blocks(padded, block, band_limit):
    top = math.ceil(band_limit) - 1
    low = list(range(top // block + 1))
    high = list(range((padded - top) // block, padded // block))
    return low + high


def body(field_real, field_imag):
    padded = 2 * N
    quarter = padded // 4
    col_total = lax.axis_size("col")
    device_total = lax.axis_size("row") * col_total
    device = lax.axis_index("row") * col_total + lax.axis_index("col")
    strip_real, strip_imag = rows_to_strip(field_real, field_imag, col_total, 1)
    ratio_sq, band_limit = optics(padded)
    fwd_outer, fwd_inner = factor_pair(padded)
    inv_outer, inv_inner = fwd_inner, fwd_outer
    band = band_blocks(padded, fwd_outer, band_limit)
    field_blocks = list(range(quarter // fwd_inner, (quarter + N) // fwd_inner))
    near_blocks = list(range(quarter // inv_outer, (quarter + N) // inv_outer))
    pick_real, pick_imag = transform_blocks(
        strip_real, strip_imag, -1.0, padded, fwd_outer, field_blocks, band
    )
    column_real, column_imag = (
        lax.all_to_all(pick_real, ("row", "col"), split_axis=1, concat_axis=0, tiled=True),
        lax.all_to_all(pick_imag, ("row", "col"), split_axis=1, concat_axis=0, tiled=True),
    )
    col_width = column_real.shape[1]
    turned_real = column_real.T
    turned_imag = column_imag.T
    spec_real, spec_imag = transform_blocks(
        turned_real, turned_imag, -1.0, padded, fwd_outer, field_blocks, band
    )
    band_arr = jnp.asarray(band, jnp.int32)
    band_pos = jnp.arange(len(band) * fwd_outer, dtype=jnp.int32)
    freq_ids = band_arr[band_pos // fwd_outer] * fwd_outer + band_pos % fwd_outer
    freq_signed = signed_index(freq_ids, padded).astype(jnp.float32)
    col_pos = device * col_width + jnp.arange(col_width, dtype=jnp.int32)
    col_ids = band_arr[col_pos // fwd_outer] * fwd_outer + col_pos % fwd_outer
    col_signed = signed_index(col_ids, padded).astype(jnp.float32)
    gain_real, gain_imag = transfer(col_signed, freq_signed, ratio_sq, band_limit)
    mixed_real = spec_real * gain_real - spec_imag * gain_imag
    mixed_imag = spec_real * gain_imag + spec_imag * gain_real
    inv_real, inv_imag = transform_blocks(
        mixed_real, mixed_imag, 1.0, padded, inv_outer, band, near_blocks
    )
    back_real = inv_real.T
    back_imag = inv_imag.T
    line_real, line_imag = (
        lax.all_to_all(back_real, ("row", "col"), split_axis=0, concat_axis=1, tiled=True),
        lax.all_to_all(back_imag, ("row", "col"), split_axis=0, concat_axis=1, tiled=True),
    )
    line_rows = line_real.shape[0]
    near_real, near_imag = transform_blocks(
        line_real, line_imag, 1.0, padded, inv_outer, band, near_blocks
    )
    amplitude = jnp.sqrt(near_real * near_real + near_imag * near_imag)
    row_total = lax.axis_size("row")
    peak_tile = jnp.full((8, 128), jnp.max(amplitude), jnp.float32)
    peak = global_max(peak_tile, row_total, col_total)[0, 0]
    row_ids = device * line_rows + jnp.arange(line_rows, dtype=jnp.int32)
    col_all = jnp.arange(N, dtype=jnp.int32)
    even_cell = (row_ids[:, None] + col_all[None, :]) % 2 == 0
    slm_real, slm_imag = encode(near_real, near_imag, amplitude, peak, even_cell)
    tile_real, tile_imag = strip_to_rows(slm_real, slm_imag, col_total, 2)
    return (tile_real, tile_imag)


def solution(mesh):
    in_specs = (P("row", "col"), P("row", "col"))
    out_specs = (P("row", "col"), P("row", "col"))
    return jax.shard_map(body, mesh=mesh, in_specs=in_specs, out_specs=out_specs, check_vma=False)
```

```python
from functools import partial
import math

import jax
import jax.numpy as jnp
from jax import lax
from jax.sharding import PartitionSpec as P
from jax.experimental import pallas as pl
from jax.experimental.pallas import tpu as pltpu
import functools

N = 4096


wavelength = 5.2e-07
distance = 0.2


def optics(padded_side):
    pitch = 2e-06 * math.sqrt(8192.0 / padded_side)
    extent = padded_side * pitch
    ratio_sq = (wavelength / extent) ** 2
    band_limit = extent / (wavelength * math.sqrt((2.0 * distance / extent) ** 2 + 1.0))
    return (ratio_sq, band_limit)


def factor_pair(length):
    bit_count = length.bit_length() - 1
    inner_size = 2 ** ((bit_count + 1) // 2)
    return (length // inner_size, inner_size)


def signed_index(index_ids, modulus):
    return jnp.where(index_ids >= modulus // 2, index_ids - modulus, index_ids)


def transfer(row_signed, col_signed, ratio_sq, band_limit):
    square = row_signed[:, None] * row_signed[:, None] + col_signed[None, :] * col_signed[None, :]
    scaled = ratio_sq * square
    phase_angle = -2.0 * math.pi * distance / wavelength * scaled / (1.0 + jnp.sqrt(1.0 - scaled))
    gauss_gain = jnp.exp(square * (-2.0 / (band_limit * band_limit)))
    inside = (jnp.abs(row_signed)[:, None] < band_limit) & (
        jnp.abs(col_signed)[None, :] < band_limit
    )
    total_gain = jnp.where(inside, gauss_gain, 0.0)
    return (total_gain * jnp.cos(phase_angle), total_gain * jnp.sin(phase_angle))


def encode(near_real, near_imag, amplitude, peak, even_cell):
    amp_level = 0.8 * amplitude / peak
    amp_floor = jnp.maximum(amplitude, 0.05 * peak)
    unit_real = near_real / amp_floor
    unit_imag = near_imag / amp_floor
    lift_part = jnp.sqrt(1.0 - amp_level * amp_level)
    cell_sign = jnp.where(even_cell, 1.0, -1.0)
    out_real = unit_real * amp_level + cell_sign * unit_imag * lift_part
    out_imag = unit_imag * amp_level - cell_sign * unit_real * lift_part
    return (out_real, out_imag)


def index_range(range_start, id_count):
    return jnp.arange(id_count, dtype=jnp.int32) + range_start


def phase_table(first_ids, second_ids, modulus, exponent_sign):
    product = first_ids[:, None] * second_ids[None, :] % modulus
    phase_arg = exponent_sign * 2.0 * math.pi / modulus * product.astype(jnp.float32)
    return (jnp.cos(phase_arg), jnp.sin(phase_arg))


def complex_einsum(form, left_real, left_imag, right_real, right_imag):
    real_dot = partial(jnp.einsum, form, precision=lax.Precision.HIGH)
    out_real = real_dot(left_real, right_real) - real_dot(left_imag, right_imag)
    out_imag = real_dot(left_real, right_imag) + real_dot(left_imag, right_real)
    return (out_real, out_imag)


def transform_last(values_real, values_imag, exponent_sign, in_start, out_start, out_count, length):
    outer_size, inner_size = factor_pair(length)
    row_count = values_real.shape[0]
    blocks_in = values_real.shape[1] // inner_size
    first_block = in_start // inner_size
    cube_real = values_real.reshape(row_count, blocks_in, inner_size)
    cube_imag = values_imag.reshape(row_count, blocks_in, inner_size)
    step_real, step_imag = phase_table(
        index_range(first_block, blocks_in), index_range(0, outer_size), outer_size, exponent_sign
    )
    mid_real, mid_imag = complex_einsum("rnq,nk->rkq", cube_real, cube_imag, step_real, step_imag)
    twist_real, twist_imag = phase_table(
        index_range(0, outer_size), index_range(0, inner_size), length, exponent_sign
    )
    mid_real, mid_imag = (
        mid_real * twist_real - mid_imag * twist_imag,
        mid_real * twist_imag + mid_imag * twist_real,
    )
    blocks_out = out_count // outer_size
    second_block = out_start // outer_size
    last_real, last_imag = phase_table(
        index_range(0, inner_size), index_range(second_block, blocks_out), inner_size, exponent_sign
    )
    done_real, done_imag = complex_einsum("rkq,qj->rjk", mid_real, mid_imag, last_real, last_imag)
    return (
        done_real.reshape(row_count, blocks_out * outer_size),
        done_imag.reshape(row_count, blocks_out * outer_size),
    )


def _allmax_kernel(nr, nc, x_ref, o_ref, buf_c, buf_r, part, ssem_c, rsem_c, ssem_r, rsem_r):
    me_r = lax.axis_index("row")
    me_c = lax.axis_index("col")
    mesh_t = pl.DeviceIdType.MESH
    barrier = pltpu.get_barrier_semaphore()
    for k in range(1, nc):
        pl.semaphore_signal(barrier, inc=1, device_id=(me_r, lax.rem(me_c + k, nc)), device_id_type=mesh_t)
    for k in range(1, nr):
        pl.semaphore_signal(barrier, inc=1, device_id=(lax.rem(me_r + k, nr), me_c), device_id_type=mesh_t)
    pl.semaphore_wait(barrier, (nc - 1) + (nr - 1))

    def col_copy(dst_c, slot):
        return pltpu.make_async_remote_copy(
            src_ref=x_ref, dst_ref=buf_c.at[slot], send_sem=ssem_c.at[dst_c],
            recv_sem=rsem_c.at[slot], device_id=(me_r, dst_c), device_id_type=mesh_t)
    sends = []
    for k in range(1, nc):
        cp = col_copy(lax.rem(me_c + k, nc), me_c)
        cp.start()
        sends.append(cp)
    acc = x_ref[...]
    for k in range(1, nc):
        src = lax.rem(me_c + nc - k, nc)
        col_copy(src, src).wait_recv()
        acc = jnp.maximum(acc, buf_c[src])
    for cp in sends:
        cp.wait_send()
    part[...] = acc

    def row_copy(dst_r, slot):
        return pltpu.make_async_remote_copy(
            src_ref=part, dst_ref=buf_r.at[slot], send_sem=ssem_r.at[dst_r],
            recv_sem=rsem_r.at[slot], device_id=(dst_r, me_c), device_id_type=mesh_t)
    sends = []
    for k in range(1, nr):
        cp = row_copy(lax.rem(me_r + k, nr), me_r)
        cp.start()
        sends.append(cp)
    for k in range(1, nr):
        src = lax.rem(me_r + nr - k, nr)
        row_copy(src, src).wait_recv()
        acc = jnp.maximum(acc, buf_r[src])
    for cp in sends:
        cp.wait_send()
    o_ref[...] = acc


def global_max(tile, nr, nc):
    return pl.pallas_call(
        functools.partial(_allmax_kernel, nr, nc),
        out_shape=jax.ShapeDtypeStruct(tile.shape, tile.dtype),
        in_specs=[pl.BlockSpec(memory_space=pltpu.VMEM)],
        out_specs=pl.BlockSpec(memory_space=pltpu.VMEM),
        scratch_shapes=[
            pltpu.VMEM((nc,) + tile.shape, tile.dtype),
            pltpu.VMEM((nr,) + tile.shape, tile.dtype),
            pltpu.VMEM(tile.shape, tile.dtype),
            pltpu.SemaphoreType.DMA((nc,)),
            pltpu.SemaphoreType.DMA((nc,)),
            pltpu.SemaphoreType.DMA((nr,)),
            pltpu.SemaphoreType.DMA((nr,)),
        ],
        compiler_params=pltpu.CompilerParams(collective_id=0, has_side_effects=True),
    )(tile)


def _col_exchange_kernel(nc, piece, place, re_ref, im_ref, re_out, im_out, send_sem, recv_sem, own_sem):
    me_r = lax.axis_index("row")
    me = lax.axis_index("col")
    mesh_t = pl.DeviceIdType.MESH
    barrier = pltpu.get_barrier_semaphore()
    for k in range(1, nc):
        pl.semaphore_signal(barrier, inc=1, device_id=(me_r, lax.rem(me + k, nc)), device_id_type=mesh_t)
    pl.semaphore_wait(barrier, nc - 1)
    srcs = (re_ref, im_ref)
    dsts = (re_out, im_out)

    def remote(peer, slot, part):
        return pltpu.make_async_remote_copy(
            src_ref=piece(srcs[part], peer), dst_ref=place(dsts[part], slot),
            send_sem=send_sem.at[peer, part], recv_sem=recv_sem.at[slot, part],
            device_id=(me_r, peer), device_id_type=mesh_t)

    sends = []
    for k in range(1, nc):
        peer = lax.rem(me + k, nc)
        for part in range(2):
            cp = remote(peer, me, part)
            cp.start()
            sends.append(cp)
    owns = []
    for part in range(2):
        cp = pltpu.make_async_copy(piece(srcs[part], me), place(dsts[part], me), own_sem.at[part])
        cp.start()
        owns.append(cp)
    for cp in owns:
        cp.wait()
    for k in range(1, nc):
        src = lax.rem(me + nc - k, nc)
        for part in range(2):
            remote(src, src, part).wait_recv()
    for cp in sends:
        cp.wait_send()


def col_exchange(re, im, out_rows, out_cols, piece, place, nc, cid):
    out = jax.ShapeDtypeStruct((out_rows, out_cols), re.dtype)
    return pl.pallas_call(
        functools.partial(_col_exchange_kernel, nc, piece, place),
        out_shape=(out, out),
        in_specs=[pl.BlockSpec(memory_space=pl.ANY)] * 2,
        out_specs=(pl.BlockSpec(memory_space=pl.ANY),) * 2,
        scratch_shapes=[
            pltpu.SemaphoreType.DMA((nc, 2)),
            pltpu.SemaphoreType.DMA((nc, 2)),
            pltpu.SemaphoreType.DMA((2,)),
        ],
        compiler_params=pltpu.CompilerParams(collective_id=cid, has_side_effects=True),
    )(re, im)


def rows_to_strip(re, im, nc, cid):
    rows, cols = re.shape
    band = rows // nc
    piece = lambda ref, p: ref.at[pl.ds(p * band, band), :]
    place = lambda ref, s: ref.at[:, pl.ds(s * cols, cols)]
    return col_exchange(re, im, band, cols * nc, piece, place, nc, cid)


def strip_to_rows(re, im, nc, cid):
    rows, cols = re.shape
    width = cols // nc
    piece = lambda ref, p: ref.at[:, pl.ds(p * width, width)]
    place = lambda ref, s: ref.at[pl.ds(s * rows, rows), :]
    return col_exchange(re, im, rows * nc, width, piece, place, nc, cid)


def transform_blocks(values_real, values_imag, exponent_sign, length, outer_size, in_blocks, out_blocks):
    inner_size = length // outer_size
    row_count = values_real.shape[0]
    cube_real = values_real.reshape(row_count, len(in_blocks), inner_size)
    cube_imag = values_imag.reshape(row_count, len(in_blocks), inner_size)
    step_real, step_imag = phase_table(
        jnp.asarray(in_blocks, jnp.int32), index_range(0, outer_size), outer_size, exponent_sign
    )
    mid_real, mid_imag = complex_einsum("rnq,nk->rkq", cube_real, cube_imag, step_real, step_imag)
    twist_real, twist_imag = phase_table(
        index_range(0, outer_size), index_range(0, inner_size), length, exponent_sign
    )
    mid_real, mid_imag = (
        mid_real * twist_real - mid_imag * twist_imag,
        mid_real * twist_imag + mid_imag * twist_real,
    )
    last_real, last_imag = phase_table(
        index_range(0, inner_size), jnp.asarray(out_blocks, jnp.int32), inner_size, exponent_sign
    )
    done_real, done_imag = complex_einsum("rkq,qj->rjk", mid_real, mid_imag, last_real, last_imag)
    return (
        done_real.reshape(row_count, len(out_blocks) * outer_size),
        done_imag.reshape(row_count, len(out_blocks) * outer_size),
    )


def band_blocks(padded, block, band_limit):
    top = math.ceil(band_limit) - 1
    low = list(range(top // block + 1))
    high = list(range((padded - top) // block, padded // block))
    return low + high


def body(field_real, field_imag):
    padded = 2 * N
    quarter = padded // 4
    col_total = lax.axis_size("col")
    device_total = lax.axis_size("row") * col_total
    device = lax.axis_index("row") * col_total + lax.axis_index("col")
    strip_real, strip_imag = rows_to_strip(field_real, field_imag, col_total, 1)
    ratio_sq, band_limit = optics(padded)
    fwd_outer, fwd_inner = factor_pair(padded)
    inv_outer, inv_inner = fwd_inner, fwd_outer
    band = band_blocks(padded, fwd_outer, band_limit)
    field_blocks = list(range(quarter // fwd_inner, (quarter + N) // fwd_inner))
    near_blocks = list(range(quarter // inv_outer, (quarter + N) // inv_outer))
    pick_real, pick_imag = transform_blocks(
        strip_real, strip_imag, -1.0, padded, fwd_outer, field_blocks, band
    )
    column_real, column_imag = (
        lax.all_to_all(pick_real, ("row", "col"), split_axis=1, concat_axis=0, tiled=True),
        lax.all_to_all(pick_imag, ("row", "col"), split_axis=1, concat_axis=0, tiled=True),
    )
    col_width = column_real.shape[1]
    turned_real = column_real.T
    turned_imag = column_imag.T
    spec_real, spec_imag = transform_blocks(
        turned_real, turned_imag, -1.0, padded, fwd_outer, field_blocks, band
    )
    band_arr = jnp.asarray(band, jnp.int32)
    band_pos = jnp.arange(len(band) * fwd_outer, dtype=jnp.int32)
    freq_ids = band_arr[band_pos // fwd_outer] * fwd_outer + band_pos % fwd_outer
    freq_signed = signed_index(freq_ids, padded).astype(jnp.float32)
    col_pos = device * col_width + jnp.arange(col_width, dtype=jnp.int32)
    col_ids = band_arr[col_pos // fwd_outer] * fwd_outer + col_pos % fwd_outer
    col_signed = signed_index(col_ids, padded).astype(jnp.float32)
    gain_real, gain_imag = transfer(col_signed, freq_signed, ratio_sq, band_limit)
    mixed_real = spec_real * gain_real - spec_imag * gain_imag
    mixed_imag = spec_real * gain_imag + spec_imag * gain_real
    inv_real, inv_imag = transform_blocks(
        mixed_real, mixed_imag, 1.0, padded, inv_outer, band, near_blocks
    )
    back_real = inv_real.T
    back_imag = inv_imag.T
    line_real, line_imag = (
        lax.all_to_all(back_real, ("row", "col"), split_axis=0, concat_axis=1, tiled=True),
        lax.all_to_all(back_imag, ("row", "col"), split_axis=0, concat_axis=1, tiled=True),
    )
    line_rows = line_real.shape[0]
    near_real, near_imag = transform_blocks(
        line_real, line_imag, 1.0, padded, inv_outer, band, near_blocks
    )
    amplitude = jnp.sqrt(near_real * near_real + near_imag * near_imag)
    row_total = lax.axis_size("row")
    peak_tile = jnp.full((8, 128), jnp.max(amplitude), jnp.float32)
    peak = global_max(peak_tile, row_total, col_total)[0, 0]
    row_ids = device * line_rows + jnp.arange(line_rows, dtype=jnp.int32)
    col_all = jnp.arange(N, dtype=jnp.int32)
    even_cell = (row_ids[:, None] + col_all[None, :]) % 2 == 0
    slm_real, slm_imag = encode(near_real, near_imag, amplitude, peak, even_cell)
    tile_real, tile_imag = strip_to_rows(slm_real, slm_imag, col_total, 2)
    return (tile_real, tile_imag)


def solution(mesh):
    in_specs = (P("row", "col"), P("row", "col"))
    out_specs = (P("row", "col"), P("row", "col"))
    return jax.shard_map(body, mesh=mesh, in_specs=in_specs, out_specs=out_specs, check_vma=False)
```

```python
from functools import partial
import math

import jax
import jax.numpy as jnp
from jax import lax
from jax.sharding import PartitionSpec as P
from jax.experimental import pallas as pl
from jax.experimental.pallas import tpu as pltpu
import functools

N = 4096


wavelength = 5.2e-07
distance = 0.2


def optics(padded_side):
    pitch = 2e-06 * math.sqrt(8192.0 / padded_side)
    extent = padded_side * pitch
    ratio_sq = (wavelength / extent) ** 2
    band_limit = extent / (wavelength * math.sqrt((2.0 * distance / extent) ** 2 + 1.0))
    return (ratio_sq, band_limit)


def factor_pair(length):
    bit_count = length.bit_length() - 1
    inner_size = 2 ** ((bit_count + 1) // 2)
    return (length // inner_size, inner_size)


def signed_index(index_ids, modulus):
    return jnp.where(index_ids >= modulus // 2, index_ids - modulus, index_ids)


def transfer(row_signed, col_signed, ratio_sq, band_limit):
    square = row_signed[:, None] * row_signed[:, None] + col_signed[None, :] * col_signed[None, :]
    scaled = ratio_sq * square
    phase_angle = -2.0 * math.pi * distance / wavelength * scaled / (1.0 + jnp.sqrt(1.0 - scaled))
    gauss_gain = jnp.exp(square * (-2.0 / (band_limit * band_limit)))
    inside = (jnp.abs(row_signed)[:, None] < band_limit) & (
        jnp.abs(col_signed)[None, :] < band_limit
    )
    total_gain = jnp.where(inside, gauss_gain, 0.0)
    return (total_gain * jnp.cos(phase_angle), total_gain * jnp.sin(phase_angle))


def encode(near_real, near_imag, amplitude, peak, even_cell):
    amp_level = 0.8 * amplitude / peak
    amp_floor = jnp.maximum(amplitude, 0.05 * peak)
    unit_real = near_real / amp_floor
    unit_imag = near_imag / amp_floor
    lift_part = jnp.sqrt(1.0 - amp_level * amp_level)
    cell_sign = jnp.where(even_cell, 1.0, -1.0)
    out_real = unit_real * amp_level + cell_sign * unit_imag * lift_part
    out_imag = unit_imag * amp_level - cell_sign * unit_real * lift_part
    return (out_real, out_imag)


def index_range(range_start, id_count):
    return jnp.arange(id_count, dtype=jnp.int32) + range_start


def phase_table(first_ids, second_ids, modulus, exponent_sign):
    product = first_ids[:, None] * second_ids[None, :] % modulus
    phase_arg = exponent_sign * 2.0 * math.pi / modulus * product.astype(jnp.float32)
    return (jnp.cos(phase_arg), jnp.sin(phase_arg))


def complex_einsum(form, left_real, left_imag, right_real, right_imag):
    real_dot = partial(jnp.einsum, form, precision=lax.Precision.HIGH)
    out_real = real_dot(left_real, right_real) - real_dot(left_imag, right_imag)
    out_imag = real_dot(left_real, right_imag) + real_dot(left_imag, right_real)
    return (out_real, out_imag)


def transform_last(values_real, values_imag, exponent_sign, in_start, out_start, out_count, length):
    outer_size, inner_size = factor_pair(length)
    row_count = values_real.shape[0]
    blocks_in = values_real.shape[1] // inner_size
    first_block = in_start // inner_size
    cube_real = values_real.reshape(row_count, blocks_in, inner_size)
    cube_imag = values_imag.reshape(row_count, blocks_in, inner_size)
    step_real, step_imag = phase_table(
        index_range(first_block, blocks_in), index_range(0, outer_size), outer_size, exponent_sign
    )
    mid_real, mid_imag = complex_einsum("rnq,nk->rkq", cube_real, cube_imag, step_real, step_imag)
    twist_real, twist_imag = phase_table(
        index_range(0, outer_size), index_range(0, inner_size), length, exponent_sign
    )
    mid_real, mid_imag = (
        mid_real * twist_real - mid_imag * twist_imag,
        mid_real * twist_imag + mid_imag * twist_real,
    )
    blocks_out = out_count // outer_size
    second_block = out_start // outer_size
    last_real, last_imag = phase_table(
        index_range(0, inner_size), index_range(second_block, blocks_out), inner_size, exponent_sign
    )
    done_real, done_imag = complex_einsum("rkq,qj->rjk", mid_real, mid_imag, last_real, last_imag)
    return (
        done_real.reshape(row_count, blocks_out * outer_size),
        done_imag.reshape(row_count, blocks_out * outer_size),
    )


def _allmax_kernel(nr, nc, x_ref, o_ref, buf_c, buf_r, part, ssem_c, rsem_c, ssem_r, rsem_r):
    me_r = lax.axis_index("row")
    me_c = lax.axis_index("col")
    mesh_t = pl.DeviceIdType.MESH
    barrier = pltpu.get_barrier_semaphore()
    for k in range(1, nc):
        pl.semaphore_signal(barrier, inc=1, device_id=(me_r, lax.rem(me_c + k, nc)), device_id_type=mesh_t)
    for k in range(1, nr):
        pl.semaphore_signal(barrier, inc=1, device_id=(lax.rem(me_r + k, nr), me_c), device_id_type=mesh_t)
    pl.semaphore_wait(barrier, (nc - 1) + (nr - 1))

    def col_copy(dst_c, slot):
        return pltpu.make_async_remote_copy(
            src_ref=x_ref, dst_ref=buf_c.at[slot], send_sem=ssem_c.at[dst_c],
            recv_sem=rsem_c.at[slot], device_id=(me_r, dst_c), device_id_type=mesh_t)
    sends = []
    for k in range(1, nc):
        cp = col_copy(lax.rem(me_c + k, nc), me_c)
        cp.start()
        sends.append(cp)
    acc = x_ref[...]
    for k in range(1, nc):
        src = lax.rem(me_c + nc - k, nc)
        col_copy(src, src).wait_recv()
        acc = jnp.maximum(acc, buf_c[src])
    for cp in sends:
        cp.wait_send()
    part[...] = acc

    def row_copy(dst_r, slot):
        return pltpu.make_async_remote_copy(
            src_ref=part, dst_ref=buf_r.at[slot], send_sem=ssem_r.at[dst_r],
            recv_sem=rsem_r.at[slot], device_id=(dst_r, me_c), device_id_type=mesh_t)
    sends = []
    for k in range(1, nr):
        cp = row_copy(lax.rem(me_r + k, nr), me_r)
        cp.start()
        sends.append(cp)
    for k in range(1, nr):
        src = lax.rem(me_r + nr - k, nr)
        row_copy(src, src).wait_recv()
        acc = jnp.maximum(acc, buf_r[src])
    for cp in sends:
        cp.wait_send()
    o_ref[...] = acc


def global_max(tile, nr, nc):
    return pl.pallas_call(
        functools.partial(_allmax_kernel, nr, nc),
        out_shape=jax.ShapeDtypeStruct(tile.shape, tile.dtype),
        in_specs=[pl.BlockSpec(memory_space=pltpu.VMEM)],
        out_specs=pl.BlockSpec(memory_space=pltpu.VMEM),
        scratch_shapes=[
            pltpu.VMEM((nc,) + tile.shape, tile.dtype),
            pltpu.VMEM((nr,) + tile.shape, tile.dtype),
            pltpu.VMEM(tile.shape, tile.dtype),
            pltpu.SemaphoreType.DMA((nc,)),
            pltpu.SemaphoreType.DMA((nc,)),
            pltpu.SemaphoreType.DMA((nr,)),
            pltpu.SemaphoreType.DMA((nr,)),
        ],
        compiler_params=pltpu.CompilerParams(collective_id=0, has_side_effects=True),
    )(tile)


def _col_exchange_kernel(nc, piece, place, re_ref, im_ref, re_out, im_out, send_sem, recv_sem, own_sem):
    me_r = lax.axis_index("row")
    me = lax.axis_index("col")
    mesh_t = pl.DeviceIdType.MESH
    barrier = pltpu.get_barrier_semaphore()
    for k in range(1, nc):
        pl.semaphore_signal(barrier, inc=1, device_id=(me_r, lax.rem(me + k, nc)), device_id_type=mesh_t)
    pl.semaphore_wait(barrier, nc - 1)
    srcs = (re_ref, im_ref)
    dsts = (re_out, im_out)

    def remote(peer, slot, part):
        return pltpu.make_async_remote_copy(
            src_ref=piece(srcs[part], peer), dst_ref=place(dsts[part], slot),
            send_sem=send_sem.at[peer, part], recv_sem=recv_sem.at[slot, part],
            device_id=(me_r, peer), device_id_type=mesh_t)

    sends = []
    for k in range(1, nc):
        peer = lax.rem(me + k, nc)
        for part in range(2):
            cp = remote(peer, me, part)
            cp.start()
            sends.append(cp)
    owns = []
    for part in range(2):
        cp = pltpu.make_async_copy(piece(srcs[part], me), place(dsts[part], me), own_sem.at[part])
        cp.start()
        owns.append(cp)
    for cp in owns:
        cp.wait()
    for k in range(1, nc):
        src = lax.rem(me + nc - k, nc)
        for part in range(2):
            remote(src, src, part).wait_recv()
    for cp in sends:
        cp.wait_send()


def col_exchange(re, im, out_rows, out_cols, piece, place, nc, cid):
    out = jax.ShapeDtypeStruct((out_rows, out_cols), re.dtype)
    return pl.pallas_call(
        functools.partial(_col_exchange_kernel, nc, piece, place),
        out_shape=(out, out),
        in_specs=[pl.BlockSpec(memory_space=pl.ANY)] * 2,
        out_specs=(pl.BlockSpec(memory_space=pl.ANY),) * 2,
        scratch_shapes=[
            pltpu.SemaphoreType.DMA((nc, 2)),
            pltpu.SemaphoreType.DMA((nc, 2)),
            pltpu.SemaphoreType.DMA((2,)),
        ],
        compiler_params=pltpu.CompilerParams(collective_id=cid, has_side_effects=True),
    )(re, im)


def rows_to_strip(re, im, nc, cid):
    rows, cols = re.shape
    band = rows // nc
    piece = lambda ref, p: ref.at[pl.ds(p * band, band), :]
    place = lambda ref, s: ref.at[:, pl.ds(s * cols, cols)]
    return col_exchange(re, im, band, cols * nc, piece, place, nc, cid)


def strip_to_rows(re, im, nc, cid):
    rows, cols = re.shape
    width = cols // nc
    piece = lambda ref, p: ref.at[:, pl.ds(p * width, width)]
    place = lambda ref, s: ref.at[pl.ds(s * rows, rows), :]
    return col_exchange(re, im, rows * nc, width, piece, place, nc, cid)


def _finish_kernel(nr, nc, re_ref, im_ref, peak_ref, re_out, im_out, top_out,
                   buf_c, buf_r, part, send_sem, recv_sem, own_sem, ssem_c, rsem_c, ssem_r, rsem_r):
    me_r = lax.axis_index("row")
    me = lax.axis_index("col")
    mesh_t = pl.DeviceIdType.MESH
    barrier = pltpu.get_barrier_semaphore()
    for k in range(1, nc):
        pl.semaphore_signal(barrier, inc=1, device_id=(me_r, lax.rem(me + k, nc)), device_id_type=mesh_t)
    for k in range(1, nr):
        pl.semaphore_signal(barrier, inc=1, device_id=(lax.rem(me_r + k, nr), me), device_id_type=mesh_t)
    pl.semaphore_wait(barrier, (nc - 1) + (nr - 1))

    def col_top(peer, slot):
        return pltpu.make_async_remote_copy(
            src_ref=peak_ref, dst_ref=buf_c.at[slot], send_sem=ssem_c.at[peer],
            recv_sem=rsem_c.at[slot], device_id=(me_r, peer), device_id_type=mesh_t)

    for k in range(1, nc):
        col_top(lax.rem(me + k, nc), me).start()

    rows = re_ref.shape[0]
    width = re_ref.shape[1] // nc
    srcs = (re_ref, im_ref)
    dsts = (re_out, im_out)

    def data(peer, slot, part_id):
        return pltpu.make_async_remote_copy(
            src_ref=srcs[part_id].at[:, pl.ds(peer * width, width)],
            dst_ref=dsts[part_id].at[pl.ds(slot * rows, rows), :],
            send_sem=send_sem.at[peer, part_id], recv_sem=recv_sem.at[slot, part_id],
            device_id=(me_r, peer), device_id_type=mesh_t)

    for k in range(1, nc):
        for part_id in range(2):
            data(lax.rem(me + k, nc), me, part_id).start()
    owns = []
    for part_id in range(2):
        cp = pltpu.make_async_copy(
            srcs[part_id].at[:, pl.ds(me * width, width)],
            dsts[part_id].at[pl.ds(me * rows, rows), :], own_sem.at[part_id])
        cp.start()
        owns.append(cp)

    acc = peak_ref[...]
    for k in range(1, nc):
        src = lax.rem(me + nc - k, nc)
        col_top(src, src).wait_recv()
        acc = jnp.maximum(acc, buf_c[src])
    for k in range(1, nc):
        col_top(lax.rem(me + k, nc), me).wait_send()
    part[...] = acc

    def row_top(peer, slot):
        return pltpu.make_async_remote_copy(
            src_ref=part, dst_ref=buf_r.at[slot], send_sem=ssem_r.at[peer],
            recv_sem=rsem_r.at[slot], device_id=(peer, me), device_id_type=mesh_t)

    for k in range(1, nr):
        row_top(lax.rem(me_r + k, nr), me_r).start()
    for k in range(1, nr):
        src = lax.rem(me_r + nr - k, nr)
        row_top(src, src).wait_recv()
        acc = jnp.maximum(acc, buf_r[src])
    for k in range(1, nr):
        row_top(lax.rem(me_r + k, nr), me_r).wait_send()
    top_out[...] = acc

    for cp in owns:
        cp.wait()
    for k in range(1, nc):
        src = lax.rem(me + nc - k, nc)
        for part_id in range(2):
            data(src, src, part_id).wait_recv()
            data(lax.rem(me + k, nc), me, part_id).wait_send()


def finish_exchange(re, im, peak_tile, nr, nc, cid):
    rows, cols = re.shape
    out = jax.ShapeDtypeStruct((rows * nc, cols // nc), re.dtype)
    top = jax.ShapeDtypeStruct(peak_tile.shape, peak_tile.dtype)
    return pl.pallas_call(
        functools.partial(_finish_kernel, nr, nc),
        out_shape=(out, out, top),
        in_specs=[pl.BlockSpec(memory_space=pl.ANY)] * 2 + [pl.BlockSpec(memory_space=pltpu.VMEM)],
        out_specs=(pl.BlockSpec(memory_space=pl.ANY),) * 2 + (pl.BlockSpec(memory_space=pltpu.VMEM),),
        scratch_shapes=[
            pltpu.VMEM((nc,) + peak_tile.shape, peak_tile.dtype),
            pltpu.VMEM((nr,) + peak_tile.shape, peak_tile.dtype),
            pltpu.VMEM(peak_tile.shape, peak_tile.dtype),
            pltpu.SemaphoreType.DMA((nc, 2)),
            pltpu.SemaphoreType.DMA((nc, 2)),
            pltpu.SemaphoreType.DMA((2,)),
            pltpu.SemaphoreType.DMA((nc,)),
            pltpu.SemaphoreType.DMA((nc,)),
            pltpu.SemaphoreType.DMA((nr,)),
            pltpu.SemaphoreType.DMA((nr,)),
        ],
        compiler_params=pltpu.CompilerParams(collective_id=cid, has_side_effects=True),
    )(re, im, peak_tile)


def transform_blocks(values_real, values_imag, exponent_sign, length, outer_size, in_blocks, out_blocks):
    inner_size = length // outer_size
    row_count = values_real.shape[0]
    cube_real = values_real.reshape(row_count, len(in_blocks), inner_size)
    cube_imag = values_imag.reshape(row_count, len(in_blocks), inner_size)
    step_real, step_imag = phase_table(
        jnp.asarray(in_blocks, jnp.int32), index_range(0, outer_size), outer_size, exponent_sign
    )
    mid_real, mid_imag = complex_einsum("rnq,nk->rkq", cube_real, cube_imag, step_real, step_imag)
    twist_real, twist_imag = phase_table(
        index_range(0, outer_size), index_range(0, inner_size), length, exponent_sign
    )
    mid_real, mid_imag = (
        mid_real * twist_real - mid_imag * twist_imag,
        mid_real * twist_imag + mid_imag * twist_real,
    )
    last_real, last_imag = phase_table(
        index_range(0, inner_size), jnp.asarray(out_blocks, jnp.int32), inner_size, exponent_sign
    )
    done_real, done_imag = complex_einsum("rkq,qj->rjk", mid_real, mid_imag, last_real, last_imag)
    return (
        done_real.reshape(row_count, len(out_blocks) * outer_size),
        done_imag.reshape(row_count, len(out_blocks) * outer_size),
    )


def band_blocks(padded, block, band_limit):
    top = math.ceil(band_limit) - 1
    low = list(range(top // block + 1))
    high = list(range((padded - top) // block, padded // block))
    return low + high


def body(field_real, field_imag):
    padded = 2 * N
    quarter = padded // 4
    col_total = lax.axis_size("col")
    device_total = lax.axis_size("row") * col_total
    device = lax.axis_index("row") * col_total + lax.axis_index("col")
    strip_real, strip_imag = rows_to_strip(field_real, field_imag, col_total, 1)
    ratio_sq, band_limit = optics(padded)
    fwd_outer, fwd_inner = factor_pair(padded)
    inv_outer, inv_inner = fwd_inner, fwd_outer
    band = band_blocks(padded, fwd_outer, band_limit)
    field_blocks = list(range(quarter // fwd_inner, (quarter + N) // fwd_inner))
    near_blocks = list(range(quarter // inv_outer, (quarter + N) // inv_outer))
    pick_real, pick_imag = transform_blocks(
        strip_real, strip_imag, -1.0, padded, fwd_outer, field_blocks, band
    )
    column_real, column_imag = (
        lax.all_to_all(pick_real, ("row", "col"), split_axis=1, concat_axis=0, tiled=True),
        lax.all_to_all(pick_imag, ("row", "col"), split_axis=1, concat_axis=0, tiled=True),
    )
    col_width = column_real.shape[1]
    turned_real = column_real.T
    turned_imag = column_imag.T
    spec_real, spec_imag = transform_blocks(
        turned_real, turned_imag, -1.0, padded, fwd_outer, field_blocks, band
    )
    band_arr = jnp.asarray(band, jnp.int32)
    band_pos = jnp.arange(len(band) * fwd_outer, dtype=jnp.int32)
    freq_ids = band_arr[band_pos // fwd_outer] * fwd_outer + band_pos % fwd_outer
    freq_signed = signed_index(freq_ids, padded).astype(jnp.float32)
    col_pos = device * col_width + jnp.arange(col_width, dtype=jnp.int32)
    col_ids = band_arr[col_pos // fwd_outer] * fwd_outer + col_pos % fwd_outer
    col_signed = signed_index(col_ids, padded).astype(jnp.float32)
    gain_real, gain_imag = transfer(col_signed, freq_signed, ratio_sq, band_limit)
    mixed_real = spec_real * gain_real - spec_imag * gain_imag
    mixed_imag = spec_real * gain_imag + spec_imag * gain_real
    inv_real, inv_imag = transform_blocks(
        mixed_real, mixed_imag, 1.0, padded, inv_outer, band, near_blocks
    )
    back_real = inv_real.T
    back_imag = inv_imag.T
    line_real, line_imag = (
        lax.all_to_all(back_real, ("row", "col"), split_axis=0, concat_axis=1, tiled=True),
        lax.all_to_all(back_imag, ("row", "col"), split_axis=0, concat_axis=1, tiled=True),
    )
    line_rows = line_real.shape[0]
    near_real, near_imag = transform_blocks(
        line_real, line_imag, 1.0, padded, inv_outer, band, near_blocks
    )
    local_amp = jnp.sqrt(near_real * near_real + near_imag * near_imag)
    peak_tile = jnp.full((8, 128), jnp.max(local_amp), jnp.float32)
    tile_near_real, tile_near_imag, top = finish_exchange(
        near_real, near_imag, peak_tile, lax.axis_size("row"), col_total, 3
    )
    peak = top[0, 0]
    amplitude = jnp.sqrt(tile_near_real * tile_near_real + tile_near_imag * tile_near_imag)
    tile_rows, tile_cols = tile_near_real.shape
    row_ids = lax.axis_index("row") * tile_rows + jnp.arange(tile_rows, dtype=jnp.int32)
    col_ids_out = lax.axis_index("col") * tile_cols + jnp.arange(tile_cols, dtype=jnp.int32)
    even_cell = (row_ids[:, None] + col_ids_out[None, :]) % 2 == 0
    tile_real, tile_imag = encode(tile_near_real, tile_near_imag, amplitude, peak, even_cell)
    return (tile_real, tile_imag)


def solution(mesh):
    in_specs = (P("row", "col"), P("row", "col"))
    out_specs = (P("row", "col"), P("row", "col"))
    return jax.shard_map(body, mesh=mesh, in_specs=in_specs, out_specs=out_specs, check_vma=False)
```

```python
from functools import partial
import math

import jax
import jax.numpy as jnp
from jax import lax
from jax.sharding import PartitionSpec as P
from jax.experimental import pallas as pl
from jax.experimental.pallas import tpu as pltpu
import functools

N = 4096


wavelength = 5.2e-07
distance = 0.2


def optics(padded_side):
    pitch = 2e-06 * math.sqrt(8192.0 / padded_side)
    extent = padded_side * pitch
    ratio_sq = (wavelength / extent) ** 2
    band_limit = extent / (wavelength * math.sqrt((2.0 * distance / extent) ** 2 + 1.0))
    return (ratio_sq, band_limit)


def factor_pair(length):
    bit_count = length.bit_length() - 1
    inner_size = 2 ** ((bit_count + 1) // 2)
    return (length // inner_size, inner_size)


def signed_index(index_ids, modulus):
    return jnp.where(index_ids >= modulus // 2, index_ids - modulus, index_ids)


def transfer(row_signed, col_signed, ratio_sq, band_limit):
    square = row_signed[:, None] * row_signed[:, None] + col_signed[None, :] * col_signed[None, :]
    scaled = ratio_sq * square
    phase_angle = -2.0 * math.pi * distance / wavelength * scaled / (1.0 + jnp.sqrt(1.0 - scaled))
    gauss_gain = jnp.exp(square * (-2.0 / (band_limit * band_limit)))
    inside = (jnp.abs(row_signed)[:, None] < band_limit) & (
        jnp.abs(col_signed)[None, :] < band_limit
    )
    total_gain = jnp.where(inside, gauss_gain, 0.0)
    return (total_gain * jnp.cos(phase_angle), total_gain * jnp.sin(phase_angle))


def encode(near_real, near_imag, amplitude, peak, even_cell):
    amp_level = 0.8 * amplitude / peak
    amp_floor = jnp.maximum(amplitude, 0.05 * peak)
    unit_real = near_real / amp_floor
    unit_imag = near_imag / amp_floor
    lift_part = jnp.sqrt(1.0 - amp_level * amp_level)
    cell_sign = jnp.where(even_cell, 1.0, -1.0)
    out_real = unit_real * amp_level + cell_sign * unit_imag * lift_part
    out_imag = unit_imag * amp_level - cell_sign * unit_real * lift_part
    return (out_real, out_imag)


def index_range(range_start, id_count):
    return jnp.arange(id_count, dtype=jnp.int32) + range_start


def phase_table(first_ids, second_ids, modulus, exponent_sign):
    product = first_ids[:, None] * second_ids[None, :] % modulus
    phase_arg = exponent_sign * 2.0 * math.pi / modulus * product.astype(jnp.float32)
    return (jnp.cos(phase_arg), jnp.sin(phase_arg))


def complex_einsum(form, left_real, left_imag, right_real, right_imag):
    real_dot = partial(jnp.einsum, form, precision=lax.Precision.HIGH)
    out_real = real_dot(left_real, right_real) - real_dot(left_imag, right_imag)
    out_imag = real_dot(left_real, right_imag) + real_dot(left_imag, right_real)
    return (out_real, out_imag)


def transform_last(values_real, values_imag, exponent_sign, in_start, out_start, out_count, length):
    outer_size, inner_size = factor_pair(length)
    row_count = values_real.shape[0]
    blocks_in = values_real.shape[1] // inner_size
    first_block = in_start // inner_size
    cube_real = values_real.reshape(row_count, blocks_in, inner_size)
    cube_imag = values_imag.reshape(row_count, blocks_in, inner_size)
    step_real, step_imag = phase_table(
        index_range(first_block, blocks_in), index_range(0, outer_size), outer_size, exponent_sign
    )
    mid_real, mid_imag = complex_einsum("rnq,nk->rkq", cube_real, cube_imag, step_real, step_imag)
    twist_real, twist_imag = phase_table(
        index_range(0, outer_size), index_range(0, inner_size), length, exponent_sign
    )
    mid_real, mid_imag = (
        mid_real * twist_real - mid_imag * twist_imag,
        mid_real * twist_imag + mid_imag * twist_real,
    )
    blocks_out = out_count // outer_size
    second_block = out_start // outer_size
    last_real, last_imag = phase_table(
        index_range(0, inner_size), index_range(second_block, blocks_out), inner_size, exponent_sign
    )
    done_real, done_imag = complex_einsum("rkq,qj->rjk", mid_real, mid_imag, last_real, last_imag)
    return (
        done_real.reshape(row_count, blocks_out * outer_size),
        done_imag.reshape(row_count, blocks_out * outer_size),
    )


def _allmax_kernel(nr, nc, x_ref, o_ref, buf_c, buf_r, part, ssem_c, rsem_c, ssem_r, rsem_r):
    me_r = lax.axis_index("row")
    me_c = lax.axis_index("col")
    mesh_t = pl.DeviceIdType.MESH
    barrier = pltpu.get_barrier_semaphore()
    for k in range(1, nc):
        pl.semaphore_signal(barrier, inc=1, device_id=(me_r, lax.rem(me_c + k, nc)), device_id_type=mesh_t)
    for k in range(1, nr):
        pl.semaphore_signal(barrier, inc=1, device_id=(lax.rem(me_r + k, nr), me_c), device_id_type=mesh_t)
    pl.semaphore_wait(barrier, (nc - 1) + (nr - 1))

    def col_copy(dst_c, slot):
        return pltpu.make_async_remote_copy(
            src_ref=x_ref, dst_ref=buf_c.at[slot], send_sem=ssem_c.at[dst_c],
            recv_sem=rsem_c.at[slot], device_id=(me_r, dst_c), device_id_type=mesh_t)
    sends = []
    for k in range(1, nc):
        cp = col_copy(lax.rem(me_c + k, nc), me_c)
        cp.start()
        sends.append(cp)
    acc = x_ref[...]
    for k in range(1, nc):
        src = lax.rem(me_c + nc - k, nc)
        col_copy(src, src).wait_recv()
        acc = jnp.maximum(acc, buf_c[src])
    for cp in sends:
        cp.wait_send()
    part[...] = acc

    def row_copy(dst_r, slot):
        return pltpu.make_async_remote_copy(
            src_ref=part, dst_ref=buf_r.at[slot], send_sem=ssem_r.at[dst_r],
            recv_sem=rsem_r.at[slot], device_id=(dst_r, me_c), device_id_type=mesh_t)
    sends = []
    for k in range(1, nr):
        cp = row_copy(lax.rem(me_r + k, nr), me_r)
        cp.start()
        sends.append(cp)
    for k in range(1, nr):
        src = lax.rem(me_r + nr - k, nr)
        row_copy(src, src).wait_recv()
        acc = jnp.maximum(acc, buf_r[src])
    for cp in sends:
        cp.wait_send()
    o_ref[...] = acc


def global_max(tile, nr, nc):
    return pl.pallas_call(
        functools.partial(_allmax_kernel, nr, nc),
        out_shape=jax.ShapeDtypeStruct(tile.shape, tile.dtype),
        in_specs=[pl.BlockSpec(memory_space=pltpu.VMEM)],
        out_specs=pl.BlockSpec(memory_space=pltpu.VMEM),
        scratch_shapes=[
            pltpu.VMEM((nc,) + tile.shape, tile.dtype),
            pltpu.VMEM((nr,) + tile.shape, tile.dtype),
            pltpu.VMEM(tile.shape, tile.dtype),
            pltpu.SemaphoreType.DMA((nc,)),
            pltpu.SemaphoreType.DMA((nc,)),
            pltpu.SemaphoreType.DMA((nr,)),
            pltpu.SemaphoreType.DMA((nr,)),
        ],
        compiler_params=pltpu.CompilerParams(collective_id=0, has_side_effects=True),
    )(tile)


def _col_exchange_kernel(nc, piece, place, re_ref, im_ref, re_out, im_out, send_sem, recv_sem, own_sem):
    me_r = lax.axis_index("row")
    me = lax.axis_index("col")
    mesh_t = pl.DeviceIdType.MESH
    barrier = pltpu.get_barrier_semaphore()
    for k in range(1, nc):
        pl.semaphore_signal(barrier, inc=1, device_id=(me_r, lax.rem(me + k, nc)), device_id_type=mesh_t)
    pl.semaphore_wait(barrier, nc - 1)
    srcs = (re_ref, im_ref)
    dsts = (re_out, im_out)

    def remote(peer, slot, part):
        return pltpu.make_async_remote_copy(
            src_ref=piece(srcs[part], peer), dst_ref=place(dsts[part], slot),
            send_sem=send_sem.at[peer, part], recv_sem=recv_sem.at[slot, part],
            device_id=(me_r, peer), device_id_type=mesh_t)

    sends = []
    for k in range(1, nc):
        peer = lax.rem(me + k, nc)
        for part in range(2):
            cp = remote(peer, me, part)
            cp.start()
            sends.append(cp)
    owns = []
    for part in range(2):
        cp = pltpu.make_async_copy(piece(srcs[part], me), place(dsts[part], me), own_sem.at[part])
        cp.start()
        owns.append(cp)
    for cp in owns:
        cp.wait()
    for k in range(1, nc):
        src = lax.rem(me + nc - k, nc)
        for part in range(2):
            remote(src, src, part).wait_recv()
    for cp in sends:
        cp.wait_send()


def col_exchange(re, im, out_rows, out_cols, piece, place, nc, cid):
    out = jax.ShapeDtypeStruct((out_rows, out_cols), re.dtype)
    return pl.pallas_call(
        functools.partial(_col_exchange_kernel, nc, piece, place),
        out_shape=(out, out),
        in_specs=[pl.BlockSpec(memory_space=pl.ANY)] * 2,
        out_specs=(pl.BlockSpec(memory_space=pl.ANY),) * 2,
        scratch_shapes=[
            pltpu.SemaphoreType.DMA((nc, 2)),
            pltpu.SemaphoreType.DMA((nc, 2)),
            pltpu.SemaphoreType.DMA((2,)),
        ],
        compiler_params=pltpu.CompilerParams(collective_id=cid, has_side_effects=True),
    )(re, im)


def rows_to_strip(re, im, nc, cid):
    rows, cols = re.shape
    band = rows // nc
    piece = lambda ref, p: ref.at[pl.ds(p * band, band), :]
    place = lambda ref, s: ref.at[:, pl.ds(s * cols, cols)]
    return col_exchange(re, im, band, cols * nc, piece, place, nc, cid)


def strip_to_rows(re, im, nc, cid):
    rows, cols = re.shape
    width = cols // nc
    piece = lambda ref, p: ref.at[:, pl.ds(p * width, width)]
    place = lambda ref, s: ref.at[pl.ds(s * rows, rows), :]
    return col_exchange(re, im, rows * nc, width, piece, place, nc, cid)


def _finish_kernel(nr, nc, re_ref, im_ref, peak_ref, re_out, im_out, top_out,
                   buf_c, buf_r, part, send_sem, recv_sem, own_sem, ssem_c, rsem_c, ssem_r, rsem_r):
    me_r = lax.axis_index("row")
    me = lax.axis_index("col")
    mesh_t = pl.DeviceIdType.MESH
    barrier = pltpu.get_barrier_semaphore()
    for k in range(1, nc):
        pl.semaphore_signal(barrier, inc=1, device_id=(me_r, lax.rem(me + k, nc)), device_id_type=mesh_t)
    for k in range(1, nr):
        pl.semaphore_signal(barrier, inc=1, device_id=(lax.rem(me_r + k, nr), me), device_id_type=mesh_t)
    pl.semaphore_wait(barrier, (nc - 1) + (nr - 1))

    def col_top(peer, slot):
        return pltpu.make_async_remote_copy(
            src_ref=peak_ref, dst_ref=buf_c.at[slot], send_sem=ssem_c.at[peer],
            recv_sem=rsem_c.at[slot], device_id=(me_r, peer), device_id_type=mesh_t)

    for k in range(1, nc):
        col_top(lax.rem(me + k, nc), me).start()

    rows = re_ref.shape[0]
    width = re_ref.shape[1] // nc
    srcs = (re_ref, im_ref)
    dsts = (re_out, im_out)

    def data(peer, slot, part_id):
        return pltpu.make_async_remote_copy(
            src_ref=srcs[part_id].at[:, pl.ds(peer * width, width)],
            dst_ref=dsts[part_id].at[pl.ds(slot * rows, rows), :],
            send_sem=send_sem.at[peer, part_id], recv_sem=recv_sem.at[slot, part_id],
            device_id=(me_r, peer), device_id_type=mesh_t)

    for k in range(1, nc):
        for part_id in range(2):
            data(lax.rem(me + k, nc), me, part_id).start()
    owns = []
    for part_id in range(2):
        cp = pltpu.make_async_copy(
            srcs[part_id].at[:, pl.ds(me * width, width)],
            dsts[part_id].at[pl.ds(me * rows, rows), :], own_sem.at[part_id])
        cp.start()
        owns.append(cp)

    acc = peak_ref[...]
    for k in range(1, nc):
        src = lax.rem(me + nc - k, nc)
        col_top(src, src).wait_recv()
        acc = jnp.maximum(acc, buf_c[src])
    for k in range(1, nc):
        col_top(lax.rem(me + k, nc), me).wait_send()
    part[...] = acc

    def row_top(peer, slot):
        return pltpu.make_async_remote_copy(
            src_ref=part, dst_ref=buf_r.at[slot], send_sem=ssem_r.at[peer],
            recv_sem=rsem_r.at[slot], device_id=(peer, me), device_id_type=mesh_t)

    for k in range(1, nr):
        row_top(lax.rem(me_r + k, nr), me_r).start()
    for k in range(1, nr):
        src = lax.rem(me_r + nr - k, nr)
        row_top(src, src).wait_recv()
        acc = jnp.maximum(acc, buf_r[src])
    for k in range(1, nr):
        row_top(lax.rem(me_r + k, nr), me_r).wait_send()
    top_out[...] = acc

    for cp in owns:
        cp.wait()
    for k in range(1, nc):
        src = lax.rem(me + nc - k, nc)
        for part_id in range(2):
            data(src, src, part_id).wait_recv()
            data(lax.rem(me + k, nc), me, part_id).wait_send()


def finish_exchange(re, im, peak_tile, nr, nc, cid):
    rows, cols = re.shape
    out = jax.ShapeDtypeStruct((rows * nc, cols // nc), re.dtype)
    top = jax.ShapeDtypeStruct(peak_tile.shape, peak_tile.dtype)
    return pl.pallas_call(
        functools.partial(_finish_kernel, nr, nc),
        out_shape=(out, out, top),
        in_specs=[pl.BlockSpec(memory_space=pl.ANY)] * 2 + [pl.BlockSpec(memory_space=pltpu.VMEM)],
        out_specs=(pl.BlockSpec(memory_space=pl.ANY),) * 2 + (pl.BlockSpec(memory_space=pltpu.VMEM),),
        scratch_shapes=[
            pltpu.VMEM((nc,) + peak_tile.shape, peak_tile.dtype),
            pltpu.VMEM((nr,) + peak_tile.shape, peak_tile.dtype),
            pltpu.VMEM(peak_tile.shape, peak_tile.dtype),
            pltpu.SemaphoreType.DMA((nc, 2)),
            pltpu.SemaphoreType.DMA((nc, 2)),
            pltpu.SemaphoreType.DMA((2,)),
            pltpu.SemaphoreType.DMA((nc,)),
            pltpu.SemaphoreType.DMA((nc,)),
            pltpu.SemaphoreType.DMA((nr,)),
            pltpu.SemaphoreType.DMA((nr,)),
        ],
        compiler_params=pltpu.CompilerParams(collective_id=cid, has_side_effects=True),
    )(re, im, peak_tile)


def transform_blocks(values_real, values_imag, exponent_sign, length, outer_size, in_blocks, out_blocks):
    inner_size = length // outer_size
    row_count = values_real.shape[0]
    cube_real = values_real.reshape(row_count, len(in_blocks), inner_size)
    cube_imag = values_imag.reshape(row_count, len(in_blocks), inner_size)
    step_real, step_imag = phase_table(
        jnp.asarray(in_blocks, jnp.int32), index_range(0, outer_size), outer_size, exponent_sign
    )
    mid_real, mid_imag = complex_einsum("rnq,nk->rkq", cube_real, cube_imag, step_real, step_imag)
    twist_real, twist_imag = phase_table(
        index_range(0, outer_size), index_range(0, inner_size), length, exponent_sign
    )
    mid_real, mid_imag = (
        mid_real * twist_real - mid_imag * twist_imag,
        mid_real * twist_imag + mid_imag * twist_real,
    )
    last_real, last_imag = phase_table(
        index_range(0, inner_size), jnp.asarray(out_blocks, jnp.int32), inner_size, exponent_sign
    )
    done_real, done_imag = complex_einsum("rkq,qj->rjk", mid_real, mid_imag, last_real, last_imag)
    return (
        done_real.reshape(row_count, len(out_blocks) * outer_size),
        done_imag.reshape(row_count, len(out_blocks) * outer_size),
    )


def band_blocks(padded, block, band_limit):
    top = math.ceil(band_limit) - 1
    low = list(range(top // block + 1))
    high = list(range((padded - top) // block, padded // block))
    return low + high


def body(field_real, field_imag):
    padded = 2 * N
    quarter = padded // 4
    col_total = lax.axis_size("col")
    device_total = lax.axis_size("row") * col_total
    device = lax.axis_index("row") * col_total + lax.axis_index("col")
    strip_real, strip_imag = rows_to_strip(field_real, field_imag, col_total, 1)
    ratio_sq, band_limit = optics(padded)
    fwd_outer, fwd_inner = factor_pair(padded)
    inv_outer, inv_inner = fwd_inner, fwd_outer
    band = band_blocks(padded, fwd_outer, band_limit)
    field_blocks = list(range(quarter // fwd_inner, (quarter + N) // fwd_inner))
    near_blocks = list(range(quarter // inv_outer, (quarter + N) // inv_outer))
    pick_real, pick_imag = transform_blocks(
        strip_real, strip_imag, -1.0, padded, fwd_outer, field_blocks, band
    )
    column = lax.all_to_all(
        jnp.stack([pick_real, pick_imag]), ("row", "col"), split_axis=2, concat_axis=1, tiled=True
    )
    column_real, column_imag = column[0], column[1]
    col_width = column_real.shape[1]
    turned_real = column_real.T
    turned_imag = column_imag.T
    spec_real, spec_imag = transform_blocks(
        turned_real, turned_imag, -1.0, padded, fwd_outer, field_blocks, band
    )
    band_arr = jnp.asarray(band, jnp.int32)
    band_pos = jnp.arange(len(band) * fwd_outer, dtype=jnp.int32)
    freq_ids = band_arr[band_pos // fwd_outer] * fwd_outer + band_pos % fwd_outer
    freq_signed = signed_index(freq_ids, padded).astype(jnp.float32)
    col_pos = device * col_width + jnp.arange(col_width, dtype=jnp.int32)
    col_ids = band_arr[col_pos // fwd_outer] * fwd_outer + col_pos % fwd_outer
    col_signed = signed_index(col_ids, padded).astype(jnp.float32)
    gain_real, gain_imag = transfer(col_signed, freq_signed, ratio_sq, band_limit)
    mixed_real = spec_real * gain_real - spec_imag * gain_imag
    mixed_imag = spec_real * gain_imag + spec_imag * gain_real
    inv_real, inv_imag = transform_blocks(
        mixed_real, mixed_imag, 1.0, padded, inv_outer, band, near_blocks
    )
    back_real = inv_real.T
    back_imag = inv_imag.T
    line = lax.all_to_all(
        jnp.stack([back_real, back_imag]), ("row", "col"), split_axis=1, concat_axis=2, tiled=True
    )
    line_real, line_imag = line[0], line[1]
    line_rows = line_real.shape[0]
    near_real, near_imag = transform_blocks(
        line_real, line_imag, 1.0, padded, inv_outer, band, near_blocks
    )
    local_amp = jnp.sqrt(near_real * near_real + near_imag * near_imag)
    peak_tile = jnp.full((8, 128), jnp.max(local_amp), jnp.float32)
    tile_near_real, tile_near_imag, top = finish_exchange(
        near_real, near_imag, peak_tile, lax.axis_size("row"), col_total, 3
    )
    peak = top[0, 0]
    amplitude = jnp.sqrt(tile_near_real * tile_near_real + tile_near_imag * tile_near_imag)
    tile_rows, tile_cols = tile_near_real.shape
    row_ids = lax.axis_index("row") * tile_rows + jnp.arange(tile_rows, dtype=jnp.int32)
    col_ids_out = lax.axis_index("col") * tile_cols + jnp.arange(tile_cols, dtype=jnp.int32)
    even_cell = (row_ids[:, None] + col_ids_out[None, :]) % 2 == 0
    tile_real, tile_imag = encode(tile_near_real, tile_near_imag, amplitude, peak, even_cell)
    return (tile_real, tile_imag)


def solution(mesh):
    in_specs = (P("row", "col"), P("row", "col"))
    out_specs = (P("row", "col"), P("row", "col"))
    return jax.shard_map(body, mesh=mesh, in_specs=in_specs, out_specs=out_specs, check_vma=False)
```

```python
from functools import partial
import math

import jax
import jax.numpy as jnp
from jax import lax
from jax.sharding import PartitionSpec as P
from jax.experimental import pallas as pl
from jax.experimental.pallas import tpu as pltpu
import functools

import numpy as np

N = 4096


wavelength = 5.2e-07
distance = 0.2


def optics(padded_side):
    pitch = 2e-06 * math.sqrt(8192.0 / padded_side)
    extent = padded_side * pitch
    ratio_sq = (wavelength / extent) ** 2
    band_limit = extent / (wavelength * math.sqrt((2.0 * distance / extent) ** 2 + 1.0))
    return (ratio_sq, band_limit)


def factor_pair(length):
    bit_count = length.bit_length() - 1
    inner_size = 2 ** ((bit_count + 1) // 2)
    return (length // inner_size, inner_size)


def signed_index(index_ids, modulus):
    return jnp.where(index_ids >= modulus // 2, index_ids - modulus, index_ids)


def transfer(row_signed, col_signed, ratio_sq, band_limit):
    square = row_signed[:, None] * row_signed[:, None] + col_signed[None, :] * col_signed[None, :]
    scaled = ratio_sq * square
    phase_angle = -2.0 * math.pi * distance / wavelength * scaled / (1.0 + jnp.sqrt(1.0 - scaled))
    gauss_gain = jnp.exp(square * (-2.0 / (band_limit * band_limit)))
    inside = (jnp.abs(row_signed)[:, None] < band_limit) & (
        jnp.abs(col_signed)[None, :] < band_limit
    )
    total_gain = jnp.where(inside, gauss_gain, 0.0)
    return (total_gain * jnp.cos(phase_angle), total_gain * jnp.sin(phase_angle))


def encode(near_real, near_imag, amplitude, peak, even_cell):
    amp_level = 0.8 * amplitude / peak
    amp_floor = jnp.maximum(amplitude, 0.05 * peak)
    unit_real = near_real / amp_floor
    unit_imag = near_imag / amp_floor
    lift_part = jnp.sqrt(1.0 - amp_level * amp_level)
    cell_sign = jnp.where(even_cell, 1.0, -1.0)
    out_real = unit_real * amp_level + cell_sign * unit_imag * lift_part
    out_imag = unit_imag * amp_level - cell_sign * unit_real * lift_part
    return (out_real, out_imag)


def index_range(range_start, id_count):
    return jnp.arange(id_count, dtype=jnp.int32) + range_start


def phase_table(first_ids, second_ids, modulus, exponent_sign):
    product = first_ids[:, None] * second_ids[None, :] % modulus
    phase_arg = exponent_sign * 2.0 * math.pi / modulus * product.astype(jnp.float32)
    return (jnp.cos(phase_arg), jnp.sin(phase_arg))


def complex_einsum(form, left_real, left_imag, right_real, right_imag):
    real_dot = partial(jnp.einsum, form, precision=lax.Precision.HIGH)
    out_real = real_dot(left_real, right_real) - real_dot(left_imag, right_imag)
    out_imag = real_dot(left_real, right_imag) + real_dot(left_imag, right_real)
    return (out_real, out_imag)


def transform_last(values_real, values_imag, exponent_sign, in_start, out_start, out_count, length):
    outer_size, inner_size = factor_pair(length)
    row_count = values_real.shape[0]
    blocks_in = values_real.shape[1] // inner_size
    first_block = in_start // inner_size
    cube_real = values_real.reshape(row_count, blocks_in, inner_size)
    cube_imag = values_imag.reshape(row_count, blocks_in, inner_size)
    step_real, step_imag = phase_table(
        index_range(first_block, blocks_in), index_range(0, outer_size), outer_size, exponent_sign
    )
    mid_real, mid_imag = complex_einsum("rnq,nk->rkq", cube_real, cube_imag, step_real, step_imag)
    twist_real, twist_imag = phase_table(
        index_range(0, outer_size), index_range(0, inner_size), length, exponent_sign
    )
    mid_real, mid_imag = (
        mid_real * twist_real - mid_imag * twist_imag,
        mid_real * twist_imag + mid_imag * twist_real,
    )
    blocks_out = out_count // outer_size
    second_block = out_start // outer_size
    last_real, last_imag = phase_table(
        index_range(0, inner_size), index_range(second_block, blocks_out), inner_size, exponent_sign
    )
    done_real, done_imag = complex_einsum("rkq,qj->rjk", mid_real, mid_imag, last_real, last_imag)
    return (
        done_real.reshape(row_count, blocks_out * outer_size),
        done_imag.reshape(row_count, blocks_out * outer_size),
    )


def _allmax_kernel(nr, nc, x_ref, o_ref, buf_c, buf_r, part, ssem_c, rsem_c, ssem_r, rsem_r):
    me_r = lax.axis_index("row")
    me_c = lax.axis_index("col")
    mesh_t = pl.DeviceIdType.MESH
    barrier = pltpu.get_barrier_semaphore()
    for k in range(1, nc):
        pl.semaphore_signal(barrier, inc=1, device_id=(me_r, lax.rem(me_c + k, nc)), device_id_type=mesh_t)
    for k in range(1, nr):
        pl.semaphore_signal(barrier, inc=1, device_id=(lax.rem(me_r + k, nr), me_c), device_id_type=mesh_t)
    pl.semaphore_wait(barrier, (nc - 1) + (nr - 1))

    def col_copy(dst_c, slot):
        return pltpu.make_async_remote_copy(
            src_ref=x_ref, dst_ref=buf_c.at[slot], send_sem=ssem_c.at[dst_c],
            recv_sem=rsem_c.at[slot], device_id=(me_r, dst_c), device_id_type=mesh_t)
    sends = []
    for k in range(1, nc):
        cp = col_copy(lax.rem(me_c + k, nc), me_c)
        cp.start()
        sends.append(cp)
    acc = x_ref[...]
    for k in range(1, nc):
        src = lax.rem(me_c + nc - k, nc)
        col_copy(src, src).wait_recv()
        acc = jnp.maximum(acc, buf_c[src])
    for cp in sends:
        cp.wait_send()
    part[...] = acc

    def row_copy(dst_r, slot):
        return pltpu.make_async_remote_copy(
            src_ref=part, dst_ref=buf_r.at[slot], send_sem=ssem_r.at[dst_r],
            recv_sem=rsem_r.at[slot], device_id=(dst_r, me_c), device_id_type=mesh_t)
    sends = []
    for k in range(1, nr):
        cp = row_copy(lax.rem(me_r + k, nr), me_r)
        cp.start()
        sends.append(cp)
    for k in range(1, nr):
        src = lax.rem(me_r + nr - k, nr)
        row_copy(src, src).wait_recv()
        acc = jnp.maximum(acc, buf_r[src])
    for cp in sends:
        cp.wait_send()
    o_ref[...] = acc


def global_max(tile, nr, nc):
    return pl.pallas_call(
        functools.partial(_allmax_kernel, nr, nc),
        out_shape=jax.ShapeDtypeStruct(tile.shape, tile.dtype),
        in_specs=[pl.BlockSpec(memory_space=pltpu.VMEM)],
        out_specs=pl.BlockSpec(memory_space=pltpu.VMEM),
        scratch_shapes=[
            pltpu.VMEM((nc,) + tile.shape, tile.dtype),
            pltpu.VMEM((nr,) + tile.shape, tile.dtype),
            pltpu.VMEM(tile.shape, tile.dtype),
            pltpu.SemaphoreType.DMA((nc,)),
            pltpu.SemaphoreType.DMA((nc,)),
            pltpu.SemaphoreType.DMA((nr,)),
            pltpu.SemaphoreType.DMA((nr,)),
        ],
        compiler_params=pltpu.CompilerParams(collective_id=0, has_side_effects=True),
    )(tile)


def _col_exchange_kernel(nc, piece, place, re_ref, im_ref, re_out, im_out, send_sem, recv_sem, own_sem):
    me_r = lax.axis_index("row")
    me = lax.axis_index("col")
    mesh_t = pl.DeviceIdType.MESH
    barrier = pltpu.get_barrier_semaphore()
    for k in range(1, nc):
        pl.semaphore_signal(barrier, inc=1, device_id=(me_r, lax.rem(me + k, nc)), device_id_type=mesh_t)
    pl.semaphore_wait(barrier, nc - 1)
    srcs = (re_ref, im_ref)
    dsts = (re_out, im_out)

    def remote(peer, slot, part):
        return pltpu.make_async_remote_copy(
            src_ref=piece(srcs[part], peer), dst_ref=place(dsts[part], slot),
            send_sem=send_sem.at[peer, part], recv_sem=recv_sem.at[slot, part],
            device_id=(me_r, peer), device_id_type=mesh_t)

    sends = []
    for k in range(1, nc):
        peer = lax.rem(me + k, nc)
        for part in range(2):
            cp = remote(peer, me, part)
            cp.start()
            sends.append(cp)
    owns = []
    for part in range(2):
        cp = pltpu.make_async_copy(piece(srcs[part], me), place(dsts[part], me), own_sem.at[part])
        cp.start()
        owns.append(cp)
    for cp in owns:
        cp.wait()
    for k in range(1, nc):
        src = lax.rem(me + nc - k, nc)
        for part in range(2):
            remote(src, src, part).wait_recv()
    for cp in sends:
        cp.wait_send()


def col_exchange(re, im, out_rows, out_cols, piece, place, nc, cid):
    out = jax.ShapeDtypeStruct((out_rows, out_cols), re.dtype)
    return pl.pallas_call(
        functools.partial(_col_exchange_kernel, nc, piece, place),
        out_shape=(out, out),
        in_specs=[pl.BlockSpec(memory_space=pl.ANY)] * 2,
        out_specs=(pl.BlockSpec(memory_space=pl.ANY),) * 2,
        scratch_shapes=[
            pltpu.SemaphoreType.DMA((nc, 2)),
            pltpu.SemaphoreType.DMA((nc, 2)),
            pltpu.SemaphoreType.DMA((2,)),
        ],
        compiler_params=pltpu.CompilerParams(collective_id=cid, has_side_effects=True),
    )(re, im)


def rows_to_strip(re, im, nc, cid):
    rows, cols = re.shape
    band = rows // nc
    piece = lambda ref, p: ref.at[pl.ds(p * band, band), :]
    place = lambda ref, s: ref.at[:, pl.ds(s * cols, cols)]
    return col_exchange(re, im, band, cols * nc, piece, place, nc, cid)


def strip_to_rows(re, im, nc, cid):
    rows, cols = re.shape
    width = cols // nc
    piece = lambda ref, p: ref.at[:, pl.ds(p * width, width)]
    place = lambda ref, s: ref.at[pl.ds(s * rows, rows), :]
    return col_exchange(re, im, rows * nc, width, piece, place, nc, cid)


def _finish_kernel(nr, nc, re_ref, im_ref, peak_ref, re_out, im_out, top_out,
                   buf_c, buf_r, part, send_sem, recv_sem, own_sem, ssem_c, rsem_c, ssem_r, rsem_r):
    me_r = lax.axis_index("row")
    me = lax.axis_index("col")
    mesh_t = pl.DeviceIdType.MESH
    barrier = pltpu.get_barrier_semaphore()
    for k in range(1, nc):
        pl.semaphore_signal(barrier, inc=1, device_id=(me_r, lax.rem(me + k, nc)), device_id_type=mesh_t)
    for k in range(1, nr):
        pl.semaphore_signal(barrier, inc=1, device_id=(lax.rem(me_r + k, nr), me), device_id_type=mesh_t)
    pl.semaphore_wait(barrier, (nc - 1) + (nr - 1))

    def col_top(peer, slot):
        return pltpu.make_async_remote_copy(
            src_ref=peak_ref, dst_ref=buf_c.at[slot], send_sem=ssem_c.at[peer],
            recv_sem=rsem_c.at[slot], device_id=(me_r, peer), device_id_type=mesh_t)

    for k in range(1, nc):
        col_top(lax.rem(me + k, nc), me).start()

    rows = re_ref.shape[0]
    width = re_ref.shape[1] // nc
    srcs = (re_ref, im_ref)
    dsts = (re_out, im_out)

    def data(peer, slot, part_id):
        return pltpu.make_async_remote_copy(
            src_ref=srcs[part_id].at[:, pl.ds(peer * width, width)],
            dst_ref=dsts[part_id].at[pl.ds(slot * rows, rows), :],
            send_sem=send_sem.at[peer, part_id], recv_sem=recv_sem.at[slot, part_id],
            device_id=(me_r, peer), device_id_type=mesh_t)

    for k in range(1, nc):
        for part_id in range(2):
            data(lax.rem(me + k, nc), me, part_id).start()
    owns = []
    for part_id in range(2):
        cp = pltpu.make_async_copy(
            srcs[part_id].at[:, pl.ds(me * width, width)],
            dsts[part_id].at[pl.ds(me * rows, rows), :], own_sem.at[part_id])
        cp.start()
        owns.append(cp)

    acc = peak_ref[...]
    for k in range(1, nc):
        src = lax.rem(me + nc - k, nc)
        col_top(src, src).wait_recv()
        acc = jnp.maximum(acc, buf_c[src])
    for k in range(1, nc):
        col_top(lax.rem(me + k, nc), me).wait_send()
    part[...] = acc

    def row_top(peer, slot):
        return pltpu.make_async_remote_copy(
            src_ref=part, dst_ref=buf_r.at[slot], send_sem=ssem_r.at[peer],
            recv_sem=rsem_r.at[slot], device_id=(peer, me), device_id_type=mesh_t)

    for k in range(1, nr):
        row_top(lax.rem(me_r + k, nr), me_r).start()
    for k in range(1, nr):
        src = lax.rem(me_r + nr - k, nr)
        row_top(src, src).wait_recv()
        acc = jnp.maximum(acc, buf_r[src])
    for k in range(1, nr):
        row_top(lax.rem(me_r + k, nr), me_r).wait_send()
    top_out[...] = acc

    for cp in owns:
        cp.wait()
    for k in range(1, nc):
        src = lax.rem(me + nc - k, nc)
        for part_id in range(2):
            data(src, src, part_id).wait_recv()
            data(lax.rem(me + k, nc), me, part_id).wait_send()


def finish_exchange(re, im, peak_tile, nr, nc, cid):
    rows, cols = re.shape
    out = jax.ShapeDtypeStruct((rows * nc, cols // nc), re.dtype)
    top = jax.ShapeDtypeStruct(peak_tile.shape, peak_tile.dtype)
    return pl.pallas_call(
        functools.partial(_finish_kernel, nr, nc),
        out_shape=(out, out, top),
        in_specs=[pl.BlockSpec(memory_space=pl.ANY)] * 2 + [pl.BlockSpec(memory_space=pltpu.VMEM)],
        out_specs=(pl.BlockSpec(memory_space=pl.ANY),) * 2 + (pl.BlockSpec(memory_space=pltpu.VMEM),),
        scratch_shapes=[
            pltpu.VMEM((nc,) + peak_tile.shape, peak_tile.dtype),
            pltpu.VMEM((nr,) + peak_tile.shape, peak_tile.dtype),
            pltpu.VMEM(peak_tile.shape, peak_tile.dtype),
            pltpu.SemaphoreType.DMA((nc, 2)),
            pltpu.SemaphoreType.DMA((nc, 2)),
            pltpu.SemaphoreType.DMA((2,)),
            pltpu.SemaphoreType.DMA((nc,)),
            pltpu.SemaphoreType.DMA((nc,)),
            pltpu.SemaphoreType.DMA((nr,)),
            pltpu.SemaphoreType.DMA((nr,)),
        ],
        compiler_params=pltpu.CompilerParams(collective_id=cid, has_side_effects=True),
    )(re, im, peak_tile)


def transform_blocks(values_real, values_imag, exponent_sign, length, outer_size, in_blocks, out_blocks):
    inner_size = length // outer_size
    row_count = values_real.shape[0]
    cube_real = values_real.reshape(row_count, len(in_blocks), inner_size)
    cube_imag = values_imag.reshape(row_count, len(in_blocks), inner_size)
    step_real, step_imag = phase_table(
        jnp.asarray(in_blocks, jnp.int32), index_range(0, outer_size), outer_size, exponent_sign
    )
    mid_real, mid_imag = complex_einsum("rnq,nk->rkq", cube_real, cube_imag, step_real, step_imag)
    twist_real, twist_imag = phase_table(
        index_range(0, outer_size), index_range(0, inner_size), length, exponent_sign
    )
    mid_real, mid_imag = (
        mid_real * twist_real - mid_imag * twist_imag,
        mid_real * twist_imag + mid_imag * twist_real,
    )
    last_real, last_imag = phase_table(
        index_range(0, inner_size), jnp.asarray(out_blocks, jnp.int32), inner_size, exponent_sign
    )
    done_real, done_imag = complex_einsum("rkq,qj->rjk", mid_real, mid_imag, last_real, last_imag)
    return (
        done_real.reshape(row_count, len(out_blocks) * outer_size),
        done_imag.reshape(row_count, len(out_blocks) * outer_size),
    )


def band_blocks(padded, block, band_limit):
    top = math.ceil(band_limit) - 1
    low = list(range(top // block + 1))
    high = list(range((padded - top) // block, padded // block))
    return low + high


def body(field_real, field_imag):
    padded = 2 * N
    quarter = padded // 4
    col_total = lax.axis_size("col")
    device_total = lax.axis_size("row") * col_total
    device = lax.axis_index("row") * col_total + lax.axis_index("col")
    strip_real, strip_imag = rows_to_strip(field_real, field_imag, col_total, 1)
    ratio_sq, band_limit = optics(padded)
    fwd_outer, fwd_inner = factor_pair(padded)
    inv_outer, inv_inner = fwd_inner, fwd_outer
    band = band_blocks(padded, fwd_outer, band_limit)
    field_blocks = list(range(quarter // fwd_inner, (quarter + N) // fwd_inner))
    near_blocks = list(range(quarter // inv_outer, (quarter + N) // inv_outer))
    pick_real, pick_imag = transform_blocks(
        strip_real, strip_imag, -1.0, padded, fwd_outer, field_blocks, band
    )
    column_real, column_imag = (
        lax.all_to_all(pick_real, ("row", "col"), split_axis=1, concat_axis=0, tiled=True),
        lax.all_to_all(pick_imag, ("row", "col"), split_axis=1, concat_axis=0, tiled=True),
    )
    col_width = column_real.shape[1]
    turned_real = column_real.T
    turned_imag = column_imag.T
    spec_real, spec_imag = transform_blocks(
        turned_real, turned_imag, -1.0, padded, fwd_outer, field_blocks, band
    )
    band_freqs = np.array(band, np.int32)[:, None] * fwd_outer + np.arange(fwd_outer, dtype=np.int32)
    freq_ids = jnp.asarray(band_freqs.reshape(-1))
    freq_signed = signed_index(freq_ids, padded).astype(jnp.float32)
    col_ids = lax.dynamic_slice(freq_ids, (device * col_width,), (col_width,))
    col_signed = signed_index(col_ids, padded).astype(jnp.float32)
    gain_real, gain_imag = transfer(col_signed, freq_signed, ratio_sq, band_limit)
    mixed_real = spec_real * gain_real - spec_imag * gain_imag
    mixed_imag = spec_real * gain_imag + spec_imag * gain_real
    inv_real, inv_imag = transform_blocks(
        mixed_real, mixed_imag, 1.0, padded, inv_outer, band, near_blocks
    )
    back_real = inv_real.T
    back_imag = inv_imag.T
    line_real, line_imag = (
        lax.all_to_all(back_real, ("row", "col"), split_axis=0, concat_axis=1, tiled=True),
        lax.all_to_all(back_imag, ("row", "col"), split_axis=0, concat_axis=1, tiled=True),
    )
    line_rows = line_real.shape[0]
    near_real, near_imag = transform_blocks(
        line_real, line_imag, 1.0, padded, inv_outer, band, near_blocks
    )
    local_amp = jnp.sqrt(near_real * near_real + near_imag * near_imag)
    peak_tile = jnp.full((8, 128), jnp.max(local_amp), jnp.float32)
    tile_near_real, tile_near_imag, top = finish_exchange(
        near_real, near_imag, peak_tile, lax.axis_size("row"), col_total, 3
    )
    peak = top[0, 0]
    amplitude = jnp.sqrt(tile_near_real * tile_near_real + tile_near_imag * tile_near_imag)
    tile_rows, tile_cols = tile_near_real.shape
    row_ids = lax.axis_index("row") * tile_rows + jnp.arange(tile_rows, dtype=jnp.int32)
    col_ids_out = lax.axis_index("col") * tile_cols + jnp.arange(tile_cols, dtype=jnp.int32)
    even_cell = (row_ids[:, None] + col_ids_out[None, :]) % 2 == 0
    tile_real, tile_imag = encode(tile_near_real, tile_near_imag, amplitude, peak, even_cell)
    return (tile_real, tile_imag)


def solution(mesh):
    in_specs = (P("row", "col"), P("row", "col"))
    out_specs = (P("row", "col"), P("row", "col"))
    return jax.shard_map(body, mesh=mesh, in_specs=in_specs, out_specs=out_specs, check_vma=False)
```

```python
from functools import partial
import math

import jax
import jax.numpy as jnp
from jax import lax
from jax.sharding import PartitionSpec as P
from jax.experimental import pallas as pl
from jax.experimental.pallas import tpu as pltpu
import functools

import numpy as np

N = 4096


wavelength = 5.2e-07
distance = 0.2


def optics(padded_side):
    pitch = 2e-06 * math.sqrt(8192.0 / padded_side)
    extent = padded_side * pitch
    ratio_sq = (wavelength / extent) ** 2
    band_limit = extent / (wavelength * math.sqrt((2.0 * distance / extent) ** 2 + 1.0))
    return (ratio_sq, band_limit)


def factor_pair(length):
    bit_count = length.bit_length() - 1
    inner_size = 2 ** ((bit_count + 1) // 2)
    return (length // inner_size, inner_size)


def signed_index(index_ids, modulus):
    return jnp.where(index_ids >= modulus // 2, index_ids - modulus, index_ids)


def transfer(row_signed, col_signed, ratio_sq, band_limit):
    square = row_signed[:, None] * row_signed[:, None] + col_signed[None, :] * col_signed[None, :]
    scaled = ratio_sq * square
    phase_angle = -2.0 * math.pi * distance / wavelength * scaled / (1.0 + jnp.sqrt(1.0 - scaled))
    gauss_gain = jnp.exp(square * (-2.0 / (band_limit * band_limit)))
    inside = (jnp.abs(row_signed)[:, None] < band_limit) & (
        jnp.abs(col_signed)[None, :] < band_limit
    )
    total_gain = jnp.where(inside, gauss_gain, 0.0)
    return (total_gain * jnp.cos(phase_angle), total_gain * jnp.sin(phase_angle))


def encode(near_real, near_imag, amplitude, peak, even_cell):
    amp_level = 0.8 * amplitude / peak
    amp_floor = jnp.maximum(amplitude, 0.05 * peak)
    unit_real = near_real / amp_floor
    unit_imag = near_imag / amp_floor
    lift_part = jnp.sqrt(1.0 - amp_level * amp_level)
    cell_sign = jnp.where(even_cell, 1.0, -1.0)
    out_real = unit_real * amp_level + cell_sign * unit_imag * lift_part
    out_imag = unit_imag * amp_level - cell_sign * unit_real * lift_part
    return (out_real, out_imag)


def index_range(range_start, id_count):
    return jnp.arange(id_count, dtype=jnp.int32) + range_start


def phase_table(first_ids, second_ids, modulus, exponent_sign):
    product = first_ids[:, None] * second_ids[None, :] % modulus
    phase_arg = exponent_sign * 2.0 * math.pi / modulus * product.astype(jnp.float32)
    return (jnp.cos(phase_arg), jnp.sin(phase_arg))


def complex_einsum(form, left_real, left_imag, right_real, right_imag):
    real_dot = partial(jnp.einsum, form, precision=lax.Precision.HIGH)
    out_real = real_dot(left_real, right_real) - real_dot(left_imag, right_imag)
    out_imag = real_dot(left_real, right_imag) + real_dot(left_imag, right_real)
    return (out_real, out_imag)


def transform_last(values_real, values_imag, exponent_sign, in_start, out_start, out_count, length):
    outer_size, inner_size = factor_pair(length)
    row_count = values_real.shape[0]
    blocks_in = values_real.shape[1] // inner_size
    first_block = in_start // inner_size
    cube_real = values_real.reshape(row_count, blocks_in, inner_size)
    cube_imag = values_imag.reshape(row_count, blocks_in, inner_size)
    step_real, step_imag = phase_table(
        index_range(first_block, blocks_in), index_range(0, outer_size), outer_size, exponent_sign
    )
    mid_real, mid_imag = complex_einsum("rnq,nk->rkq", cube_real, cube_imag, step_real, step_imag)
    twist_real, twist_imag = phase_table(
        index_range(0, outer_size), index_range(0, inner_size), length, exponent_sign
    )
    mid_real, mid_imag = (
        mid_real * twist_real - mid_imag * twist_imag,
        mid_real * twist_imag + mid_imag * twist_real,
    )
    blocks_out = out_count // outer_size
    second_block = out_start // outer_size
    last_real, last_imag = phase_table(
        index_range(0, inner_size), index_range(second_block, blocks_out), inner_size, exponent_sign
    )
    done_real, done_imag = complex_einsum("rkq,qj->rjk", mid_real, mid_imag, last_real, last_imag)
    return (
        done_real.reshape(row_count, blocks_out * outer_size),
        done_imag.reshape(row_count, blocks_out * outer_size),
    )


def _allmax_kernel(nr, nc, x_ref, o_ref, buf_c, buf_r, part, ssem_c, rsem_c, ssem_r, rsem_r):
    me_r = lax.axis_index("row")
    me_c = lax.axis_index("col")
    mesh_t = pl.DeviceIdType.MESH
    barrier = pltpu.get_barrier_semaphore()
    for k in range(1, nc):
        pl.semaphore_signal(barrier, inc=1, device_id=(me_r, lax.rem(me_c + k, nc)), device_id_type=mesh_t)
    for k in range(1, nr):
        pl.semaphore_signal(barrier, inc=1, device_id=(lax.rem(me_r + k, nr), me_c), device_id_type=mesh_t)
    pl.semaphore_wait(barrier, (nc - 1) + (nr - 1))

    def col_copy(dst_c, slot):
        return pltpu.make_async_remote_copy(
            src_ref=x_ref, dst_ref=buf_c.at[slot], send_sem=ssem_c.at[dst_c],
            recv_sem=rsem_c.at[slot], device_id=(me_r, dst_c), device_id_type=mesh_t)
    sends = []
    for k in range(1, nc):
        cp = col_copy(lax.rem(me_c + k, nc), me_c)
        cp.start()
        sends.append(cp)
    acc = x_ref[...]
    for k in range(1, nc):
        src = lax.rem(me_c + nc - k, nc)
        col_copy(src, src).wait_recv()
        acc = jnp.maximum(acc, buf_c[src])
    for cp in sends:
        cp.wait_send()
    part[...] = acc

    def row_copy(dst_r, slot):
        return pltpu.make_async_remote_copy(
            src_ref=part, dst_ref=buf_r.at[slot], send_sem=ssem_r.at[dst_r],
            recv_sem=rsem_r.at[slot], device_id=(dst_r, me_c), device_id_type=mesh_t)
    sends = []
    for k in range(1, nr):
        cp = row_copy(lax.rem(me_r + k, nr), me_r)
        cp.start()
        sends.append(cp)
    for k in range(1, nr):
        src = lax.rem(me_r + nr - k, nr)
        row_copy(src, src).wait_recv()
        acc = jnp.maximum(acc, buf_r[src])
    for cp in sends:
        cp.wait_send()
    o_ref[...] = acc


def global_max(tile, nr, nc):
    return pl.pallas_call(
        functools.partial(_allmax_kernel, nr, nc),
        out_shape=jax.ShapeDtypeStruct(tile.shape, tile.dtype),
        in_specs=[pl.BlockSpec(memory_space=pltpu.VMEM)],
        out_specs=pl.BlockSpec(memory_space=pltpu.VMEM),
        scratch_shapes=[
            pltpu.VMEM((nc,) + tile.shape, tile.dtype),
            pltpu.VMEM((nr,) + tile.shape, tile.dtype),
            pltpu.VMEM(tile.shape, tile.dtype),
            pltpu.SemaphoreType.DMA((nc,)),
            pltpu.SemaphoreType.DMA((nc,)),
            pltpu.SemaphoreType.DMA((nr,)),
            pltpu.SemaphoreType.DMA((nr,)),
        ],
        compiler_params=pltpu.CompilerParams(collective_id=0, has_side_effects=True),
    )(tile)


def _col_exchange_kernel(nc, piece, place, re_ref, im_ref, re_out, im_out, send_sem, recv_sem, own_sem):
    me_r = lax.axis_index("row")
    me = lax.axis_index("col")
    mesh_t = pl.DeviceIdType.MESH
    barrier = pltpu.get_barrier_semaphore()
    for k in range(1, nc):
        pl.semaphore_signal(barrier, inc=1, device_id=(me_r, lax.rem(me + k, nc)), device_id_type=mesh_t)
    pl.semaphore_wait(barrier, nc - 1)
    srcs = (re_ref, im_ref)
    dsts = (re_out, im_out)

    def remote(peer, slot, part):
        return pltpu.make_async_remote_copy(
            src_ref=piece(srcs[part], peer), dst_ref=place(dsts[part], slot),
            send_sem=send_sem.at[peer, part], recv_sem=recv_sem.at[slot, part],
            device_id=(me_r, peer), device_id_type=mesh_t)

    sends = []
    for k in range(1, nc):
        peer = lax.rem(me + k, nc)
        for part in range(2):
            cp = remote(peer, me, part)
            cp.start()
            sends.append(cp)
    owns = []
    for part in range(2):
        cp = pltpu.make_async_copy(piece(srcs[part], me), place(dsts[part], me), own_sem.at[part])
        cp.start()
        owns.append(cp)
    for cp in owns:
        cp.wait()
    for k in range(1, nc):
        src = lax.rem(me + nc - k, nc)
        for part in range(2):
            remote(src, src, part).wait_recv()
    for cp in sends:
        cp.wait_send()


def col_exchange(re, im, out_rows, out_cols, piece, place, nc, cid):
    out = jax.ShapeDtypeStruct((out_rows, out_cols), re.dtype)
    return pl.pallas_call(
        functools.partial(_col_exchange_kernel, nc, piece, place),
        out_shape=(out, out),
        in_specs=[pl.BlockSpec(memory_space=pl.ANY)] * 2,
        out_specs=(pl.BlockSpec(memory_space=pl.ANY),) * 2,
        scratch_shapes=[
            pltpu.SemaphoreType.DMA((nc, 2)),
            pltpu.SemaphoreType.DMA((nc, 2)),
            pltpu.SemaphoreType.DMA((2,)),
        ],
        compiler_params=pltpu.CompilerParams(collective_id=cid, has_side_effects=True),
    )(re, im)


def rows_to_strip(re, im, nc, cid):
    rows, cols = re.shape
    band = rows // nc
    piece = lambda ref, p: ref.at[pl.ds(p * band, band), :]
    place = lambda ref, s: ref.at[:, pl.ds(s * cols, cols)]
    return col_exchange(re, im, band, cols * nc, piece, place, nc, cid)


def strip_to_rows(re, im, nc, cid):
    rows, cols = re.shape
    width = cols // nc
    piece = lambda ref, p: ref.at[:, pl.ds(p * width, width)]
    place = lambda ref, s: ref.at[pl.ds(s * rows, rows), :]
    return col_exchange(re, im, rows * nc, width, piece, place, nc, cid)


def _finish_kernel(nr, nc, re_ref, im_ref, peak_ref, re_out, im_out, top_out,
                   buf_c, buf_r, part, send_sem, recv_sem, own_sem, ssem_c, rsem_c, ssem_r, rsem_r):
    me_r = lax.axis_index("row")
    me = lax.axis_index("col")
    mesh_t = pl.DeviceIdType.MESH
    barrier = pltpu.get_barrier_semaphore()
    for k in range(1, nc):
        pl.semaphore_signal(barrier, inc=1, device_id=(me_r, lax.rem(me + k, nc)), device_id_type=mesh_t)
    for k in range(1, nr):
        pl.semaphore_signal(barrier, inc=1, device_id=(lax.rem(me_r + k, nr), me), device_id_type=mesh_t)
    pl.semaphore_wait(barrier, (nc - 1) + (nr - 1))

    def col_top(peer, slot):
        return pltpu.make_async_remote_copy(
            src_ref=peak_ref, dst_ref=buf_c.at[slot], send_sem=ssem_c.at[peer],
            recv_sem=rsem_c.at[slot], device_id=(me_r, peer), device_id_type=mesh_t)

    for k in range(1, nc):
        col_top(lax.rem(me + k, nc), me).start()

    rows = re_ref.shape[0]
    width = re_ref.shape[1] // nc
    srcs = (re_ref, im_ref)
    dsts = (re_out, im_out)

    def data(peer, slot, part_id):
        return pltpu.make_async_remote_copy(
            src_ref=srcs[part_id].at[:, pl.ds(peer * width, width)],
            dst_ref=dsts[part_id].at[pl.ds(slot * rows, rows), :],
            send_sem=send_sem.at[peer, part_id], recv_sem=recv_sem.at[slot, part_id],
            device_id=(me_r, peer), device_id_type=mesh_t)

    for k in range(1, nc):
        for part_id in range(2):
            data(lax.rem(me + k, nc), me, part_id).start()
    owns = []
    for part_id in range(2):
        cp = pltpu.make_async_copy(
            srcs[part_id].at[:, pl.ds(me * width, width)],
            dsts[part_id].at[pl.ds(me * rows, rows), :], own_sem.at[part_id])
        cp.start()
        owns.append(cp)

    acc = peak_ref[...]
    for k in range(1, nc):
        src = lax.rem(me + nc - k, nc)
        col_top(src, src).wait_recv()
        acc = jnp.maximum(acc, buf_c[src])
    for k in range(1, nc):
        col_top(lax.rem(me + k, nc), me).wait_send()
    part[...] = acc

    def row_top(peer, slot):
        return pltpu.make_async_remote_copy(
            src_ref=part, dst_ref=buf_r.at[slot], send_sem=ssem_r.at[peer],
            recv_sem=rsem_r.at[slot], device_id=(peer, me), device_id_type=mesh_t)

    for k in range(1, nr):
        row_top(lax.rem(me_r + k, nr), me_r).start()
    for k in range(1, nr):
        src = lax.rem(me_r + nr - k, nr)
        row_top(src, src).wait_recv()
        acc = jnp.maximum(acc, buf_r[src])
    for k in range(1, nr):
        row_top(lax.rem(me_r + k, nr), me_r).wait_send()
    top_out[...] = acc

    for cp in owns:
        cp.wait()
    for k in range(1, nc):
        src = lax.rem(me + nc - k, nc)
        for part_id in range(2):
            data(src, src, part_id).wait_recv()
            data(lax.rem(me + k, nc), me, part_id).wait_send()


def finish_exchange(re, im, peak_tile, nr, nc, cid):
    rows, cols = re.shape
    out = jax.ShapeDtypeStruct((rows * nc, cols // nc), re.dtype)
    top = jax.ShapeDtypeStruct(peak_tile.shape, peak_tile.dtype)
    return pl.pallas_call(
        functools.partial(_finish_kernel, nr, nc),
        out_shape=(out, out, top),
        in_specs=[pl.BlockSpec(memory_space=pl.ANY)] * 2 + [pl.BlockSpec(memory_space=pltpu.VMEM)],
        out_specs=(pl.BlockSpec(memory_space=pl.ANY),) * 2 + (pl.BlockSpec(memory_space=pltpu.VMEM),),
        scratch_shapes=[
            pltpu.VMEM((nc,) + peak_tile.shape, peak_tile.dtype),
            pltpu.VMEM((nr,) + peak_tile.shape, peak_tile.dtype),
            pltpu.VMEM(peak_tile.shape, peak_tile.dtype),
            pltpu.SemaphoreType.DMA((nc, 2)),
            pltpu.SemaphoreType.DMA((nc, 2)),
            pltpu.SemaphoreType.DMA((2,)),
            pltpu.SemaphoreType.DMA((nc,)),
            pltpu.SemaphoreType.DMA((nc,)),
            pltpu.SemaphoreType.DMA((nr,)),
            pltpu.SemaphoreType.DMA((nr,)),
        ],
        compiler_params=pltpu.CompilerParams(collective_id=cid, has_side_effects=True),
    )(re, im, peak_tile)


def transform_blocks(
    values_real, values_imag, exponent_sign, length, outer_size, in_blocks, out_blocks,
    lead_in=False, lead_out=False,
):
    inner_size = length // outer_size
    if lead_in:
        row_count = values_real.shape[1]
        cube_real = values_real.reshape(len(in_blocks), inner_size, row_count)
        cube_imag = values_imag.reshape(len(in_blocks), inner_size, row_count)
        first_form = "nqr,nk->rkq"
    else:
        row_count = values_real.shape[0]
        cube_real = values_real.reshape(row_count, len(in_blocks), inner_size)
        cube_imag = values_imag.reshape(row_count, len(in_blocks), inner_size)
        first_form = "rnq,nk->rkq"
    step_real, step_imag = phase_table(
        jnp.asarray(in_blocks, jnp.int32), index_range(0, outer_size), outer_size, exponent_sign
    )
    mid_real, mid_imag = complex_einsum(first_form, cube_real, cube_imag, step_real, step_imag)
    twist_real, twist_imag = phase_table(
        index_range(0, outer_size), index_range(0, inner_size), length, exponent_sign
    )
    mid_real, mid_imag = (
        mid_real * twist_real - mid_imag * twist_imag,
        mid_real * twist_imag + mid_imag * twist_real,
    )
    last_real, last_imag = phase_table(
        index_range(0, inner_size), jnp.asarray(out_blocks, jnp.int32), inner_size, exponent_sign
    )
    if lead_out:
        done_real, done_imag = complex_einsum(
            "rkq,qj->jkr", mid_real, mid_imag, last_real, last_imag
        )
        return (
            done_real.reshape(len(out_blocks) * outer_size, row_count),
            done_imag.reshape(len(out_blocks) * outer_size, row_count),
        )
    done_real, done_imag = complex_einsum("rkq,qj->rjk", mid_real, mid_imag, last_real, last_imag)
    return (
        done_real.reshape(row_count, len(out_blocks) * outer_size),
        done_imag.reshape(row_count, len(out_blocks) * outer_size),
    )


def band_blocks(padded, block, band_limit):
    top = math.ceil(band_limit) - 1
    low = list(range(top // block + 1))
    high = list(range((padded - top) // block, padded // block))
    return low + high


def body(field_real, field_imag):
    padded = 2 * N
    quarter = padded // 4
    col_total = lax.axis_size("col")
    device_total = lax.axis_size("row") * col_total
    device = lax.axis_index("row") * col_total + lax.axis_index("col")
    strip_real, strip_imag = rows_to_strip(field_real, field_imag, col_total, 1)
    ratio_sq, band_limit = optics(padded)
    fwd_outer, fwd_inner = factor_pair(padded)
    inv_outer, inv_inner = fwd_inner, fwd_outer
    band = band_blocks(padded, fwd_outer, band_limit)
    field_blocks = list(range(quarter // fwd_inner, (quarter + N) // fwd_inner))
    near_blocks = list(range(quarter // inv_outer, (quarter + N) // inv_outer))
    pick_real, pick_imag = transform_blocks(
        strip_real, strip_imag, -1.0, padded, fwd_outer, field_blocks, band, lead_out=True
    )
    turned_real, turned_imag = (
        lax.all_to_all(pick_real, ("row", "col"), split_axis=0, concat_axis=1, tiled=True),
        lax.all_to_all(pick_imag, ("row", "col"), split_axis=0, concat_axis=1, tiled=True),
    )
    col_width = turned_real.shape[0]
    spec_real, spec_imag = transform_blocks(
        turned_real, turned_imag, -1.0, padded, fwd_outer, field_blocks, band
    )
    band_freqs = np.array(band, np.int32)[:, None] * fwd_outer + np.arange(fwd_outer, dtype=np.int32)
    freq_ids = jnp.asarray(band_freqs.reshape(-1))
    freq_signed = signed_index(freq_ids, padded).astype(jnp.float32)
    col_ids = lax.dynamic_slice(freq_ids, (device * col_width,), (col_width,))
    col_signed = signed_index(col_ids, padded).astype(jnp.float32)
    gain_real, gain_imag = transfer(col_signed, freq_signed, ratio_sq, band_limit)
    mixed_real = spec_real * gain_real - spec_imag * gain_imag
    mixed_imag = spec_real * gain_imag + spec_imag * gain_real
    inv_real, inv_imag = transform_blocks(
        mixed_real, mixed_imag, 1.0, padded, inv_outer, band, near_blocks
    )
    line_real, line_imag = (
        lax.all_to_all(inv_real, ("row", "col"), split_axis=1, concat_axis=0, tiled=True),
        lax.all_to_all(inv_imag, ("row", "col"), split_axis=1, concat_axis=0, tiled=True),
    )
    near_real, near_imag = transform_blocks(
        line_real, line_imag, 1.0, padded, inv_outer, band, near_blocks, lead_in=True
    )
    local_amp = jnp.sqrt(near_real * near_real + near_imag * near_imag)
    peak_tile = jnp.full((8, 128), jnp.max(local_amp), jnp.float32)
    tile_near_real, tile_near_imag, top = finish_exchange(
        near_real, near_imag, peak_tile, lax.axis_size("row"), col_total, 3
    )
    peak = top[0, 0]
    amplitude = jnp.sqrt(tile_near_real * tile_near_real + tile_near_imag * tile_near_imag)
    tile_rows, tile_cols = tile_near_real.shape
    row_ids = lax.axis_index("row") * tile_rows + jnp.arange(tile_rows, dtype=jnp.int32)
    col_ids_out = lax.axis_index("col") * tile_cols + jnp.arange(tile_cols, dtype=jnp.int32)
    even_cell = (row_ids[:, None] + col_ids_out[None, :]) % 2 == 0
    tile_real, tile_imag = encode(tile_near_real, tile_near_imag, amplitude, peak, even_cell)
    return (tile_real, tile_imag)


def solution(mesh):
    in_specs = (P("row", "col"), P("row", "col"))
    out_specs = (P("row", "col"), P("row", "col"))
    return jax.shard_map(body, mesh=mesh, in_specs=in_specs, out_specs=out_specs, check_vma=False)
```

```python
from functools import partial
import math

import jax
import jax.numpy as jnp
from jax import lax
from jax.sharding import PartitionSpec as P
from jax.experimental import pallas as pl
from jax.experimental.pallas import tpu as pltpu
import functools

import numpy as np

N = 4096


wavelength = 5.2e-07
distance = 0.2


def optics(padded_side):
    pitch = 2e-06 * math.sqrt(8192.0 / padded_side)
    extent = padded_side * pitch
    ratio_sq = (wavelength / extent) ** 2
    band_limit = extent / (wavelength * math.sqrt((2.0 * distance / extent) ** 2 + 1.0))
    return (ratio_sq, band_limit)


def factor_pair(length):
    bit_count = length.bit_length() - 1
    inner_size = 2 ** ((bit_count + 1) // 2)
    return (length // inner_size, inner_size)


def signed_index(index_ids, modulus):
    return jnp.where(index_ids >= modulus // 2, index_ids - modulus, index_ids)


def transfer(row_signed, col_signed, ratio_sq, band_limit):
    square = row_signed[:, None] * row_signed[:, None] + col_signed[None, :] * col_signed[None, :]
    scaled = ratio_sq * square
    phase_angle = -2.0 * math.pi * distance / wavelength * scaled / (1.0 + jnp.sqrt(1.0 - scaled))
    gauss_gain = jnp.exp(square * (-2.0 / (band_limit * band_limit)))
    inside = (jnp.abs(row_signed)[:, None] < band_limit) & (
        jnp.abs(col_signed)[None, :] < band_limit
    )
    total_gain = jnp.where(inside, gauss_gain, 0.0)
    return (total_gain * jnp.cos(phase_angle), total_gain * jnp.sin(phase_angle))


def encode(near_real, near_imag, amplitude, peak, even_cell):
    amp_level = 0.8 * amplitude / peak
    amp_floor = jnp.maximum(amplitude, 0.05 * peak)
    unit_real = near_real / amp_floor
    unit_imag = near_imag / amp_floor
    lift_part = jnp.sqrt(1.0 - amp_level * amp_level)
    cell_sign = jnp.where(even_cell, 1.0, -1.0)
    out_real = unit_real * amp_level + cell_sign * unit_imag * lift_part
    out_imag = unit_imag * amp_level - cell_sign * unit_real * lift_part
    return (out_real, out_imag)


def index_range(range_start, id_count):
    return jnp.arange(id_count, dtype=jnp.int32) + range_start


def phase_table(first_ids, second_ids, modulus, exponent_sign):
    product = first_ids[:, None] * second_ids[None, :] % modulus
    phase_arg = exponent_sign * 2.0 * math.pi / modulus * product.astype(jnp.float32)
    return (jnp.cos(phase_arg), jnp.sin(phase_arg))


def complex_einsum(form, left_real, left_imag, right_real, right_imag):
    real_dot = partial(jnp.einsum, form, precision=lax.Precision.HIGH)
    out_real = real_dot(left_real, right_real) - real_dot(left_imag, right_imag)
    out_imag = real_dot(left_real, right_imag) + real_dot(left_imag, right_real)
    return (out_real, out_imag)


def transform_last(values_real, values_imag, exponent_sign, in_start, out_start, out_count, length):
    outer_size, inner_size = factor_pair(length)
    row_count = values_real.shape[0]
    blocks_in = values_real.shape[1] // inner_size
    first_block = in_start // inner_size
    cube_real = values_real.reshape(row_count, blocks_in, inner_size)
    cube_imag = values_imag.reshape(row_count, blocks_in, inner_size)
    step_real, step_imag = phase_table(
        index_range(first_block, blocks_in), index_range(0, outer_size), outer_size, exponent_sign
    )
    mid_real, mid_imag = complex_einsum("rnq,nk->rkq", cube_real, cube_imag, step_real, step_imag)
    twist_real, twist_imag = phase_table(
        index_range(0, outer_size), index_range(0, inner_size), length, exponent_sign
    )
    mid_real, mid_imag = (
        mid_real * twist_real - mid_imag * twist_imag,
        mid_real * twist_imag + mid_imag * twist_real,
    )
    blocks_out = out_count // outer_size
    second_block = out_start // outer_size
    last_real, last_imag = phase_table(
        index_range(0, inner_size), index_range(second_block, blocks_out), inner_size, exponent_sign
    )
    done_real, done_imag = complex_einsum("rkq,qj->rjk", mid_real, mid_imag, last_real, last_imag)
    return (
        done_real.reshape(row_count, blocks_out * outer_size),
        done_imag.reshape(row_count, blocks_out * outer_size),
    )


def _allmax_kernel(nr, nc, x_ref, o_ref, buf_c, buf_r, part, ssem_c, rsem_c, ssem_r, rsem_r):
    me_r = lax.axis_index("row")
    me_c = lax.axis_index("col")
    mesh_t = pl.DeviceIdType.MESH
    barrier = pltpu.get_barrier_semaphore()
    for k in range(1, nc):
        pl.semaphore_signal(barrier, inc=1, device_id=(me_r, lax.rem(me_c + k, nc)), device_id_type=mesh_t)
    for k in range(1, nr):
        pl.semaphore_signal(barrier, inc=1, device_id=(lax.rem(me_r + k, nr), me_c), device_id_type=mesh_t)
    pl.semaphore_wait(barrier, (nc - 1) + (nr - 1))

    def col_copy(dst_c, slot):
        return pltpu.make_async_remote_copy(
            src_ref=x_ref, dst_ref=buf_c.at[slot], send_sem=ssem_c.at[dst_c],
            recv_sem=rsem_c.at[slot], device_id=(me_r, dst_c), device_id_type=mesh_t)
    sends = []
    for k in range(1, nc):
        cp = col_copy(lax.rem(me_c + k, nc), me_c)
        cp.start()
        sends.append(cp)
    acc = x_ref[...]
    for k in range(1, nc):
        src = lax.rem(me_c + nc - k, nc)
        col_copy(src, src).wait_recv()
        acc = jnp.maximum(acc, buf_c[src])
    for cp in sends:
        cp.wait_send()
    part[...] = acc

    def row_copy(dst_r, slot):
        return pltpu.make_async_remote_copy(
            src_ref=part, dst_ref=buf_r.at[slot], send_sem=ssem_r.at[dst_r],
            recv_sem=rsem_r.at[slot], device_id=(dst_r, me_c), device_id_type=mesh_t)
    sends = []
    for k in range(1, nr):
        cp = row_copy(lax.rem(me_r + k, nr), me_r)
        cp.start()
        sends.append(cp)
    for k in range(1, nr):
        src = lax.rem(me_r + nr - k, nr)
        row_copy(src, src).wait_recv()
        acc = jnp.maximum(acc, buf_r[src])
    for cp in sends:
        cp.wait_send()
    o_ref[...] = acc


def global_max(tile, nr, nc):
    return pl.pallas_call(
        functools.partial(_allmax_kernel, nr, nc),
        out_shape=jax.ShapeDtypeStruct(tile.shape, tile.dtype),
        in_specs=[pl.BlockSpec(memory_space=pltpu.VMEM)],
        out_specs=pl.BlockSpec(memory_space=pltpu.VMEM),
        scratch_shapes=[
            pltpu.VMEM((nc,) + tile.shape, tile.dtype),
            pltpu.VMEM((nr,) + tile.shape, tile.dtype),
            pltpu.VMEM(tile.shape, tile.dtype),
            pltpu.SemaphoreType.DMA((nc,)),
            pltpu.SemaphoreType.DMA((nc,)),
            pltpu.SemaphoreType.DMA((nr,)),
            pltpu.SemaphoreType.DMA((nr,)),
        ],
        compiler_params=pltpu.CompilerParams(collective_id=0, has_side_effects=True),
    )(tile)


def _col_exchange_kernel(nc, piece, place, re_ref, im_ref, re_out, im_out, send_sem, recv_sem, own_sem):
    me_r = lax.axis_index("row")
    me = lax.axis_index("col")
    mesh_t = pl.DeviceIdType.MESH
    barrier = pltpu.get_barrier_semaphore()
    for k in range(1, nc):
        pl.semaphore_signal(barrier, inc=1, device_id=(me_r, lax.rem(me + k, nc)), device_id_type=mesh_t)
    pl.semaphore_wait(barrier, nc - 1)
    srcs = (re_ref, im_ref)
    dsts = (re_out, im_out)

    def remote(peer, slot, part):
        return pltpu.make_async_remote_copy(
            src_ref=piece(srcs[part], peer), dst_ref=place(dsts[part], slot),
            send_sem=send_sem.at[peer, part], recv_sem=recv_sem.at[slot, part],
            device_id=(me_r, peer), device_id_type=mesh_t)

    sends = []
    for k in range(1, nc):
        peer = lax.rem(me + k, nc)
        for part in range(2):
            cp = remote(peer, me, part)
            cp.start()
            sends.append(cp)
    owns = []
    for part in range(2):
        cp = pltpu.make_async_copy(piece(srcs[part], me), place(dsts[part], me), own_sem.at[part])
        cp.start()
        owns.append(cp)
    for cp in owns:
        cp.wait()
    for k in range(1, nc):
        src = lax.rem(me + nc - k, nc)
        for part in range(2):
            remote(src, src, part).wait_recv()
    for cp in sends:
        cp.wait_send()


def col_exchange(re, im, out_rows, out_cols, piece, place, nc, cid):
    out = jax.ShapeDtypeStruct((out_rows, out_cols), re.dtype)
    return pl.pallas_call(
        functools.partial(_col_exchange_kernel, nc, piece, place),
        out_shape=(out, out),
        in_specs=[pl.BlockSpec(memory_space=pl.ANY)] * 2,
        out_specs=(pl.BlockSpec(memory_space=pl.ANY),) * 2,
        scratch_shapes=[
            pltpu.SemaphoreType.DMA((nc, 2)),
            pltpu.SemaphoreType.DMA((nc, 2)),
            pltpu.SemaphoreType.DMA((2,)),
        ],
        compiler_params=pltpu.CompilerParams(collective_id=cid, has_side_effects=True),
    )(re, im)


def rows_to_strip(re, im, nc, cid):
    rows, cols = re.shape
    band = rows // nc
    piece = lambda ref, p: ref.at[pl.ds(p * band, band), :]
    place = lambda ref, s: ref.at[:, pl.ds(s * cols, cols)]
    return col_exchange(re, im, band, cols * nc, piece, place, nc, cid)


def strip_to_rows(re, im, nc, cid):
    rows, cols = re.shape
    width = cols // nc
    piece = lambda ref, p: ref.at[:, pl.ds(p * width, width)]
    place = lambda ref, s: ref.at[pl.ds(s * rows, rows), :]
    return col_exchange(re, im, rows * nc, width, piece, place, nc, cid)


def _finish_kernel(nr, nc, re_ref, im_ref, peak_ref, re_out, im_out, top_out,
                   buf_c, buf_r, part, send_sem, recv_sem, own_sem, ssem_c, rsem_c, ssem_r, rsem_r):
    me_r = lax.axis_index("row")
    me = lax.axis_index("col")
    mesh_t = pl.DeviceIdType.MESH
    barrier = pltpu.get_barrier_semaphore()
    for k in range(1, nc):
        pl.semaphore_signal(barrier, inc=1, device_id=(me_r, lax.rem(me + k, nc)), device_id_type=mesh_t)
    for k in range(1, nr):
        pl.semaphore_signal(barrier, inc=1, device_id=(lax.rem(me_r + k, nr), me), device_id_type=mesh_t)
    pl.semaphore_wait(barrier, (nc - 1) + (nr - 1))

    def col_top(peer, slot):
        return pltpu.make_async_remote_copy(
            src_ref=peak_ref, dst_ref=buf_c.at[slot], send_sem=ssem_c.at[peer],
            recv_sem=rsem_c.at[slot], device_id=(me_r, peer), device_id_type=mesh_t)

    for k in range(1, nc):
        col_top(lax.rem(me + k, nc), me).start()

    rows = re_ref.shape[0]
    width = re_ref.shape[1] // nc
    srcs = (re_ref, im_ref)
    dsts = (re_out, im_out)

    def data(peer, slot, part_id):
        return pltpu.make_async_remote_copy(
            src_ref=srcs[part_id].at[:, pl.ds(peer * width, width)],
            dst_ref=dsts[part_id].at[pl.ds(slot * rows, rows), :],
            send_sem=send_sem.at[peer, part_id], recv_sem=recv_sem.at[slot, part_id],
            device_id=(me_r, peer), device_id_type=mesh_t)

    for k in range(1, nc):
        for part_id in range(2):
            data(lax.rem(me + k, nc), me, part_id).start()
    owns = []
    for part_id in range(2):
        cp = pltpu.make_async_copy(
            srcs[part_id].at[:, pl.ds(me * width, width)],
            dsts[part_id].at[pl.ds(me * rows, rows), :], own_sem.at[part_id])
        cp.start()
        owns.append(cp)

    acc = peak_ref[...]
    for k in range(1, nc):
        src = lax.rem(me + nc - k, nc)
        col_top(src, src).wait_recv()
        acc = jnp.maximum(acc, buf_c[src])
    for k in range(1, nc):
        col_top(lax.rem(me + k, nc), me).wait_send()
    part[...] = acc

    def row_top(peer, slot):
        return pltpu.make_async_remote_copy(
            src_ref=part, dst_ref=buf_r.at[slot], send_sem=ssem_r.at[peer],
            recv_sem=rsem_r.at[slot], device_id=(peer, me), device_id_type=mesh_t)

    for k in range(1, nr):
        row_top(lax.rem(me_r + k, nr), me_r).start()
    for k in range(1, nr):
        src = lax.rem(me_r + nr - k, nr)
        row_top(src, src).wait_recv()
        acc = jnp.maximum(acc, buf_r[src])
    for k in range(1, nr):
        row_top(lax.rem(me_r + k, nr), me_r).wait_send()
    top_out[...] = acc

    for cp in owns:
        cp.wait()
    for k in range(1, nc):
        src = lax.rem(me + nc - k, nc)
        for part_id in range(2):
            data(src, src, part_id).wait_recv()
            data(lax.rem(me + k, nc), me, part_id).wait_send()


def finish_exchange(re, im, peak_tile, nr, nc, cid):
    rows, cols = re.shape
    out = jax.ShapeDtypeStruct((rows * nc, cols // nc), re.dtype)
    top = jax.ShapeDtypeStruct(peak_tile.shape, peak_tile.dtype)
    return pl.pallas_call(
        functools.partial(_finish_kernel, nr, nc),
        out_shape=(out, out, top),
        in_specs=[pl.BlockSpec(memory_space=pl.ANY)] * 2 + [pl.BlockSpec(memory_space=pltpu.VMEM)],
        out_specs=(pl.BlockSpec(memory_space=pl.ANY),) * 2 + (pl.BlockSpec(memory_space=pltpu.VMEM),),
        scratch_shapes=[
            pltpu.VMEM((nc,) + peak_tile.shape, peak_tile.dtype),
            pltpu.VMEM((nr,) + peak_tile.shape, peak_tile.dtype),
            pltpu.VMEM(peak_tile.shape, peak_tile.dtype),
            pltpu.SemaphoreType.DMA((nc, 2)),
            pltpu.SemaphoreType.DMA((nc, 2)),
            pltpu.SemaphoreType.DMA((2,)),
            pltpu.SemaphoreType.DMA((nc,)),
            pltpu.SemaphoreType.DMA((nc,)),
            pltpu.SemaphoreType.DMA((nr,)),
            pltpu.SemaphoreType.DMA((nr,)),
        ],
        compiler_params=pltpu.CompilerParams(collective_id=cid, has_side_effects=True),
    )(re, im, peak_tile)


def _one_exchange_kernel(nr, nc, x_ref, x_out, send_sem, recv_sem, own_sem):
    n = nr * nc
    me = lax.axis_index("row") * nc + lax.axis_index("col")
    mesh_t = pl.DeviceIdType.MESH
    barrier = pltpu.get_barrier_semaphore()

    def where(p):
        return (p // nc, lax.rem(p, nc))

    def greet(k, carry):
        pl.semaphore_signal(barrier, inc=1, device_id=where(lax.rem(me + k, n)), device_id_type=mesh_t)
        return carry

    lax.fori_loop(1, n, greet, 0)
    pl.semaphore_wait(barrier, n - 1)

    def remote(peer, slot):
        return pltpu.make_async_remote_copy(
            src_ref=x_ref.at[peer], dst_ref=x_out.at[slot],
            send_sem=send_sem.at[peer], recv_sem=recv_sem.at[slot],
            device_id=where(peer), device_id_type=mesh_t)

    def send(k, carry):
        remote(lax.rem(me + k, n), me).start()
        return carry

    lax.fori_loop(1, n, send, 0)
    own = pltpu.make_async_copy(x_ref.at[me], x_out.at[me], own_sem.at[0])
    own.start()
    own.wait()

    def recv(k, carry):
        remote(lax.rem(me + n - k, n), lax.rem(me + n - k, n)).wait_recv()
        remote(lax.rem(me + k, n), me).wait_send()
        return carry

    lax.fori_loop(1, n, recv, 0)


def one_exchange(x, nr, nc, cid):
    n = nr * nc
    return pl.pallas_call(
        functools.partial(_one_exchange_kernel, nr, nc),
        out_shape=jax.ShapeDtypeStruct(x.shape, x.dtype),
        in_specs=[pl.BlockSpec(memory_space=pl.ANY)],
        out_specs=pl.BlockSpec(memory_space=pl.ANY),
        scratch_shapes=[
            pltpu.SemaphoreType.DMA((n,)),
            pltpu.SemaphoreType.DMA((n,)),
            pltpu.SemaphoreType.DMA((1,)),
        ],
        compiler_params=pltpu.CompilerParams(collective_id=cid, has_side_effects=True),
    )(x)


def transform_blocks(
    values_real, values_imag, exponent_sign, length, outer_size, in_blocks, out_blocks,
    lead_in=False, lead_out=False,
):
    inner_size = length // outer_size
    if lead_in:
        row_count = values_real.shape[1]
        cube_real = values_real.reshape(len(in_blocks), inner_size, row_count)
        cube_imag = values_imag.reshape(len(in_blocks), inner_size, row_count)
        first_form = "nqr,nk->rkq"
    else:
        row_count = values_real.shape[0]
        cube_real = values_real.reshape(row_count, len(in_blocks), inner_size)
        cube_imag = values_imag.reshape(row_count, len(in_blocks), inner_size)
        first_form = "rnq,nk->rkq"
    step_real, step_imag = phase_table(
        jnp.asarray(in_blocks, jnp.int32), index_range(0, outer_size), outer_size, exponent_sign
    )
    mid_real, mid_imag = complex_einsum(first_form, cube_real, cube_imag, step_real, step_imag)
    twist_real, twist_imag = phase_table(
        index_range(0, outer_size), index_range(0, inner_size), length, exponent_sign
    )
    mid_real, mid_imag = (
        mid_real * twist_real - mid_imag * twist_imag,
        mid_real * twist_imag + mid_imag * twist_real,
    )
    last_real, last_imag = phase_table(
        index_range(0, inner_size), jnp.asarray(out_blocks, jnp.int32), inner_size, exponent_sign
    )
    if lead_out:
        done_real, done_imag = complex_einsum(
            "rkq,qj->jkr", mid_real, mid_imag, last_real, last_imag
        )
        return (
            done_real.reshape(len(out_blocks) * outer_size, row_count),
            done_imag.reshape(len(out_blocks) * outer_size, row_count),
        )
    done_real, done_imag = complex_einsum("rkq,qj->rjk", mid_real, mid_imag, last_real, last_imag)
    return (
        done_real.reshape(row_count, len(out_blocks) * outer_size),
        done_imag.reshape(row_count, len(out_blocks) * outer_size),
    )


def band_blocks(padded, block, band_limit, multiple):
    top = math.ceil(band_limit) - 1
    low = list(range(top // block + 1))
    high = list(range((padded - top) // block, padded // block))
    while (len(low) + len(high)) * block % multiple:
        if len(low) <= len(high):
            low.append(low[-1] + 1)
        else:
            high.insert(0, high[0] - 1)
    return low + high


def pack_chunks(first, second, device_total, lead):
    if lead:
        width = first.shape[0] // device_total
        both = jnp.stack([first, second]).reshape(2, device_total, width, first.shape[1])
        both = both.transpose(1, 0, 2, 3)
    else:
        width = first.shape[1] // device_total
        both = jnp.stack([first, second]).reshape(2, first.shape[0], device_total, width)
        both = both.transpose(2, 0, 1, 3)
    return both.reshape(device_total, -1, 128)


def body(field_real, field_imag):
    padded = 2 * N
    quarter = padded // 4
    col_total = lax.axis_size("col")
    device_total = lax.axis_size("row") * col_total
    device = lax.axis_index("row") * col_total + lax.axis_index("col")
    strip_real, strip_imag = rows_to_strip(field_real, field_imag, col_total, 1)
    ratio_sq, band_limit = optics(padded)
    fwd_outer, fwd_inner = factor_pair(padded)
    inv_outer, inv_inner = fwd_inner, fwd_outer
    band = band_blocks(padded, fwd_outer, band_limit, device_total * 2)
    field_blocks = list(range(quarter // fwd_inner, (quarter + N) // fwd_inner))
    near_blocks = list(range(quarter // inv_outer, (quarter + N) // inv_outer))
    pick_real, pick_imag = transform_blocks(
        strip_real, strip_imag, -1.0, padded, fwd_outer, field_blocks, band, lead_out=True
    )
    col_width = pick_real.shape[0] // device_total
    strip_rows = pick_real.shape[1]
    arrived = one_exchange(
        pack_chunks(pick_real, pick_imag, device_total, True), lax.axis_size("row"), col_total, 4
    )
    arrived = arrived.reshape(device_total, 2, col_width, strip_rows).transpose(1, 2, 0, 3)
    arrived = arrived.reshape(2, col_width, device_total * strip_rows)
    turned_real, turned_imag = arrived[0], arrived[1]
    spec_real, spec_imag = transform_blocks(
        turned_real, turned_imag, -1.0, padded, fwd_outer, field_blocks, band
    )
    band_freqs = np.array(band, np.int32)[:, None] * fwd_outer + np.arange(fwd_outer, dtype=np.int32)
    freq_ids = jnp.asarray(band_freqs.reshape(-1))
    freq_signed = signed_index(freq_ids, padded).astype(jnp.float32)
    col_ids = lax.dynamic_slice(freq_ids, (device * col_width,), (col_width,))
    col_signed = signed_index(col_ids, padded).astype(jnp.float32)
    gain_real, gain_imag = transfer(col_signed, freq_signed, ratio_sq, band_limit)
    mixed_real = spec_real * gain_real - spec_imag * gain_imag
    mixed_imag = spec_real * gain_imag + spec_imag * gain_real
    inv_real, inv_imag = transform_blocks(
        mixed_real, mixed_imag, 1.0, padded, inv_outer, band, near_blocks
    )
    returned = one_exchange(
        pack_chunks(inv_real, inv_imag, device_total, False), lax.axis_size("row"), col_total, 5
    )
    returned = returned.reshape(device_total, 2, col_width, strip_rows).transpose(1, 0, 2, 3)
    returned = returned.reshape(2, device_total * col_width, strip_rows)
    line_real, line_imag = returned[0], returned[1]
    near_real, near_imag = transform_blocks(
        line_real, line_imag, 1.0, padded, inv_outer, band, near_blocks, lead_in=True
    )
    local_amp = jnp.sqrt(near_real * near_real + near_imag * near_imag)
    peak_tile = jnp.full((8, 128), jnp.max(local_amp), jnp.float32)
    tile_near_real, tile_near_imag, top = finish_exchange(
        near_real, near_imag, peak_tile, lax.axis_size("row"), col_total, 3
    )
    peak = top[0, 0]
    amplitude = jnp.sqrt(tile_near_real * tile_near_real + tile_near_imag * tile_near_imag)
    tile_rows, tile_cols = tile_near_real.shape
    row_ids = lax.axis_index("row") * tile_rows + jnp.arange(tile_rows, dtype=jnp.int32)
    col_ids_out = lax.axis_index("col") * tile_cols + jnp.arange(tile_cols, dtype=jnp.int32)
    even_cell = (row_ids[:, None] + col_ids_out[None, :]) % 2 == 0
    tile_real, tile_imag = encode(tile_near_real, tile_near_imag, amplitude, peak, even_cell)
    return (tile_real, tile_imag)


def solution(mesh):
    in_specs = (P("row", "col"), P("row", "col"))
    out_specs = (P("row", "col"), P("row", "col"))
    return jax.shard_map(body, mesh=mesh, in_specs=in_specs, out_specs=out_specs, check_vma=False)
```

```python
from functools import partial
import math

import jax
import jax.numpy as jnp
from jax import lax
from jax.sharding import PartitionSpec as P
from jax.experimental import pallas as pl
from jax.experimental.pallas import tpu as pltpu
import functools

import numpy as np

N = 4096


wavelength = 5.2e-07
distance = 0.2


def optics(padded_side):
    pitch = 2e-06 * math.sqrt(8192.0 / padded_side)
    extent = padded_side * pitch
    ratio_sq = (wavelength / extent) ** 2
    band_limit = extent / (wavelength * math.sqrt((2.0 * distance / extent) ** 2 + 1.0))
    return (ratio_sq, band_limit)


def factor_pair(length):
    bit_count = length.bit_length() - 1
    inner_size = 2 ** ((bit_count + 1) // 2)
    return (length // inner_size, inner_size)


def signed_index(index_ids, modulus):
    return jnp.where(index_ids >= modulus // 2, index_ids - modulus, index_ids)


def transfer(row_signed, col_signed, ratio_sq, band_limit):
    square = row_signed[:, None] * row_signed[:, None] + col_signed[None, :] * col_signed[None, :]
    scaled = ratio_sq * square
    phase_angle = -2.0 * math.pi * distance / wavelength * scaled / (1.0 + jnp.sqrt(1.0 - scaled))
    gauss_gain = jnp.exp(square * (-2.0 / (band_limit * band_limit)))
    inside = (jnp.abs(row_signed)[:, None] < band_limit) & (
        jnp.abs(col_signed)[None, :] < band_limit
    )
    total_gain = jnp.where(inside, gauss_gain, 0.0)
    return (total_gain * jnp.cos(phase_angle), total_gain * jnp.sin(phase_angle))


def encode(near_real, near_imag, amplitude, peak, even_cell):
    amp_level = 0.8 * amplitude / peak
    amp_floor = jnp.maximum(amplitude, 0.05 * peak)
    unit_real = near_real / amp_floor
    unit_imag = near_imag / amp_floor
    lift_part = jnp.sqrt(1.0 - amp_level * amp_level)
    cell_sign = jnp.where(even_cell, 1.0, -1.0)
    out_real = unit_real * amp_level + cell_sign * unit_imag * lift_part
    out_imag = unit_imag * amp_level - cell_sign * unit_real * lift_part
    return (out_real, out_imag)


def index_range(range_start, id_count):
    return jnp.arange(id_count, dtype=jnp.int32) + range_start


def phase_table(first_ids, second_ids, modulus, exponent_sign):
    product = first_ids[:, None] * second_ids[None, :] % modulus
    phase_arg = exponent_sign * 2.0 * math.pi / modulus * product.astype(jnp.float32)
    return (jnp.cos(phase_arg), jnp.sin(phase_arg))


def complex_einsum(form, left_real, left_imag, right_real, right_imag):
    real_dot = partial(jnp.einsum, form, precision=lax.Precision.HIGH)
    out_real = real_dot(left_real, right_real) - real_dot(left_imag, right_imag)
    out_imag = real_dot(left_real, right_imag) + real_dot(left_imag, right_real)
    return (out_real, out_imag)


def transform_last(values_real, values_imag, exponent_sign, in_start, out_start, out_count, length):
    outer_size, inner_size = factor_pair(length)
    row_count = values_real.shape[0]
    blocks_in = values_real.shape[1] // inner_size
    first_block = in_start // inner_size
    cube_real = values_real.reshape(row_count, blocks_in, inner_size)
    cube_imag = values_imag.reshape(row_count, blocks_in, inner_size)
    step_real, step_imag = phase_table(
        index_range(first_block, blocks_in), index_range(0, outer_size), outer_size, exponent_sign
    )
    mid_real, mid_imag = complex_einsum("rnq,nk->rkq", cube_real, cube_imag, step_real, step_imag)
    twist_real, twist_imag = phase_table(
        index_range(0, outer_size), index_range(0, inner_size), length, exponent_sign
    )
    mid_real, mid_imag = (
        mid_real * twist_real - mid_imag * twist_imag,
        mid_real * twist_imag + mid_imag * twist_real,
    )
    blocks_out = out_count // outer_size
    second_block = out_start // outer_size
    last_real, last_imag = phase_table(
        index_range(0, inner_size), index_range(second_block, blocks_out), inner_size, exponent_sign
    )
    done_real, done_imag = complex_einsum("rkq,qj->rjk", mid_real, mid_imag, last_real, last_imag)
    return (
        done_real.reshape(row_count, blocks_out * outer_size),
        done_imag.reshape(row_count, blocks_out * outer_size),
    )


def _allmax_kernel(nr, nc, x_ref, o_ref, buf_c, buf_r, part, ssem_c, rsem_c, ssem_r, rsem_r):
    me_r = lax.axis_index("row")
    me_c = lax.axis_index("col")
    mesh_t = pl.DeviceIdType.MESH
    barrier = pltpu.get_barrier_semaphore()
    for k in range(1, nc):
        pl.semaphore_signal(barrier, inc=1, device_id=(me_r, lax.rem(me_c + k, nc)), device_id_type=mesh_t)
    for k in range(1, nr):
        pl.semaphore_signal(barrier, inc=1, device_id=(lax.rem(me_r + k, nr), me_c), device_id_type=mesh_t)
    pl.semaphore_wait(barrier, (nc - 1) + (nr - 1))

    def col_copy(dst_c, slot):
        return pltpu.make_async_remote_copy(
            src_ref=x_ref, dst_ref=buf_c.at[slot], send_sem=ssem_c.at[dst_c],
            recv_sem=rsem_c.at[slot], device_id=(me_r, dst_c), device_id_type=mesh_t)
    sends = []
    for k in range(1, nc):
        cp = col_copy(lax.rem(me_c + k, nc), me_c)
        cp.start()
        sends.append(cp)
    acc = x_ref[...]
    for k in range(1, nc):
        src = lax.rem(me_c + nc - k, nc)
        col_copy(src, src).wait_recv()
        acc = jnp.maximum(acc, buf_c[src])
    for cp in sends:
        cp.wait_send()
    part[...] = acc

    def row_copy(dst_r, slot):
        return pltpu.make_async_remote_copy(
            src_ref=part, dst_ref=buf_r.at[slot], send_sem=ssem_r.at[dst_r],
            recv_sem=rsem_r.at[slot], device_id=(dst_r, me_c), device_id_type=mesh_t)
    sends = []
    for k in range(1, nr):
        cp = row_copy(lax.rem(me_r + k, nr), me_r)
        cp.start()
        sends.append(cp)
    for k in range(1, nr):
        src = lax.rem(me_r + nr - k, nr)
        row_copy(src, src).wait_recv()
        acc = jnp.maximum(acc, buf_r[src])
    for cp in sends:
        cp.wait_send()
    o_ref[...] = acc


def global_max(tile, nr, nc):
    return pl.pallas_call(
        functools.partial(_allmax_kernel, nr, nc),
        out_shape=jax.ShapeDtypeStruct(tile.shape, tile.dtype),
        in_specs=[pl.BlockSpec(memory_space=pltpu.VMEM)],
        out_specs=pl.BlockSpec(memory_space=pltpu.VMEM),
        scratch_shapes=[
            pltpu.VMEM((nc,) + tile.shape, tile.dtype),
            pltpu.VMEM((nr,) + tile.shape, tile.dtype),
            pltpu.VMEM(tile.shape, tile.dtype),
            pltpu.SemaphoreType.DMA((nc,)),
            pltpu.SemaphoreType.DMA((nc,)),
            pltpu.SemaphoreType.DMA((nr,)),
            pltpu.SemaphoreType.DMA((nr,)),
        ],
        compiler_params=pltpu.CompilerParams(collective_id=0, has_side_effects=True),
    )(tile)


def _col_exchange_kernel(nc, piece, place, re_ref, im_ref, re_out, im_out, send_sem, recv_sem, own_sem):
    me_r = lax.axis_index("row")
    me = lax.axis_index("col")
    mesh_t = pl.DeviceIdType.MESH
    barrier = pltpu.get_barrier_semaphore()
    for k in range(1, nc):
        pl.semaphore_signal(barrier, inc=1, device_id=(me_r, lax.rem(me + k, nc)), device_id_type=mesh_t)
    pl.semaphore_wait(barrier, nc - 1)
    srcs = (re_ref, im_ref)
    dsts = (re_out, im_out)

    def remote(peer, slot, part):
        return pltpu.make_async_remote_copy(
            src_ref=piece(srcs[part], peer), dst_ref=place(dsts[part], slot),
            send_sem=send_sem.at[peer, part], recv_sem=recv_sem.at[slot, part],
            device_id=(me_r, peer), device_id_type=mesh_t)

    sends = []
    for k in range(1, nc):
        peer = lax.rem(me + k, nc)
        for part in range(2):
            cp = remote(peer, me, part)
            cp.start()
            sends.append(cp)
    owns = []
    for part in range(2):
        cp = pltpu.make_async_copy(piece(srcs[part], me), place(dsts[part], me), own_sem.at[part])
        cp.start()
        owns.append(cp)
    for cp in owns:
        cp.wait()
    for k in range(1, nc):
        src = lax.rem(me + nc - k, nc)
        for part in range(2):
            remote(src, src, part).wait_recv()
    for cp in sends:
        cp.wait_send()


def col_exchange(re, im, out_rows, out_cols, piece, place, nc, cid):
    out = jax.ShapeDtypeStruct((out_rows, out_cols), re.dtype)
    return pl.pallas_call(
        functools.partial(_col_exchange_kernel, nc, piece, place),
        out_shape=(out, out),
        in_specs=[pl.BlockSpec(memory_space=pl.ANY)] * 2,
        out_specs=(pl.BlockSpec(memory_space=pl.ANY),) * 2,
        scratch_shapes=[
            pltpu.SemaphoreType.DMA((nc, 2)),
            pltpu.SemaphoreType.DMA((nc, 2)),
            pltpu.SemaphoreType.DMA((2,)),
        ],
        compiler_params=pltpu.CompilerParams(collective_id=cid, has_side_effects=True),
    )(re, im)


def rows_to_strip(re, im, nc, cid):
    rows, cols = re.shape
    band = rows // nc
    piece = lambda ref, p: ref.at[pl.ds(p * band, band), :]
    place = lambda ref, s: ref.at[:, pl.ds(s * cols, cols)]
    return col_exchange(re, im, band, cols * nc, piece, place, nc, cid)


def strip_to_rows(re, im, nc, cid):
    rows, cols = re.shape
    width = cols // nc
    piece = lambda ref, p: ref.at[:, pl.ds(p * width, width)]
    place = lambda ref, s: ref.at[pl.ds(s * rows, rows), :]
    return col_exchange(re, im, rows * nc, width, piece, place, nc, cid)


def _finish_kernel(nr, nc, re_ref, im_ref, peak_ref, re_out, im_out, top_out,
                   buf_c, buf_r, part, send_sem, recv_sem, own_sem, ssem_c, rsem_c, ssem_r, rsem_r):
    me_r = lax.axis_index("row")
    me = lax.axis_index("col")
    mesh_t = pl.DeviceIdType.MESH
    barrier = pltpu.get_barrier_semaphore()
    for k in range(1, nc):
        pl.semaphore_signal(barrier, inc=1, device_id=(me_r, lax.rem(me + k, nc)), device_id_type=mesh_t)
    for k in range(1, nr):
        pl.semaphore_signal(barrier, inc=1, device_id=(lax.rem(me_r + k, nr), me), device_id_type=mesh_t)
    pl.semaphore_wait(barrier, (nc - 1) + (nr - 1))

    def col_top(peer, slot):
        return pltpu.make_async_remote_copy(
            src_ref=peak_ref, dst_ref=buf_c.at[slot], send_sem=ssem_c.at[peer],
            recv_sem=rsem_c.at[slot], device_id=(me_r, peer), device_id_type=mesh_t)

    for k in range(1, nc):
        col_top(lax.rem(me + k, nc), me).start()

    rows = re_ref.shape[0]
    width = re_ref.shape[1] // nc
    srcs = (re_ref, im_ref)
    dsts = (re_out, im_out)

    def data(peer, slot, part_id):
        return pltpu.make_async_remote_copy(
            src_ref=srcs[part_id].at[:, pl.ds(peer * width, width)],
            dst_ref=dsts[part_id].at[pl.ds(slot * rows, rows), :],
            send_sem=send_sem.at[peer, part_id], recv_sem=recv_sem.at[slot, part_id],
            device_id=(me_r, peer), device_id_type=mesh_t)

    for k in range(1, nc):
        for part_id in range(2):
            data(lax.rem(me + k, nc), me, part_id).start()
    owns = []
    for part_id in range(2):
        cp = pltpu.make_async_copy(
            srcs[part_id].at[:, pl.ds(me * width, width)],
            dsts[part_id].at[pl.ds(me * rows, rows), :], own_sem.at[part_id])
        cp.start()
        owns.append(cp)

    acc = peak_ref[...]
    for k in range(1, nc):
        src = lax.rem(me + nc - k, nc)
        col_top(src, src).wait_recv()
        acc = jnp.maximum(acc, buf_c[src])
    for k in range(1, nc):
        col_top(lax.rem(me + k, nc), me).wait_send()
    part[...] = acc

    def row_top(peer, slot):
        return pltpu.make_async_remote_copy(
            src_ref=part, dst_ref=buf_r.at[slot], send_sem=ssem_r.at[peer],
            recv_sem=rsem_r.at[slot], device_id=(peer, me), device_id_type=mesh_t)

    for k in range(1, nr):
        row_top(lax.rem(me_r + k, nr), me_r).start()
    for k in range(1, nr):
        src = lax.rem(me_r + nr - k, nr)
        row_top(src, src).wait_recv()
        acc = jnp.maximum(acc, buf_r[src])
    for k in range(1, nr):
        row_top(lax.rem(me_r + k, nr), me_r).wait_send()
    top_out[...] = acc

    for cp in owns:
        cp.wait()
    for k in range(1, nc):
        src = lax.rem(me + nc - k, nc)
        for part_id in range(2):
            data(src, src, part_id).wait_recv()
            data(lax.rem(me + k, nc), me, part_id).wait_send()


def finish_exchange(re, im, peak_tile, nr, nc, cid):
    rows, cols = re.shape
    out = jax.ShapeDtypeStruct((rows * nc, cols // nc), re.dtype)
    top = jax.ShapeDtypeStruct(peak_tile.shape, peak_tile.dtype)
    return pl.pallas_call(
        functools.partial(_finish_kernel, nr, nc),
        out_shape=(out, out, top),
        in_specs=[pl.BlockSpec(memory_space=pl.ANY)] * 2 + [pl.BlockSpec(memory_space=pltpu.VMEM)],
        out_specs=(pl.BlockSpec(memory_space=pl.ANY),) * 2 + (pl.BlockSpec(memory_space=pltpu.VMEM),),
        scratch_shapes=[
            pltpu.VMEM((nc,) + peak_tile.shape, peak_tile.dtype),
            pltpu.VMEM((nr,) + peak_tile.shape, peak_tile.dtype),
            pltpu.VMEM(peak_tile.shape, peak_tile.dtype),
            pltpu.SemaphoreType.DMA((nc, 2)),
            pltpu.SemaphoreType.DMA((nc, 2)),
            pltpu.SemaphoreType.DMA((2,)),
            pltpu.SemaphoreType.DMA((nc,)),
            pltpu.SemaphoreType.DMA((nc,)),
            pltpu.SemaphoreType.DMA((nr,)),
            pltpu.SemaphoreType.DMA((nr,)),
        ],
        compiler_params=pltpu.CompilerParams(collective_id=cid, has_side_effects=True),
    )(re, im, peak_tile)


def _one_exchange_kernel(nr, nc, x_ref, x_out, send_sem, recv_sem, own_sem):
    n = nr * nc
    me = lax.axis_index("row") * nc + lax.axis_index("col")
    mesh_t = pl.DeviceIdType.MESH
    barrier = pltpu.get_barrier_semaphore()

    def where(p):
        return (p // nc, lax.rem(p, nc))

    def greet(k, carry):
        pl.semaphore_signal(barrier, inc=1, device_id=where(lax.rem(me + k, n)), device_id_type=mesh_t)
        return carry

    lax.fori_loop(1, n, greet, 0)
    pl.semaphore_wait(barrier, n - 1)

    def remote(peer, slot):
        return pltpu.make_async_remote_copy(
            src_ref=x_ref.at[peer], dst_ref=x_out.at[slot],
            send_sem=send_sem.at[peer], recv_sem=recv_sem.at[slot],
            device_id=where(peer), device_id_type=mesh_t)

    def send(k, carry):
        remote(lax.rem(me + k, n), me).start()
        return carry

    lax.fori_loop(1, n, send, 0)
    own = pltpu.make_async_copy(x_ref.at[me], x_out.at[me], own_sem.at[0])
    own.start()
    own.wait()

    def recv(k, carry):
        remote(lax.rem(me + n - k, n), lax.rem(me + n - k, n)).wait_recv()
        remote(lax.rem(me + k, n), me).wait_send()
        return carry

    lax.fori_loop(1, n, recv, 0)


def one_exchange(x, nr, nc, cid):
    n = nr * nc
    return pl.pallas_call(
        functools.partial(_one_exchange_kernel, nr, nc),
        out_shape=jax.ShapeDtypeStruct(x.shape, x.dtype),
        in_specs=[pl.BlockSpec(memory_space=pl.ANY)],
        out_specs=pl.BlockSpec(memory_space=pl.ANY),
        scratch_shapes=[
            pltpu.SemaphoreType.DMA((n,)),
            pltpu.SemaphoreType.DMA((n,)),
            pltpu.SemaphoreType.DMA((1,)),
        ],
        compiler_params=pltpu.CompilerParams(collective_id=cid, has_side_effects=True),
    )(x)


def transform_blocks(
    values_real, values_imag, exponent_sign, length, outer_size, in_blocks, out_blocks,
    lead_in=False, lead_out=False,
):
    inner_size = length // outer_size
    if lead_in:
        row_count = values_real.shape[1]
        cube_real = values_real.reshape(len(in_blocks), inner_size, row_count)
        cube_imag = values_imag.reshape(len(in_blocks), inner_size, row_count)
        first_form = "nqr,nk->rkq"
    else:
        row_count = values_real.shape[0]
        cube_real = values_real.reshape(row_count, len(in_blocks), inner_size)
        cube_imag = values_imag.reshape(row_count, len(in_blocks), inner_size)
        first_form = "rnq,nk->rkq"
    step_real, step_imag = phase_table(
        jnp.asarray(in_blocks, jnp.int32), index_range(0, outer_size), outer_size, exponent_sign
    )
    mid_real, mid_imag = complex_einsum(first_form, cube_real, cube_imag, step_real, step_imag)
    twist_real, twist_imag = phase_table(
        index_range(0, outer_size), index_range(0, inner_size), length, exponent_sign
    )
    mid_real, mid_imag = (
        mid_real * twist_real - mid_imag * twist_imag,
        mid_real * twist_imag + mid_imag * twist_real,
    )
    last_real, last_imag = phase_table(
        index_range(0, inner_size), jnp.asarray(out_blocks, jnp.int32), inner_size, exponent_sign
    )
    if lead_out:
        done_real, done_imag = complex_einsum(
            "rkq,qj->jkr", mid_real, mid_imag, last_real, last_imag
        )
        return (
            done_real.reshape(len(out_blocks) * outer_size, row_count),
            done_imag.reshape(len(out_blocks) * outer_size, row_count),
        )
    done_real, done_imag = complex_einsum("rkq,qj->rjk", mid_real, mid_imag, last_real, last_imag)
    return (
        done_real.reshape(row_count, len(out_blocks) * outer_size),
        done_imag.reshape(row_count, len(out_blocks) * outer_size),
    )


def band_blocks(padded, block, band_limit, multiple):
    top = math.ceil(band_limit) - 1
    low = list(range(top // block + 1))
    high = list(range((padded - top) // block, padded // block))
    while (len(low) + len(high)) * block % multiple:
        if len(low) <= len(high):
            low.append(low[-1] + 1)
        else:
            high.insert(0, high[0] - 1)
    return low + high


def pack_chunks(first, second, device_total, lead):
    if lead:
        width = first.shape[0] // device_total
        both = jnp.stack([first, second]).reshape(2, device_total, width, first.shape[1])
        both = both.transpose(1, 0, 2, 3)
    else:
        width = first.shape[1] // device_total
        both = jnp.stack([first, second]).reshape(2, first.shape[0], device_total, width)
        both = both.transpose(2, 0, 1, 3)
    return both.reshape(device_total, -1, 128)


def body(field_real, field_imag):
    padded = 2 * N
    quarter = padded // 4
    col_total = lax.axis_size("col")
    device_total = lax.axis_size("row") * col_total
    device = lax.axis_index("row") * col_total + lax.axis_index("col")
    strip_real, strip_imag = rows_to_strip(field_real, field_imag, col_total, 1)
    ratio_sq, band_limit = optics(padded)
    fwd_outer, fwd_inner = factor_pair(padded)
    inv_outer, inv_inner = fwd_inner, fwd_outer
    band = band_blocks(padded, fwd_outer, band_limit, device_total * 2)
    field_blocks = list(range(quarter // fwd_inner, (quarter + N) // fwd_inner))
    near_blocks = list(range(quarter // inv_outer, (quarter + N) // inv_outer))
    pick_real, pick_imag = transform_blocks(
        strip_real, strip_imag, -1.0, padded, fwd_outer, field_blocks, band
    )
    strip_rows = pick_real.shape[0]
    col_width = pick_real.shape[1] // device_total
    packed = jnp.stack([pick_real, pick_imag]).reshape(2, strip_rows, device_total, col_width)
    packed = packed.transpose(2, 0, 1, 3).reshape(device_total, -1, 128)
    arrived = one_exchange(packed, lax.axis_size("row"), col_total, 4)
    arrived = arrived.reshape(device_total, 2, strip_rows, col_width).transpose(1, 0, 2, 3)
    arrived = arrived.reshape(2, device_total * strip_rows, col_width)
    turned_real, turned_imag = arrived[0], arrived[1]
    spec_real, spec_imag = transform_blocks(
        turned_real, turned_imag, -1.0, padded, fwd_outer, field_blocks, band, lead_in=True
    )
    band_freqs = np.array(band, np.int32)[:, None] * fwd_outer + np.arange(fwd_outer, dtype=np.int32)
    freq_ids = jnp.asarray(band_freqs.reshape(-1))
    freq_signed = signed_index(freq_ids, padded).astype(jnp.float32)
    col_ids = lax.dynamic_slice(freq_ids, (device * col_width,), (col_width,))
    col_signed = signed_index(col_ids, padded).astype(jnp.float32)
    gain_real, gain_imag = transfer(col_signed, freq_signed, ratio_sq, band_limit)
    mixed_real = spec_real * gain_real - spec_imag * gain_imag
    mixed_imag = spec_real * gain_imag + spec_imag * gain_real
    inv_real, inv_imag = transform_blocks(
        mixed_real, mixed_imag, 1.0, padded, inv_outer, band, near_blocks
    )
    returned = one_exchange(
        pack_chunks(inv_real, inv_imag, device_total, False), lax.axis_size("row"), col_total, 5
    )
    returned = returned.reshape(device_total, 2, col_width, strip_rows).transpose(1, 0, 2, 3)
    returned = returned.reshape(2, device_total * col_width, strip_rows)
    line_real, line_imag = returned[0], returned[1]
    near_real, near_imag = transform_blocks(
        line_real, line_imag, 1.0, padded, inv_outer, band, near_blocks, lead_in=True
    )
    local_amp = jnp.sqrt(near_real * near_real + near_imag * near_imag)
    peak_tile = jnp.full((8, 128), jnp.max(local_amp), jnp.float32)
    tile_near_real, tile_near_imag, top = finish_exchange(
        near_real, near_imag, peak_tile, lax.axis_size("row"), col_total, 3
    )
    peak = top[0, 0]
    amplitude = jnp.sqrt(tile_near_real * tile_near_real + tile_near_imag * tile_near_imag)
    tile_rows, tile_cols = tile_near_real.shape
    row_ids = lax.axis_index("row") * tile_rows + jnp.arange(tile_rows, dtype=jnp.int32)
    col_ids_out = lax.axis_index("col") * tile_cols + jnp.arange(tile_cols, dtype=jnp.int32)
    even_cell = (row_ids[:, None] + col_ids_out[None, :]) % 2 == 0
    tile_real, tile_imag = encode(tile_near_real, tile_near_imag, amplitude, peak, even_cell)
    return (tile_real, tile_imag)


def solution(mesh):
    in_specs = (P("row", "col"), P("row", "col"))
    out_specs = (P("row", "col"), P("row", "col"))
    return jax.shard_map(body, mesh=mesh, in_specs=in_specs, out_specs=out_specs, check_vma=False)
```

```python
from functools import partial
import math

import jax
import jax.numpy as jnp
from jax import lax
from jax.sharding import PartitionSpec as P
from jax.experimental import pallas as pl
from jax.experimental.pallas import tpu as pltpu
import functools

import numpy as np

N = 4096


wavelength = 5.2e-07
distance = 0.2


def optics(padded_side):
    pitch = 2e-06 * math.sqrt(8192.0 / padded_side)
    extent = padded_side * pitch
    ratio_sq = (wavelength / extent) ** 2
    band_limit = extent / (wavelength * math.sqrt((2.0 * distance / extent) ** 2 + 1.0))
    return (ratio_sq, band_limit)


def factor_pair(length):
    bit_count = length.bit_length() - 1
    inner_size = 2 ** ((bit_count + 1) // 2)
    return (length // inner_size, inner_size)


def signed_index(index_ids, modulus):
    return jnp.where(index_ids >= modulus // 2, index_ids - modulus, index_ids)


def transfer(row_signed, col_signed, ratio_sq, band_limit):
    square = row_signed[:, None] * row_signed[:, None] + col_signed[None, :] * col_signed[None, :]
    scaled = ratio_sq * square
    phase_angle = -2.0 * math.pi * distance / wavelength * scaled / (1.0 + jnp.sqrt(1.0 - scaled))
    gauss_gain = jnp.exp(square * (-2.0 / (band_limit * band_limit)))
    inside = (jnp.abs(row_signed)[:, None] < band_limit) & (
        jnp.abs(col_signed)[None, :] < band_limit
    )
    total_gain = jnp.where(inside, gauss_gain, 0.0)
    return (total_gain * jnp.cos(phase_angle), total_gain * jnp.sin(phase_angle))


def encode(near_real, near_imag, amplitude, peak, even_cell):
    amp_level = 0.8 * amplitude / peak
    amp_floor = jnp.maximum(amplitude, 0.05 * peak)
    unit_real = near_real / amp_floor
    unit_imag = near_imag / amp_floor
    lift_part = jnp.sqrt(1.0 - amp_level * amp_level)
    cell_sign = jnp.where(even_cell, 1.0, -1.0)
    out_real = unit_real * amp_level + cell_sign * unit_imag * lift_part
    out_imag = unit_imag * amp_level - cell_sign * unit_real * lift_part
    return (out_real, out_imag)


def index_range(range_start, id_count):
    return jnp.arange(id_count, dtype=jnp.int32) + range_start


def phase_table(first_ids, second_ids, modulus, exponent_sign):
    product = first_ids[:, None] * second_ids[None, :] % modulus
    phase_arg = exponent_sign * 2.0 * math.pi / modulus * product.astype(jnp.float32)
    return (jnp.cos(phase_arg), jnp.sin(phase_arg))


def complex_einsum(form, left_real, left_imag, right_real, right_imag):
    real_dot = partial(jnp.einsum, form, precision=lax.Precision.HIGH)
    out_real = real_dot(left_real, right_real) - real_dot(left_imag, right_imag)
    out_imag = real_dot(left_real, right_imag) + real_dot(left_imag, right_real)
    return (out_real, out_imag)


def transform_last(values_real, values_imag, exponent_sign, in_start, out_start, out_count, length):
    outer_size, inner_size = factor_pair(length)
    row_count = values_real.shape[0]
    blocks_in = values_real.shape[1] // inner_size
    first_block = in_start // inner_size
    cube_real = values_real.reshape(row_count, blocks_in, inner_size)
    cube_imag = values_imag.reshape(row_count, blocks_in, inner_size)
    step_real, step_imag = phase_table(
        index_range(first_block, blocks_in), index_range(0, outer_size), outer_size, exponent_sign
    )
    mid_real, mid_imag = complex_einsum("rnq,nk->rkq", cube_real, cube_imag, step_real, step_imag)
    twist_real, twist_imag = phase_table(
        index_range(0, outer_size), index_range(0, inner_size), length, exponent_sign
    )
    mid_real, mid_imag = (
        mid_real * twist_real - mid_imag * twist_imag,
        mid_real * twist_imag + mid_imag * twist_real,
    )
    blocks_out = out_count // outer_size
    second_block = out_start // outer_size
    last_real, last_imag = phase_table(
        index_range(0, inner_size), index_range(second_block, blocks_out), inner_size, exponent_sign
    )
    done_real, done_imag = complex_einsum("rkq,qj->rjk", mid_real, mid_imag, last_real, last_imag)
    return (
        done_real.reshape(row_count, blocks_out * outer_size),
        done_imag.reshape(row_count, blocks_out * outer_size),
    )


def _allmax_kernel(nr, nc, x_ref, o_ref, buf_c, buf_r, part, ssem_c, rsem_c, ssem_r, rsem_r):
    me_r = lax.axis_index("row")
    me_c = lax.axis_index("col")
    mesh_t = pl.DeviceIdType.MESH
    barrier = pltpu.get_barrier_semaphore()
    for k in range(1, nc):
        pl.semaphore_signal(barrier, inc=1, device_id=(me_r, lax.rem(me_c + k, nc)), device_id_type=mesh_t)
    for k in range(1, nr):
        pl.semaphore_signal(barrier, inc=1, device_id=(lax.rem(me_r + k, nr), me_c), device_id_type=mesh_t)
    pl.semaphore_wait(barrier, (nc - 1) + (nr - 1))

    def col_copy(dst_c, slot):
        return pltpu.make_async_remote_copy(
            src_ref=x_ref, dst_ref=buf_c.at[slot], send_sem=ssem_c.at[dst_c],
            recv_sem=rsem_c.at[slot], device_id=(me_r, dst_c), device_id_type=mesh_t)
    sends = []
    for k in range(1, nc):
        cp = col_copy(lax.rem(me_c + k, nc), me_c)
        cp.start()
        sends.append(cp)
    acc = x_ref[...]
    for k in range(1, nc):
        src = lax.rem(me_c + nc - k, nc)
        col_copy(src, src).wait_recv()
        acc = jnp.maximum(acc, buf_c[src])
    for cp in sends:
        cp.wait_send()
    part[...] = acc

    def row_copy(dst_r, slot):
        return pltpu.make_async_remote_copy(
            src_ref=part, dst_ref=buf_r.at[slot], send_sem=ssem_r.at[dst_r],
            recv_sem=rsem_r.at[slot], device_id=(dst_r, me_c), device_id_type=mesh_t)
    sends = []
    for k in range(1, nr):
        cp = row_copy(lax.rem(me_r + k, nr), me_r)
        cp.start()
        sends.append(cp)
    for k in range(1, nr):
        src = lax.rem(me_r + nr - k, nr)
        row_copy(src, src).wait_recv()
        acc = jnp.maximum(acc, buf_r[src])
    for cp in sends:
        cp.wait_send()
    o_ref[...] = acc


def global_max(tile, nr, nc):
    return pl.pallas_call(
        functools.partial(_allmax_kernel, nr, nc),
        out_shape=jax.ShapeDtypeStruct(tile.shape, tile.dtype),
        in_specs=[pl.BlockSpec(memory_space=pltpu.VMEM)],
        out_specs=pl.BlockSpec(memory_space=pltpu.VMEM),
        scratch_shapes=[
            pltpu.VMEM((nc,) + tile.shape, tile.dtype),
            pltpu.VMEM((nr,) + tile.shape, tile.dtype),
            pltpu.VMEM(tile.shape, tile.dtype),
            pltpu.SemaphoreType.DMA((nc,)),
            pltpu.SemaphoreType.DMA((nc,)),
            pltpu.SemaphoreType.DMA((nr,)),
            pltpu.SemaphoreType.DMA((nr,)),
        ],
        compiler_params=pltpu.CompilerParams(collective_id=0, has_side_effects=True),
    )(tile)


def _col_exchange_kernel(nc, piece, place, re_ref, im_ref, re_out, im_out, send_sem, recv_sem, own_sem):
    me_r = lax.axis_index("row")
    me = lax.axis_index("col")
    mesh_t = pl.DeviceIdType.MESH
    barrier = pltpu.get_barrier_semaphore()
    for k in range(1, nc):
        pl.semaphore_signal(barrier, inc=1, device_id=(me_r, lax.rem(me + k, nc)), device_id_type=mesh_t)
    pl.semaphore_wait(barrier, nc - 1)
    srcs = (re_ref, im_ref)
    dsts = (re_out, im_out)

    def remote(peer, slot, part):
        return pltpu.make_async_remote_copy(
            src_ref=piece(srcs[part], peer), dst_ref=place(dsts[part], slot),
            send_sem=send_sem.at[peer, part], recv_sem=recv_sem.at[slot, part],
            device_id=(me_r, peer), device_id_type=mesh_t)

    sends = []
    for k in range(1, nc):
        peer = lax.rem(me + k, nc)
        for part in range(2):
            cp = remote(peer, me, part)
            cp.start()
            sends.append(cp)
    owns = []
    for part in range(2):
        cp = pltpu.make_async_copy(piece(srcs[part], me), place(dsts[part], me), own_sem.at[part])
        cp.start()
        owns.append(cp)
    for cp in owns:
        cp.wait()
    for k in range(1, nc):
        src = lax.rem(me + nc - k, nc)
        for part in range(2):
            remote(src, src, part).wait_recv()
    for cp in sends:
        cp.wait_send()


def col_exchange(re, im, out_rows, out_cols, piece, place, nc, cid):
    out = jax.ShapeDtypeStruct((out_rows, out_cols), re.dtype)
    return pl.pallas_call(
        functools.partial(_col_exchange_kernel, nc, piece, place),
        out_shape=(out, out),
        in_specs=[pl.BlockSpec(memory_space=pl.ANY)] * 2,
        out_specs=(pl.BlockSpec(memory_space=pl.ANY),) * 2,
        scratch_shapes=[
            pltpu.SemaphoreType.DMA((nc, 2)),
            pltpu.SemaphoreType.DMA((nc, 2)),
            pltpu.SemaphoreType.DMA((2,)),
        ],
        compiler_params=pltpu.CompilerParams(collective_id=cid, has_side_effects=True),
    )(re, im)


def rows_to_strip(re, im, nc, cid):
    rows, cols = re.shape
    band = rows // nc
    piece = lambda ref, p: ref.at[pl.ds(p * band, band), :]
    place = lambda ref, s: ref.at[:, pl.ds(s * cols, cols)]
    return col_exchange(re, im, band, cols * nc, piece, place, nc, cid)


def strip_to_rows(re, im, nc, cid):
    rows, cols = re.shape
    width = cols // nc
    piece = lambda ref, p: ref.at[:, pl.ds(p * width, width)]
    place = lambda ref, s: ref.at[pl.ds(s * rows, rows), :]
    return col_exchange(re, im, rows * nc, width, piece, place, nc, cid)


def _finish_kernel(nr, nc, re_ref, im_ref, peak_ref, re_out, im_out, top_out,
                   buf_c, buf_r, part, send_sem, recv_sem, own_sem, ssem_c, rsem_c, ssem_r, rsem_r):
    me_r = lax.axis_index("row")
    me = lax.axis_index("col")
    mesh_t = pl.DeviceIdType.MESH
    barrier = pltpu.get_barrier_semaphore()
    for k in range(1, nc):
        pl.semaphore_signal(barrier, inc=1, device_id=(me_r, lax.rem(me + k, nc)), device_id_type=mesh_t)
    for k in range(1, nr):
        pl.semaphore_signal(barrier, inc=1, device_id=(lax.rem(me_r + k, nr), me), device_id_type=mesh_t)
    pl.semaphore_wait(barrier, (nc - 1) + (nr - 1))

    def col_top(peer, slot):
        return pltpu.make_async_remote_copy(
            src_ref=peak_ref, dst_ref=buf_c.at[slot], send_sem=ssem_c.at[peer],
            recv_sem=rsem_c.at[slot], device_id=(me_r, peer), device_id_type=mesh_t)

    for k in range(1, nc):
        col_top(lax.rem(me + k, nc), me).start()

    rows = re_ref.shape[0]
    width = re_ref.shape[1] // nc
    srcs = (re_ref, im_ref)
    dsts = (re_out, im_out)

    def data(peer, slot, part_id):
        return pltpu.make_async_remote_copy(
            src_ref=srcs[part_id].at[:, pl.ds(peer * width, width)],
            dst_ref=dsts[part_id].at[pl.ds(slot * rows, rows), :],
            send_sem=send_sem.at[peer, part_id], recv_sem=recv_sem.at[slot, part_id],
            device_id=(me_r, peer), device_id_type=mesh_t)

    for k in range(1, nc):
        for part_id in range(2):
            data(lax.rem(me + k, nc), me, part_id).start()
    owns = []
    for part_id in range(2):
        cp = pltpu.make_async_copy(
            srcs[part_id].at[:, pl.ds(me * width, width)],
            dsts[part_id].at[pl.ds(me * rows, rows), :], own_sem.at[part_id])
        cp.start()
        owns.append(cp)

    acc = peak_ref[...]
    for k in range(1, nc):
        src = lax.rem(me + nc - k, nc)
        col_top(src, src).wait_recv()
        acc = jnp.maximum(acc, buf_c[src])
    for k in range(1, nc):
        col_top(lax.rem(me + k, nc), me).wait_send()
    part[...] = acc

    def row_top(peer, slot):
        return pltpu.make_async_remote_copy(
            src_ref=part, dst_ref=buf_r.at[slot], send_sem=ssem_r.at[peer],
            recv_sem=rsem_r.at[slot], device_id=(peer, me), device_id_type=mesh_t)

    for k in range(1, nr):
        row_top(lax.rem(me_r + k, nr), me_r).start()
    for k in range(1, nr):
        src = lax.rem(me_r + nr - k, nr)
        row_top(src, src).wait_recv()
        acc = jnp.maximum(acc, buf_r[src])
    for k in range(1, nr):
        row_top(lax.rem(me_r + k, nr), me_r).wait_send()
    top_out[...] = acc

    for cp in owns:
        cp.wait()
    for k in range(1, nc):
        src = lax.rem(me + nc - k, nc)
        for part_id in range(2):
            data(src, src, part_id).wait_recv()
            data(lax.rem(me + k, nc), me, part_id).wait_send()


def finish_exchange(re, im, peak_tile, nr, nc, cid):
    rows, cols = re.shape
    out = jax.ShapeDtypeStruct((rows * nc, cols // nc), re.dtype)
    top = jax.ShapeDtypeStruct(peak_tile.shape, peak_tile.dtype)
    return pl.pallas_call(
        functools.partial(_finish_kernel, nr, nc),
        out_shape=(out, out, top),
        in_specs=[pl.BlockSpec(memory_space=pl.ANY)] * 2 + [pl.BlockSpec(memory_space=pltpu.VMEM)],
        out_specs=(pl.BlockSpec(memory_space=pl.ANY),) * 2 + (pl.BlockSpec(memory_space=pltpu.VMEM),),
        scratch_shapes=[
            pltpu.VMEM((nc,) + peak_tile.shape, peak_tile.dtype),
            pltpu.VMEM((nr,) + peak_tile.shape, peak_tile.dtype),
            pltpu.VMEM(peak_tile.shape, peak_tile.dtype),
            pltpu.SemaphoreType.DMA((nc, 2)),
            pltpu.SemaphoreType.DMA((nc, 2)),
            pltpu.SemaphoreType.DMA((2,)),
            pltpu.SemaphoreType.DMA((nc,)),
            pltpu.SemaphoreType.DMA((nc,)),
            pltpu.SemaphoreType.DMA((nr,)),
            pltpu.SemaphoreType.DMA((nr,)),
        ],
        compiler_params=pltpu.CompilerParams(collective_id=cid, has_side_effects=True),
    )(re, im, peak_tile)


def _one_exchange_kernel(nr, nc, x_ref, x_out, send_sem, recv_sem, own_sem):
    n = nr * nc
    me = lax.axis_index("row") * nc + lax.axis_index("col")
    mesh_t = pl.DeviceIdType.MESH
    barrier = pltpu.get_barrier_semaphore()

    def where(p):
        return (p // nc, lax.rem(p, nc))

    def greet(k, carry):
        pl.semaphore_signal(barrier, inc=1, device_id=where(lax.rem(me + k, n)), device_id_type=mesh_t)
        return carry

    lax.fori_loop(1, n, greet, 0)
    pl.semaphore_wait(barrier, n - 1)

    def remote(peer, slot):
        return pltpu.make_async_remote_copy(
            src_ref=x_ref.at[peer], dst_ref=x_out.at[slot],
            send_sem=send_sem.at[peer], recv_sem=recv_sem.at[slot],
            device_id=where(peer), device_id_type=mesh_t)

    def send(k, carry):
        remote(lax.rem(me + k, n), me).start()
        return carry

    lax.fori_loop(1, n, send, 0)
    own = pltpu.make_async_copy(x_ref.at[me], x_out.at[me], own_sem.at[0])
    own.start()
    own.wait()

    def recv(k, carry):
        remote(lax.rem(me + n - k, n), lax.rem(me + n - k, n)).wait_recv()
        remote(lax.rem(me + k, n), me).wait_send()
        return carry

    lax.fori_loop(1, n, recv, 0)


def one_exchange(x, nr, nc, cid):
    n = nr * nc
    return pl.pallas_call(
        functools.partial(_one_exchange_kernel, nr, nc),
        out_shape=jax.ShapeDtypeStruct(x.shape, x.dtype),
        in_specs=[pl.BlockSpec(memory_space=pl.ANY)],
        out_specs=pl.BlockSpec(memory_space=pl.ANY),
        scratch_shapes=[
            pltpu.SemaphoreType.DMA((n,)),
            pltpu.SemaphoreType.DMA((n,)),
            pltpu.SemaphoreType.DMA((1,)),
        ],
        compiler_params=pltpu.CompilerParams(collective_id=cid, has_side_effects=True),
    )(x)


def transform_blocks(
    values_real, values_imag, exponent_sign, length, outer_size, in_blocks, out_blocks,
    lead_in=False, lead_out=False,
):
    inner_size = length // outer_size
    if lead_in:
        row_count = values_real.shape[1]
        cube_real = values_real.reshape(len(in_blocks), inner_size, row_count)
        cube_imag = values_imag.reshape(len(in_blocks), inner_size, row_count)
        first_form = "nqr,nk->rkq"
    else:
        row_count = values_real.shape[0]
        cube_real = values_real.reshape(row_count, len(in_blocks), inner_size)
        cube_imag = values_imag.reshape(row_count, len(in_blocks), inner_size)
        first_form = "rnq,nk->rkq"
    step_real, step_imag = phase_table(
        jnp.asarray(in_blocks, jnp.int32), index_range(0, outer_size), outer_size, exponent_sign
    )
    mid_real, mid_imag = complex_einsum(first_form, cube_real, cube_imag, step_real, step_imag)
    twist_real, twist_imag = phase_table(
        index_range(0, outer_size), index_range(0, inner_size), length, exponent_sign
    )
    mid_real, mid_imag = (
        mid_real * twist_real - mid_imag * twist_imag,
        mid_real * twist_imag + mid_imag * twist_real,
    )
    last_real, last_imag = phase_table(
        index_range(0, inner_size), jnp.asarray(out_blocks, jnp.int32), inner_size, exponent_sign
    )
    if lead_out:
        done_real, done_imag = complex_einsum(
            "rkq,qj->jkr", mid_real, mid_imag, last_real, last_imag
        )
        return (
            done_real.reshape(len(out_blocks) * outer_size, row_count),
            done_imag.reshape(len(out_blocks) * outer_size, row_count),
        )
    done_real, done_imag = complex_einsum("rkq,qj->rjk", mid_real, mid_imag, last_real, last_imag)
    return (
        done_real.reshape(row_count, len(out_blocks) * outer_size),
        done_imag.reshape(row_count, len(out_blocks) * outer_size),
    )


def band_blocks(padded, block, band_limit, multiple):
    top = math.ceil(band_limit) - 1
    low = list(range(top // block + 1))
    high = list(range((padded - top) // block, padded // block))
    while (len(low) + len(high)) * block % multiple:
        if len(low) <= len(high):
            low.append(low[-1] + 1)
        else:
            high.insert(0, high[0] - 1)
    return low + high


def pack_chunks(first, second, device_total, lead):
    if lead:
        width = first.shape[0] // device_total
        both = jnp.stack([first, second]).reshape(2, device_total, width, first.shape[1])
        both = both.transpose(1, 0, 2, 3)
    else:
        width = first.shape[1] // device_total
        both = jnp.stack([first, second]).reshape(2, first.shape[0], device_total, width)
        both = both.transpose(2, 0, 1, 3)
    return both.reshape(device_total, -1, 128)


def body(field_real, field_imag):
    padded = 2 * N
    quarter = padded // 4
    col_total = lax.axis_size("col")
    device_total = lax.axis_size("row") * col_total
    device = lax.axis_index("row") * col_total + lax.axis_index("col")
    strip_real, strip_imag = rows_to_strip(field_real, field_imag, col_total, 1)
    ratio_sq, band_limit = optics(padded)
    fwd_outer, fwd_inner = factor_pair(padded)
    inv_outer, inv_inner = fwd_inner, fwd_outer
    band = band_blocks(padded, fwd_outer, band_limit, device_total * 2)
    field_blocks = list(range(quarter // fwd_inner, (quarter + N) // fwd_inner))
    near_blocks = list(range(quarter // inv_outer, (quarter + N) // inv_outer))
    pick_real, pick_imag = transform_blocks(
        strip_real, strip_imag, -1.0, padded, fwd_outer, field_blocks, band
    )
    strip_rows = pick_real.shape[0]
    col_width = pick_real.shape[1] // device_total
    packed = jnp.stack([pick_real, pick_imag]).reshape(2, strip_rows, device_total, col_width)
    packed = packed.transpose(2, 0, 1, 3).reshape(device_total, -1, 128)
    arrived = one_exchange(packed, lax.axis_size("row"), col_total, 4)
    arrived = arrived.reshape(device_total, 2, strip_rows, col_width).transpose(1, 0, 2, 3)
    arrived = arrived.reshape(2, device_total * strip_rows, col_width)
    turned_real, turned_imag = arrived[0], arrived[1]
    spec_real, spec_imag = transform_blocks(
        turned_real, turned_imag, -1.0, padded, fwd_outer, field_blocks, band, lead_in=True
    )
    band_freqs = np.array(band, np.int32)[:, None] * fwd_outer + np.arange(fwd_outer, dtype=np.int32)
    freq_ids = jnp.asarray(band_freqs.reshape(-1))
    freq_signed = signed_index(freq_ids, padded).astype(jnp.float32)
    col_ids = lax.dynamic_slice(freq_ids, (device * col_width,), (col_width,))
    col_signed = signed_index(col_ids, padded).astype(jnp.float32)
    gain_real, gain_imag = transfer(col_signed, freq_signed, ratio_sq, band_limit)
    mixed_real = spec_real * gain_real - spec_imag * gain_imag
    mixed_imag = spec_real * gain_imag + spec_imag * gain_real
    inv_real, inv_imag = transform_blocks(
        mixed_real, mixed_imag, 1.0, padded, inv_outer, band, near_blocks, lead_out=True
    )
    packed = jnp.stack([inv_real, inv_imag]).reshape(2, device_total, strip_rows, col_width)
    packed = packed.transpose(1, 0, 2, 3).reshape(device_total, -1, 128)
    returned = one_exchange(packed, lax.axis_size("row"), col_total, 5)
    returned = returned.reshape(device_total, 2, strip_rows, col_width).transpose(1, 2, 0, 3)
    returned = returned.reshape(2, strip_rows, device_total * col_width)
    line_real, line_imag = returned[0], returned[1]
    near_real, near_imag = transform_blocks(
        line_real, line_imag, 1.0, padded, inv_outer, band, near_blocks
    )
    local_amp = jnp.sqrt(near_real * near_real + near_imag * near_imag)
    peak_tile = jnp.full((8, 128), jnp.max(local_amp), jnp.float32)
    tile_near_real, tile_near_imag, top = finish_exchange(
        near_real, near_imag, peak_tile, lax.axis_size("row"), col_total, 3
    )
    peak = top[0, 0]
    amplitude = jnp.sqrt(tile_near_real * tile_near_real + tile_near_imag * tile_near_imag)
    tile_rows, tile_cols = tile_near_real.shape
    row_ids = lax.axis_index("row") * tile_rows + jnp.arange(tile_rows, dtype=jnp.int32)
    col_ids_out = lax.axis_index("col") * tile_cols + jnp.arange(tile_cols, dtype=jnp.int32)
    even_cell = (row_ids[:, None] + col_ids_out[None, :]) % 2 == 0
    tile_real, tile_imag = encode(tile_near_real, tile_near_imag, amplitude, peak, even_cell)
    return (tile_real, tile_imag)


def solution(mesh):
    in_specs = (P("row", "col"), P("row", "col"))
    out_specs = (P("row", "col"), P("row", "col"))
    return jax.shard_map(body, mesh=mesh, in_specs=in_specs, out_specs=out_specs, check_vma=False)
```

```python
from functools import partial
import math

import jax
import jax.numpy as jnp
from jax import lax
from jax.sharding import PartitionSpec as P
from jax.experimental import pallas as pl
from jax.experimental.pallas import tpu as pltpu
import functools

import numpy as np

N = 4096


wavelength = 5.2e-07
distance = 0.2


def optics(padded_side):
    pitch = 2e-06 * math.sqrt(8192.0 / padded_side)
    extent = padded_side * pitch
    ratio_sq = (wavelength / extent) ** 2
    band_limit = extent / (wavelength * math.sqrt((2.0 * distance / extent) ** 2 + 1.0))
    return (ratio_sq, band_limit)


def factor_pair(length):
    bit_count = length.bit_length() - 1
    inner_size = 2 ** ((bit_count + 1) // 2)
    return (length // inner_size, inner_size)


def signed_index(index_ids, modulus):
    return jnp.where(index_ids >= modulus // 2, index_ids - modulus, index_ids)


def transfer(row_signed, col_signed, ratio_sq, band_limit):
    square = row_signed[:, None] * row_signed[:, None] + col_signed[None, :] * col_signed[None, :]
    scaled = ratio_sq * square
    phase_angle = -2.0 * math.pi * distance / wavelength * scaled / (1.0 + jnp.sqrt(1.0 - scaled))
    gauss_gain = jnp.exp(square * (-2.0 / (band_limit * band_limit)))
    inside = (jnp.abs(row_signed)[:, None] < band_limit) & (
        jnp.abs(col_signed)[None, :] < band_limit
    )
    total_gain = jnp.where(inside, gauss_gain, 0.0)
    return (total_gain * jnp.cos(phase_angle), total_gain * jnp.sin(phase_angle))


def encode(near_real, near_imag, amplitude, peak, even_cell):
    amp_level = 0.8 * amplitude / peak
    amp_floor = jnp.maximum(amplitude, 0.05 * peak)
    unit_real = near_real / amp_floor
    unit_imag = near_imag / amp_floor
    lift_part = jnp.sqrt(1.0 - amp_level * amp_level)
    cell_sign = jnp.where(even_cell, 1.0, -1.0)
    out_real = unit_real * amp_level + cell_sign * unit_imag * lift_part
    out_imag = unit_imag * amp_level - cell_sign * unit_real * lift_part
    return (out_real, out_imag)


def index_range(range_start, id_count):
    return jnp.arange(id_count, dtype=jnp.int32) + range_start


def phase_table(first_ids, second_ids, modulus, exponent_sign):
    product = first_ids[:, None] * second_ids[None, :] % modulus
    phase_arg = exponent_sign * 2.0 * math.pi / modulus * product.astype(jnp.float32)
    return (jnp.cos(phase_arg), jnp.sin(phase_arg))


def complex_einsum(form, left_real, left_imag, right_real, right_imag):
    real_dot = partial(jnp.einsum, form, precision=lax.Precision.HIGH)
    shared = real_dot(left_real + left_imag, right_real)
    out_real = shared - real_dot(left_imag, right_real + right_imag)
    out_imag = shared + real_dot(left_real, right_imag - right_real)
    return (out_real, out_imag)


def transform_last(values_real, values_imag, exponent_sign, in_start, out_start, out_count, length):
    outer_size, inner_size = factor_pair(length)
    row_count = values_real.shape[0]
    blocks_in = values_real.shape[1] // inner_size
    first_block = in_start // inner_size
    cube_real = values_real.reshape(row_count, blocks_in, inner_size)
    cube_imag = values_imag.reshape(row_count, blocks_in, inner_size)
    step_real, step_imag = phase_table(
        index_range(first_block, blocks_in), index_range(0, outer_size), outer_size, exponent_sign
    )
    mid_real, mid_imag = complex_einsum("rnq,nk->rkq", cube_real, cube_imag, step_real, step_imag)
    twist_real, twist_imag = phase_table(
        index_range(0, outer_size), index_range(0, inner_size), length, exponent_sign
    )
    mid_real, mid_imag = (
        mid_real * twist_real - mid_imag * twist_imag,
        mid_real * twist_imag + mid_imag * twist_real,
    )
    blocks_out = out_count // outer_size
    second_block = out_start // outer_size
    last_real, last_imag = phase_table(
        index_range(0, inner_size), index_range(second_block, blocks_out), inner_size, exponent_sign
    )
    done_real, done_imag = complex_einsum("rkq,qj->rjk", mid_real, mid_imag, last_real, last_imag)
    return (
        done_real.reshape(row_count, blocks_out * outer_size),
        done_imag.reshape(row_count, blocks_out * outer_size),
    )


def _allmax_kernel(nr, nc, x_ref, o_ref, buf_c, buf_r, part, ssem_c, rsem_c, ssem_r, rsem_r):
    me_r = lax.axis_index("row")
    me_c = lax.axis_index("col")
    mesh_t = pl.DeviceIdType.MESH
    barrier = pltpu.get_barrier_semaphore()
    for k in range(1, nc):
        pl.semaphore_signal(barrier, inc=1, device_id=(me_r, lax.rem(me_c + k, nc)), device_id_type=mesh_t)
    for k in range(1, nr):
        pl.semaphore_signal(barrier, inc=1, device_id=(lax.rem(me_r + k, nr), me_c), device_id_type=mesh_t)
    pl.semaphore_wait(barrier, (nc - 1) + (nr - 1))

    def col_copy(dst_c, slot):
        return pltpu.make_async_remote_copy(
            src_ref=x_ref, dst_ref=buf_c.at[slot], send_sem=ssem_c.at[dst_c],
            recv_sem=rsem_c.at[slot], device_id=(me_r, dst_c), device_id_type=mesh_t)
    sends = []
    for k in range(1, nc):
        cp = col_copy(lax.rem(me_c + k, nc), me_c)
        cp.start()
        sends.append(cp)
    acc = x_ref[...]
    for k in range(1, nc):
        src = lax.rem(me_c + nc - k, nc)
        col_copy(src, src).wait_recv()
        acc = jnp.maximum(acc, buf_c[src])
    for cp in sends:
        cp.wait_send()
    part[...] = acc

    def row_copy(dst_r, slot):
        return pltpu.make_async_remote_copy(
            src_ref=part, dst_ref=buf_r.at[slot], send_sem=ssem_r.at[dst_r],
            recv_sem=rsem_r.at[slot], device_id=(dst_r, me_c), device_id_type=mesh_t)
    sends = []
    for k in range(1, nr):
        cp = row_copy(lax.rem(me_r + k, nr), me_r)
        cp.start()
        sends.append(cp)
    for k in range(1, nr):
        src = lax.rem(me_r + nr - k, nr)
        row_copy(src, src).wait_recv()
        acc = jnp.maximum(acc, buf_r[src])
    for cp in sends:
        cp.wait_send()
    o_ref[...] = acc


def global_max(tile, nr, nc):
    return pl.pallas_call(
        functools.partial(_allmax_kernel, nr, nc),
        out_shape=jax.ShapeDtypeStruct(tile.shape, tile.dtype),
        in_specs=[pl.BlockSpec(memory_space=pltpu.VMEM)],
        out_specs=pl.BlockSpec(memory_space=pltpu.VMEM),
        scratch_shapes=[
            pltpu.VMEM((nc,) + tile.shape, tile.dtype),
            pltpu.VMEM((nr,) + tile.shape, tile.dtype),
            pltpu.VMEM(tile.shape, tile.dtype),
            pltpu.SemaphoreType.DMA((nc,)),
            pltpu.SemaphoreType.DMA((nc,)),
            pltpu.SemaphoreType.DMA((nr,)),
            pltpu.SemaphoreType.DMA((nr,)),
        ],
        compiler_params=pltpu.CompilerParams(collective_id=0, has_side_effects=True),
    )(tile)


def _col_exchange_kernel(nc, piece, place, re_ref, im_ref, re_out, im_out, send_sem, recv_sem, own_sem):
    me_r = lax.axis_index("row")
    me = lax.axis_index("col")
    mesh_t = pl.DeviceIdType.MESH
    barrier = pltpu.get_barrier_semaphore()
    for k in range(1, nc):
        pl.semaphore_signal(barrier, inc=1, device_id=(me_r, lax.rem(me + k, nc)), device_id_type=mesh_t)
    pl.semaphore_wait(barrier, nc - 1)
    srcs = (re_ref, im_ref)
    dsts = (re_out, im_out)

    def remote(peer, slot, part):
        return pltpu.make_async_remote_copy(
            src_ref=piece(srcs[part], peer), dst_ref=place(dsts[part], slot),
            send_sem=send_sem.at[peer, part], recv_sem=recv_sem.at[slot, part],
            device_id=(me_r, peer), device_id_type=mesh_t)

    sends = []
    for k in range(1, nc):
        peer = lax.rem(me + k, nc)
        for part in range(2):
            cp = remote(peer, me, part)
            cp.start()
            sends.append(cp)
    owns = []
    for part in range(2):
        cp = pltpu.make_async_copy(piece(srcs[part], me), place(dsts[part], me), own_sem.at[part])
        cp.start()
        owns.append(cp)
    for cp in owns:
        cp.wait()
    for k in range(1, nc):
        src = lax.rem(me + nc - k, nc)
        for part in range(2):
            remote(src, src, part).wait_recv()
    for cp in sends:
        cp.wait_send()


def col_exchange(re, im, out_rows, out_cols, piece, place, nc, cid):
    out = jax.ShapeDtypeStruct((out_rows, out_cols), re.dtype)
    return pl.pallas_call(
        functools.partial(_col_exchange_kernel, nc, piece, place),
        out_shape=(out, out),
        in_specs=[pl.BlockSpec(memory_space=pl.ANY)] * 2,
        out_specs=(pl.BlockSpec(memory_space=pl.ANY),) * 2,
        scratch_shapes=[
            pltpu.SemaphoreType.DMA((nc, 2)),
            pltpu.SemaphoreType.DMA((nc, 2)),
            pltpu.SemaphoreType.DMA((2,)),
        ],
        compiler_params=pltpu.CompilerParams(collective_id=cid, has_side_effects=True),
    )(re, im)


def rows_to_strip(re, im, nc, cid):
    rows, cols = re.shape
    band = rows // nc
    piece = lambda ref, p: ref.at[pl.ds(p * band, band), :]
    place = lambda ref, s: ref.at[:, pl.ds(s * cols, cols)]
    return col_exchange(re, im, band, cols * nc, piece, place, nc, cid)


def strip_to_rows(re, im, nc, cid):
    rows, cols = re.shape
    width = cols // nc
    piece = lambda ref, p: ref.at[:, pl.ds(p * width, width)]
    place = lambda ref, s: ref.at[pl.ds(s * rows, rows), :]
    return col_exchange(re, im, rows * nc, width, piece, place, nc, cid)


def _finish_kernel(nr, nc, re_ref, im_ref, peak_ref, re_out, im_out, top_out,
                   buf_c, buf_r, part, send_sem, recv_sem, own_sem, ssem_c, rsem_c, ssem_r, rsem_r):
    me_r = lax.axis_index("row")
    me = lax.axis_index("col")
    mesh_t = pl.DeviceIdType.MESH
    barrier = pltpu.get_barrier_semaphore()
    for k in range(1, nc):
        pl.semaphore_signal(barrier, inc=1, device_id=(me_r, lax.rem(me + k, nc)), device_id_type=mesh_t)
    for k in range(1, nr):
        pl.semaphore_signal(barrier, inc=1, device_id=(lax.rem(me_r + k, nr), me), device_id_type=mesh_t)
    pl.semaphore_wait(barrier, (nc - 1) + (nr - 1))

    def col_top(peer, slot):
        return pltpu.make_async_remote_copy(
            src_ref=peak_ref, dst_ref=buf_c.at[slot], send_sem=ssem_c.at[peer],
            recv_sem=rsem_c.at[slot], device_id=(me_r, peer), device_id_type=mesh_t)

    for k in range(1, nc):
        col_top(lax.rem(me + k, nc), me).start()

    rows = re_ref.shape[0]
    width = re_ref.shape[1] // nc
    srcs = (re_ref, im_ref)
    dsts = (re_out, im_out)

    def data(peer, slot, part_id):
        return pltpu.make_async_remote_copy(
            src_ref=srcs[part_id].at[:, pl.ds(peer * width, width)],
            dst_ref=dsts[part_id].at[pl.ds(slot * rows, rows), :],
            send_sem=send_sem.at[peer, part_id], recv_sem=recv_sem.at[slot, part_id],
            device_id=(me_r, peer), device_id_type=mesh_t)

    for k in range(1, nc):
        for part_id in range(2):
            data(lax.rem(me + k, nc), me, part_id).start()
    owns = []
    for part_id in range(2):
        cp = pltpu.make_async_copy(
            srcs[part_id].at[:, pl.ds(me * width, width)],
            dsts[part_id].at[pl.ds(me * rows, rows), :], own_sem.at[part_id])
        cp.start()
        owns.append(cp)

    acc = peak_ref[...]
    for k in range(1, nc):
        src = lax.rem(me + nc - k, nc)
        col_top(src, src).wait_recv()
        acc = jnp.maximum(acc, buf_c[src])
    for k in range(1, nc):
        col_top(lax.rem(me + k, nc), me).wait_send()
    part[...] = acc

    def row_top(peer, slot):
        return pltpu.make_async_remote_copy(
            src_ref=part, dst_ref=buf_r.at[slot], send_sem=ssem_r.at[peer],
            recv_sem=rsem_r.at[slot], device_id=(peer, me), device_id_type=mesh_t)

    for k in range(1, nr):
        row_top(lax.rem(me_r + k, nr), me_r).start()
    for k in range(1, nr):
        src = lax.rem(me_r + nr - k, nr)
        row_top(src, src).wait_recv()
        acc = jnp.maximum(acc, buf_r[src])
    for k in range(1, nr):
        row_top(lax.rem(me_r + k, nr), me_r).wait_send()
    top_out[...] = acc

    for cp in owns:
        cp.wait()
    for k in range(1, nc):
        src = lax.rem(me + nc - k, nc)
        for part_id in range(2):
            data(src, src, part_id).wait_recv()
            data(lax.rem(me + k, nc), me, part_id).wait_send()


def finish_exchange(re, im, peak_tile, nr, nc, cid):
    rows, cols = re.shape
    out = jax.ShapeDtypeStruct((rows * nc, cols // nc), re.dtype)
    top = jax.ShapeDtypeStruct(peak_tile.shape, peak_tile.dtype)
    return pl.pallas_call(
        functools.partial(_finish_kernel, nr, nc),
        out_shape=(out, out, top),
        in_specs=[pl.BlockSpec(memory_space=pl.ANY)] * 2 + [pl.BlockSpec(memory_space=pltpu.VMEM)],
        out_specs=(pl.BlockSpec(memory_space=pl.ANY),) * 2 + (pl.BlockSpec(memory_space=pltpu.VMEM),),
        scratch_shapes=[
            pltpu.VMEM((nc,) + peak_tile.shape, peak_tile.dtype),
            pltpu.VMEM((nr,) + peak_tile.shape, peak_tile.dtype),
            pltpu.VMEM(peak_tile.shape, peak_tile.dtype),
            pltpu.SemaphoreType.DMA((nc, 2)),
            pltpu.SemaphoreType.DMA((nc, 2)),
            pltpu.SemaphoreType.DMA((2,)),
            pltpu.SemaphoreType.DMA((nc,)),
            pltpu.SemaphoreType.DMA((nc,)),
            pltpu.SemaphoreType.DMA((nr,)),
            pltpu.SemaphoreType.DMA((nr,)),
        ],
        compiler_params=pltpu.CompilerParams(collective_id=cid, has_side_effects=True),
    )(re, im, peak_tile)


def _one_exchange_kernel(nr, nc, x_ref, x_out, send_sem, recv_sem, own_sem):
    n = nr * nc
    me = lax.axis_index("row") * nc + lax.axis_index("col")
    mesh_t = pl.DeviceIdType.MESH
    barrier = pltpu.get_barrier_semaphore()

    def where(p):
        return (p // nc, lax.rem(p, nc))

    def greet(k, carry):
        pl.semaphore_signal(barrier, inc=1, device_id=where(lax.rem(me + k, n)), device_id_type=mesh_t)
        return carry

    lax.fori_loop(1, n, greet, 0)
    pl.semaphore_wait(barrier, n - 1)

    def remote(peer, slot):
        return pltpu.make_async_remote_copy(
            src_ref=x_ref.at[peer], dst_ref=x_out.at[slot],
            send_sem=send_sem.at[peer], recv_sem=recv_sem.at[slot],
            device_id=where(peer), device_id_type=mesh_t)

    def send(k, carry):
        remote(lax.rem(me + k, n), me).start()
        return carry

    lax.fori_loop(1, n, send, 0)
    own = pltpu.make_async_copy(x_ref.at[me], x_out.at[me], own_sem.at[0])
    own.start()
    own.wait()

    def recv(k, carry):
        remote(lax.rem(me + n - k, n), lax.rem(me + n - k, n)).wait_recv()
        remote(lax.rem(me + k, n), me).wait_send()
        return carry

    lax.fori_loop(1, n, recv, 0)


def one_exchange(x, nr, nc, cid):
    n = nr * nc
    return pl.pallas_call(
        functools.partial(_one_exchange_kernel, nr, nc),
        out_shape=jax.ShapeDtypeStruct(x.shape, x.dtype),
        in_specs=[pl.BlockSpec(memory_space=pl.ANY)],
        out_specs=pl.BlockSpec(memory_space=pl.ANY),
        scratch_shapes=[
            pltpu.SemaphoreType.DMA((n,)),
            pltpu.SemaphoreType.DMA((n,)),
            pltpu.SemaphoreType.DMA((1,)),
        ],
        compiler_params=pltpu.CompilerParams(collective_id=cid, has_side_effects=True),
    )(x)


def transform_blocks(
    values_real, values_imag, exponent_sign, length, outer_size, in_blocks, out_blocks,
    lead_in=False, lead_out=False,
):
    inner_size = length // outer_size
    if lead_in:
        row_count = values_real.shape[1]
        cube_real = values_real.reshape(len(in_blocks), inner_size, row_count)
        cube_imag = values_imag.reshape(len(in_blocks), inner_size, row_count)
        first_form = "nqr,nk->rkq"
    else:
        row_count = values_real.shape[0]
        cube_real = values_real.reshape(row_count, len(in_blocks), inner_size)
        cube_imag = values_imag.reshape(row_count, len(in_blocks), inner_size)
        first_form = "rnq,nk->rkq"
    step_real, step_imag = phase_table(
        jnp.asarray(in_blocks, jnp.int32), index_range(0, outer_size), outer_size, exponent_sign
    )
    mid_real, mid_imag = complex_einsum(first_form, cube_real, cube_imag, step_real, step_imag)
    twist_real, twist_imag = phase_table(
        index_range(0, outer_size), index_range(0, inner_size), length, exponent_sign
    )
    mid_real, mid_imag = (
        mid_real * twist_real - mid_imag * twist_imag,
        mid_real * twist_imag + mid_imag * twist_real,
    )
    last_real, last_imag = phase_table(
        index_range(0, inner_size), jnp.asarray(out_blocks, jnp.int32), inner_size, exponent_sign
    )
    if lead_out:
        done_real, done_imag = complex_einsum(
            "rkq,qj->jkr", mid_real, mid_imag, last_real, last_imag
        )
        return (
            done_real.reshape(len(out_blocks) * outer_size, row_count),
            done_imag.reshape(len(out_blocks) * outer_size, row_count),
        )
    done_real, done_imag = complex_einsum("rkq,qj->rjk", mid_real, mid_imag, last_real, last_imag)
    return (
        done_real.reshape(row_count, len(out_blocks) * outer_size),
        done_imag.reshape(row_count, len(out_blocks) * outer_size),
    )


def band_blocks(padded, block, band_limit, multiple):
    top = math.ceil(band_limit) - 1
    low = list(range(top // block + 1))
    high = list(range((padded - top) // block, padded // block))
    while (len(low) + len(high)) * block % multiple:
        if len(low) <= len(high):
            low.append(low[-1] + 1)
        else:
            high.insert(0, high[0] - 1)
    return low + high


def pack_chunks(first, second, device_total, lead):
    if lead:
        width = first.shape[0] // device_total
        both = jnp.stack([first, second]).reshape(2, device_total, width, first.shape[1])
        both = both.transpose(1, 0, 2, 3)
    else:
        width = first.shape[1] // device_total
        both = jnp.stack([first, second]).reshape(2, first.shape[0], device_total, width)
        both = both.transpose(2, 0, 1, 3)
    return both.reshape(device_total, -1, 128)


def body(field_real, field_imag):
    padded = 2 * N
    quarter = padded // 4
    col_total = lax.axis_size("col")
    device_total = lax.axis_size("row") * col_total
    device = lax.axis_index("row") * col_total + lax.axis_index("col")
    strip_real, strip_imag = rows_to_strip(field_real, field_imag, col_total, 1)
    ratio_sq, band_limit = optics(padded)
    fwd_outer, fwd_inner = factor_pair(padded)
    inv_outer, inv_inner = fwd_inner, fwd_outer
    band = band_blocks(padded, fwd_outer, band_limit, device_total * 2)
    field_blocks = list(range(quarter // fwd_inner, (quarter + N) // fwd_inner))
    near_blocks = list(range(quarter // inv_outer, (quarter + N) // inv_outer))
    pick_real, pick_imag = transform_blocks(
        strip_real, strip_imag, -1.0, padded, fwd_outer, field_blocks, band
    )
    strip_rows = pick_real.shape[0]
    col_width = pick_real.shape[1] // device_total
    packed = jnp.stack([pick_real, pick_imag]).reshape(2, strip_rows, device_total, col_width)
    packed = packed.transpose(2, 0, 1, 3).reshape(device_total, -1, 128)
    arrived = one_exchange(packed, lax.axis_size("row"), col_total, 4)
    arrived = arrived.reshape(device_total, 2, strip_rows, col_width).transpose(1, 0, 2, 3)
    arrived = arrived.reshape(2, device_total * strip_rows, col_width)
    turned_real, turned_imag = arrived[0], arrived[1]
    spec_real, spec_imag = transform_blocks(
        turned_real, turned_imag, -1.0, padded, fwd_outer, field_blocks, band, lead_in=True
    )
    band_freqs = np.array(band, np.int32)[:, None] * fwd_outer + np.arange(fwd_outer, dtype=np.int32)
    freq_ids = jnp.asarray(band_freqs.reshape(-1))
    freq_signed = signed_index(freq_ids, padded).astype(jnp.float32)
    col_ids = lax.dynamic_slice(freq_ids, (device * col_width,), (col_width,))
    col_signed = signed_index(col_ids, padded).astype(jnp.float32)
    gain_real, gain_imag = transfer(col_signed, freq_signed, ratio_sq, band_limit)
    mixed_real = spec_real * gain_real - spec_imag * gain_imag
    mixed_imag = spec_real * gain_imag + spec_imag * gain_real
    inv_real, inv_imag = transform_blocks(
        mixed_real, mixed_imag, 1.0, padded, inv_outer, band, near_blocks
    )
    returned = one_exchange(
        pack_chunks(inv_real, inv_imag, device_total, False), lax.axis_size("row"), col_total, 5
    )
    returned = returned.reshape(device_total, 2, col_width, strip_rows).transpose(1, 0, 2, 3)
    returned = returned.reshape(2, device_total * col_width, strip_rows)
    line_real, line_imag = returned[0], returned[1]
    near_real, near_imag = transform_blocks(
        line_real, line_imag, 1.0, padded, inv_outer, band, near_blocks, lead_in=True
    )
    local_amp = jnp.sqrt(near_real * near_real + near_imag * near_imag)
    peak_tile = jnp.full((8, 128), jnp.max(local_amp), jnp.float32)
    tile_near_real, tile_near_imag, top = finish_exchange(
        near_real, near_imag, peak_tile, lax.axis_size("row"), col_total, 3
    )
    peak = top[0, 0]
    amplitude = jnp.sqrt(tile_near_real * tile_near_real + tile_near_imag * tile_near_imag)
    tile_rows, tile_cols = tile_near_real.shape
    row_ids = lax.axis_index("row") * tile_rows + jnp.arange(tile_rows, dtype=jnp.int32)
    col_ids_out = lax.axis_index("col") * tile_cols + jnp.arange(tile_cols, dtype=jnp.int32)
    even_cell = (row_ids[:, None] + col_ids_out[None, :]) % 2 == 0
    tile_real, tile_imag = encode(tile_near_real, tile_near_imag, amplitude, peak, even_cell)
    return (tile_real, tile_imag)


def solution(mesh):
    in_specs = (P("row", "col"), P("row", "col"))
    out_specs = (P("row", "col"), P("row", "col"))
    return jax.shard_map(body, mesh=mesh, in_specs=in_specs, out_specs=out_specs, check_vma=False)
```

```python
from functools import partial
import math

import jax
import jax.numpy as jnp
from jax import lax
from jax.sharding import PartitionSpec as P
from jax.experimental import pallas as pl
from jax.experimental.pallas import tpu as pltpu
import functools

import numpy as np

N = 4096


wavelength = 5.2e-07
distance = 0.2


def optics(padded_side):
    pitch = 2e-06 * math.sqrt(8192.0 / padded_side)
    extent = padded_side * pitch
    ratio_sq = (wavelength / extent) ** 2
    band_limit = extent / (wavelength * math.sqrt((2.0 * distance / extent) ** 2 + 1.0))
    return (ratio_sq, band_limit)


def factor_pair(length):
    bit_count = length.bit_length() - 1
    inner_size = 2 ** ((bit_count + 1) // 2)
    return (length // inner_size, inner_size)


def signed_index(index_ids, modulus):
    return jnp.where(index_ids >= modulus // 2, index_ids - modulus, index_ids)


def transfer(row_signed, col_signed, ratio_sq, band_limit):
    square = row_signed[:, None] * row_signed[:, None] + col_signed[None, :] * col_signed[None, :]
    scaled = ratio_sq * square
    phase_angle = -2.0 * math.pi * distance / wavelength * scaled / (1.0 + jnp.sqrt(1.0 - scaled))
    gauss_gain = jnp.exp(square * (-2.0 / (band_limit * band_limit)))
    inside = (jnp.abs(row_signed)[:, None] < band_limit) & (
        jnp.abs(col_signed)[None, :] < band_limit
    )
    total_gain = jnp.where(inside, gauss_gain, 0.0)
    return (total_gain * jnp.cos(phase_angle), total_gain * jnp.sin(phase_angle))


def encode(near_real, near_imag, amplitude, peak, even_cell):
    amp_level = 0.8 * amplitude / peak
    amp_floor = jnp.maximum(amplitude, 0.05 * peak)
    unit_real = near_real / amp_floor
    unit_imag = near_imag / amp_floor
    lift_part = jnp.sqrt(1.0 - amp_level * amp_level)
    cell_sign = jnp.where(even_cell, 1.0, -1.0)
    out_real = unit_real * amp_level + cell_sign * unit_imag * lift_part
    out_imag = unit_imag * amp_level - cell_sign * unit_real * lift_part
    return (out_real, out_imag)


def index_range(range_start, id_count):
    return jnp.arange(id_count, dtype=jnp.int32) + range_start


def phase_table(first_ids, second_ids, modulus, exponent_sign):
    product = first_ids[:, None] * second_ids[None, :] % modulus
    phase_arg = exponent_sign * 2.0 * math.pi / modulus * product.astype(jnp.float32)
    return (jnp.cos(phase_arg), jnp.sin(phase_arg))


def complex_einsum(form, left_real, left_imag, right_real, right_imag):
    real_dot = partial(jnp.einsum, form, precision=lax.Precision.HIGH)
    shared = real_dot(left_real + left_imag, right_real)
    out_real = shared - real_dot(left_imag, right_real + right_imag)
    out_imag = shared + real_dot(left_real, right_imag - right_real)
    return (out_real, out_imag)


def transform_last(values_real, values_imag, exponent_sign, in_start, out_start, out_count, length):
    outer_size, inner_size = factor_pair(length)
    row_count = values_real.shape[0]
    blocks_in = values_real.shape[1] // inner_size
    first_block = in_start // inner_size
    cube_real = values_real.reshape(row_count, blocks_in, inner_size)
    cube_imag = values_imag.reshape(row_count, blocks_in, inner_size)
    step_real, step_imag = phase_table(
        index_range(first_block, blocks_in), index_range(0, outer_size), outer_size, exponent_sign
    )
    mid_real, mid_imag = complex_einsum("rnq,nk->rkq", cube_real, cube_imag, step_real, step_imag)
    twist_real, twist_imag = phase_table(
        index_range(0, outer_size), index_range(0, inner_size), length, exponent_sign
    )
    mid_real, mid_imag = (
        mid_real * twist_real - mid_imag * twist_imag,
        mid_real * twist_imag + mid_imag * twist_real,
    )
    blocks_out = out_count // outer_size
    second_block = out_start // outer_size
    last_real, last_imag = phase_table(
        index_range(0, inner_size), index_range(second_block, blocks_out), inner_size, exponent_sign
    )
    done_real, done_imag = complex_einsum("rkq,qj->rjk", mid_real, mid_imag, last_real, last_imag)
    return (
        done_real.reshape(row_count, blocks_out * outer_size),
        done_imag.reshape(row_count, blocks_out * outer_size),
    )


def _allmax_kernel(nr, nc, x_ref, o_ref, buf_c, buf_r, part, ssem_c, rsem_c, ssem_r, rsem_r):
    me_r = lax.axis_index("row")
    me_c = lax.axis_index("col")
    mesh_t = pl.DeviceIdType.MESH
    barrier = pltpu.get_barrier_semaphore()
    for k in range(1, nc):
        pl.semaphore_signal(barrier, inc=1, device_id=(me_r, lax.rem(me_c + k, nc)), device_id_type=mesh_t)
    for k in range(1, nr):
        pl.semaphore_signal(barrier, inc=1, device_id=(lax.rem(me_r + k, nr), me_c), device_id_type=mesh_t)
    pl.semaphore_wait(barrier, (nc - 1) + (nr - 1))

    def col_copy(dst_c, slot):
        return pltpu.make_async_remote_copy(
            src_ref=x_ref, dst_ref=buf_c.at[slot], send_sem=ssem_c.at[dst_c],
            recv_sem=rsem_c.at[slot], device_id=(me_r, dst_c), device_id_type=mesh_t)
    sends = []
    for k in range(1, nc):
        cp = col_copy(lax.rem(me_c + k, nc), me_c)
        cp.start()
        sends.append(cp)
    acc = x_ref[...]
    for k in range(1, nc):
        src = lax.rem(me_c + nc - k, nc)
        col_copy(src, src).wait_recv()
        acc = jnp.maximum(acc, buf_c[src])
    for cp in sends:
        cp.wait_send()
    part[...] = acc

    def row_copy(dst_r, slot):
        return pltpu.make_async_remote_copy(
            src_ref=part, dst_ref=buf_r.at[slot], send_sem=ssem_r.at[dst_r],
            recv_sem=rsem_r.at[slot], device_id=(dst_r, me_c), device_id_type=mesh_t)
    sends = []
    for k in range(1, nr):
        cp = row_copy(lax.rem(me_r + k, nr), me_r)
        cp.start()
        sends.append(cp)
    for k in range(1, nr):
        src = lax.rem(me_r + nr - k, nr)
        row_copy(src, src).wait_recv()
        acc = jnp.maximum(acc, buf_r[src])
    for cp in sends:
        cp.wait_send()
    o_ref[...] = acc


def global_max(tile, nr, nc):
    return pl.pallas_call(
        functools.partial(_allmax_kernel, nr, nc),
        out_shape=jax.ShapeDtypeStruct(tile.shape, tile.dtype),
        in_specs=[pl.BlockSpec(memory_space=pltpu.VMEM)],
        out_specs=pl.BlockSpec(memory_space=pltpu.VMEM),
        scratch_shapes=[
            pltpu.VMEM((nc,) + tile.shape, tile.dtype),
            pltpu.VMEM((nr,) + tile.shape, tile.dtype),
            pltpu.VMEM(tile.shape, tile.dtype),
            pltpu.SemaphoreType.DMA((nc,)),
            pltpu.SemaphoreType.DMA((nc,)),
            pltpu.SemaphoreType.DMA((nr,)),
            pltpu.SemaphoreType.DMA((nr,)),
        ],
        compiler_params=pltpu.CompilerParams(collective_id=0, has_side_effects=True),
    )(tile)


def _col_exchange_kernel(nc, piece, place, re_ref, im_ref, re_out, im_out, send_sem, recv_sem, own_sem):
    me_r = lax.axis_index("row")
    me = lax.axis_index("col")
    mesh_t = pl.DeviceIdType.MESH
    barrier = pltpu.get_barrier_semaphore()
    for k in range(1, nc):
        pl.semaphore_signal(barrier, inc=1, device_id=(me_r, lax.rem(me + k, nc)), device_id_type=mesh_t)
    pl.semaphore_wait(barrier, nc - 1)
    srcs = (re_ref, im_ref)
    dsts = (re_out, im_out)

    def remote(peer, slot, part):
        return pltpu.make_async_remote_copy(
            src_ref=piece(srcs[part], peer), dst_ref=place(dsts[part], slot),
            send_sem=send_sem.at[peer, part], recv_sem=recv_sem.at[slot, part],
            device_id=(me_r, peer), device_id_type=mesh_t)

    sends = []
    for k in range(1, nc):
        peer = lax.rem(me + k, nc)
        for part in range(2):
            cp = remote(peer, me, part)
            cp.start()
            sends.append(cp)
    owns = []
    for part in range(2):
        cp = pltpu.make_async_copy(piece(srcs[part], me), place(dsts[part], me), own_sem.at[part])
        cp.start()
        owns.append(cp)
    for cp in owns:
        cp.wait()
    for k in range(1, nc):
        src = lax.rem(me + nc - k, nc)
        for part in range(2):
            remote(src, src, part).wait_recv()
    for cp in sends:
        cp.wait_send()


def col_exchange(re, im, out_rows, out_cols, piece, place, nc, cid):
    out = jax.ShapeDtypeStruct((out_rows, out_cols), re.dtype)
    return pl.pallas_call(
        functools.partial(_col_exchange_kernel, nc, piece, place),
        out_shape=(out, out),
        in_specs=[pl.BlockSpec(memory_space=pl.ANY)] * 2,
        out_specs=(pl.BlockSpec(memory_space=pl.ANY),) * 2,
        scratch_shapes=[
            pltpu.SemaphoreType.DMA((nc, 2)),
            pltpu.SemaphoreType.DMA((nc, 2)),
            pltpu.SemaphoreType.DMA((2,)),
        ],
        compiler_params=pltpu.CompilerParams(collective_id=cid, has_side_effects=True),
    )(re, im)


def rows_to_strip(re, im, nc, cid):
    rows, cols = re.shape
    band = rows // nc
    piece = lambda ref, p: ref.at[pl.ds(p * band, band), :]
    place = lambda ref, s: ref.at[:, pl.ds(s * cols, cols)]
    return col_exchange(re, im, band, cols * nc, piece, place, nc, cid)


def strip_to_rows(re, im, nc, cid):
    rows, cols = re.shape
    width = cols // nc
    piece = lambda ref, p: ref.at[:, pl.ds(p * width, width)]
    place = lambda ref, s: ref.at[pl.ds(s * rows, rows), :]
    return col_exchange(re, im, rows * nc, width, piece, place, nc, cid)


def _finish_kernel(nr, nc, re_ref, im_ref, peak_ref, re_out, im_out, top_out,
                   buf_c, buf_r, part, send_sem, recv_sem, own_sem, ssem_c, rsem_c, ssem_r, rsem_r):
    me_r = lax.axis_index("row")
    me = lax.axis_index("col")
    mesh_t = pl.DeviceIdType.MESH
    barrier = pltpu.get_barrier_semaphore()
    for k in range(1, nc):
        pl.semaphore_signal(barrier, inc=1, device_id=(me_r, lax.rem(me + k, nc)), device_id_type=mesh_t)
    for k in range(1, nr):
        pl.semaphore_signal(barrier, inc=1, device_id=(lax.rem(me_r + k, nr), me), device_id_type=mesh_t)
    pl.semaphore_wait(barrier, (nc - 1) + (nr - 1))

    def col_top(peer, slot):
        return pltpu.make_async_remote_copy(
            src_ref=peak_ref, dst_ref=buf_c.at[slot], send_sem=ssem_c.at[peer],
            recv_sem=rsem_c.at[slot], device_id=(me_r, peer), device_id_type=mesh_t)

    for k in range(1, nc):
        col_top(lax.rem(me + k, nc), me).start()

    rows = re_ref.shape[0]
    width = re_ref.shape[1] // nc
    srcs = (re_ref, im_ref)
    dsts = (re_out, im_out)

    def data(peer, slot, part_id):
        return pltpu.make_async_remote_copy(
            src_ref=srcs[part_id].at[:, pl.ds(peer * width, width)],
            dst_ref=dsts[part_id].at[pl.ds(slot * rows, rows), :],
            send_sem=send_sem.at[peer, part_id], recv_sem=recv_sem.at[slot, part_id],
            device_id=(me_r, peer), device_id_type=mesh_t)

    for k in range(1, nc):
        for part_id in range(2):
            data(lax.rem(me + k, nc), me, part_id).start()
    owns = []
    for part_id in range(2):
        cp = pltpu.make_async_copy(
            srcs[part_id].at[:, pl.ds(me * width, width)],
            dsts[part_id].at[pl.ds(me * rows, rows), :], own_sem.at[part_id])
        cp.start()
        owns.append(cp)

    acc = peak_ref[...]
    for k in range(1, nc):
        src = lax.rem(me + nc - k, nc)
        col_top(src, src).wait_recv()
        acc = jnp.maximum(acc, buf_c[src])
    for k in range(1, nc):
        col_top(lax.rem(me + k, nc), me).wait_send()
    part[...] = acc

    def row_top(peer, slot):
        return pltpu.make_async_remote_copy(
            src_ref=part, dst_ref=buf_r.at[slot], send_sem=ssem_r.at[peer],
            recv_sem=rsem_r.at[slot], device_id=(peer, me), device_id_type=mesh_t)

    for k in range(1, nr):
        row_top(lax.rem(me_r + k, nr), me_r).start()
    for k in range(1, nr):
        src = lax.rem(me_r + nr - k, nr)
        row_top(src, src).wait_recv()
        acc = jnp.maximum(acc, buf_r[src])
    for k in range(1, nr):
        row_top(lax.rem(me_r + k, nr), me_r).wait_send()
    top_out[...] = acc

    for cp in owns:
        cp.wait()
    for k in range(1, nc):
        src = lax.rem(me + nc - k, nc)
        for part_id in range(2):
            data(src, src, part_id).wait_recv()
            data(lax.rem(me + k, nc), me, part_id).wait_send()


def finish_exchange(re, im, peak_tile, nr, nc, cid):
    rows, cols = re.shape
    out = jax.ShapeDtypeStruct((rows * nc, cols // nc), re.dtype)
    top = jax.ShapeDtypeStruct(peak_tile.shape, peak_tile.dtype)
    return pl.pallas_call(
        functools.partial(_finish_kernel, nr, nc),
        out_shape=(out, out, top),
        in_specs=[pl.BlockSpec(memory_space=pl.ANY)] * 2 + [pl.BlockSpec(memory_space=pltpu.VMEM)],
        out_specs=(pl.BlockSpec(memory_space=pl.ANY),) * 2 + (pl.BlockSpec(memory_space=pltpu.VMEM),),
        scratch_shapes=[
            pltpu.VMEM((nc,) + peak_tile.shape, peak_tile.dtype),
            pltpu.VMEM((nr,) + peak_tile.shape, peak_tile.dtype),
            pltpu.VMEM(peak_tile.shape, peak_tile.dtype),
            pltpu.SemaphoreType.DMA((nc, 2)),
            pltpu.SemaphoreType.DMA((nc, 2)),
            pltpu.SemaphoreType.DMA((2,)),
            pltpu.SemaphoreType.DMA((nc,)),
            pltpu.SemaphoreType.DMA((nc,)),
            pltpu.SemaphoreType.DMA((nr,)),
            pltpu.SemaphoreType.DMA((nr,)),
        ],
        compiler_params=pltpu.CompilerParams(collective_id=cid, has_side_effects=True),
    )(re, im, peak_tile)


def _one_exchange_kernel(nr, nc, x_ref, x_out, send_sem, recv_sem, own_sem):
    n = nr * nc
    me = lax.axis_index("row") * nc + lax.axis_index("col")
    mesh_t = pl.DeviceIdType.MESH
    barrier = pltpu.get_barrier_semaphore()

    def where(p):
        return (p // nc, lax.rem(p, nc))

    def greet(k, carry):
        pl.semaphore_signal(barrier, inc=1, device_id=where(lax.rem(me + k, n)), device_id_type=mesh_t)
        return carry

    lax.fori_loop(1, n, greet, 0)
    pl.semaphore_wait(barrier, n - 1)

    def remote(peer, slot):
        return pltpu.make_async_remote_copy(
            src_ref=x_ref.at[peer], dst_ref=x_out.at[slot],
            send_sem=send_sem.at[peer], recv_sem=recv_sem.at[slot],
            device_id=where(peer), device_id_type=mesh_t)

    def send(k, carry):
        remote(lax.rem(me + k, n), me).start()
        return carry

    lax.fori_loop(1, n, send, 0)
    own = pltpu.make_async_copy(x_ref.at[me], x_out.at[me], own_sem.at[0])
    own.start()
    own.wait()

    def recv(k, carry):
        remote(lax.rem(me + n - k, n), lax.rem(me + n - k, n)).wait_recv()
        remote(lax.rem(me + k, n), me).wait_send()
        return carry

    lax.fori_loop(1, n, recv, 0)


def one_exchange(x, nr, nc, cid):
    n = nr * nc
    return pl.pallas_call(
        functools.partial(_one_exchange_kernel, nr, nc),
        out_shape=jax.ShapeDtypeStruct(x.shape, x.dtype),
        in_specs=[pl.BlockSpec(memory_space=pl.ANY)],
        out_specs=pl.BlockSpec(memory_space=pl.ANY),
        scratch_shapes=[
            pltpu.SemaphoreType.DMA((n,)),
            pltpu.SemaphoreType.DMA((n,)),
            pltpu.SemaphoreType.DMA((1,)),
        ],
        compiler_params=pltpu.CompilerParams(collective_id=cid, has_side_effects=True),
    )(x)


def transform_blocks(
    values_real, values_imag, exponent_sign, length, outer_size, in_blocks, out_blocks,
    lead_in=False, lead_out=False,
):
    inner_size = length // outer_size
    if lead_in:
        row_count = values_real.shape[1]
        cube_real = values_real.reshape(len(in_blocks), inner_size, row_count)
        cube_imag = values_imag.reshape(len(in_blocks), inner_size, row_count)
        first_form = "nqr,nk->rkq"
    else:
        row_count = values_real.shape[0]
        cube_real = values_real.reshape(row_count, len(in_blocks), inner_size)
        cube_imag = values_imag.reshape(row_count, len(in_blocks), inner_size)
        first_form = "rnq,nk->rkq"
    step_real, step_imag = phase_table(
        jnp.asarray(in_blocks, jnp.int32), index_range(0, outer_size), outer_size, exponent_sign
    )
    mid_real, mid_imag = complex_einsum(first_form, cube_real, cube_imag, step_real, step_imag)
    twist_real, twist_imag = phase_table(
        index_range(0, outer_size), index_range(0, inner_size), length, exponent_sign
    )
    mid_real, mid_imag = (
        mid_real * twist_real - mid_imag * twist_imag,
        mid_real * twist_imag + mid_imag * twist_real,
    )
    last_real, last_imag = phase_table(
        index_range(0, inner_size), jnp.asarray(out_blocks, jnp.int32), inner_size, exponent_sign
    )
    if lead_out:
        done_real, done_imag = complex_einsum(
            "rkq,qj->jkr", mid_real, mid_imag, last_real, last_imag
        )
        return (
            done_real.reshape(len(out_blocks) * outer_size, row_count),
            done_imag.reshape(len(out_blocks) * outer_size, row_count),
        )
    done_real, done_imag = complex_einsum("rkq,qj->rjk", mid_real, mid_imag, last_real, last_imag)
    return (
        done_real.reshape(row_count, len(out_blocks) * outer_size),
        done_imag.reshape(row_count, len(out_blocks) * outer_size),
    )


def band_blocks(padded, block, band_limit, multiple):
    top = math.ceil(band_limit) - 1
    low = list(range(top // block + 1))
    high = list(range((padded - top) // block, padded // block))
    while (len(low) + len(high)) * block % multiple:
        if len(low) <= len(high):
            low.append(low[-1] + 1)
        else:
            high.insert(0, high[0] - 1)
    return low + high


def pack_chunks(first, second, device_total, lead):
    if lead:
        width = first.shape[0] // device_total
        both = jnp.stack([first, second]).reshape(2, device_total, width, first.shape[1])
        both = both.transpose(1, 0, 2, 3)
    else:
        width = first.shape[1] // device_total
        both = jnp.stack([first, second]).reshape(2, first.shape[0], device_total, width)
        both = both.transpose(2, 0, 1, 3)
    return both.reshape(device_total, -1, 128)


def body(field_real, field_imag):
    padded = 2 * N
    quarter = padded // 4
    col_total = lax.axis_size("col")
    device_total = lax.axis_size("row") * col_total
    device = lax.axis_index("row") * col_total + lax.axis_index("col")
    strip_real, strip_imag = rows_to_strip(field_real, field_imag, col_total, 1)
    ratio_sq, band_limit = optics(padded)
    fwd_outer, fwd_inner = factor_pair(padded)
    inv_outer, inv_inner = fwd_inner, fwd_outer
    band = band_blocks(padded, fwd_outer, band_limit, device_total * 2)
    field_blocks = list(range(quarter // fwd_inner, (quarter + N) // fwd_inner))
    near_blocks = list(range(quarter // inv_outer, (quarter + N) // inv_outer))
    pick_real, pick_imag = transform_blocks(
        strip_real, strip_imag, -1.0, padded, fwd_outer, field_blocks, band
    )
    strip_rows = pick_real.shape[0]
    col_width = pick_real.shape[1] // device_total
    packed = jnp.stack([pick_real, pick_imag]).reshape(2, strip_rows, device_total, col_width)
    packed = packed.transpose(2, 0, 1, 3).reshape(device_total, -1, 128)
    arrived = one_exchange(packed, lax.axis_size("row"), col_total, 4)
    arrived = arrived.reshape(device_total, 2, strip_rows, col_width).transpose(1, 0, 2, 3)
    arrived = arrived.reshape(2, device_total * strip_rows, col_width)
    turned_real, turned_imag = arrived[0], arrived[1]
    spec_real, spec_imag = transform_blocks(
        turned_real, turned_imag, -1.0, padded, fwd_outer, field_blocks, band, lead_in=True
    )
    band_freqs = np.array(band, np.int32)[:, None] * fwd_outer + np.arange(fwd_outer, dtype=np.int32)
    freq_ids = jnp.asarray(band_freqs.reshape(-1))
    freq_signed = signed_index(freq_ids, padded).astype(jnp.float32)
    col_ids = lax.dynamic_slice(freq_ids, (device * col_width,), (col_width,))
    col_signed = signed_index(col_ids, padded).astype(jnp.float32)
    gain_real, gain_imag = transfer(col_signed, freq_signed, ratio_sq, band_limit)
    mixed_real = spec_real * gain_real - spec_imag * gain_imag
    mixed_imag = spec_real * gain_imag + spec_imag * gain_real
    inv_real, inv_imag = transform_blocks(
        mixed_real, mixed_imag, 1.0, padded, inv_outer, band, near_blocks
    )
    returned = one_exchange(
        pack_chunks(inv_real, inv_imag, device_total, False), lax.axis_size("row"), col_total, 5
    )
    returned = returned.reshape(device_total, 2, col_width, strip_rows).transpose(1, 0, 2, 3)
    returned = returned.reshape(2, device_total * col_width, strip_rows)
    line_real, line_imag = returned[0], returned[1]
    near_real, near_imag = transform_blocks(
        line_real, line_imag, 1.0, padded, inv_outer, band, near_blocks, lead_in=True
    )
    local_amp = jnp.sqrt(near_real * near_real + near_imag * near_imag)
    peak_tile = jnp.max(local_amp.reshape(-1, 8, 128), axis=0)
    tile_near_real, tile_near_imag, top = finish_exchange(
        near_real, near_imag, peak_tile, lax.axis_size("row"), col_total, 3
    )
    peak = jnp.max(top)
    amplitude = jnp.sqrt(tile_near_real * tile_near_real + tile_near_imag * tile_near_imag)
    tile_rows, tile_cols = tile_near_real.shape
    row_ids = lax.axis_index("row") * tile_rows + jnp.arange(tile_rows, dtype=jnp.int32)
    col_ids_out = lax.axis_index("col") * tile_cols + jnp.arange(tile_cols, dtype=jnp.int32)
    even_cell = (row_ids[:, None] + col_ids_out[None, :]) % 2 == 0
    tile_real, tile_imag = encode(tile_near_real, tile_near_imag, amplitude, peak, even_cell)
    return (tile_real, tile_imag)


def solution(mesh):
    in_specs = (P("row", "col"), P("row", "col"))
    out_specs = (P("row", "col"), P("row", "col"))
    return jax.shard_map(body, mesh=mesh, in_specs=in_specs, out_specs=out_specs, check_vma=False)
```

```python
from functools import partial
import math

import jax
import jax.numpy as jnp
from jax import lax
from jax.sharding import PartitionSpec as P
from jax.experimental import pallas as pl
from jax.experimental.pallas import tpu as pltpu
import functools

import numpy as np

N = 4096


wavelength = 5.2e-07
distance = 0.2


def optics(padded_side):
    pitch = 2e-06 * math.sqrt(8192.0 / padded_side)
    extent = padded_side * pitch
    ratio_sq = (wavelength / extent) ** 2
    band_limit = extent / (wavelength * math.sqrt((2.0 * distance / extent) ** 2 + 1.0))
    return (ratio_sq, band_limit)


def factor_pair(length):
    bit_count = length.bit_length() - 1
    inner_size = 2 ** ((bit_count + 1) // 2)
    return (length // inner_size, inner_size)


def signed_index(index_ids, modulus):
    return jnp.where(index_ids >= modulus // 2, index_ids - modulus, index_ids)


def transfer(row_signed, col_signed, ratio_sq, band_limit):
    square = row_signed[:, None] * row_signed[:, None] + col_signed[None, :] * col_signed[None, :]
    scaled = ratio_sq * square
    phase_angle = -2.0 * math.pi * distance / wavelength * scaled / (1.0 + jnp.sqrt(1.0 - scaled))
    gauss_gain = jnp.exp(square * (-2.0 / (band_limit * band_limit)))
    inside = (jnp.abs(row_signed)[:, None] < band_limit) & (
        jnp.abs(col_signed)[None, :] < band_limit
    )
    total_gain = jnp.where(inside, gauss_gain, 0.0)
    return (total_gain * jnp.cos(phase_angle), total_gain * jnp.sin(phase_angle))


def encode(near_real, near_imag, amplitude, peak, even_cell):
    amp_level = 0.8 * amplitude / peak
    amp_floor = jnp.maximum(amplitude, 0.05 * peak)
    unit_real = near_real / amp_floor
    unit_imag = near_imag / amp_floor
    lift_part = jnp.sqrt(1.0 - amp_level * amp_level)
    cell_sign = jnp.where(even_cell, 1.0, -1.0)
    out_real = unit_real * amp_level + cell_sign * unit_imag * lift_part
    out_imag = unit_imag * amp_level - cell_sign * unit_real * lift_part
    return (out_real, out_imag)


def index_range(range_start, id_count):
    return jnp.arange(id_count, dtype=jnp.int32) + range_start


def phase_table(first_ids, second_ids, modulus, exponent_sign):
    product = first_ids[:, None] * second_ids[None, :] % modulus
    phase_arg = exponent_sign * 2.0 * math.pi / modulus * product.astype(jnp.float32)
    return (jnp.cos(phase_arg), jnp.sin(phase_arg))


def complex_einsum(form, left_real, left_imag, right_real, right_imag):
    real_dot = partial(jnp.einsum, form, precision=lax.Precision.HIGH)
    shared = real_dot(left_real + left_imag, right_real)
    out_real = shared - real_dot(left_imag, right_real + right_imag)
    out_imag = shared + real_dot(left_real, right_imag - right_real)
    return (out_real, out_imag)


def transform_last(values_real, values_imag, exponent_sign, in_start, out_start, out_count, length):
    outer_size, inner_size = factor_pair(length)
    row_count = values_real.shape[0]
    blocks_in = values_real.shape[1] // inner_size
    first_block = in_start // inner_size
    cube_real = values_real.reshape(row_count, blocks_in, inner_size)
    cube_imag = values_imag.reshape(row_count, blocks_in, inner_size)
    step_real, step_imag = phase_table(
        index_range(first_block, blocks_in), index_range(0, outer_size), outer_size, exponent_sign
    )
    mid_real, mid_imag = complex_einsum("rnq,nk->rkq", cube_real, cube_imag, step_real, step_imag)
    twist_real, twist_imag = phase_table(
        index_range(0, outer_size), index_range(0, inner_size), length, exponent_sign
    )
    mid_real, mid_imag = (
        mid_real * twist_real - mid_imag * twist_imag,
        mid_real * twist_imag + mid_imag * twist_real,
    )
    blocks_out = out_count // outer_size
    second_block = out_start // outer_size
    last_real, last_imag = phase_table(
        index_range(0, inner_size), index_range(second_block, blocks_out), inner_size, exponent_sign
    )
    done_real, done_imag = complex_einsum("rkq,qj->rjk", mid_real, mid_imag, last_real, last_imag)
    return (
        done_real.reshape(row_count, blocks_out * outer_size),
        done_imag.reshape(row_count, blocks_out * outer_size),
    )


def _allmax_kernel(nr, nc, x_ref, o_ref, buf_c, buf_r, part, ssem_c, rsem_c, ssem_r, rsem_r):
    me_r = lax.axis_index("row")
    me_c = lax.axis_index("col")
    mesh_t = pl.DeviceIdType.MESH
    barrier = pltpu.get_barrier_semaphore()
    for k in range(1, nc):
        pl.semaphore_signal(barrier, inc=1, device_id=(me_r, lax.rem(me_c + k, nc)), device_id_type=mesh_t)
    for k in range(1, nr):
        pl.semaphore_signal(barrier, inc=1, device_id=(lax.rem(me_r + k, nr), me_c), device_id_type=mesh_t)
    pl.semaphore_wait(barrier, (nc - 1) + (nr - 1))

    def col_copy(dst_c, slot):
        return pltpu.make_async_remote_copy(
            src_ref=x_ref, dst_ref=buf_c.at[slot], send_sem=ssem_c.at[dst_c],
            recv_sem=rsem_c.at[slot], device_id=(me_r, dst_c), device_id_type=mesh_t)
    sends = []
    for k in range(1, nc):
        cp = col_copy(lax.rem(me_c + k, nc), me_c)
        cp.start()
        sends.append(cp)
    acc = x_ref[...]
    for k in range(1, nc):
        src = lax.rem(me_c + nc - k, nc)
        col_copy(src, src).wait_recv()
        acc = jnp.maximum(acc, buf_c[src])
    for cp in sends:
        cp.wait_send()
    part[...] = acc

    def row_copy(dst_r, slot):
        return pltpu.make_async_remote_copy(
            src_ref=part, dst_ref=buf_r.at[slot], send_sem=ssem_r.at[dst_r],
            recv_sem=rsem_r.at[slot], device_id=(dst_r, me_c), device_id_type=mesh_t)
    sends = []
    for k in range(1, nr):
        cp = row_copy(lax.rem(me_r + k, nr), me_r)
        cp.start()
        sends.append(cp)
    for k in range(1, nr):
        src = lax.rem(me_r + nr - k, nr)
        row_copy(src, src).wait_recv()
        acc = jnp.maximum(acc, buf_r[src])
    for cp in sends:
        cp.wait_send()
    o_ref[...] = acc


def global_max(tile, nr, nc):
    return pl.pallas_call(
        functools.partial(_allmax_kernel, nr, nc),
        out_shape=jax.ShapeDtypeStruct(tile.shape, tile.dtype),
        in_specs=[pl.BlockSpec(memory_space=pltpu.VMEM)],
        out_specs=pl.BlockSpec(memory_space=pltpu.VMEM),
        scratch_shapes=[
            pltpu.VMEM((nc,) + tile.shape, tile.dtype),
            pltpu.VMEM((nr,) + tile.shape, tile.dtype),
            pltpu.VMEM(tile.shape, tile.dtype),
            pltpu.SemaphoreType.DMA((nc,)),
            pltpu.SemaphoreType.DMA((nc,)),
            pltpu.SemaphoreType.DMA((nr,)),
            pltpu.SemaphoreType.DMA((nr,)),
        ],
        compiler_params=pltpu.CompilerParams(collective_id=0, has_side_effects=True),
    )(tile)


def _col_exchange_kernel(nc, piece, place, re_ref, im_ref, re_out, im_out, send_sem, recv_sem, own_sem):
    me_r = lax.axis_index("row")
    me = lax.axis_index("col")
    mesh_t = pl.DeviceIdType.MESH
    barrier = pltpu.get_barrier_semaphore()
    for k in range(1, nc):
        pl.semaphore_signal(barrier, inc=1, device_id=(me_r, lax.rem(me + k, nc)), device_id_type=mesh_t)
    pl.semaphore_wait(barrier, nc - 1)
    srcs = (re_ref, im_ref)
    dsts = (re_out, im_out)

    def remote(peer, slot, part):
        return pltpu.make_async_remote_copy(
            src_ref=piece(srcs[part], peer), dst_ref=place(dsts[part], slot),
            send_sem=send_sem.at[peer, part], recv_sem=recv_sem.at[slot, part],
            device_id=(me_r, peer), device_id_type=mesh_t)

    sends = []
    for k in range(1, nc):
        peer = lax.rem(me + k, nc)
        for part in range(2):
            cp = remote(peer, me, part)
            cp.start()
            sends.append(cp)
    owns = []
    for part in range(2):
        cp = pltpu.make_async_copy(piece(srcs[part], me), place(dsts[part], me), own_sem.at[part])
        cp.start()
        owns.append(cp)
    for cp in owns:
        cp.wait()
    for k in range(1, nc):
        src = lax.rem(me + nc - k, nc)
        for part in range(2):
            remote(src, src, part).wait_recv()
    for cp in sends:
        cp.wait_send()


def col_exchange(re, im, out_rows, out_cols, piece, place, nc, cid, out_shape=None):
    out = jax.ShapeDtypeStruct(out_shape or (out_rows, out_cols), re.dtype)
    return pl.pallas_call(
        functools.partial(_col_exchange_kernel, nc, piece, place),
        out_shape=(out, out),
        in_specs=[pl.BlockSpec(memory_space=pl.ANY)] * 2,
        out_specs=(pl.BlockSpec(memory_space=pl.ANY),) * 2,
        scratch_shapes=[
            pltpu.SemaphoreType.DMA((nc, 2)),
            pltpu.SemaphoreType.DMA((nc, 2)),
            pltpu.SemaphoreType.DMA((2,)),
        ],
        compiler_params=pltpu.CompilerParams(collective_id=cid, has_side_effects=True),
    )(re, im)


def rows_to_strip(re, im, nc, cid):
    rows, cols = re.shape
    band = rows // nc
    piece = lambda ref, p: ref.at[pl.ds(p * band, band), :]
    place = lambda ref, s: ref.at[s]
    blocks = col_exchange(re, im, band, cols * nc, piece, place, nc, cid, (nc, band, cols))
    return tuple(b.transpose(1, 0, 2).reshape(band, nc * cols) for b in blocks)


def strip_to_rows(re, im, nc, cid):
    rows, cols = re.shape
    width = cols // nc
    piece = lambda ref, p: ref.at[:, pl.ds(p * width, width)]
    place = lambda ref, s: ref.at[pl.ds(s * rows, rows), :]
    return col_exchange(re, im, rows * nc, width, piece, place, nc, cid)


def _finish_kernel(nr, nc, re_ref, im_ref, peak_ref, re_out, im_out, top_out,
                   buf_c, buf_r, part, send_sem, recv_sem, own_sem, ssem_c, rsem_c, ssem_r, rsem_r):
    me_r = lax.axis_index("row")
    me = lax.axis_index("col")
    mesh_t = pl.DeviceIdType.MESH
    barrier = pltpu.get_barrier_semaphore()
    for k in range(1, nc):
        pl.semaphore_signal(barrier, inc=1, device_id=(me_r, lax.rem(me + k, nc)), device_id_type=mesh_t)
    for k in range(1, nr):
        pl.semaphore_signal(barrier, inc=1, device_id=(lax.rem(me_r + k, nr), me), device_id_type=mesh_t)
    pl.semaphore_wait(barrier, (nc - 1) + (nr - 1))

    def col_top(peer, slot):
        return pltpu.make_async_remote_copy(
            src_ref=peak_ref, dst_ref=buf_c.at[slot], send_sem=ssem_c.at[peer],
            recv_sem=rsem_c.at[slot], device_id=(me_r, peer), device_id_type=mesh_t)

    for k in range(1, nc):
        col_top(lax.rem(me + k, nc), me).start()

    rows = re_ref.shape[0]
    width = re_ref.shape[1] // nc
    srcs = (re_ref, im_ref)
    dsts = (re_out, im_out)

    def data(peer, slot, part_id):
        return pltpu.make_async_remote_copy(
            src_ref=srcs[part_id].at[:, pl.ds(peer * width, width)],
            dst_ref=dsts[part_id].at[pl.ds(slot * rows, rows), :],
            send_sem=send_sem.at[peer, part_id], recv_sem=recv_sem.at[slot, part_id],
            device_id=(me_r, peer), device_id_type=mesh_t)

    for k in range(1, nc):
        for part_id in range(2):
            data(lax.rem(me + k, nc), me, part_id).start()
    owns = []
    for part_id in range(2):
        cp = pltpu.make_async_copy(
            srcs[part_id].at[:, pl.ds(me * width, width)],
            dsts[part_id].at[pl.ds(me * rows, rows), :], own_sem.at[part_id])
        cp.start()
        owns.append(cp)

    acc = peak_ref[...]
    for k in range(1, nc):
        src = lax.rem(me + nc - k, nc)
        col_top(src, src).wait_recv()
        acc = jnp.maximum(acc, buf_c[src])
    for k in range(1, nc):
        col_top(lax.rem(me + k, nc), me).wait_send()
    part[...] = acc

    def row_top(peer, slot):
        return pltpu.make_async_remote_copy(
            src_ref=part, dst_ref=buf_r.at[slot], send_sem=ssem_r.at[peer],
            recv_sem=rsem_r.at[slot], device_id=(peer, me), device_id_type=mesh_t)

    for k in range(1, nr):
        row_top(lax.rem(me_r + k, nr), me_r).start()
    for k in range(1, nr):
        src = lax.rem(me_r + nr - k, nr)
        row_top(src, src).wait_recv()
        acc = jnp.maximum(acc, buf_r[src])
    for k in range(1, nr):
        row_top(lax.rem(me_r + k, nr), me_r).wait_send()
    top_out[...] = acc

    for cp in owns:
        cp.wait()
    for k in range(1, nc):
        src = lax.rem(me + nc - k, nc)
        for part_id in range(2):
            data(src, src, part_id).wait_recv()
            data(lax.rem(me + k, nc), me, part_id).wait_send()


def finish_exchange(re, im, peak_tile, nr, nc, cid):
    rows, cols = re.shape
    out = jax.ShapeDtypeStruct((rows * nc, cols // nc), re.dtype)
    top = jax.ShapeDtypeStruct(peak_tile.shape, peak_tile.dtype)
    return pl.pallas_call(
        functools.partial(_finish_kernel, nr, nc),
        out_shape=(out, out, top),
        in_specs=[pl.BlockSpec(memory_space=pl.ANY)] * 2 + [pl.BlockSpec(memory_space=pltpu.VMEM)],
        out_specs=(pl.BlockSpec(memory_space=pl.ANY),) * 2 + (pl.BlockSpec(memory_space=pltpu.VMEM),),
        scratch_shapes=[
            pltpu.VMEM((nc,) + peak_tile.shape, peak_tile.dtype),
            pltpu.VMEM((nr,) + peak_tile.shape, peak_tile.dtype),
            pltpu.VMEM(peak_tile.shape, peak_tile.dtype),
            pltpu.SemaphoreType.DMA((nc, 2)),
            pltpu.SemaphoreType.DMA((nc, 2)),
            pltpu.SemaphoreType.DMA((2,)),
            pltpu.SemaphoreType.DMA((nc,)),
            pltpu.SemaphoreType.DMA((nc,)),
            pltpu.SemaphoreType.DMA((nr,)),
            pltpu.SemaphoreType.DMA((nr,)),
        ],
        compiler_params=pltpu.CompilerParams(collective_id=cid, has_side_effects=True),
    )(re, im, peak_tile)


def _one_exchange_kernel(nr, nc, x_ref, x_out, send_sem, recv_sem, own_sem):
    n = nr * nc
    me = lax.axis_index("row") * nc + lax.axis_index("col")
    mesh_t = pl.DeviceIdType.MESH
    barrier = pltpu.get_barrier_semaphore()

    def where(p):
        return (p // nc, lax.rem(p, nc))

    def greet(k, carry):
        pl.semaphore_signal(barrier, inc=1, device_id=where(lax.rem(me + k, n)), device_id_type=mesh_t)
        return carry

    lax.fori_loop(1, n, greet, 0)
    pl.semaphore_wait(barrier, n - 1)

    def remote(peer, slot):
        return pltpu.make_async_remote_copy(
            src_ref=x_ref.at[peer], dst_ref=x_out.at[slot],
            send_sem=send_sem.at[peer], recv_sem=recv_sem.at[slot],
            device_id=where(peer), device_id_type=mesh_t)

    def send(k, carry):
        remote(lax.rem(me + k, n), me).start()
        return carry

    lax.fori_loop(1, n, send, 0)
    own = pltpu.make_async_copy(x_ref.at[me], x_out.at[me], own_sem.at[0])
    own.start()
    own.wait()

    def recv(k, carry):
        remote(lax.rem(me + n - k, n), lax.rem(me + n - k, n)).wait_recv()
        remote(lax.rem(me + k, n), me).wait_send()
        return carry

    lax.fori_loop(1, n, recv, 0)


def one_exchange(x, nr, nc, cid):
    n = nr * nc
    return pl.pallas_call(
        functools.partial(_one_exchange_kernel, nr, nc),
        out_shape=jax.ShapeDtypeStruct(x.shape, x.dtype),
        in_specs=[pl.BlockSpec(memory_space=pl.ANY)],
        out_specs=pl.BlockSpec(memory_space=pl.ANY),
        scratch_shapes=[
            pltpu.SemaphoreType.DMA((n,)),
            pltpu.SemaphoreType.DMA((n,)),
            pltpu.SemaphoreType.DMA((1,)),
        ],
        compiler_params=pltpu.CompilerParams(collective_id=cid, has_side_effects=True),
    )(x)


def transform_blocks(
    values_real, values_imag, exponent_sign, length, outer_size, in_blocks, out_blocks,
    lead_in=False, lead_out=False,
):
    inner_size = length // outer_size
    if lead_in:
        row_count = values_real.shape[1]
        cube_real = values_real.reshape(len(in_blocks), inner_size, row_count)
        cube_imag = values_imag.reshape(len(in_blocks), inner_size, row_count)
        first_form = "nqr,nk->rkq"
    else:
        row_count = values_real.shape[0]
        cube_real = values_real.reshape(row_count, len(in_blocks), inner_size)
        cube_imag = values_imag.reshape(row_count, len(in_blocks), inner_size)
        first_form = "rnq,nk->rkq"
    step_real, step_imag = phase_table(
        jnp.asarray(in_blocks, jnp.int32), index_range(0, outer_size), outer_size, exponent_sign
    )
    mid_real, mid_imag = complex_einsum(first_form, cube_real, cube_imag, step_real, step_imag)
    twist_real, twist_imag = phase_table(
        index_range(0, outer_size), index_range(0, inner_size), length, exponent_sign
    )
    mid_real, mid_imag = (
        mid_real * twist_real - mid_imag * twist_imag,
        mid_real * twist_imag + mid_imag * twist_real,
    )
    last_real, last_imag = phase_table(
        index_range(0, inner_size), jnp.asarray(out_blocks, jnp.int32), inner_size, exponent_sign
    )
    if lead_out:
        done_real, done_imag = complex_einsum(
            "rkq,qj->jkr", mid_real, mid_imag, last_real, last_imag
        )
        return (
            done_real.reshape(len(out_blocks) * outer_size, row_count),
            done_imag.reshape(len(out_blocks) * outer_size, row_count),
        )
    done_real, done_imag = complex_einsum("rkq,qj->rjk", mid_real, mid_imag, last_real, last_imag)
    return (
        done_real.reshape(row_count, len(out_blocks) * outer_size),
        done_imag.reshape(row_count, len(out_blocks) * outer_size),
    )


def band_blocks(padded, block, band_limit, multiple):
    top = math.ceil(band_limit) - 1
    low = list(range(top // block + 1))
    high = list(range((padded - top) // block, padded // block))
    while (len(low) + len(high)) * block % multiple:
        if len(low) <= len(high):
            low.append(low[-1] + 1)
        else:
            high.insert(0, high[0] - 1)
    return low + high


def pack_chunks(first, second, device_total, lead):
    if lead:
        width = first.shape[0] // device_total
        both = jnp.stack([first, second]).reshape(2, device_total, width, first.shape[1])
        both = both.transpose(1, 0, 2, 3)
    else:
        width = first.shape[1] // device_total
        both = jnp.stack([first, second]).reshape(2, first.shape[0], device_total, width)
        both = both.transpose(2, 0, 1, 3)
    return both.reshape(device_total, -1, 128)


def body(field_real, field_imag):
    padded = 2 * N
    quarter = padded // 4
    col_total = lax.axis_size("col")
    device_total = lax.axis_size("row") * col_total
    device = lax.axis_index("row") * col_total + lax.axis_index("col")
    strip_real, strip_imag = rows_to_strip(field_real, field_imag, col_total, 1)
    ratio_sq, band_limit = optics(padded)
    fwd_outer, fwd_inner = factor_pair(padded)
    inv_outer, inv_inner = fwd_inner, fwd_outer
    band = band_blocks(padded, fwd_outer, band_limit, device_total * 2)
    field_blocks = list(range(quarter // fwd_inner, (quarter + N) // fwd_inner))
    near_blocks = list(range(quarter // inv_outer, (quarter + N) // inv_outer))
    pick_real, pick_imag = transform_blocks(
        strip_real, strip_imag, -1.0, padded, fwd_outer, field_blocks, band
    )
    strip_rows = pick_real.shape[0]
    col_width = pick_real.shape[1] // device_total
    packed = jnp.stack([pick_real, pick_imag]).reshape(2, strip_rows, device_total, col_width)
    packed = packed.transpose(2, 0, 1, 3).reshape(device_total, -1, 128)
    arrived = one_exchange(packed, lax.axis_size("row"), col_total, 4)
    arrived = arrived.reshape(device_total, 2, strip_rows, col_width).transpose(1, 0, 2, 3)
    arrived = arrived.reshape(2, device_total * strip_rows, col_width)
    turned_real, turned_imag = arrived[0], arrived[1]
    spec_real, spec_imag = transform_blocks(
        turned_real, turned_imag, -1.0, padded, fwd_outer, field_blocks, band, lead_in=True
    )
    band_freqs = np.array(band, np.int32)[:, None] * fwd_outer + np.arange(fwd_outer, dtype=np.int32)
    freq_ids = jnp.asarray(band_freqs.reshape(-1))
    freq_signed = signed_index(freq_ids, padded).astype(jnp.float32)
    col_ids = lax.dynamic_slice(freq_ids, (device * col_width,), (col_width,))
    col_signed = signed_index(col_ids, padded).astype(jnp.float32)
    gain_real, gain_imag = transfer(col_signed, freq_signed, ratio_sq, band_limit)
    mixed_real = spec_real * gain_real - spec_imag * gain_imag
    mixed_imag = spec_real * gain_imag + spec_imag * gain_real
    inv_real, inv_imag = transform_blocks(
        mixed_real, mixed_imag, 1.0, padded, inv_outer, band, near_blocks
    )
    returned = one_exchange(
        pack_chunks(inv_real, inv_imag, device_total, False), lax.axis_size("row"), col_total, 5
    )
    returned = returned.reshape(device_total, 2, col_width, strip_rows).transpose(1, 0, 2, 3)
    returned = returned.reshape(2, device_total * col_width, strip_rows)
    line_real, line_imag = returned[0], returned[1]
    near_real, near_imag = transform_blocks(
        line_real, line_imag, 1.0, padded, inv_outer, band, near_blocks, lead_in=True
    )
    local_amp = jnp.sqrt(near_real * near_real + near_imag * near_imag)
    peak_tile = jnp.max(local_amp.reshape(-1, 8, 128), axis=0)
    tile_near_real, tile_near_imag, top = finish_exchange(
        near_real, near_imag, peak_tile, lax.axis_size("row"), col_total, 3
    )
    peak = jnp.max(top)
    amplitude = jnp.sqrt(tile_near_real * tile_near_real + tile_near_imag * tile_near_imag)
    tile_rows, tile_cols = tile_near_real.shape
    row_ids = lax.axis_index("row") * tile_rows + jnp.arange(tile_rows, dtype=jnp.int32)
    col_ids_out = lax.axis_index("col") * tile_cols + jnp.arange(tile_cols, dtype=jnp.int32)
    even_cell = (row_ids[:, None] + col_ids_out[None, :]) % 2 == 0
    tile_real, tile_imag = encode(tile_near_real, tile_near_imag, amplitude, peak, even_cell)
    return (tile_real, tile_imag)


def solution(mesh):
    in_specs = (P("row", "col"), P("row", "col"))
    out_specs = (P("row", "col"), P("row", "col"))
    return jax.shard_map(body, mesh=mesh, in_specs=in_specs, out_specs=out_specs, check_vma=False)
```

```python
from functools import partial
import math

import jax
import jax.numpy as jnp
from jax import lax
from jax.sharding import PartitionSpec as P
from jax.experimental import pallas as pl
from jax.experimental.pallas import tpu as pltpu
import functools

import numpy as np

N = 4096


wavelength = 5.2e-07
distance = 0.2


def optics(padded_side):
    pitch = 2e-06 * math.sqrt(8192.0 / padded_side)
    extent = padded_side * pitch
    ratio_sq = (wavelength / extent) ** 2
    band_limit = extent / (wavelength * math.sqrt((2.0 * distance / extent) ** 2 + 1.0))
    return (ratio_sq, band_limit)


def factor_pair(length):
    bit_count = length.bit_length() - 1
    inner_size = 2 ** ((bit_count + 1) // 2)
    return (length // inner_size, inner_size)


def signed_index(index_ids, modulus):
    return jnp.where(index_ids >= modulus // 2, index_ids - modulus, index_ids)


def transfer(row_signed, col_signed, ratio_sq, band_limit):
    square = row_signed[:, None] * row_signed[:, None] + col_signed[None, :] * col_signed[None, :]
    scaled = ratio_sq * square
    phase_angle = -2.0 * math.pi * distance / wavelength * scaled / (1.0 + jnp.sqrt(1.0 - scaled))
    gauss_gain = jnp.exp(square * (-2.0 / (band_limit * band_limit)))
    inside = (jnp.abs(row_signed)[:, None] < band_limit) & (
        jnp.abs(col_signed)[None, :] < band_limit
    )
    total_gain = jnp.where(inside, gauss_gain, 0.0)
    return (total_gain * jnp.cos(phase_angle), total_gain * jnp.sin(phase_angle))


def encode(near_real, near_imag, amplitude, peak, even_cell):
    amp_level = amplitude * (0.8 / peak)
    inv_floor = 1.0 / jnp.maximum(amplitude, 0.05 * peak)
    unit_real = near_real * inv_floor
    unit_imag = near_imag * inv_floor
    lift_part = jnp.sqrt(1.0 - amp_level * amp_level)
    cell_sign = jnp.where(even_cell, 1.0, -1.0)
    out_real = unit_real * amp_level + cell_sign * unit_imag * lift_part
    out_imag = unit_imag * amp_level - cell_sign * unit_real * lift_part
    return (out_real, out_imag)


def index_range(range_start, id_count):
    return jnp.arange(id_count, dtype=jnp.int32) + range_start


def phase_table(first_ids, second_ids, modulus, exponent_sign):
    product = first_ids[:, None] * second_ids[None, :] % modulus
    phase_arg = exponent_sign * 2.0 * math.pi / modulus * product.astype(jnp.float32)
    return (jnp.cos(phase_arg), jnp.sin(phase_arg))


def complex_einsum(form, left_real, left_imag, right_real, right_imag):
    real_dot = partial(jnp.einsum, form, precision=lax.Precision.HIGH)
    shared = real_dot(left_real + left_imag, right_real)
    out_real = shared - real_dot(left_imag, right_real + right_imag)
    out_imag = shared + real_dot(left_real, right_imag - right_real)
    return (out_real, out_imag)


def transform_last(values_real, values_imag, exponent_sign, in_start, out_start, out_count, length):
    outer_size, inner_size = factor_pair(length)
    row_count = values_real.shape[0]
    blocks_in = values_real.shape[1] // inner_size
    first_block = in_start // inner_size
    cube_real = values_real.reshape(row_count, blocks_in, inner_size)
    cube_imag = values_imag.reshape(row_count, blocks_in, inner_size)
    step_real, step_imag = phase_table(
        index_range(first_block, blocks_in), index_range(0, outer_size), outer_size, exponent_sign
    )
    mid_real, mid_imag = complex_einsum("rnq,nk->rkq", cube_real, cube_imag, step_real, step_imag)
    twist_real, twist_imag = phase_table(
        index_range(0, outer_size), index_range(0, inner_size), length, exponent_sign
    )
    mid_real, mid_imag = (
        mid_real * twist_real - mid_imag * twist_imag,
        mid_real * twist_imag + mid_imag * twist_real,
    )
    blocks_out = out_count // outer_size
    second_block = out_start // outer_size
    last_real, last_imag = phase_table(
        index_range(0, inner_size), index_range(second_block, blocks_out), inner_size, exponent_sign
    )
    done_real, done_imag = complex_einsum("rkq,qj->rjk", mid_real, mid_imag, last_real, last_imag)
    return (
        done_real.reshape(row_count, blocks_out * outer_size),
        done_imag.reshape(row_count, blocks_out * outer_size),
    )


def _allmax_kernel(nr, nc, x_ref, o_ref, buf_c, buf_r, part, ssem_c, rsem_c, ssem_r, rsem_r):
    me_r = lax.axis_index("row")
    me_c = lax.axis_index("col")
    mesh_t = pl.DeviceIdType.MESH
    barrier = pltpu.get_barrier_semaphore()
    for k in range(1, nc):
        pl.semaphore_signal(barrier, inc=1, device_id=(me_r, lax.rem(me_c + k, nc)), device_id_type=mesh_t)
    for k in range(1, nr):
        pl.semaphore_signal(barrier, inc=1, device_id=(lax.rem(me_r + k, nr), me_c), device_id_type=mesh_t)
    pl.semaphore_wait(barrier, (nc - 1) + (nr - 1))

    def col_copy(dst_c, slot):
        return pltpu.make_async_remote_copy(
            src_ref=x_ref, dst_ref=buf_c.at[slot], send_sem=ssem_c.at[dst_c],
            recv_sem=rsem_c.at[slot], device_id=(me_r, dst_c), device_id_type=mesh_t)
    sends = []
    for k in range(1, nc):
        cp = col_copy(lax.rem(me_c + k, nc), me_c)
        cp.start()
        sends.append(cp)
    acc = x_ref[...]
    for k in range(1, nc):
        src = lax.rem(me_c + nc - k, nc)
        col_copy(src, src).wait_recv()
        acc = jnp.maximum(acc, buf_c[src])
    for cp in sends:
        cp.wait_send()
    part[...] = acc

    def row_copy(dst_r, slot):
        return pltpu.make_async_remote_copy(
            src_ref=part, dst_ref=buf_r.at[slot], send_sem=ssem_r.at[dst_r],
            recv_sem=rsem_r.at[slot], device_id=(dst_r, me_c), device_id_type=mesh_t)
    sends = []
    for k in range(1, nr):
        cp = row_copy(lax.rem(me_r + k, nr), me_r)
        cp.start()
        sends.append(cp)
    for k in range(1, nr):
        src = lax.rem(me_r + nr - k, nr)
        row_copy(src, src).wait_recv()
        acc = jnp.maximum(acc, buf_r[src])
    for cp in sends:
        cp.wait_send()
    o_ref[...] = acc


def global_max(tile, nr, nc):
    return pl.pallas_call(
        functools.partial(_allmax_kernel, nr, nc),
        out_shape=jax.ShapeDtypeStruct(tile.shape, tile.dtype),
        in_specs=[pl.BlockSpec(memory_space=pltpu.VMEM)],
        out_specs=pl.BlockSpec(memory_space=pltpu.VMEM),
        scratch_shapes=[
            pltpu.VMEM((nc,) + tile.shape, tile.dtype),
            pltpu.VMEM((nr,) + tile.shape, tile.dtype),
            pltpu.VMEM(tile.shape, tile.dtype),
            pltpu.SemaphoreType.DMA((nc,)),
            pltpu.SemaphoreType.DMA((nc,)),
            pltpu.SemaphoreType.DMA((nr,)),
            pltpu.SemaphoreType.DMA((nr,)),
        ],
        compiler_params=pltpu.CompilerParams(collective_id=0, has_side_effects=True),
    )(tile)


def _col_exchange_kernel(nc, piece, place, re_ref, im_ref, re_out, im_out, send_sem, recv_sem, own_sem):
    me_r = lax.axis_index("row")
    me = lax.axis_index("col")
    mesh_t = pl.DeviceIdType.MESH
    barrier = pltpu.get_barrier_semaphore()
    for k in range(1, nc):
        pl.semaphore_signal(barrier, inc=1, device_id=(me_r, lax.rem(me + k, nc)), device_id_type=mesh_t)
    pl.semaphore_wait(barrier, nc - 1)
    srcs = (re_ref, im_ref)
    dsts = (re_out, im_out)

    def remote(peer, slot, part):
        return pltpu.make_async_remote_copy(
            src_ref=piece(srcs[part], peer), dst_ref=place(dsts[part], slot),
            send_sem=send_sem.at[peer, part], recv_sem=recv_sem.at[slot, part],
            device_id=(me_r, peer), device_id_type=mesh_t)

    sends = []
    for k in range(1, nc):
        peer = lax.rem(me + k, nc)
        for part in range(2):
            cp = remote(peer, me, part)
            cp.start()
            sends.append(cp)
    owns = []
    for part in range(2):
        cp = pltpu.make_async_copy(piece(srcs[part], me), place(dsts[part], me), own_sem.at[part])
        cp.start()
        owns.append(cp)
    for cp in owns:
        cp.wait()
    for k in range(1, nc):
        src = lax.rem(me + nc - k, nc)
        for part in range(2):
            remote(src, src, part).wait_recv()
    for cp in sends:
        cp.wait_send()


def col_exchange(re, im, out_rows, out_cols, piece, place, nc, cid):
    out = jax.ShapeDtypeStruct((out_rows, out_cols), re.dtype)
    return pl.pallas_call(
        functools.partial(_col_exchange_kernel, nc, piece, place),
        out_shape=(out, out),
        in_specs=[pl.BlockSpec(memory_space=pl.ANY)] * 2,
        out_specs=(pl.BlockSpec(memory_space=pl.ANY),) * 2,
        scratch_shapes=[
            pltpu.SemaphoreType.DMA((nc, 2)),
            pltpu.SemaphoreType.DMA((nc, 2)),
            pltpu.SemaphoreType.DMA((2,)),
        ],
        compiler_params=pltpu.CompilerParams(collective_id=cid, has_side_effects=True),
    )(re, im)


def rows_to_strip(re, im, nc, cid):
    rows, cols = re.shape
    band = rows // nc
    piece = lambda ref, p: ref.at[pl.ds(p * band, band), :]
    place = lambda ref, s: ref.at[:, pl.ds(s * cols, cols)]
    return col_exchange(re, im, band, cols * nc, piece, place, nc, cid)


def strip_to_rows(re, im, nc, cid):
    rows, cols = re.shape
    width = cols // nc
    piece = lambda ref, p: ref.at[:, pl.ds(p * width, width)]
    place = lambda ref, s: ref.at[pl.ds(s * rows, rows), :]
    return col_exchange(re, im, rows * nc, width, piece, place, nc, cid)


def _finish_kernel(nr, nc, re_ref, im_ref, peak_ref, re_out, im_out, top_out,
                   buf_c, buf_r, part, send_sem, recv_sem, own_sem, ssem_c, rsem_c, ssem_r, rsem_r):
    me_r = lax.axis_index("row")
    me = lax.axis_index("col")
    mesh_t = pl.DeviceIdType.MESH
    barrier = pltpu.get_barrier_semaphore()
    for k in range(1, nc):
        pl.semaphore_signal(barrier, inc=1, device_id=(me_r, lax.rem(me + k, nc)), device_id_type=mesh_t)
    for k in range(1, nr):
        pl.semaphore_signal(barrier, inc=1, device_id=(lax.rem(me_r + k, nr), me), device_id_type=mesh_t)
    pl.semaphore_wait(barrier, (nc - 1) + (nr - 1))

    def col_top(peer, slot):
        return pltpu.make_async_remote_copy(
            src_ref=peak_ref, dst_ref=buf_c.at[slot], send_sem=ssem_c.at[peer],
            recv_sem=rsem_c.at[slot], device_id=(me_r, peer), device_id_type=mesh_t)

    for k in range(1, nc):
        col_top(lax.rem(me + k, nc), me).start()

    rows = re_ref.shape[0]
    width = re_ref.shape[1] // nc
    srcs = (re_ref, im_ref)
    dsts = (re_out, im_out)

    def data(peer, slot, part_id):
        return pltpu.make_async_remote_copy(
            src_ref=srcs[part_id].at[:, pl.ds(peer * width, width)],
            dst_ref=dsts[part_id].at[pl.ds(slot * rows, rows), :],
            send_sem=send_sem.at[peer, part_id], recv_sem=recv_sem.at[slot, part_id],
            device_id=(me_r, peer), device_id_type=mesh_t)

    for k in range(1, nc):
        for part_id in range(2):
            data(lax.rem(me + k, nc), me, part_id).start()
    owns = []
    for part_id in range(2):
        cp = pltpu.make_async_copy(
            srcs[part_id].at[:, pl.ds(me * width, width)],
            dsts[part_id].at[pl.ds(me * rows, rows), :], own_sem.at[part_id])
        cp.start()
        owns.append(cp)

    acc = peak_ref[...]
    for k in range(1, nc):
        src = lax.rem(me + nc - k, nc)
        col_top(src, src).wait_recv()
        acc = jnp.maximum(acc, buf_c[src])
    for k in range(1, nc):
        col_top(lax.rem(me + k, nc), me).wait_send()
    part[...] = acc

    def row_top(peer, slot):
        return pltpu.make_async_remote_copy(
            src_ref=part, dst_ref=buf_r.at[slot], send_sem=ssem_r.at[peer],
            recv_sem=rsem_r.at[slot], device_id=(peer, me), device_id_type=mesh_t)

    for k in range(1, nr):
        row_top(lax.rem(me_r + k, nr), me_r).start()
    for k in range(1, nr):
        src = lax.rem(me_r + nr - k, nr)
        row_top(src, src).wait_recv()
        acc = jnp.maximum(acc, buf_r[src])
    for k in range(1, nr):
        row_top(lax.rem(me_r + k, nr), me_r).wait_send()
    top_out[...] = acc

    for cp in owns:
        cp.wait()
    for k in range(1, nc):
        src = lax.rem(me + nc - k, nc)
        for part_id in range(2):
            data(src, src, part_id).wait_recv()
            data(lax.rem(me + k, nc), me, part_id).wait_send()


def finish_exchange(re, im, peak_tile, nr, nc, cid):
    rows, cols = re.shape
    out = jax.ShapeDtypeStruct((rows * nc, cols // nc), re.dtype)
    top = jax.ShapeDtypeStruct(peak_tile.shape, peak_tile.dtype)
    return pl.pallas_call(
        functools.partial(_finish_kernel, nr, nc),
        out_shape=(out, out, top),
        in_specs=[pl.BlockSpec(memory_space=pl.ANY)] * 2 + [pl.BlockSpec(memory_space=pltpu.VMEM)],
        out_specs=(pl.BlockSpec(memory_space=pl.ANY),) * 2 + (pl.BlockSpec(memory_space=pltpu.VMEM),),
        scratch_shapes=[
            pltpu.VMEM((nc,) + peak_tile.shape, peak_tile.dtype),
            pltpu.VMEM((nr,) + peak_tile.shape, peak_tile.dtype),
            pltpu.VMEM(peak_tile.shape, peak_tile.dtype),
            pltpu.SemaphoreType.DMA((nc, 2)),
            pltpu.SemaphoreType.DMA((nc, 2)),
            pltpu.SemaphoreType.DMA((2,)),
            pltpu.SemaphoreType.DMA((nc,)),
            pltpu.SemaphoreType.DMA((nc,)),
            pltpu.SemaphoreType.DMA((nr,)),
            pltpu.SemaphoreType.DMA((nr,)),
        ],
        compiler_params=pltpu.CompilerParams(collective_id=cid, has_side_effects=True),
    )(re, im, peak_tile)


def _one_exchange_kernel(nr, nc, x_ref, x_out, send_sem, recv_sem, own_sem):
    n = nr * nc
    me = lax.axis_index("row") * nc + lax.axis_index("col")
    mesh_t = pl.DeviceIdType.MESH
    barrier = pltpu.get_barrier_semaphore()

    def where(p):
        return (p // nc, lax.rem(p, nc))

    def greet(k, carry):
        pl.semaphore_signal(barrier, inc=1, device_id=where(lax.rem(me + k, n)), device_id_type=mesh_t)
        return carry

    lax.fori_loop(1, n, greet, 0)
    pl.semaphore_wait(barrier, n - 1)

    def remote(peer, slot):
        return pltpu.make_async_remote_copy(
            src_ref=x_ref.at[peer], dst_ref=x_out.at[slot],
            send_sem=send_sem.at[peer], recv_sem=recv_sem.at[slot],
            device_id=where(peer), device_id_type=mesh_t)

    def send(k, carry):
        remote(lax.rem(me + k, n), me).start()
        return carry

    lax.fori_loop(1, n, send, 0)
    own = pltpu.make_async_copy(x_ref.at[me], x_out.at[me], own_sem.at[0])
    own.start()
    own.wait()

    def recv(k, carry):
        remote(lax.rem(me + n - k, n), lax.rem(me + n - k, n)).wait_recv()
        remote(lax.rem(me + k, n), me).wait_send()
        return carry

    lax.fori_loop(1, n, recv, 0)


def one_exchange(x, nr, nc, cid):
    n = nr * nc
    return pl.pallas_call(
        functools.partial(_one_exchange_kernel, nr, nc),
        out_shape=jax.ShapeDtypeStruct(x.shape, x.dtype),
        in_specs=[pl.BlockSpec(memory_space=pl.ANY)],
        out_specs=pl.BlockSpec(memory_space=pl.ANY),
        scratch_shapes=[
            pltpu.SemaphoreType.DMA((n,)),
            pltpu.SemaphoreType.DMA((n,)),
            pltpu.SemaphoreType.DMA((1,)),
        ],
        compiler_params=pltpu.CompilerParams(collective_id=cid, has_side_effects=True),
    )(x)


def transform_blocks(
    values_real, values_imag, exponent_sign, length, outer_size, in_blocks, out_blocks,
    lead_in=False, lead_out=False,
):
    inner_size = length // outer_size
    if lead_in:
        row_count = values_real.shape[1]
        cube_real = values_real.reshape(len(in_blocks), inner_size, row_count)
        cube_imag = values_imag.reshape(len(in_blocks), inner_size, row_count)
        first_form = "nqr,nk->rkq"
    else:
        row_count = values_real.shape[0]
        cube_real = values_real.reshape(row_count, len(in_blocks), inner_size)
        cube_imag = values_imag.reshape(row_count, len(in_blocks), inner_size)
        first_form = "rnq,nk->rkq"
    step_real, step_imag = phase_table(
        jnp.asarray(in_blocks, jnp.int32), index_range(0, outer_size), outer_size, exponent_sign
    )
    mid_real, mid_imag = complex_einsum(first_form, cube_real, cube_imag, step_real, step_imag)
    twist_real, twist_imag = phase_table(
        index_range(0, outer_size), index_range(0, inner_size), length, exponent_sign
    )
    mid_real, mid_imag = (
        mid_real * twist_real - mid_imag * twist_imag,
        mid_real * twist_imag + mid_imag * twist_real,
    )
    last_real, last_imag = phase_table(
        index_range(0, inner_size), jnp.asarray(out_blocks, jnp.int32), inner_size, exponent_sign
    )
    if lead_out:
        done_real, done_imag = complex_einsum(
            "rkq,qj->jkr", mid_real, mid_imag, last_real, last_imag
        )
        return (
            done_real.reshape(len(out_blocks) * outer_size, row_count),
            done_imag.reshape(len(out_blocks) * outer_size, row_count),
        )
    done_real, done_imag = complex_einsum("rkq,qj->rjk", mid_real, mid_imag, last_real, last_imag)
    return (
        done_real.reshape(row_count, len(out_blocks) * outer_size),
        done_imag.reshape(row_count, len(out_blocks) * outer_size),
    )


def band_blocks(padded, block, band_limit, multiple):
    top = math.ceil(band_limit) - 1
    low = list(range(top // block + 1))
    high = list(range((padded - top) // block, padded // block))
    while (len(low) + len(high)) * block % multiple:
        if len(low) <= len(high):
            low.append(low[-1] + 1)
        else:
            high.insert(0, high[0] - 1)
    return low + high


def pack_chunks(first, second, device_total, lead):
    if lead:
        width = first.shape[0] // device_total
        both = jnp.stack([first, second]).reshape(2, device_total, width, first.shape[1])
        both = both.transpose(1, 0, 2, 3)
    else:
        width = first.shape[1] // device_total
        both = jnp.stack([first, second]).reshape(2, first.shape[0], device_total, width)
        both = both.transpose(2, 0, 1, 3)
    return both.reshape(device_total, -1, 128)


def body(field_real, field_imag):
    padded = 2 * N
    quarter = padded // 4
    col_total = lax.axis_size("col")
    device_total = lax.axis_size("row") * col_total
    device = lax.axis_index("row") * col_total + lax.axis_index("col")
    strip_real, strip_imag = rows_to_strip(field_real, field_imag, col_total, 1)
    ratio_sq, band_limit = optics(padded)
    fwd_outer, fwd_inner = factor_pair(padded)
    inv_outer, inv_inner = fwd_inner, fwd_outer
    band = band_blocks(padded, fwd_outer, band_limit, device_total * 2)
    field_blocks = list(range(quarter // fwd_inner, (quarter + N) // fwd_inner))
    near_blocks = list(range(quarter // inv_outer, (quarter + N) // inv_outer))
    pick_real, pick_imag = transform_blocks(
        strip_real, strip_imag, -1.0, padded, fwd_outer, field_blocks, band
    )
    strip_rows = pick_real.shape[0]
    col_width = pick_real.shape[1] // device_total
    packed = jnp.stack([pick_real, pick_imag]).reshape(2, strip_rows, device_total, col_width)
    packed = packed.transpose(2, 0, 1, 3).reshape(device_total, -1, 128)
    arrived = one_exchange(packed, lax.axis_size("row"), col_total, 4)
    arrived = arrived.reshape(device_total, 2, strip_rows, col_width).transpose(1, 0, 2, 3)
    arrived = arrived.reshape(2, device_total * strip_rows, col_width)
    turned_real, turned_imag = arrived[0], arrived[1]
    spec_real, spec_imag = transform_blocks(
        turned_real, turned_imag, -1.0, padded, fwd_outer, field_blocks, band, lead_in=True
    )
    band_freqs = np.array(band, np.int32)[:, None] * fwd_outer + np.arange(fwd_outer, dtype=np.int32)
    freq_ids = jnp.asarray(band_freqs.reshape(-1))
    freq_signed = signed_index(freq_ids, padded).astype(jnp.float32)
    col_ids = lax.dynamic_slice(freq_ids, (device * col_width,), (col_width,))
    col_signed = signed_index(col_ids, padded).astype(jnp.float32)
    gain_real, gain_imag = transfer(col_signed, freq_signed, ratio_sq, band_limit)
    mixed_real = spec_real * gain_real - spec_imag * gain_imag
    mixed_imag = spec_real * gain_imag + spec_imag * gain_real
    inv_real, inv_imag = transform_blocks(
        mixed_real, mixed_imag, 1.0, padded, inv_outer, band, near_blocks
    )
    returned = one_exchange(
        pack_chunks(inv_real, inv_imag, device_total, False), lax.axis_size("row"), col_total, 5
    )
    returned = returned.reshape(device_total, 2, col_width, strip_rows).transpose(1, 0, 2, 3)
    returned = returned.reshape(2, device_total * col_width, strip_rows)
    line_real, line_imag = returned[0], returned[1]
    near_real, near_imag = transform_blocks(
        line_real, line_imag, 1.0, padded, inv_outer, band, near_blocks, lead_in=True
    )
    local_amp = jnp.sqrt(near_real * near_real + near_imag * near_imag)
    peak_tile = jnp.max(local_amp.reshape(-1, 8, 128), axis=0)
    tile_near_real, tile_near_imag, top = finish_exchange(
        near_real, near_imag, peak_tile, lax.axis_size("row"), col_total, 3
    )
    peak = jnp.max(top)
    amplitude = jnp.sqrt(tile_near_real * tile_near_real + tile_near_imag * tile_near_imag)
    tile_rows, tile_cols = tile_near_real.shape
    row_ids = lax.axis_index("row") * tile_rows + jnp.arange(tile_rows, dtype=jnp.int32)
    col_ids_out = lax.axis_index("col") * tile_cols + jnp.arange(tile_cols, dtype=jnp.int32)
    even_cell = (row_ids[:, None] + col_ids_out[None, :]) % 2 == 0
    tile_real, tile_imag = encode(tile_near_real, tile_near_imag, amplitude, peak, even_cell)
    return (tile_real, tile_imag)


def solution(mesh):
    in_specs = (P("row", "col"), P("row", "col"))
    out_specs = (P("row", "col"), P("row", "col"))
    return jax.shard_map(body, mesh=mesh, in_specs=in_specs, out_specs=out_specs, check_vma=False)
```

```python
from functools import partial
import math

import jax
import jax.numpy as jnp
from jax import lax
from jax.sharding import PartitionSpec as P
from jax.experimental import pallas as pl
from jax.experimental.pallas import tpu as pltpu
import functools

import numpy as np

N = 4096


wavelength = 5.2e-07
distance = 0.2


def optics(padded_side):
    pitch = 2e-06 * math.sqrt(8192.0 / padded_side)
    extent = padded_side * pitch
    ratio_sq = (wavelength / extent) ** 2
    band_limit = extent / (wavelength * math.sqrt((2.0 * distance / extent) ** 2 + 1.0))
    return (ratio_sq, band_limit)


def factor_pair(length):
    bit_count = length.bit_length() - 1
    inner_size = 2 ** ((bit_count + 1) // 2)
    return (length // inner_size, inner_size)


def signed_index(index_ids, modulus):
    return jnp.where(index_ids >= modulus // 2, index_ids - modulus, index_ids)


def transfer(row_signed, col_signed, ratio_sq, band_limit):
    square = row_signed[:, None] * row_signed[:, None] + col_signed[None, :] * col_signed[None, :]
    scaled = ratio_sq * square
    phase_angle = -2.0 * math.pi * distance / wavelength * scaled / (1.0 + jnp.sqrt(1.0 - scaled))
    gauss_gain = jnp.exp(square * (-2.0 / (band_limit * band_limit)))
    inside = (jnp.abs(row_signed)[:, None] < band_limit) & (
        jnp.abs(col_signed)[None, :] < band_limit
    )
    total_gain = jnp.where(inside, gauss_gain, 0.0)
    return (total_gain * jnp.cos(phase_angle), total_gain * jnp.sin(phase_angle))


def encode(near_real, near_imag, amplitude, peak, even_cell):
    amp_level = 0.8 * amplitude / peak
    amp_floor = jnp.maximum(amplitude, 0.05 * peak)
    unit_real = near_real / amp_floor
    unit_imag = near_imag / amp_floor
    lift_part = jnp.sqrt(1.0 - amp_level * amp_level)
    cell_sign = jnp.where(even_cell, 1.0, -1.0)
    out_real = unit_real * amp_level + cell_sign * unit_imag * lift_part
    out_imag = unit_imag * amp_level - cell_sign * unit_real * lift_part
    return (out_real, out_imag)


def index_range(range_start, id_count):
    return jnp.arange(id_count, dtype=jnp.int32) + range_start


def phase_table(first_ids, second_ids, modulus, exponent_sign):
    product = first_ids[:, None] * second_ids[None, :] % modulus
    phase_arg = exponent_sign * 2.0 * math.pi / modulus * product.astype(jnp.float32)
    return (jnp.cos(phase_arg), jnp.sin(phase_arg))


def complex_einsum(form, left_real, left_imag, right_real, right_imag):
    real_dot = partial(jnp.einsum, form, precision=lax.Precision.HIGH)
    shared = real_dot(left_real + left_imag, right_real)
    out_real = shared - real_dot(left_imag, right_real + right_imag)
    out_imag = shared + real_dot(left_real, right_imag - right_real)
    return (out_real, out_imag)


def transform_last(values_real, values_imag, exponent_sign, in_start, out_start, out_count, length):
    outer_size, inner_size = factor_pair(length)
    row_count = values_real.shape[0]
    blocks_in = values_real.shape[1] // inner_size
    first_block = in_start // inner_size
    cube_real = values_real.reshape(row_count, blocks_in, inner_size)
    cube_imag = values_imag.reshape(row_count, blocks_in, inner_size)
    step_real, step_imag = phase_table(
        index_range(first_block, blocks_in), index_range(0, outer_size), outer_size, exponent_sign
    )
    mid_real, mid_imag = complex_einsum("rnq,nk->rkq", cube_real, cube_imag, step_real, step_imag)
    twist_real, twist_imag = phase_table(
        index_range(0, outer_size), index_range(0, inner_size), length, exponent_sign
    )
    mid_real, mid_imag = (
        mid_real * twist_real - mid_imag * twist_imag,
        mid_real * twist_imag + mid_imag * twist_real,
    )
    blocks_out = out_count // outer_size
    second_block = out_start // outer_size
    last_real, last_imag = phase_table(
        index_range(0, inner_size), index_range(second_block, blocks_out), inner_size, exponent_sign
    )
    done_real, done_imag = complex_einsum("rkq,qj->rjk", mid_real, mid_imag, last_real, last_imag)
    return (
        done_real.reshape(row_count, blocks_out * outer_size),
        done_imag.reshape(row_count, blocks_out * outer_size),
    )


def _allmax_kernel(nr, nc, x_ref, o_ref, buf_c, buf_r, part, ssem_c, rsem_c, ssem_r, rsem_r):
    me_r = lax.axis_index("row")
    me_c = lax.axis_index("col")
    mesh_t = pl.DeviceIdType.MESH
    barrier = pltpu.get_barrier_semaphore()
    for k in range(1, nc):
        pl.semaphore_signal(barrier, inc=1, device_id=(me_r, lax.rem(me_c + k, nc)), device_id_type=mesh_t)
    for k in range(1, nr):
        pl.semaphore_signal(barrier, inc=1, device_id=(lax.rem(me_r + k, nr), me_c), device_id_type=mesh_t)
    pl.semaphore_wait(barrier, (nc - 1) + (nr - 1))

    def col_copy(dst_c, slot):
        return pltpu.make_async_remote_copy(
            src_ref=x_ref, dst_ref=buf_c.at[slot], send_sem=ssem_c.at[dst_c],
            recv_sem=rsem_c.at[slot], device_id=(me_r, dst_c), device_id_type=mesh_t)
    sends = []
    for k in range(1, nc):
        cp = col_copy(lax.rem(me_c + k, nc), me_c)
        cp.start()
        sends.append(cp)
    acc = x_ref[...]
    for k in range(1, nc):
        src = lax.rem(me_c + nc - k, nc)
        col_copy(src, src).wait_recv()
        acc = jnp.maximum(acc, buf_c[src])
    for cp in sends:
        cp.wait_send()
    part[...] = acc

    def row_copy(dst_r, slot):
        return pltpu.make_async_remote_copy(
            src_ref=part, dst_ref=buf_r.at[slot], send_sem=ssem_r.at[dst_r],
            recv_sem=rsem_r.at[slot], device_id=(dst_r, me_c), device_id_type=mesh_t)
    sends = []
    for k in range(1, nr):
        cp = row_copy(lax.rem(me_r + k, nr), me_r)
        cp.start()
        sends.append(cp)
    for k in range(1, nr):
        src = lax.rem(me_r + nr - k, nr)
        row_copy(src, src).wait_recv()
        acc = jnp.maximum(acc, buf_r[src])
    for cp in sends:
        cp.wait_send()
    o_ref[...] = acc


def global_max(tile, nr, nc):
    return pl.pallas_call(
        functools.partial(_allmax_kernel, nr, nc),
        out_shape=jax.ShapeDtypeStruct(tile.shape, tile.dtype),
        in_specs=[pl.BlockSpec(memory_space=pltpu.VMEM)],
        out_specs=pl.BlockSpec(memory_space=pltpu.VMEM),
        scratch_shapes=[
            pltpu.VMEM((nc,) + tile.shape, tile.dtype),
            pltpu.VMEM((nr,) + tile.shape, tile.dtype),
            pltpu.VMEM(tile.shape, tile.dtype),
            pltpu.SemaphoreType.DMA((nc,)),
            pltpu.SemaphoreType.DMA((nc,)),
            pltpu.SemaphoreType.DMA((nr,)),
            pltpu.SemaphoreType.DMA((nr,)),
        ],
        compiler_params=pltpu.CompilerParams(collective_id=0, has_side_effects=True),
    )(tile)


def _col_exchange_kernel(nc, piece, place, re_ref, im_ref, re_out, im_out, send_sem, recv_sem, own_sem):
    me_r = lax.axis_index("row")
    me = lax.axis_index("col")
    mesh_t = pl.DeviceIdType.MESH
    barrier = pltpu.get_barrier_semaphore()
    for k in range(1, nc):
        pl.semaphore_signal(barrier, inc=1, device_id=(me_r, lax.rem(me + k, nc)), device_id_type=mesh_t)
    pl.semaphore_wait(barrier, nc - 1)
    srcs = (re_ref, im_ref)
    dsts = (re_out, im_out)

    def remote(peer, slot, part):
        return pltpu.make_async_remote_copy(
            src_ref=piece(srcs[part], peer), dst_ref=place(dsts[part], slot),
            send_sem=send_sem.at[peer, part], recv_sem=recv_sem.at[slot, part],
            device_id=(me_r, peer), device_id_type=mesh_t)

    sends = []
    for k in range(1, nc):
        peer = lax.rem(me + k, nc)
        for part in range(2):
            cp = remote(peer, me, part)
            cp.start()
            sends.append(cp)
    owns = []
    for part in range(2):
        cp = pltpu.make_async_copy(piece(srcs[part], me), place(dsts[part], me), own_sem.at[part])
        cp.start()
        owns.append(cp)
    for cp in owns:
        cp.wait()
    for k in range(1, nc):
        src = lax.rem(me + nc - k, nc)
        for part in range(2):
            remote(src, src, part).wait_recv()
    for cp in sends:
        cp.wait_send()


def col_exchange(re, im, out_rows, out_cols, piece, place, nc, cid):
    out = jax.ShapeDtypeStruct((out_rows, out_cols), re.dtype)
    return pl.pallas_call(
        functools.partial(_col_exchange_kernel, nc, piece, place),
        out_shape=(out, out),
        in_specs=[pl.BlockSpec(memory_space=pl.ANY)] * 2,
        out_specs=(pl.BlockSpec(memory_space=pl.ANY),) * 2,
        scratch_shapes=[
            pltpu.SemaphoreType.DMA((nc, 2)),
            pltpu.SemaphoreType.DMA((nc, 2)),
            pltpu.SemaphoreType.DMA((2,)),
        ],
        compiler_params=pltpu.CompilerParams(collective_id=cid, has_side_effects=True),
    )(re, im)


def rows_to_strip(re, im, nc, cid):
    rows, cols = re.shape
    band = rows // nc
    piece = lambda ref, p: ref.at[pl.ds(p * band, band), :]
    place = lambda ref, s: ref.at[:, pl.ds(s * cols, cols)]
    return col_exchange(re, im, band, cols * nc, piece, place, nc, cid)


def strip_to_rows(re, im, nc, cid):
    rows, cols = re.shape
    width = cols // nc
    piece = lambda ref, p: ref.at[:, pl.ds(p * width, width)]
    place = lambda ref, s: ref.at[pl.ds(s * rows, rows), :]
    return col_exchange(re, im, rows * nc, width, piece, place, nc, cid)


def _finish_kernel(nr, nc, re_ref, im_ref, peak_ref, re_out, im_out, top_out,
                   buf_c, buf_r, part, send_sem, recv_sem, own_sem, ssem_c, rsem_c, ssem_r, rsem_r):
    me_r = lax.axis_index("row")
    me = lax.axis_index("col")
    mesh_t = pl.DeviceIdType.MESH
    barrier = pltpu.get_barrier_semaphore()
    for k in range(1, nc):
        pl.semaphore_signal(barrier, inc=1, device_id=(me_r, lax.rem(me + k, nc)), device_id_type=mesh_t)
    for k in range(1, nr):
        pl.semaphore_signal(barrier, inc=1, device_id=(lax.rem(me_r + k, nr), me), device_id_type=mesh_t)
    pl.semaphore_wait(barrier, (nc - 1) + (nr - 1))

    def col_top(peer, slot):
        return pltpu.make_async_remote_copy(
            src_ref=peak_ref, dst_ref=buf_c.at[slot], send_sem=ssem_c.at[peer],
            recv_sem=rsem_c.at[slot], device_id=(me_r, peer), device_id_type=mesh_t)

    for k in range(1, nc):
        col_top(lax.rem(me + k, nc), me).start()

    rows = re_ref.shape[0]
    width = re_ref.shape[1] // nc
    srcs = (re_ref, im_ref)
    dsts = (re_out, im_out)

    def data(peer, slot, part_id):
        return pltpu.make_async_remote_copy(
            src_ref=srcs[part_id].at[:, pl.ds(peer * width, width)],
            dst_ref=dsts[part_id].at[pl.ds(slot * rows, rows), :],
            send_sem=send_sem.at[peer, part_id], recv_sem=recv_sem.at[slot, part_id],
            device_id=(me_r, peer), device_id_type=mesh_t)

    for k in range(1, nc):
        for part_id in range(2):
            data(lax.rem(me + k, nc), me, part_id).start()
    owns = []
    for part_id in range(2):
        cp = pltpu.make_async_copy(
            srcs[part_id].at[:, pl.ds(me * width, width)],
            dsts[part_id].at[pl.ds(me * rows, rows), :], own_sem.at[part_id])
        cp.start()
        owns.append(cp)

    acc = peak_ref[...]
    for k in range(1, nc):
        src = lax.rem(me + nc - k, nc)
        col_top(src, src).wait_recv()
        acc = jnp.maximum(acc, buf_c[src])
    for k in range(1, nc):
        col_top(lax.rem(me + k, nc), me).wait_send()
    part[...] = acc

    def row_top(peer, slot):
        return pltpu.make_async_remote_copy(
            src_ref=part, dst_ref=buf_r.at[slot], send_sem=ssem_r.at[peer],
            recv_sem=rsem_r.at[slot], device_id=(peer, me), device_id_type=mesh_t)

    for k in range(1, nr):
        row_top(lax.rem(me_r + k, nr), me_r).start()
    for k in range(1, nr):
        src = lax.rem(me_r + nr - k, nr)
        row_top(src, src).wait_recv()
        acc = jnp.maximum(acc, buf_r[src])
    for k in range(1, nr):
        row_top(lax.rem(me_r + k, nr), me_r).wait_send()
    top_out[...] = acc

    for cp in owns:
        cp.wait()
    for k in range(1, nc):
        src = lax.rem(me + nc - k, nc)
        for part_id in range(2):
            data(src, src, part_id).wait_recv()
            data(lax.rem(me + k, nc), me, part_id).wait_send()


def finish_exchange(re, im, peak_tile, nr, nc, cid):
    rows, cols = re.shape
    out = jax.ShapeDtypeStruct((rows * nc, cols // nc), re.dtype)
    top = jax.ShapeDtypeStruct(peak_tile.shape, peak_tile.dtype)
    return pl.pallas_call(
        functools.partial(_finish_kernel, nr, nc),
        out_shape=(out, out, top),
        in_specs=[pl.BlockSpec(memory_space=pl.ANY)] * 2 + [pl.BlockSpec(memory_space=pltpu.VMEM)],
        out_specs=(pl.BlockSpec(memory_space=pl.ANY),) * 2 + (pl.BlockSpec(memory_space=pltpu.VMEM),),
        scratch_shapes=[
            pltpu.VMEM((nc,) + peak_tile.shape, peak_tile.dtype),
            pltpu.VMEM((nr,) + peak_tile.shape, peak_tile.dtype),
            pltpu.VMEM(peak_tile.shape, peak_tile.dtype),
            pltpu.SemaphoreType.DMA((nc, 2)),
            pltpu.SemaphoreType.DMA((nc, 2)),
            pltpu.SemaphoreType.DMA((2,)),
            pltpu.SemaphoreType.DMA((nc,)),
            pltpu.SemaphoreType.DMA((nc,)),
            pltpu.SemaphoreType.DMA((nr,)),
            pltpu.SemaphoreType.DMA((nr,)),
        ],
        compiler_params=pltpu.CompilerParams(collective_id=cid, has_side_effects=True),
    )(re, im, peak_tile)


def _one_exchange_kernel(nr, nc, x_ref, x_out, send_sem, recv_sem, own_sem):
    n = nr * nc
    me = lax.axis_index("row") * nc + lax.axis_index("col")
    mesh_t = pl.DeviceIdType.MESH
    barrier = pltpu.get_barrier_semaphore()

    def where(p):
        return (p // nc, lax.rem(p, nc))

    def greet(k, carry):
        pl.semaphore_signal(barrier, inc=1, device_id=where(lax.rem(me + k, n)), device_id_type=mesh_t)
        return carry

    lax.fori_loop(1, n, greet, 0)
    pl.semaphore_wait(barrier, n - 1)

    def remote(peer, slot):
        return pltpu.make_async_remote_copy(
            src_ref=x_ref.at[peer], dst_ref=x_out.at[slot],
            send_sem=send_sem.at[peer], recv_sem=recv_sem.at[slot],
            device_id=where(peer), device_id_type=mesh_t)

    def send(k, carry):
        remote(lax.rem(me + k, n), me).start()
        return carry

    lax.fori_loop(1, n, send, 0)
    own = pltpu.make_async_copy(x_ref.at[me], x_out.at[me], own_sem.at[0])
    own.start()
    own.wait()

    def recv(k, carry):
        remote(lax.rem(me + n - k, n), lax.rem(me + n - k, n)).wait_recv()
        remote(lax.rem(me + k, n), me).wait_send()
        return carry

    lax.fori_loop(1, n, recv, 0)


def one_exchange(x, nr, nc, cid):
    n = nr * nc
    return pl.pallas_call(
        functools.partial(_one_exchange_kernel, nr, nc),
        out_shape=jax.ShapeDtypeStruct(x.shape, x.dtype),
        in_specs=[pl.BlockSpec(memory_space=pl.ANY)],
        out_specs=pl.BlockSpec(memory_space=pl.ANY),
        scratch_shapes=[
            pltpu.SemaphoreType.DMA((n,)),
            pltpu.SemaphoreType.DMA((n,)),
            pltpu.SemaphoreType.DMA((1,)),
        ],
        compiler_params=pltpu.CompilerParams(collective_id=cid, has_side_effects=True),
    )(x)


def transform_blocks(
    values_real, values_imag, exponent_sign, length, outer_size, in_blocks, out_blocks,
    lead_in=False, lead_out=False,
):
    inner_size = length // outer_size
    if lead_in:
        row_count = values_real.shape[1]
        cube_real = values_real.reshape(len(in_blocks), inner_size, row_count)
        cube_imag = values_imag.reshape(len(in_blocks), inner_size, row_count)
        first_form = "nqr,nk->rkq"
    else:
        row_count = values_real.shape[0]
        cube_real = values_real.reshape(row_count, len(in_blocks), inner_size)
        cube_imag = values_imag.reshape(row_count, len(in_blocks), inner_size)
        first_form = "rnq,nk->rkq"
    step_real, step_imag = phase_table(
        jnp.asarray(in_blocks, jnp.int32), index_range(0, outer_size), outer_size, exponent_sign
    )
    mid_real, mid_imag = complex_einsum(first_form, cube_real, cube_imag, step_real, step_imag)
    twist_real, twist_imag = phase_table(
        index_range(0, outer_size), index_range(0, inner_size), length, exponent_sign
    )
    last_real, last_imag = phase_table(
        index_range(0, inner_size), jnp.asarray(out_blocks, jnp.int32), inner_size, exponent_sign
    )
    last_real, last_imag = (
        twist_real[:, :, None] * last_real[None] - twist_imag[:, :, None] * last_imag[None],
        twist_real[:, :, None] * last_imag[None] + twist_imag[:, :, None] * last_real[None],
    )
    if lead_out:
        done_real, done_imag = complex_einsum(
            "rkq,kqj->jkr", mid_real, mid_imag, last_real, last_imag
        )
        return (
            done_real.reshape(len(out_blocks) * outer_size, row_count),
            done_imag.reshape(len(out_blocks) * outer_size, row_count),
        )
    done_real, done_imag = complex_einsum("rkq,kqj->rjk", mid_real, mid_imag, last_real, last_imag)
    return (
        done_real.reshape(row_count, len(out_blocks) * outer_size),
        done_imag.reshape(row_count, len(out_blocks) * outer_size),
    )


def band_blocks(padded, block, band_limit, multiple):
    top = math.ceil(band_limit) - 1
    low = list(range(top // block + 1))
    high = list(range((padded - top) // block, padded // block))
    while (len(low) + len(high)) * block % multiple:
        if len(low) <= len(high):
            low.append(low[-1] + 1)
        else:
            high.insert(0, high[0] - 1)
    return low + high


def pack_chunks(first, second, device_total, lead):
    if lead:
        width = first.shape[0] // device_total
        both = jnp.stack([first, second]).reshape(2, device_total, width, first.shape[1])
        both = both.transpose(1, 0, 2, 3)
    else:
        width = first.shape[1] // device_total
        both = jnp.stack([first, second]).reshape(2, first.shape[0], device_total, width)
        both = both.transpose(2, 0, 1, 3)
    return both.reshape(device_total, -1, 128)


def body(field_real, field_imag):
    padded = 2 * N
    quarter = padded // 4
    col_total = lax.axis_size("col")
    device_total = lax.axis_size("row") * col_total
    device = lax.axis_index("row") * col_total + lax.axis_index("col")
    strip_real, strip_imag = rows_to_strip(field_real, field_imag, col_total, 1)
    ratio_sq, band_limit = optics(padded)
    fwd_outer, fwd_inner = factor_pair(padded)
    inv_outer, inv_inner = fwd_inner, fwd_outer
    band = band_blocks(padded, fwd_outer, band_limit, device_total * 2)
    field_blocks = list(range(quarter // fwd_inner, (quarter + N) // fwd_inner))
    near_blocks = list(range(quarter // inv_outer, (quarter + N) // inv_outer))
    pick_real, pick_imag = transform_blocks(
        strip_real, strip_imag, -1.0, padded, fwd_outer, field_blocks, band
    )
    strip_rows = pick_real.shape[0]
    col_width = pick_real.shape[1] // device_total
    packed = jnp.stack([pick_real, pick_imag]).reshape(2, strip_rows, device_total, col_width)
    packed = packed.transpose(2, 0, 1, 3).reshape(device_total, -1, 128)
    arrived = one_exchange(packed, lax.axis_size("row"), col_total, 4)
    arrived = arrived.reshape(device_total, 2, strip_rows, col_width).transpose(1, 0, 2, 3)
    arrived = arrived.reshape(2, device_total * strip_rows, col_width)
    turned_real, turned_imag = arrived[0], arrived[1]
    spec_real, spec_imag = transform_blocks(
        turned_real, turned_imag, -1.0, padded, fwd_outer, field_blocks, band, lead_in=True
    )
    band_freqs = np.array(band, np.int32)[:, None] * fwd_outer + np.arange(fwd_outer, dtype=np.int32)
    freq_ids = jnp.asarray(band_freqs.reshape(-1))
    freq_signed = signed_index(freq_ids, padded).astype(jnp.float32)
    col_ids = lax.dynamic_slice(freq_ids, (device * col_width,), (col_width,))
    col_signed = signed_index(col_ids, padded).astype(jnp.float32)
    gain_real, gain_imag = transfer(col_signed, freq_signed, ratio_sq, band_limit)
    mixed_real = spec_real * gain_real - spec_imag * gain_imag
    mixed_imag = spec_real * gain_imag + spec_imag * gain_real
    inv_real, inv_imag = transform_blocks(
        mixed_real, mixed_imag, 1.0, padded, inv_outer, band, near_blocks
    )
    returned = one_exchange(
        pack_chunks(inv_real, inv_imag, device_total, False), lax.axis_size("row"), col_total, 5
    )
    returned = returned.reshape(device_total, 2, col_width, strip_rows).transpose(1, 0, 2, 3)
    returned = returned.reshape(2, device_total * col_width, strip_rows)
    line_real, line_imag = returned[0], returned[1]
    near_real, near_imag = transform_blocks(
        line_real, line_imag, 1.0, padded, inv_outer, band, near_blocks, lead_in=True
    )
    local_amp = jnp.sqrt(near_real * near_real + near_imag * near_imag)
    peak_tile = jnp.max(local_amp.reshape(-1, 8, 128), axis=0)
    tile_near_real, tile_near_imag, top = finish_exchange(
        near_real, near_imag, peak_tile, lax.axis_size("row"), col_total, 3
    )
    peak = jnp.max(top)
    amplitude = jnp.sqrt(tile_near_real * tile_near_real + tile_near_imag * tile_near_imag)
    tile_rows, tile_cols = tile_near_real.shape
    row_ids = lax.axis_index("row") * tile_rows + jnp.arange(tile_rows, dtype=jnp.int32)
    col_ids_out = lax.axis_index("col") * tile_cols + jnp.arange(tile_cols, dtype=jnp.int32)
    even_cell = (row_ids[:, None] + col_ids_out[None, :]) % 2 == 0
    tile_real, tile_imag = encode(tile_near_real, tile_near_imag, amplitude, peak, even_cell)
    return (tile_real, tile_imag)


def solution(mesh):
    in_specs = (P("row", "col"), P("row", "col"))
    out_specs = (P("row", "col"), P("row", "col"))
    return jax.shard_map(body, mesh=mesh, in_specs=in_specs, out_specs=out_specs, check_vma=False)
```

```python
from functools import partial
import math

import jax
import jax.numpy as jnp
from jax import lax
from jax.sharding import PartitionSpec as P
from jax.experimental import pallas as pl
from jax.experimental.pallas import tpu as pltpu
import functools

import numpy as np

N = 4096


wavelength = 5.2e-07
distance = 0.2


def optics(padded_side):
    pitch = 2e-06 * math.sqrt(8192.0 / padded_side)
    extent = padded_side * pitch
    ratio_sq = (wavelength / extent) ** 2
    band_limit = extent / (wavelength * math.sqrt((2.0 * distance / extent) ** 2 + 1.0))
    return (ratio_sq, band_limit)


def factor_pair(length):
    bit_count = length.bit_length() - 1
    inner_size = 2 ** ((bit_count + 1) // 2)
    return (length // inner_size, inner_size)


def signed_index(index_ids, modulus):
    return jnp.where(index_ids >= modulus // 2, index_ids - modulus, index_ids)


def transfer(row_signed, col_signed, ratio_sq, band_limit):
    square = row_signed[:, None] * row_signed[:, None] + col_signed[None, :] * col_signed[None, :]
    scaled = ratio_sq * square
    phase_angle = -2.0 * math.pi * distance / wavelength * scaled / (1.0 + jnp.sqrt(1.0 - scaled))
    gauss_gain = jnp.exp(square * (-2.0 / (band_limit * band_limit)))
    inside = (jnp.abs(row_signed)[:, None] < band_limit) & (
        jnp.abs(col_signed)[None, :] < band_limit
    )
    total_gain = jnp.where(inside, gauss_gain, 0.0)
    return (total_gain * jnp.cos(phase_angle), total_gain * jnp.sin(phase_angle))


def encode(near_real, near_imag, amplitude, peak, even_cell):
    amp_level = 0.8 * amplitude / peak
    amp_floor = jnp.maximum(amplitude, 0.05 * peak)
    unit_real = near_real / amp_floor
    unit_imag = near_imag / amp_floor
    lift_part = jnp.sqrt(1.0 - amp_level * amp_level)
    cell_sign = jnp.where(even_cell, 1.0, -1.0)
    out_real = unit_real * amp_level + cell_sign * unit_imag * lift_part
    out_imag = unit_imag * amp_level - cell_sign * unit_real * lift_part
    return (out_real, out_imag)


def index_range(range_start, id_count):
    return jnp.arange(id_count, dtype=jnp.int32) + range_start


def phase_table(first_ids, second_ids, modulus, exponent_sign):
    product = first_ids[:, None] * second_ids[None, :] % modulus
    phase_arg = exponent_sign * 2.0 * math.pi / modulus * product.astype(jnp.float32)
    return (jnp.cos(phase_arg), jnp.sin(phase_arg))


def complex_einsum(form, left_real, left_imag, right_real, right_imag):
    real_dot = partial(jnp.einsum, form, precision=lax.Precision.HIGH)
    shared = real_dot(left_real + left_imag, right_real)
    out_real = shared - real_dot(left_imag, right_real + right_imag)
    out_imag = shared + real_dot(left_real, right_imag - right_real)
    return (out_real, out_imag)


def transform_last(values_real, values_imag, exponent_sign, in_start, out_start, out_count, length):
    outer_size, inner_size = factor_pair(length)
    row_count = values_real.shape[0]
    blocks_in = values_real.shape[1] // inner_size
    first_block = in_start // inner_size
    cube_real = values_real.reshape(row_count, blocks_in, inner_size)
    cube_imag = values_imag.reshape(row_count, blocks_in, inner_size)
    step_real, step_imag = phase_table(
        index_range(first_block, blocks_in), index_range(0, outer_size), outer_size, exponent_sign
    )
    mid_real, mid_imag = complex_einsum("rnq,nk->rkq", cube_real, cube_imag, step_real, step_imag)
    twist_real, twist_imag = phase_table(
        index_range(0, outer_size), index_range(0, inner_size), length, exponent_sign
    )
    mid_real, mid_imag = (
        mid_real * twist_real - mid_imag * twist_imag,
        mid_real * twist_imag + mid_imag * twist_real,
    )
    blocks_out = out_count // outer_size
    second_block = out_start // outer_size
    last_real, last_imag = phase_table(
        index_range(0, inner_size), index_range(second_block, blocks_out), inner_size, exponent_sign
    )
    done_real, done_imag = complex_einsum("rkq,qj->rjk", mid_real, mid_imag, last_real, last_imag)
    return (
        done_real.reshape(row_count, blocks_out * outer_size),
        done_imag.reshape(row_count, blocks_out * outer_size),
    )


def _allmax_kernel(nr, nc, x_ref, o_ref, buf_c, buf_r, part, ssem_c, rsem_c, ssem_r, rsem_r):
    me_r = lax.axis_index("row")
    me_c = lax.axis_index("col")
    mesh_t = pl.DeviceIdType.MESH
    barrier = pltpu.get_barrier_semaphore()
    for k in range(1, nc):
        pl.semaphore_signal(barrier, inc=1, device_id=(me_r, lax.rem(me_c + k, nc)), device_id_type=mesh_t)
    for k in range(1, nr):
        pl.semaphore_signal(barrier, inc=1, device_id=(lax.rem(me_r + k, nr), me_c), device_id_type=mesh_t)
    pl.semaphore_wait(barrier, (nc - 1) + (nr - 1))

    def col_copy(dst_c, slot):
        return pltpu.make_async_remote_copy(
            src_ref=x_ref, dst_ref=buf_c.at[slot], send_sem=ssem_c.at[dst_c],
            recv_sem=rsem_c.at[slot], device_id=(me_r, dst_c), device_id_type=mesh_t)
    sends = []
    for k in range(1, nc):
        cp = col_copy(lax.rem(me_c + k, nc), me_c)
        cp.start()
        sends.append(cp)
    acc = x_ref[...]
    for k in range(1, nc):
        src = lax.rem(me_c + nc - k, nc)
        col_copy(src, src).wait_recv()
        acc = jnp.maximum(acc, buf_c[src])
    for cp in sends:
        cp.wait_send()
    part[...] = acc

    def row_copy(dst_r, slot):
        return pltpu.make_async_remote_copy(
            src_ref=part, dst_ref=buf_r.at[slot], send_sem=ssem_r.at[dst_r],
            recv_sem=rsem_r.at[slot], device_id=(dst_r, me_c), device_id_type=mesh_t)
    sends = []
    for k in range(1, nr):
        cp = row_copy(lax.rem(me_r + k, nr), me_r)
        cp.start()
        sends.append(cp)
    for k in range(1, nr):
        src = lax.rem(me_r + nr - k, nr)
        row_copy(src, src).wait_recv()
        acc = jnp.maximum(acc, buf_r[src])
    for cp in sends:
        cp.wait_send()
    o_ref[...] = acc


def global_max(tile, nr, nc):
    return pl.pallas_call(
        functools.partial(_allmax_kernel, nr, nc),
        out_shape=jax.ShapeDtypeStruct(tile.shape, tile.dtype),
        in_specs=[pl.BlockSpec(memory_space=pltpu.VMEM)],
        out_specs=pl.BlockSpec(memory_space=pltpu.VMEM),
        scratch_shapes=[
            pltpu.VMEM((nc,) + tile.shape, tile.dtype),
            pltpu.VMEM((nr,) + tile.shape, tile.dtype),
            pltpu.VMEM(tile.shape, tile.dtype),
            pltpu.SemaphoreType.DMA((nc,)),
            pltpu.SemaphoreType.DMA((nc,)),
            pltpu.SemaphoreType.DMA((nr,)),
            pltpu.SemaphoreType.DMA((nr,)),
        ],
        compiler_params=pltpu.CompilerParams(collective_id=0, has_side_effects=True),
    )(tile)


def _col_exchange_kernel(nc, piece, place, re_ref, im_ref, re_out, im_out, send_sem, recv_sem, own_sem):
    me_r = lax.axis_index("row")
    me = lax.axis_index("col")
    mesh_t = pl.DeviceIdType.MESH
    barrier = pltpu.get_barrier_semaphore()
    for k in range(1, nc):
        pl.semaphore_signal(barrier, inc=1, device_id=(me_r, lax.rem(me + k, nc)), device_id_type=mesh_t)
    pl.semaphore_wait(barrier, nc - 1)
    srcs = (re_ref, im_ref)
    dsts = (re_out, im_out)

    def remote(peer, slot, part):
        return pltpu.make_async_remote_copy(
            src_ref=piece(srcs[part], peer), dst_ref=place(dsts[part], slot),
            send_sem=send_sem.at[peer, part], recv_sem=recv_sem.at[slot, part],
            device_id=(me_r, peer), device_id_type=mesh_t)

    sends = []
    for k in range(1, nc):
        peer = lax.rem(me + k, nc)
        for part in range(2):
            cp = remote(peer, me, part)
            cp.start()
            sends.append(cp)
    owns = []
    for part in range(2):
        cp = pltpu.make_async_copy(piece(srcs[part], me), place(dsts[part], me), own_sem.at[part])
        cp.start()
        owns.append(cp)
    for cp in owns:
        cp.wait()
    for k in range(1, nc):
        src = lax.rem(me + nc - k, nc)
        for part in range(2):
            remote(src, src, part).wait_recv()
    for cp in sends:
        cp.wait_send()


def col_exchange(re, im, out_rows, out_cols, piece, place, nc, cid):
    out = jax.ShapeDtypeStruct((out_rows, out_cols), re.dtype)
    return pl.pallas_call(
        functools.partial(_col_exchange_kernel, nc, piece, place),
        out_shape=(out, out),
        in_specs=[pl.BlockSpec(memory_space=pl.ANY)] * 2,
        out_specs=(pl.BlockSpec(memory_space=pl.ANY),) * 2,
        scratch_shapes=[
            pltpu.SemaphoreType.DMA((nc, 2)),
            pltpu.SemaphoreType.DMA((nc, 2)),
            pltpu.SemaphoreType.DMA((2,)),
        ],
        compiler_params=pltpu.CompilerParams(collective_id=cid, has_side_effects=True),
    )(re, im)


def rows_to_strip(re, im, nc, cid):
    rows, cols = re.shape
    band = rows // nc
    piece = lambda ref, p: ref.at[pl.ds(p * band, band), :]
    place = lambda ref, s: ref.at[:, pl.ds(s * cols, cols)]
    return col_exchange(re, im, band, cols * nc, piece, place, nc, cid)


def strip_to_rows(re, im, nc, cid):
    rows, cols = re.shape
    width = cols // nc
    piece = lambda ref, p: ref.at[:, pl.ds(p * width, width)]
    place = lambda ref, s: ref.at[pl.ds(s * rows, rows), :]
    return col_exchange(re, im, rows * nc, width, piece, place, nc, cid)


def _finish_kernel(nr, nc, re_ref, im_ref, peak_ref, re_out, im_out, top_out,
                   buf_c, buf_r, part, send_sem, recv_sem, own_sem, ssem_c, rsem_c, ssem_r, rsem_r):
    me_r = lax.axis_index("row")
    me = lax.axis_index("col")
    mesh_t = pl.DeviceIdType.MESH
    barrier = pltpu.get_barrier_semaphore()
    for k in range(1, nc):
        pl.semaphore_signal(barrier, inc=1, device_id=(me_r, lax.rem(me + k, nc)), device_id_type=mesh_t)
    for k in range(1, nr):
        pl.semaphore_signal(barrier, inc=1, device_id=(lax.rem(me_r + k, nr), me), device_id_type=mesh_t)
    pl.semaphore_wait(barrier, (nc - 1) + (nr - 1))

    def col_top(peer, slot):
        return pltpu.make_async_remote_copy(
            src_ref=peak_ref, dst_ref=buf_c.at[slot], send_sem=ssem_c.at[peer],
            recv_sem=rsem_c.at[slot], device_id=(me_r, peer), device_id_type=mesh_t)

    for k in range(1, nc):
        col_top(lax.rem(me + k, nc), me).start()

    rows = re_ref.shape[0]
    width = re_ref.shape[1] // nc
    srcs = (re_ref, im_ref)
    dsts = (re_out, im_out)

    def data(peer, slot, part_id):
        return pltpu.make_async_remote_copy(
            src_ref=srcs[part_id].at[:, pl.ds(peer * width, width)],
            dst_ref=dsts[part_id].at[pl.ds(slot * rows, rows), :],
            send_sem=send_sem.at[peer, part_id], recv_sem=recv_sem.at[slot, part_id],
            device_id=(me_r, peer), device_id_type=mesh_t)

    for k in range(1, nc):
        for part_id in range(2):
            data(lax.rem(me + k, nc), me, part_id).start()
    owns = []
    for part_id in range(2):
        cp = pltpu.make_async_copy(
            srcs[part_id].at[:, pl.ds(me * width, width)],
            dsts[part_id].at[pl.ds(me * rows, rows), :], own_sem.at[part_id])
        cp.start()
        owns.append(cp)

    acc = peak_ref[...]
    for k in range(1, nc):
        src = lax.rem(me + nc - k, nc)
        col_top(src, src).wait_recv()
        acc = jnp.maximum(acc, buf_c[src])
    for k in range(1, nc):
        col_top(lax.rem(me + k, nc), me).wait_send()
    part[...] = acc

    def row_top(peer, slot):
        return pltpu.make_async_remote_copy(
            src_ref=part, dst_ref=buf_r.at[slot], send_sem=ssem_r.at[peer],
            recv_sem=rsem_r.at[slot], device_id=(peer, me), device_id_type=mesh_t)

    for k in range(1, nr):
        row_top(lax.rem(me_r + k, nr), me_r).start()
    for k in range(1, nr):
        src = lax.rem(me_r + nr - k, nr)
        row_top(src, src).wait_recv()
        acc = jnp.maximum(acc, buf_r[src])
    for k in range(1, nr):
        row_top(lax.rem(me_r + k, nr), me_r).wait_send()
    top_out[...] = acc

    for cp in owns:
        cp.wait()
    for k in range(1, nc):
        src = lax.rem(me + nc - k, nc)
        for part_id in range(2):
            data(src, src, part_id).wait_recv()
            data(lax.rem(me + k, nc), me, part_id).wait_send()


def finish_exchange(re, im, peak_tile, nr, nc, cid):
    rows, cols = re.shape
    out = jax.ShapeDtypeStruct((rows * nc, cols // nc), re.dtype)
    top = jax.ShapeDtypeStruct(peak_tile.shape, peak_tile.dtype)
    return pl.pallas_call(
        functools.partial(_finish_kernel, nr, nc),
        out_shape=(out, out, top),
        in_specs=[pl.BlockSpec(memory_space=pl.ANY)] * 2 + [pl.BlockSpec(memory_space=pltpu.VMEM)],
        out_specs=(pl.BlockSpec(memory_space=pl.ANY),) * 2 + (pl.BlockSpec(memory_space=pltpu.VMEM),),
        scratch_shapes=[
            pltpu.VMEM((nc,) + peak_tile.shape, peak_tile.dtype),
            pltpu.VMEM((nr,) + peak_tile.shape, peak_tile.dtype),
            pltpu.VMEM(peak_tile.shape, peak_tile.dtype),
            pltpu.SemaphoreType.DMA((nc, 2)),
            pltpu.SemaphoreType.DMA((nc, 2)),
            pltpu.SemaphoreType.DMA((2,)),
            pltpu.SemaphoreType.DMA((nc,)),
            pltpu.SemaphoreType.DMA((nc,)),
            pltpu.SemaphoreType.DMA((nr,)),
            pltpu.SemaphoreType.DMA((nr,)),
        ],
        compiler_params=pltpu.CompilerParams(collective_id=cid, has_side_effects=True),
    )(re, im, peak_tile)


def _one_exchange_kernel(nr, nc, x_ref, x_out, send_sem, recv_sem, own_sem):
    n = nr * nc
    me = lax.axis_index("row") * nc + lax.axis_index("col")
    mesh_t = pl.DeviceIdType.MESH
    barrier = pltpu.get_barrier_semaphore()

    def where(p):
        return (p // nc, lax.rem(p, nc))

    def greet(k, carry):
        pl.semaphore_signal(barrier, inc=1, device_id=where(lax.rem(me + k, n)), device_id_type=mesh_t)
        return carry

    lax.fori_loop(1, n, greet, 0, unroll=8)
    pl.semaphore_wait(barrier, n - 1)

    def remote(peer, slot):
        return pltpu.make_async_remote_copy(
            src_ref=x_ref.at[peer], dst_ref=x_out.at[slot],
            send_sem=send_sem.at[peer], recv_sem=recv_sem.at[slot],
            device_id=where(peer), device_id_type=mesh_t)

    def send(k, carry):
        remote(lax.rem(me + k, n), me).start()
        return carry

    lax.fori_loop(1, n, send, 0, unroll=8)
    own = pltpu.make_async_copy(x_ref.at[me], x_out.at[me], own_sem.at[0])
    own.start()
    own.wait()

    def recv(k, carry):
        remote(lax.rem(me + n - k, n), lax.rem(me + n - k, n)).wait_recv()
        remote(lax.rem(me + k, n), me).wait_send()
        return carry

    lax.fori_loop(1, n, recv, 0, unroll=8)


def one_exchange(x, nr, nc, cid):
    n = nr * nc
    return pl.pallas_call(
        functools.partial(_one_exchange_kernel, nr, nc),
        out_shape=jax.ShapeDtypeStruct(x.shape, x.dtype),
        in_specs=[pl.BlockSpec(memory_space=pl.ANY)],
        out_specs=pl.BlockSpec(memory_space=pl.ANY),
        scratch_shapes=[
            pltpu.SemaphoreType.DMA((n,)),
            pltpu.SemaphoreType.DMA((n,)),
            pltpu.SemaphoreType.DMA((1,)),
        ],
        compiler_params=pltpu.CompilerParams(collective_id=cid, has_side_effects=True),
    )(x)


def transform_blocks(
    values_real, values_imag, exponent_sign, length, outer_size, in_blocks, out_blocks,
    lead_in=False, lead_out=False,
):
    inner_size = length // outer_size
    if lead_in:
        row_count = values_real.shape[1]
        cube_real = values_real.reshape(len(in_blocks), inner_size, row_count)
        cube_imag = values_imag.reshape(len(in_blocks), inner_size, row_count)
        first_form = "nqr,nk->rkq"
    else:
        row_count = values_real.shape[0]
        cube_real = values_real.reshape(row_count, len(in_blocks), inner_size)
        cube_imag = values_imag.reshape(row_count, len(in_blocks), inner_size)
        first_form = "rnq,nk->rkq"
    step_real, step_imag = phase_table(
        jnp.asarray(in_blocks, jnp.int32), index_range(0, outer_size), outer_size, exponent_sign
    )
    mid_real, mid_imag = complex_einsum(first_form, cube_real, cube_imag, step_real, step_imag)
    twist_real, twist_imag = phase_table(
        index_range(0, outer_size), index_range(0, inner_size), length, exponent_sign
    )
    mid_real, mid_imag = (
        mid_real * twist_real - mid_imag * twist_imag,
        mid_real * twist_imag + mid_imag * twist_real,
    )
    last_real, last_imag = phase_table(
        index_range(0, inner_size), jnp.asarray(out_blocks, jnp.int32), inner_size, exponent_sign
    )
    if lead_out:
        done_real, done_imag = complex_einsum(
            "rkq,qj->jkr", mid_real, mid_imag, last_real, last_imag
        )
        return (
            done_real.reshape(len(out_blocks) * outer_size, row_count),
            done_imag.reshape(len(out_blocks) * outer_size, row_count),
        )
    done_real, done_imag = complex_einsum("rkq,qj->rjk", mid_real, mid_imag, last_real, last_imag)
    return (
        done_real.reshape(row_count, len(out_blocks) * outer_size),
        done_imag.reshape(row_count, len(out_blocks) * outer_size),
    )


def band_blocks(padded, block, band_limit, multiple):
    top = math.ceil(band_limit) - 1
    low = list(range(top // block + 1))
    high = list(range((padded - top) // block, padded // block))
    while (len(low) + len(high)) * block % multiple:
        if len(low) <= len(high):
            low.append(low[-1] + 1)
        else:
            high.insert(0, high[0] - 1)
    return low + high


def pack_chunks(first, second, device_total, lead):
    if lead:
        width = first.shape[0] // device_total
        both = jnp.stack([first, second]).reshape(2, device_total, width, first.shape[1])
        both = both.transpose(1, 0, 2, 3)
    else:
        width = first.shape[1] // device_total
        both = jnp.stack([first, second]).reshape(2, first.shape[0], device_total, width)
        both = both.transpose(2, 0, 1, 3)
    return both.reshape(device_total, -1, 128)


def body(field_real, field_imag):
    padded = 2 * N
    quarter = padded // 4
    col_total = lax.axis_size("col")
    device_total = lax.axis_size("row") * col_total
    device = lax.axis_index("row") * col_total + lax.axis_index("col")
    strip_real, strip_imag = rows_to_strip(field_real, field_imag, col_total, 1)
    ratio_sq, band_limit = optics(padded)
    fwd_outer, fwd_inner = factor_pair(padded)
    inv_outer, inv_inner = fwd_inner, fwd_outer
    band = band_blocks(padded, fwd_outer, band_limit, device_total * 2)
    field_blocks = list(range(quarter // fwd_inner, (quarter + N) // fwd_inner))
    near_blocks = list(range(quarter // inv_outer, (quarter + N) // inv_outer))
    pick_real, pick_imag = transform_blocks(
        strip_real, strip_imag, -1.0, padded, fwd_outer, field_blocks, band
    )
    strip_rows = pick_real.shape[0]
    col_width = pick_real.shape[1] // device_total
    packed = jnp.stack([pick_real, pick_imag]).reshape(2, strip_rows, device_total, col_width)
    packed = packed.transpose(2, 0, 1, 3).reshape(device_total, -1, 128)
    arrived = one_exchange(packed, lax.axis_size("row"), col_total, 4)
    arrived = arrived.reshape(device_total, 2, strip_rows, col_width).transpose(1, 0, 2, 3)
    arrived = arrived.reshape(2, device_total * strip_rows, col_width)
    turned_real, turned_imag = arrived[0], arrived[1]
    spec_real, spec_imag = transform_blocks(
        turned_real, turned_imag, -1.0, padded, fwd_outer, field_blocks, band, lead_in=True
    )
    band_freqs = np.array(band, np.int32)[:, None] * fwd_outer + np.arange(fwd_outer, dtype=np.int32)
    freq_ids = jnp.asarray(band_freqs.reshape(-1))
    freq_signed = signed_index(freq_ids, padded).astype(jnp.float32)
    col_ids = lax.dynamic_slice(freq_ids, (device * col_width,), (col_width,))
    col_signed = signed_index(col_ids, padded).astype(jnp.float32)
    gain_real, gain_imag = transfer(col_signed, freq_signed, ratio_sq, band_limit)
    mixed_real = spec_real * gain_real - spec_imag * gain_imag
    mixed_imag = spec_real * gain_imag + spec_imag * gain_real
    inv_real, inv_imag = transform_blocks(
        mixed_real, mixed_imag, 1.0, padded, inv_outer, band, near_blocks
    )
    returned = one_exchange(
        pack_chunks(inv_real, inv_imag, device_total, False), lax.axis_size("row"), col_total, 5
    )
    returned = returned.reshape(device_total, 2, col_width, strip_rows).transpose(1, 0, 2, 3)
    returned = returned.reshape(2, device_total * col_width, strip_rows)
    line_real, line_imag = returned[0], returned[1]
    near_real, near_imag = transform_blocks(
        line_real, line_imag, 1.0, padded, inv_outer, band, near_blocks, lead_in=True
    )
    local_amp = jnp.sqrt(near_real * near_real + near_imag * near_imag)
    peak_tile = jnp.max(local_amp.reshape(-1, 8, 128), axis=0)
    tile_near_real, tile_near_imag, top = finish_exchange(
        near_real, near_imag, peak_tile, lax.axis_size("row"), col_total, 3
    )
    peak = jnp.max(top)
    amplitude = jnp.sqrt(tile_near_real * tile_near_real + tile_near_imag * tile_near_imag)
    tile_rows, tile_cols = tile_near_real.shape
    row_ids = lax.axis_index("row") * tile_rows + jnp.arange(tile_rows, dtype=jnp.int32)
    col_ids_out = lax.axis_index("col") * tile_cols + jnp.arange(tile_cols, dtype=jnp.int32)
    even_cell = (row_ids[:, None] + col_ids_out[None, :]) % 2 == 0
    tile_real, tile_imag = encode(tile_near_real, tile_near_imag, amplitude, peak, even_cell)
    return (tile_real, tile_imag)


def solution(mesh):
    in_specs = (P("row", "col"), P("row", "col"))
    out_specs = (P("row", "col"), P("row", "col"))
    return jax.shard_map(body, mesh=mesh, in_specs=in_specs, out_specs=out_specs, check_vma=False)
```

```python
from functools import partial
import math

import jax
import jax.numpy as jnp
from jax import lax
from jax.sharding import PartitionSpec as P
from jax.experimental import pallas as pl
from jax.experimental.pallas import tpu as pltpu
import functools

import numpy as np

N = 4096


wavelength = 5.2e-07
distance = 0.2


def optics(padded_side):
    pitch = 2e-06 * math.sqrt(8192.0 / padded_side)
    extent = padded_side * pitch
    ratio_sq = (wavelength / extent) ** 2
    band_limit = extent / (wavelength * math.sqrt((2.0 * distance / extent) ** 2 + 1.0))
    return (ratio_sq, band_limit)


def factor_pair(length):
    bit_count = length.bit_length() - 1
    inner_size = 2 ** ((bit_count + 1) // 2)
    return (length // inner_size, inner_size)


def signed_index(index_ids, modulus):
    return jnp.where(index_ids >= modulus // 2, index_ids - modulus, index_ids)


def transfer(row_signed, col_signed, ratio_sq, band_limit):
    square = row_signed[:, None] * row_signed[:, None] + col_signed[None, :] * col_signed[None, :]
    scaled = ratio_sq * square
    phase_angle = -2.0 * math.pi * distance / wavelength * scaled / (1.0 + jnp.sqrt(1.0 - scaled))
    gauss_gain = jnp.exp(square * (-2.0 / (band_limit * band_limit)))
    inside = (jnp.abs(row_signed)[:, None] < band_limit) & (
        jnp.abs(col_signed)[None, :] < band_limit
    )
    total_gain = jnp.where(inside, gauss_gain, 0.0)
    return (total_gain * jnp.cos(phase_angle), total_gain * jnp.sin(phase_angle))


def encode(near_real, near_imag, amplitude, peak, even_cell):
    amp_level = 0.8 * amplitude / peak
    amp_floor = jnp.maximum(amplitude, 0.05 * peak)
    unit_real = near_real / amp_floor
    unit_imag = near_imag / amp_floor
    lift_part = jnp.sqrt(1.0 - amp_level * amp_level)
    cell_sign = jnp.where(even_cell, 1.0, -1.0)
    out_real = unit_real * amp_level + cell_sign * unit_imag * lift_part
    out_imag = unit_imag * amp_level - cell_sign * unit_real * lift_part
    return (out_real, out_imag)


def index_range(range_start, id_count):
    return jnp.arange(id_count, dtype=jnp.int32) + range_start


def phase_table(first_ids, second_ids, modulus, exponent_sign):
    product = first_ids[:, None] * second_ids[None, :] % modulus
    phase_arg = exponent_sign * 2.0 * math.pi / modulus * product.astype(jnp.float32)
    return (jnp.cos(phase_arg), jnp.sin(phase_arg))


def complex_einsum(form, left_real, left_imag, right_real, right_imag):
    real_dot = partial(jnp.einsum, form, precision=lax.Precision.HIGH)
    shared = real_dot(left_real + left_imag, right_real)
    out_real = shared - real_dot(left_imag, right_real + right_imag)
    out_imag = shared + real_dot(left_real, right_imag - right_real)
    return (out_real, out_imag)


def transform_last(values_real, values_imag, exponent_sign, in_start, out_start, out_count, length):
    outer_size, inner_size = factor_pair(length)
    row_count = values_real.shape[0]
    blocks_in = values_real.shape[1] // inner_size
    first_block = in_start // inner_size
    cube_real = values_real.reshape(row_count, blocks_in, inner_size)
    cube_imag = values_imag.reshape(row_count, blocks_in, inner_size)
    step_real, step_imag = phase_table(
        index_range(first_block, blocks_in), index_range(0, outer_size), outer_size, exponent_sign
    )
    mid_real, mid_imag = complex_einsum("rnq,nk->rkq", cube_real, cube_imag, step_real, step_imag)
    twist_real, twist_imag = phase_table(
        index_range(0, outer_size), index_range(0, inner_size), length, exponent_sign
    )
    mid_real, mid_imag = (
        mid_real * twist_real - mid_imag * twist_imag,
        mid_real * twist_imag + mid_imag * twist_real,
    )
    blocks_out = out_count // outer_size
    second_block = out_start // outer_size
    last_real, last_imag = phase_table(
        index_range(0, inner_size), index_range(second_block, blocks_out), inner_size, exponent_sign
    )
    done_real, done_imag = complex_einsum("rkq,qj->rjk", mid_real, mid_imag, last_real, last_imag)
    return (
        done_real.reshape(row_count, blocks_out * outer_size),
        done_imag.reshape(row_count, blocks_out * outer_size),
    )


def _allmax_kernel(nr, nc, x_ref, o_ref, buf_c, buf_r, part, ssem_c, rsem_c, ssem_r, rsem_r):
    me_r = lax.axis_index("row")
    me_c = lax.axis_index("col")
    mesh_t = pl.DeviceIdType.MESH
    barrier = pltpu.get_barrier_semaphore()
    for k in range(1, nc):
        pl.semaphore_signal(barrier, inc=1, device_id=(me_r, lax.rem(me_c + k, nc)), device_id_type=mesh_t)
    for k in range(1, nr):
        pl.semaphore_signal(barrier, inc=1, device_id=(lax.rem(me_r + k, nr), me_c), device_id_type=mesh_t)
    pl.semaphore_wait(barrier, (nc - 1) + (nr - 1))

    def col_copy(dst_c, slot):
        return pltpu.make_async_remote_copy(
            src_ref=x_ref, dst_ref=buf_c.at[slot], send_sem=ssem_c.at[dst_c],
            recv_sem=rsem_c.at[slot], device_id=(me_r, dst_c), device_id_type=mesh_t)
    sends = []
    for k in range(1, nc):
        cp = col_copy(lax.rem(me_c + k, nc), me_c)
        cp.start()
        sends.append(cp)
    acc = x_ref[...]
    for k in range(1, nc):
        src = lax.rem(me_c + nc - k, nc)
        col_copy(src, src).wait_recv()
        acc = jnp.maximum(acc, buf_c[src])
    for cp in sends:
        cp.wait_send()
    part[...] = acc

    def row_copy(dst_r, slot):
        return pltpu.make_async_remote_copy(
            src_ref=part, dst_ref=buf_r.at[slot], send_sem=ssem_r.at[dst_r],
            recv_sem=rsem_r.at[slot], device_id=(dst_r, me_c), device_id_type=mesh_t)
    sends = []
    for k in range(1, nr):
        cp = row_copy(lax.rem(me_r + k, nr), me_r)
        cp.start()
        sends.append(cp)
    for k in range(1, nr):
        src = lax.rem(me_r + nr - k, nr)
        row_copy(src, src).wait_recv()
        acc = jnp.maximum(acc, buf_r[src])
    for cp in sends:
        cp.wait_send()
    o_ref[...] = acc


def global_max(tile, nr, nc):
    return pl.pallas_call(
        functools.partial(_allmax_kernel, nr, nc),
        out_shape=jax.ShapeDtypeStruct(tile.shape, tile.dtype),
        in_specs=[pl.BlockSpec(memory_space=pltpu.VMEM)],
        out_specs=pl.BlockSpec(memory_space=pltpu.VMEM),
        scratch_shapes=[
            pltpu.VMEM((nc,) + tile.shape, tile.dtype),
            pltpu.VMEM((nr,) + tile.shape, tile.dtype),
            pltpu.VMEM(tile.shape, tile.dtype),
            pltpu.SemaphoreType.DMA((nc,)),
            pltpu.SemaphoreType.DMA((nc,)),
            pltpu.SemaphoreType.DMA((nr,)),
            pltpu.SemaphoreType.DMA((nr,)),
        ],
        compiler_params=pltpu.CompilerParams(collective_id=0, has_side_effects=True),
    )(tile)


def _col_exchange_kernel(nc, piece, place, re_ref, im_ref, re_out, im_out, send_sem, recv_sem, own_sem):
    me_r = lax.axis_index("row")
    me = lax.axis_index("col")
    mesh_t = pl.DeviceIdType.MESH
    barrier = pltpu.get_barrier_semaphore()
    for k in range(1, nc):
        pl.semaphore_signal(barrier, inc=1, device_id=(me_r, lax.rem(me + k, nc)), device_id_type=mesh_t)
    pl.semaphore_wait(barrier, nc - 1)
    srcs = (re_ref, im_ref)
    dsts = (re_out, im_out)

    def remote(peer, slot, part):
        return pltpu.make_async_remote_copy(
            src_ref=piece(srcs[part], peer), dst_ref=place(dsts[part], slot),
            send_sem=send_sem.at[peer, part], recv_sem=recv_sem.at[slot, part],
            device_id=(me_r, peer), device_id_type=mesh_t)

    sends = []
    for k in range(1, nc):
        peer = lax.rem(me + k, nc)
        for part in range(2):
            cp = remote(peer, me, part)
            cp.start()
            sends.append(cp)
    owns = []
    for part in range(2):
        cp = pltpu.make_async_copy(piece(srcs[part], me), place(dsts[part], me), own_sem.at[part])
        cp.start()
        owns.append(cp)
    for cp in owns:
        cp.wait()
    for k in range(1, nc):
        src = lax.rem(me + nc - k, nc)
        for part in range(2):
            remote(src, src, part).wait_recv()
    for cp in sends:
        cp.wait_send()


def col_exchange(re, im, out_rows, out_cols, piece, place, nc, cid):
    out = jax.ShapeDtypeStruct((out_rows, out_cols), re.dtype)
    return pl.pallas_call(
        functools.partial(_col_exchange_kernel, nc, piece, place),
        out_shape=(out, out),
        in_specs=[pl.BlockSpec(memory_space=pl.ANY)] * 2,
        out_specs=(pl.BlockSpec(memory_space=pl.ANY),) * 2,
        scratch_shapes=[
            pltpu.SemaphoreType.DMA((nc, 2)),
            pltpu.SemaphoreType.DMA((nc, 2)),
            pltpu.SemaphoreType.DMA((2,)),
        ],
        compiler_params=pltpu.CompilerParams(collective_id=cid, has_side_effects=True),
    )(re, im)


def rows_to_strip(re, im, nc, cid):
    rows, cols = re.shape
    band = rows // nc
    piece = lambda ref, p: ref.at[pl.ds(p * band, band), :]
    place = lambda ref, s: ref.at[:, pl.ds(s * cols, cols)]
    return col_exchange(re, im, band, cols * nc, piece, place, nc, cid)


def strip_to_rows(re, im, nc, cid):
    rows, cols = re.shape
    width = cols // nc
    piece = lambda ref, p: ref.at[:, pl.ds(p * width, width)]
    place = lambda ref, s: ref.at[pl.ds(s * rows, rows), :]
    return col_exchange(re, im, rows * nc, width, piece, place, nc, cid)


def _finish_kernel(nr, nc, re_ref, im_ref, peak_ref, re_out, im_out, top_out,
                   buf_c, buf_r, part, send_sem, recv_sem, own_sem, ssem_c, rsem_c, ssem_r, rsem_r):
    me_r = lax.axis_index("row")
    me = lax.axis_index("col")
    mesh_t = pl.DeviceIdType.MESH
    barrier = pltpu.get_barrier_semaphore()
    for k in range(1, nc):
        pl.semaphore_signal(barrier, inc=1, device_id=(me_r, lax.rem(me + k, nc)), device_id_type=mesh_t)
    for k in range(1, nr):
        pl.semaphore_signal(barrier, inc=1, device_id=(lax.rem(me_r + k, nr), me), device_id_type=mesh_t)
    pl.semaphore_wait(barrier, (nc - 1) + (nr - 1))

    def col_top(peer, slot):
        return pltpu.make_async_remote_copy(
            src_ref=peak_ref, dst_ref=buf_c.at[slot], send_sem=ssem_c.at[peer],
            recv_sem=rsem_c.at[slot], device_id=(me_r, peer), device_id_type=mesh_t)

    for k in range(1, nc):
        col_top(lax.rem(me + k, nc), me).start()

    rows = re_ref.shape[0]
    width = re_ref.shape[1] // nc
    srcs = (re_ref, im_ref)
    dsts = (re_out, im_out)

    def data(peer, slot, part_id):
        return pltpu.make_async_remote_copy(
            src_ref=srcs[part_id].at[:, pl.ds(peer * width, width)],
            dst_ref=dsts[part_id].at[pl.ds(slot * rows, rows), :],
            send_sem=send_sem.at[peer, part_id], recv_sem=recv_sem.at[slot, part_id],
            device_id=(me_r, peer), device_id_type=mesh_t)

    for k in range(1, nc):
        for part_id in range(2):
            data(lax.rem(me + k, nc), me, part_id).start()
    owns = []
    for part_id in range(2):
        cp = pltpu.make_async_copy(
            srcs[part_id].at[:, pl.ds(me * width, width)],
            dsts[part_id].at[pl.ds(me * rows, rows), :], own_sem.at[part_id])
        cp.start()
        owns.append(cp)

    acc = peak_ref[...]
    for k in range(1, nc):
        src = lax.rem(me + nc - k, nc)
        col_top(src, src).wait_recv()
        acc = jnp.maximum(acc, buf_c[src])
    for k in range(1, nc):
        col_top(lax.rem(me + k, nc), me).wait_send()
    part[...] = acc

    def row_top(peer, slot):
        return pltpu.make_async_remote_copy(
            src_ref=part, dst_ref=buf_r.at[slot], send_sem=ssem_r.at[peer],
            recv_sem=rsem_r.at[slot], device_id=(peer, me), device_id_type=mesh_t)

    for k in range(1, nr):
        row_top(lax.rem(me_r + k, nr), me_r).start()
    for k in range(1, nr):
        src = lax.rem(me_r + nr - k, nr)
        row_top(src, src).wait_recv()
        acc = jnp.maximum(acc, buf_r[src])
    for k in range(1, nr):
        row_top(lax.rem(me_r + k, nr), me_r).wait_send()
    top_out[...] = acc

    for cp in owns:
        cp.wait()
    for k in range(1, nc):
        src = lax.rem(me + nc - k, nc)
        for part_id in range(2):
            data(src, src, part_id).wait_recv()
            data(lax.rem(me + k, nc), me, part_id).wait_send()


def finish_exchange(re, im, peak_tile, nr, nc, cid):
    rows, cols = re.shape
    out = jax.ShapeDtypeStruct((rows * nc, cols // nc), re.dtype)
    top = jax.ShapeDtypeStruct(peak_tile.shape, peak_tile.dtype)
    return pl.pallas_call(
        functools.partial(_finish_kernel, nr, nc),
        out_shape=(out, out, top),
        in_specs=[pl.BlockSpec(memory_space=pl.ANY)] * 2 + [pl.BlockSpec(memory_space=pltpu.VMEM)],
        out_specs=(pl.BlockSpec(memory_space=pl.ANY),) * 2 + (pl.BlockSpec(memory_space=pltpu.VMEM),),
        scratch_shapes=[
            pltpu.VMEM((nc,) + peak_tile.shape, peak_tile.dtype),
            pltpu.VMEM((nr,) + peak_tile.shape, peak_tile.dtype),
            pltpu.VMEM(peak_tile.shape, peak_tile.dtype),
            pltpu.SemaphoreType.DMA((nc, 2)),
            pltpu.SemaphoreType.DMA((nc, 2)),
            pltpu.SemaphoreType.DMA((2,)),
            pltpu.SemaphoreType.DMA((nc,)),
            pltpu.SemaphoreType.DMA((nc,)),
            pltpu.SemaphoreType.DMA((nr,)),
            pltpu.SemaphoreType.DMA((nr,)),
        ],
        compiler_params=pltpu.CompilerParams(collective_id=cid, has_side_effects=True),
    )(re, im, peak_tile)


def _one_exchange_kernel(nr, nc, x_ref, x_out, send_sem, recv_sem, own_sem):
    n = nr * nc
    me = lax.axis_index("row") * nc + lax.axis_index("col")
    mesh_t = pl.DeviceIdType.MESH
    barrier = pltpu.get_barrier_semaphore()

    def where(p):
        return (p // nc, lax.rem(p, nc))

    def greet(k, carry):
        pl.semaphore_signal(barrier, inc=1, device_id=where(lax.rem(me + k, n)), device_id_type=mesh_t)
        return carry

    lax.fori_loop(1, n, greet, 0, unroll=8)
    pl.semaphore_wait(barrier, n - 1)

    def remote(peer, slot):
        return pltpu.make_async_remote_copy(
            src_ref=x_ref.at[peer], dst_ref=x_out.at[slot],
            send_sem=send_sem.at[peer], recv_sem=recv_sem.at[slot],
            device_id=where(peer), device_id_type=mesh_t)

    def send(k, carry):
        remote(lax.rem(me + k, n), me).start()
        return carry

    lax.fori_loop(1, n, send, 0, unroll=8)
    own = pltpu.make_async_copy(x_ref.at[me], x_out.at[me], own_sem.at[0])
    own.start()
    own.wait()

    def recv(k, carry):
        remote(lax.rem(me + n - k, n), lax.rem(me + n - k, n)).wait_recv()
        remote(lax.rem(me + k, n), me).wait_send()
        return carry

    lax.fori_loop(1, n, recv, 0, unroll=8)


def one_exchange(x, nr, nc, cid):
    n = nr * nc
    return pl.pallas_call(
        functools.partial(_one_exchange_kernel, nr, nc),
        out_shape=jax.ShapeDtypeStruct(x.shape, x.dtype),
        in_specs=[pl.BlockSpec(memory_space=pl.ANY)],
        out_specs=pl.BlockSpec(memory_space=pl.ANY),
        scratch_shapes=[
            pltpu.SemaphoreType.DMA((n,)),
            pltpu.SemaphoreType.DMA((n,)),
            pltpu.SemaphoreType.DMA((1,)),
        ],
        compiler_params=pltpu.CompilerParams(collective_id=cid, has_side_effects=True),
    )(x)


def transform_blocks(
    values_real, values_imag, exponent_sign, length, outer_size, in_blocks, out_blocks,
    lead_in=False, lead_out=False,
):
    inner_size = length // outer_size
    if lead_in:
        row_count = values_real.shape[1]
        cube_real = values_real.reshape(len(in_blocks), inner_size, row_count)
        cube_imag = values_imag.reshape(len(in_blocks), inner_size, row_count)
        first_form = "nqr,nk->rkq"
    else:
        row_count = values_real.shape[0]
        cube_real = values_real.reshape(row_count, len(in_blocks), inner_size)
        cube_imag = values_imag.reshape(row_count, len(in_blocks), inner_size)
        first_form = "rnq,nk->rkq"
    step_real, step_imag = phase_table(
        jnp.asarray(in_blocks, jnp.int32), index_range(0, outer_size), outer_size, exponent_sign
    )
    mid_real, mid_imag = complex_einsum(first_form, cube_real, cube_imag, step_real, step_imag)
    twist_real, twist_imag = phase_table(
        index_range(0, outer_size), index_range(0, inner_size), length, exponent_sign
    )
    mid_real, mid_imag = (
        mid_real * twist_real - mid_imag * twist_imag,
        mid_real * twist_imag + mid_imag * twist_real,
    )
    last_real, last_imag = phase_table(
        index_range(0, inner_size), jnp.asarray(out_blocks, jnp.int32), inner_size, exponent_sign
    )
    if lead_out:
        done_real, done_imag = complex_einsum(
            "rkq,qj->jkr", mid_real, mid_imag, last_real, last_imag
        )
        return (
            done_real.reshape(len(out_blocks) * outer_size, row_count),
            done_imag.reshape(len(out_blocks) * outer_size, row_count),
        )
    done_real, done_imag = complex_einsum("rkq,qj->rjk", mid_real, mid_imag, last_real, last_imag)
    return (
        done_real.reshape(row_count, len(out_blocks) * outer_size),
        done_imag.reshape(row_count, len(out_blocks) * outer_size),
    )


def band_blocks(padded, block, band_limit, multiple):
    top = math.ceil(band_limit) - 1
    low = list(range(top // block + 1))
    high = list(range((padded - top) // block, padded // block))
    while (len(low) + len(high)) * block % multiple:
        if len(low) <= len(high):
            low.append(low[-1] + 1)
        else:
            high.insert(0, high[0] - 1)
    return low + high


def pack_chunks(first, second, device_total, lead):
    if lead:
        width = first.shape[0] // device_total
        both = jnp.stack([first, second]).reshape(2, device_total, width, first.shape[1])
        both = both.transpose(1, 0, 2, 3)
    else:
        width = first.shape[1] // device_total
        both = jnp.stack([first, second]).reshape(2, first.shape[0], device_total, width)
        both = both.transpose(2, 0, 1, 3)
    return both.reshape(device_total, -1, 128)


def body(field_real, field_imag):
    padded = 2 * N
    quarter = padded // 4
    col_total = lax.axis_size("col")
    device_total = lax.axis_size("row") * col_total
    device = lax.axis_index("row") * col_total + lax.axis_index("col")
    strip_real, strip_imag = rows_to_strip(field_real, field_imag, col_total, 1)
    ratio_sq, band_limit = optics(padded)
    fwd_outer, fwd_inner = factor_pair(padded)
    inv_outer, inv_inner = fwd_outer, fwd_inner
    band = band_blocks(padded, fwd_outer, band_limit, device_total * 2)
    field_blocks = list(range(quarter // fwd_inner, (quarter + N) // fwd_inner))
    near_blocks = list(range(quarter // inv_outer, (quarter + N) // inv_outer))
    inv_band = band[::2] if all(b % 2 == 0 and band[i * 2 + 1] == b + 1 for i, b in enumerate(band[::2])) else None
    inv_band = [b // 2 for b in inv_band]
    pick_real, pick_imag = transform_blocks(
        strip_real, strip_imag, -1.0, padded, fwd_outer, field_blocks, band
    )
    strip_rows = pick_real.shape[0]
    col_width = pick_real.shape[1] // device_total
    packed = jnp.stack([pick_real, pick_imag]).reshape(2, strip_rows, device_total, col_width)
    packed = packed.transpose(2, 0, 1, 3).reshape(device_total, -1, 128)
    arrived = one_exchange(packed, lax.axis_size("row"), col_total, 4)
    arrived = arrived.reshape(device_total, 2, strip_rows, col_width).transpose(1, 0, 2, 3)
    arrived = arrived.reshape(2, device_total * strip_rows, col_width)
    turned_real, turned_imag = arrived[0], arrived[1]
    spec_real, spec_imag = transform_blocks(
        turned_real, turned_imag, -1.0, padded, fwd_outer, field_blocks, band, lead_in=True
    )
    band_freqs = np.array(band, np.int32)[:, None] * fwd_outer + np.arange(fwd_outer, dtype=np.int32)
    freq_ids = jnp.asarray(band_freqs.reshape(-1))
    freq_signed = signed_index(freq_ids, padded).astype(jnp.float32)
    col_ids = lax.dynamic_slice(freq_ids, (device * col_width,), (col_width,))
    col_signed = signed_index(col_ids, padded).astype(jnp.float32)
    gain_real, gain_imag = transfer(col_signed, freq_signed, ratio_sq, band_limit)
    mixed_real = spec_real * gain_real - spec_imag * gain_imag
    mixed_imag = spec_real * gain_imag + spec_imag * gain_real
    inv_real, inv_imag = transform_blocks(
        mixed_real, mixed_imag, 1.0, padded, inv_outer, inv_band, near_blocks
    )
    returned = one_exchange(
        pack_chunks(inv_real, inv_imag, device_total, False), lax.axis_size("row"), col_total, 5
    )
    returned = returned.reshape(device_total, 2, col_width, strip_rows).transpose(1, 0, 2, 3)
    returned = returned.reshape(2, device_total * col_width, strip_rows)
    line_real, line_imag = returned[0], returned[1]
    near_real, near_imag = transform_blocks(
        line_real, line_imag, 1.0, padded, inv_outer, inv_band, near_blocks, lead_in=True
    )
    local_amp = jnp.sqrt(near_real * near_real + near_imag * near_imag)
    peak_tile = jnp.max(local_amp.reshape(-1, 8, 128), axis=0)
    tile_near_real, tile_near_imag, top = finish_exchange(
        near_real, near_imag, peak_tile, lax.axis_size("row"), col_total, 3
    )
    peak = jnp.max(top)
    amplitude = jnp.sqrt(tile_near_real * tile_near_real + tile_near_imag * tile_near_imag)
    tile_rows, tile_cols = tile_near_real.shape
    row_ids = lax.axis_index("row") * tile_rows + jnp.arange(tile_rows, dtype=jnp.int32)
    col_ids_out = lax.axis_index("col") * tile_cols + jnp.arange(tile_cols, dtype=jnp.int32)
    even_cell = (row_ids[:, None] + col_ids_out[None, :]) % 2 == 0
    tile_real, tile_imag = encode(tile_near_real, tile_near_imag, amplitude, peak, even_cell)
    return (tile_real, tile_imag)


def solution(mesh):
    in_specs = (P("row", "col"), P("row", "col"))
    out_specs = (P("row", "col"), P("row", "col"))
    return jax.shard_map(body, mesh=mesh, in_specs=in_specs, out_specs=out_specs, check_vma=False)
```

```python
from functools import partial
import math

import jax
import jax.numpy as jnp
from jax import lax
from jax.sharding import PartitionSpec as P
from jax.experimental import pallas as pl
from jax.experimental.pallas import tpu as pltpu
import functools

import numpy as np

N = 4096


wavelength = 5.2e-07
distance = 0.2


def optics(padded_side):
    pitch = 2e-06 * math.sqrt(8192.0 / padded_side)
    extent = padded_side * pitch
    ratio_sq = (wavelength / extent) ** 2
    band_limit = extent / (wavelength * math.sqrt((2.0 * distance / extent) ** 2 + 1.0))
    return (ratio_sq, band_limit)


def factor_pair(length):
    bit_count = length.bit_length() - 1
    inner_size = 2 ** ((bit_count + 1) // 2)
    return (length // inner_size, inner_size)


def signed_index(index_ids, modulus):
    return jnp.where(index_ids >= modulus // 2, index_ids - modulus, index_ids)


def transfer(row_signed, col_signed, ratio_sq, band_limit):
    square = row_signed[:, None] * row_signed[:, None] + col_signed[None, :] * col_signed[None, :]
    scaled = ratio_sq * square
    phase_angle = -2.0 * math.pi * distance / wavelength * scaled / (1.0 + jnp.sqrt(1.0 - scaled))
    gauss_gain = jnp.exp(square * (-2.0 / (band_limit * band_limit)))
    inside = (jnp.abs(row_signed)[:, None] < band_limit) & (
        jnp.abs(col_signed)[None, :] < band_limit
    )
    total_gain = jnp.where(inside, gauss_gain, 0.0)
    return (total_gain * jnp.cos(phase_angle), total_gain * jnp.sin(phase_angle))


def encode(near_real, near_imag, amplitude, peak, even_cell):
    amp_level = 0.8 * amplitude / peak
    amp_floor = jnp.maximum(amplitude, 0.05 * peak)
    unit_real = near_real / amp_floor
    unit_imag = near_imag / amp_floor
    lift_part = jnp.sqrt(1.0 - amp_level * amp_level)
    cell_sign = jnp.where(even_cell, 1.0, -1.0)
    out_real = unit_real * amp_level + cell_sign * unit_imag * lift_part
    out_imag = unit_imag * amp_level - cell_sign * unit_real * lift_part
    return (out_real, out_imag)


def index_range(range_start, id_count):
    return jnp.arange(id_count, dtype=jnp.int32) + range_start


def phase_table(first_ids, second_ids, modulus, exponent_sign):
    product = first_ids[:, None] * second_ids[None, :] % modulus
    phase_arg = exponent_sign * 2.0 * math.pi / modulus * product.astype(jnp.float32)
    return (jnp.cos(phase_arg), jnp.sin(phase_arg))


def complex_einsum(form, left_real, left_imag, right_real, right_imag):
    real_dot = partial(jnp.einsum, form, precision=lax.Precision.HIGH)
    out_form = form.split("->")[1]
    axis = out_form.index(form.split("->")[0].split(",")[1][-1])
    width = right_real.shape[-1]
    both = jnp.concatenate([right_real, right_imag], axis=-1)
    from_real = real_dot(left_real, both)
    from_imag = real_dot(left_imag, both)
    real_part = partial(lax.slice_in_dim, start_index=0, limit_index=width, axis=axis)
    imag_part = partial(lax.slice_in_dim, start_index=width, limit_index=2 * width, axis=axis)
    out_real = real_part(from_real) - imag_part(from_imag)
    out_imag = imag_part(from_real) + real_part(from_imag)
    return (out_real, out_imag)


def transform_last(values_real, values_imag, exponent_sign, in_start, out_start, out_count, length):
    outer_size, inner_size = factor_pair(length)
    row_count = values_real.shape[0]
    blocks_in = values_real.shape[1] // inner_size
    first_block = in_start // inner_size
    cube_real = values_real.reshape(row_count, blocks_in, inner_size)
    cube_imag = values_imag.reshape(row_count, blocks_in, inner_size)
    step_real, step_imag = phase_table(
        index_range(first_block, blocks_in), index_range(0, outer_size), outer_size, exponent_sign
    )
    mid_real, mid_imag = complex_einsum("rnq,nk->rkq", cube_real, cube_imag, step_real, step_imag)
    twist_real, twist_imag = phase_table(
        index_range(0, outer_size), index_range(0, inner_size), length, exponent_sign
    )
    mid_real, mid_imag = (
        mid_real * twist_real - mid_imag * twist_imag,
        mid_real * twist_imag + mid_imag * twist_real,
    )
    blocks_out = out_count // outer_size
    second_block = out_start // outer_size
    last_real, last_imag = phase_table(
        index_range(0, inner_size), index_range(second_block, blocks_out), inner_size, exponent_sign
    )
    done_real, done_imag = complex_einsum("rkq,qj->rjk", mid_real, mid_imag, last_real, last_imag)
    return (
        done_real.reshape(row_count, blocks_out * outer_size),
        done_imag.reshape(row_count, blocks_out * outer_size),
    )


def _allmax_kernel(nr, nc, x_ref, o_ref, buf_c, buf_r, part, ssem_c, rsem_c, ssem_r, rsem_r):
    me_r = lax.axis_index("row")
    me_c = lax.axis_index("col")
    mesh_t = pl.DeviceIdType.MESH
    barrier = pltpu.get_barrier_semaphore()
    for k in range(1, nc):
        pl.semaphore_signal(barrier, inc=1, device_id=(me_r, lax.rem(me_c + k, nc)), device_id_type=mesh_t)
    for k in range(1, nr):
        pl.semaphore_signal(barrier, inc=1, device_id=(lax.rem(me_r + k, nr), me_c), device_id_type=mesh_t)
    pl.semaphore_wait(barrier, (nc - 1) + (nr - 1))

    def col_copy(dst_c, slot):
        return pltpu.make_async_remote_copy(
            src_ref=x_ref, dst_ref=buf_c.at[slot], send_sem=ssem_c.at[dst_c],
            recv_sem=rsem_c.at[slot], device_id=(me_r, dst_c), device_id_type=mesh_t)
    sends = []
    for k in range(1, nc):
        cp = col_copy(lax.rem(me_c + k, nc), me_c)
        cp.start()
        sends.append(cp)
    acc = x_ref[...]
    for k in range(1, nc):
        src = lax.rem(me_c + nc - k, nc)
        col_copy(src, src).wait_recv()
        acc = jnp.maximum(acc, buf_c[src])
    for cp in sends:
        cp.wait_send()
    part[...] = acc

    def row_copy(dst_r, slot):
        return pltpu.make_async_remote_copy(
            src_ref=part, dst_ref=buf_r.at[slot], send_sem=ssem_r.at[dst_r],
            recv_sem=rsem_r.at[slot], device_id=(dst_r, me_c), device_id_type=mesh_t)
    sends = []
    for k in range(1, nr):
        cp = row_copy(lax.rem(me_r + k, nr), me_r)
        cp.start()
        sends.append(cp)
    for k in range(1, nr):
        src = lax.rem(me_r + nr - k, nr)
        row_copy(src, src).wait_recv()
        acc = jnp.maximum(acc, buf_r[src])
    for cp in sends:
        cp.wait_send()
    o_ref[...] = acc


def global_max(tile, nr, nc):
    return pl.pallas_call(
        functools.partial(_allmax_kernel, nr, nc),
        out_shape=jax.ShapeDtypeStruct(tile.shape, tile.dtype),
        in_specs=[pl.BlockSpec(memory_space=pltpu.VMEM)],
        out_specs=pl.BlockSpec(memory_space=pltpu.VMEM),
        scratch_shapes=[
            pltpu.VMEM((nc,) + tile.shape, tile.dtype),
            pltpu.VMEM((nr,) + tile.shape, tile.dtype),
            pltpu.VMEM(tile.shape, tile.dtype),
            pltpu.SemaphoreType.DMA((nc,)),
            pltpu.SemaphoreType.DMA((nc,)),
            pltpu.SemaphoreType.DMA((nr,)),
            pltpu.SemaphoreType.DMA((nr,)),
        ],
        compiler_params=pltpu.CompilerParams(collective_id=0, has_side_effects=True),
    )(tile)


def _col_exchange_kernel(nc, piece, place, re_ref, im_ref, re_out, im_out, send_sem, recv_sem, own_sem):
    me_r = lax.axis_index("row")
    me = lax.axis_index("col")
    mesh_t = pl.DeviceIdType.MESH
    barrier = pltpu.get_barrier_semaphore()
    for k in range(1, nc):
        pl.semaphore_signal(barrier, inc=1, device_id=(me_r, lax.rem(me + k, nc)), device_id_type=mesh_t)
    pl.semaphore_wait(barrier, nc - 1)
    srcs = (re_ref, im_ref)
    dsts = (re_out, im_out)

    def remote(peer, slot, part):
        return pltpu.make_async_remote_copy(
            src_ref=piece(srcs[part], peer), dst_ref=place(dsts[part], slot),
            send_sem=send_sem.at[peer, part], recv_sem=recv_sem.at[slot, part],
            device_id=(me_r, peer), device_id_type=mesh_t)

    sends = []
    for k in range(1, nc):
        peer = lax.rem(me + k, nc)
        for part in range(2):
            cp = remote(peer, me, part)
            cp.start()
            sends.append(cp)
    owns = []
    for part in range(2):
        cp = pltpu.make_async_copy(piece(srcs[part], me), place(dsts[part], me), own_sem.at[part])
        cp.start()
        owns.append(cp)
    for cp in owns:
        cp.wait()
    for k in range(1, nc):
        src = lax.rem(me + nc - k, nc)
        for part in range(2):
            remote(src, src, part).wait_recv()
    for cp in sends:
        cp.wait_send()


def col_exchange(re, im, out_rows, out_cols, piece, place, nc, cid):
    out = jax.ShapeDtypeStruct((out_rows, out_cols), re.dtype)
    return pl.pallas_call(
        functools.partial(_col_exchange_kernel, nc, piece, place),
        out_shape=(out, out),
        in_specs=[pl.BlockSpec(memory_space=pl.ANY)] * 2,
        out_specs=(pl.BlockSpec(memory_space=pl.ANY),) * 2,
        scratch_shapes=[
            pltpu.SemaphoreType.DMA((nc, 2)),
            pltpu.SemaphoreType.DMA((nc, 2)),
            pltpu.SemaphoreType.DMA((2,)),
        ],
        compiler_params=pltpu.CompilerParams(collective_id=cid, has_side_effects=True),
    )(re, im)


def rows_to_strip(re, im, nc, cid):
    rows, cols = re.shape
    band = rows // nc
    piece = lambda ref, p: ref.at[pl.ds(p * band, band), :]
    place = lambda ref, s: ref.at[:, pl.ds(s * cols, cols)]
    return col_exchange(re, im, band, cols * nc, piece, place, nc, cid)


def strip_to_rows(re, im, nc, cid):
    rows, cols = re.shape
    width = cols // nc
    piece = lambda ref, p: ref.at[:, pl.ds(p * width, width)]
    place = lambda ref, s: ref.at[pl.ds(s * rows, rows), :]
    return col_exchange(re, im, rows * nc, width, piece, place, nc, cid)


def _finish_kernel(nr, nc, re_ref, im_ref, peak_ref, re_out, im_out, top_out,
                   buf_c, buf_r, part, send_sem, recv_sem, own_sem, ssem_c, rsem_c, ssem_r, rsem_r):
    me_r = lax.axis_index("row")
    me = lax.axis_index("col")
    mesh_t = pl.DeviceIdType.MESH
    barrier = pltpu.get_barrier_semaphore()
    for k in range(1, nc):
        pl.semaphore_signal(barrier, inc=1, device_id=(me_r, lax.rem(me + k, nc)), device_id_type=mesh_t)
    for k in range(1, nr):
        pl.semaphore_signal(barrier, inc=1, device_id=(lax.rem(me_r + k, nr), me), device_id_type=mesh_t)
    pl.semaphore_wait(barrier, (nc - 1) + (nr - 1))

    def col_top(peer, slot):
        return pltpu.make_async_remote_copy(
            src_ref=peak_ref, dst_ref=buf_c.at[slot], send_sem=ssem_c.at[peer],
            recv_sem=rsem_c.at[slot], device_id=(me_r, peer), device_id_type=mesh_t)

    for k in range(1, nc):
        col_top(lax.rem(me + k, nc), me).start()

    rows = re_ref.shape[0]
    width = re_ref.shape[1] // nc
    srcs = (re_ref, im_ref)
    dsts = (re_out, im_out)

    def data(peer, slot, part_id):
        return pltpu.make_async_remote_copy(
            src_ref=srcs[part_id].at[:, pl.ds(peer * width, width)],
            dst_ref=dsts[part_id].at[pl.ds(slot * rows, rows), :],
            send_sem=send_sem.at[peer, part_id], recv_sem=recv_sem.at[slot, part_id],
            device_id=(me_r, peer), device_id_type=mesh_t)

    for k in range(1, nc):
        for part_id in range(2):
            data(lax.rem(me + k, nc), me, part_id).start()
    owns = []
    for part_id in range(2):
        cp = pltpu.make_async_copy(
            srcs[part_id].at[:, pl.ds(me * width, width)],
            dsts[part_id].at[pl.ds(me * rows, rows), :], own_sem.at[part_id])
        cp.start()
        owns.append(cp)

    acc = peak_ref[...]
    for k in range(1, nc):
        src = lax.rem(me + nc - k, nc)
        col_top(src, src).wait_recv()
        acc = jnp.maximum(acc, buf_c[src])
    for k in range(1, nc):
        col_top(lax.rem(me + k, nc), me).wait_send()
    part[...] = acc

    def row_top(peer, slot):
        return pltpu.make_async_remote_copy(
            src_ref=part, dst_ref=buf_r.at[slot], send_sem=ssem_r.at[peer],
            recv_sem=rsem_r.at[slot], device_id=(peer, me), device_id_type=mesh_t)

    for k in range(1, nr):
        row_top(lax.rem(me_r + k, nr), me_r).start()
    for k in range(1, nr):
        src = lax.rem(me_r + nr - k, nr)
        row_top(src, src).wait_recv()
        acc = jnp.maximum(acc, buf_r[src])
    for k in range(1, nr):
        row_top(lax.rem(me_r + k, nr), me_r).wait_send()
    top_out[...] = acc

    for cp in owns:
        cp.wait()
    for k in range(1, nc):
        src = lax.rem(me + nc - k, nc)
        for part_id in range(2):
            data(src, src, part_id).wait_recv()
            data(lax.rem(me + k, nc), me, part_id).wait_send()


def finish_exchange(re, im, peak_tile, nr, nc, cid):
    rows, cols = re.shape
    out = jax.ShapeDtypeStruct((rows * nc, cols // nc), re.dtype)
    top = jax.ShapeDtypeStruct(peak_tile.shape, peak_tile.dtype)
    return pl.pallas_call(
        functools.partial(_finish_kernel, nr, nc),
        out_shape=(out, out, top),
        in_specs=[pl.BlockSpec(memory_space=pl.ANY)] * 2 + [pl.BlockSpec(memory_space=pltpu.VMEM)],
        out_specs=(pl.BlockSpec(memory_space=pl.ANY),) * 2 + (pl.BlockSpec(memory_space=pltpu.VMEM),),
        scratch_shapes=[
            pltpu.VMEM((nc,) + peak_tile.shape, peak_tile.dtype),
            pltpu.VMEM((nr,) + peak_tile.shape, peak_tile.dtype),
            pltpu.VMEM(peak_tile.shape, peak_tile.dtype),
            pltpu.SemaphoreType.DMA((nc, 2)),
            pltpu.SemaphoreType.DMA((nc, 2)),
            pltpu.SemaphoreType.DMA((2,)),
            pltpu.SemaphoreType.DMA((nc,)),
            pltpu.SemaphoreType.DMA((nc,)),
            pltpu.SemaphoreType.DMA((nr,)),
            pltpu.SemaphoreType.DMA((nr,)),
        ],
        compiler_params=pltpu.CompilerParams(collective_id=cid, has_side_effects=True),
    )(re, im, peak_tile)


def _one_exchange_kernel(nr, nc, x_ref, x_out, send_sem, recv_sem, own_sem):
    n = nr * nc
    me = lax.axis_index("row") * nc + lax.axis_index("col")
    mesh_t = pl.DeviceIdType.MESH
    barrier = pltpu.get_barrier_semaphore()

    def where(p):
        return (p // nc, lax.rem(p, nc))

    def greet(k, carry):
        pl.semaphore_signal(barrier, inc=1, device_id=where(lax.rem(me + k, n)), device_id_type=mesh_t)
        return carry

    lax.fori_loop(1, n, greet, 0, unroll=8)
    pl.semaphore_wait(barrier, n - 1)

    def remote(peer, slot):
        return pltpu.make_async_remote_copy(
            src_ref=x_ref.at[peer], dst_ref=x_out.at[slot],
            send_sem=send_sem.at[peer], recv_sem=recv_sem.at[slot],
            device_id=where(peer), device_id_type=mesh_t)

    def send(k, carry):
        remote(lax.rem(me + k, n), me).start()
        return carry

    lax.fori_loop(1, n, send, 0, unroll=8)
    own = pltpu.make_async_copy(x_ref.at[me], x_out.at[me], own_sem.at[0])
    own.start()
    own.wait()

    def recv(k, carry):
        remote(lax.rem(me + n - k, n), lax.rem(me + n - k, n)).wait_recv()
        remote(lax.rem(me + k, n), me).wait_send()
        return carry

    lax.fori_loop(1, n, recv, 0, unroll=8)


def one_exchange(x, nr, nc, cid):
    n = nr * nc
    return pl.pallas_call(
        functools.partial(_one_exchange_kernel, nr, nc),
        out_shape=jax.ShapeDtypeStruct(x.shape, x.dtype),
        in_specs=[pl.BlockSpec(memory_space=pl.ANY)],
        out_specs=pl.BlockSpec(memory_space=pl.ANY),
        scratch_shapes=[
            pltpu.SemaphoreType.DMA((n,)),
            pltpu.SemaphoreType.DMA((n,)),
            pltpu.SemaphoreType.DMA((1,)),
        ],
        compiler_params=pltpu.CompilerParams(collective_id=cid, has_side_effects=True),
    )(x)


def transform_blocks(
    values_real, values_imag, exponent_sign, length, outer_size, in_blocks, out_blocks,
    lead_in=False, lead_out=False,
):
    inner_size = length // outer_size
    if lead_in:
        row_count = values_real.shape[1]
        cube_real = values_real.reshape(len(in_blocks), inner_size, row_count)
        cube_imag = values_imag.reshape(len(in_blocks), inner_size, row_count)
        first_form = "nqr,nk->rkq"
    else:
        row_count = values_real.shape[0]
        cube_real = values_real.reshape(row_count, len(in_blocks), inner_size)
        cube_imag = values_imag.reshape(row_count, len(in_blocks), inner_size)
        first_form = "rnq,nk->rkq"
    step_real, step_imag = phase_table(
        jnp.asarray(in_blocks, jnp.int32), index_range(0, outer_size), outer_size, exponent_sign
    )
    mid_real, mid_imag = complex_einsum(first_form, cube_real, cube_imag, step_real, step_imag)
    twist_real, twist_imag = phase_table(
        index_range(0, outer_size), index_range(0, inner_size), length, exponent_sign
    )
    mid_real, mid_imag = (
        mid_real * twist_real - mid_imag * twist_imag,
        mid_real * twist_imag + mid_imag * twist_real,
    )
    last_real, last_imag = phase_table(
        index_range(0, inner_size), jnp.asarray(out_blocks, jnp.int32), inner_size, exponent_sign
    )
    if lead_out:
        done_real, done_imag = complex_einsum(
            "rkq,qj->jkr", mid_real, mid_imag, last_real, last_imag
        )
        return (
            done_real.reshape(len(out_blocks) * outer_size, row_count),
            done_imag.reshape(len(out_blocks) * outer_size, row_count),
        )
    done_real, done_imag = complex_einsum("rkq,qj->rjk", mid_real, mid_imag, last_real, last_imag)
    return (
        done_real.reshape(row_count, len(out_blocks) * outer_size),
        done_imag.reshape(row_count, len(out_blocks) * outer_size),
    )


def band_blocks(padded, block, band_limit, multiple):
    top = math.ceil(band_limit) - 1
    low = list(range(top // block + 1))
    high = list(range((padded - top) // block, padded // block))
    while (len(low) + len(high)) * block % multiple:
        if len(low) <= len(high):
            low.append(low[-1] + 1)
        else:
            high.insert(0, high[0] - 1)
    return low + high


def pack_chunks(first, second, device_total, lead):
    if lead:
        width = first.shape[0] // device_total
        both = jnp.stack([first, second]).reshape(2, device_total, width, first.shape[1])
        both = both.transpose(1, 0, 2, 3)
    else:
        width = first.shape[1] // device_total
        both = jnp.stack([first, second]).reshape(2, first.shape[0], device_total, width)
        both = both.transpose(2, 0, 1, 3)
    return both.reshape(device_total, -1, 128)


def body(field_real, field_imag):
    padded = 2 * N
    quarter = padded // 4
    col_total = lax.axis_size("col")
    device_total = lax.axis_size("row") * col_total
    device = lax.axis_index("row") * col_total + lax.axis_index("col")
    strip_real, strip_imag = rows_to_strip(field_real, field_imag, col_total, 1)
    ratio_sq, band_limit = optics(padded)
    fwd_outer, fwd_inner = factor_pair(padded)
    inv_outer, inv_inner = fwd_outer, fwd_inner
    band = band_blocks(padded, fwd_outer, band_limit, device_total * 2)
    field_blocks = list(range(quarter // fwd_inner, (quarter + N) // fwd_inner))
    near_blocks = list(range(quarter // inv_outer, (quarter + N) // inv_outer))
    inv_band = band[::2] if all(b % 2 == 0 and band[i * 2 + 1] == b + 1 for i, b in enumerate(band[::2])) else None
    inv_band = [b // 2 for b in inv_band]
    pick_real, pick_imag = transform_blocks(
        strip_real, strip_imag, -1.0, padded, fwd_outer, field_blocks, band
    )
    strip_rows = pick_real.shape[0]
    col_width = pick_real.shape[1] // device_total
    packed = jnp.stack([pick_real, pick_imag]).reshape(2, strip_rows, device_total, col_width)
    packed = packed.transpose(2, 0, 1, 3).reshape(device_total, -1, 128)
    arrived = one_exchange(packed, lax.axis_size("row"), col_total, 4)
    arrived = arrived.reshape(device_total, 2, strip_rows, col_width).transpose(1, 0, 2, 3)
    arrived = arrived.reshape(2, device_total * strip_rows, col_width)
    turned_real, turned_imag = arrived[0], arrived[1]
    spec_real, spec_imag = transform_blocks(
        turned_real, turned_imag, -1.0, padded, fwd_outer, field_blocks, band, lead_in=True
    )
    band_freqs = np.array(band, np.int32)[:, None] * fwd_outer + np.arange(fwd_outer, dtype=np.int32)
    freq_ids = jnp.asarray(band_freqs.reshape(-1))
    freq_signed = signed_index(freq_ids, padded).astype(jnp.float32)
    col_ids = lax.dynamic_slice(freq_ids, (device * col_width,), (col_width,))
    col_signed = signed_index(col_ids, padded).astype(jnp.float32)
    gain_real, gain_imag = transfer(col_signed, freq_signed, ratio_sq, band_limit)
    mixed_real = spec_real * gain_real - spec_imag * gain_imag
    mixed_imag = spec_real * gain_imag + spec_imag * gain_real
    inv_real, inv_imag = transform_blocks(
        mixed_real, mixed_imag, 1.0, padded, inv_outer, inv_band, near_blocks
    )
    returned = one_exchange(
        pack_chunks(inv_real, inv_imag, device_total, False), lax.axis_size("row"), col_total, 5
    )
    returned = returned.reshape(device_total, 2, col_width, strip_rows).transpose(1, 0, 2, 3)
    returned = returned.reshape(2, device_total * col_width, strip_rows)
    line_real, line_imag = returned[0], returned[1]
    near_real, near_imag = transform_blocks(
        line_real, line_imag, 1.0, padded, inv_outer, inv_band, near_blocks, lead_in=True
    )
    local_amp = jnp.sqrt(near_real * near_real + near_imag * near_imag)
    peak_tile = jnp.max(local_amp.reshape(-1, 8, 128), axis=0)
    tile_near_real, tile_near_imag, top = finish_exchange(
        near_real, near_imag, peak_tile, lax.axis_size("row"), col_total, 3
    )
    peak = jnp.max(top)
    amplitude = jnp.sqrt(tile_near_real * tile_near_real + tile_near_imag * tile_near_imag)
    tile_rows, tile_cols = tile_near_real.shape
    row_ids = lax.axis_index("row") * tile_rows + jnp.arange(tile_rows, dtype=jnp.int32)
    col_ids_out = lax.axis_index("col") * tile_cols + jnp.arange(tile_cols, dtype=jnp.int32)
    even_cell = (row_ids[:, None] + col_ids_out[None, :]) % 2 == 0
    tile_real, tile_imag = encode(tile_near_real, tile_near_imag, amplitude, peak, even_cell)
    return (tile_real, tile_imag)


def solution(mesh):
    in_specs = (P("row", "col"), P("row", "col"))
    out_specs = (P("row", "col"), P("row", "col"))
    return jax.shard_map(body, mesh=mesh, in_specs=in_specs, out_specs=out_specs, check_vma=False)
```

```python
from functools import partial
import math

import jax
import jax.numpy as jnp
from jax import lax
from jax.sharding import PartitionSpec as P
from jax.experimental import pallas as pl
from jax.experimental.pallas import tpu as pltpu
import functools

import numpy as np

N = 4096


wavelength = 5.2e-07
distance = 0.2


def optics(padded_side):
    pitch = 2e-06 * math.sqrt(8192.0 / padded_side)
    extent = padded_side * pitch
    ratio_sq = (wavelength / extent) ** 2
    band_limit = extent / (wavelength * math.sqrt((2.0 * distance / extent) ** 2 + 1.0))
    return (ratio_sq, band_limit)


def factor_pair(length):
    bit_count = length.bit_length() - 1
    inner_size = 2 ** ((bit_count + 1) // 2)
    return (length // inner_size, inner_size)


def signed_index(index_ids, modulus):
    return jnp.where(index_ids >= modulus // 2, index_ids - modulus, index_ids)


def transfer(row_signed, col_signed, ratio_sq, band_limit):
    square = row_signed[:, None] * row_signed[:, None] + col_signed[None, :] * col_signed[None, :]
    scaled = ratio_sq * square
    phase_angle = -2.0 * math.pi * distance / wavelength * scaled / (1.0 + jnp.sqrt(1.0 - scaled))
    gauss_gain = jnp.exp(square * (-2.0 / (band_limit * band_limit)))
    inside = (jnp.abs(row_signed)[:, None] < band_limit) & (
        jnp.abs(col_signed)[None, :] < band_limit
    )
    total_gain = jnp.where(inside, gauss_gain, 0.0)
    return (total_gain * jnp.cos(phase_angle), total_gain * jnp.sin(phase_angle))


def encode(near_real, near_imag, amplitude, peak, even_cell):
    amp_level = 0.8 * amplitude / peak
    amp_floor = jnp.maximum(amplitude, 0.05 * peak)
    unit_real = near_real / amp_floor
    unit_imag = near_imag / amp_floor
    lift_part = jnp.sqrt(1.0 - amp_level * amp_level)
    cell_sign = jnp.where(even_cell, 1.0, -1.0)
    out_real = unit_real * amp_level + cell_sign * unit_imag * lift_part
    out_imag = unit_imag * amp_level - cell_sign * unit_real * lift_part
    return (out_real, out_imag)


def index_range(range_start, id_count):
    return jnp.arange(id_count, dtype=jnp.int32) + range_start


def phase_table(first_ids, second_ids, modulus, exponent_sign):
    product = first_ids[:, None] * second_ids[None, :] % modulus
    phase_arg = exponent_sign * 2.0 * math.pi / modulus * product.astype(jnp.float32)
    return (jnp.cos(phase_arg), jnp.sin(phase_arg))


def complex_einsum(form, left_real, left_imag, right_real, right_imag):
    real_dot = partial(jnp.einsum, form, precision=lax.Precision.HIGH)
    out_form = form.split("->")[1]
    axis = out_form.index(form.split("->")[0].split(",")[1][-1])
    width = right_real.shape[-1]
    both = jnp.concatenate([right_real, right_imag], axis=-1)
    from_real = real_dot(left_real, both)
    from_imag = real_dot(left_imag, both)
    real_part = partial(lax.slice_in_dim, start_index=0, limit_index=width, axis=axis)
    imag_part = partial(lax.slice_in_dim, start_index=width, limit_index=2 * width, axis=axis)
    out_real = real_part(from_real) - imag_part(from_imag)
    out_imag = imag_part(from_real) + real_part(from_imag)
    return (out_real, out_imag)


def transform_last(values_real, values_imag, exponent_sign, in_start, out_start, out_count, length):
    outer_size, inner_size = factor_pair(length)
    row_count = values_real.shape[0]
    blocks_in = values_real.shape[1] // inner_size
    first_block = in_start // inner_size
    cube_real = values_real.reshape(row_count, blocks_in, inner_size)
    cube_imag = values_imag.reshape(row_count, blocks_in, inner_size)
    step_real, step_imag = phase_table(
        index_range(first_block, blocks_in), index_range(0, outer_size), outer_size, exponent_sign
    )
    mid_real, mid_imag = complex_einsum("rnq,nk->rkq", cube_real, cube_imag, step_real, step_imag)
    twist_real, twist_imag = phase_table(
        index_range(0, outer_size), index_range(0, inner_size), length, exponent_sign
    )
    mid_real, mid_imag = (
        mid_real * twist_real - mid_imag * twist_imag,
        mid_real * twist_imag + mid_imag * twist_real,
    )
    blocks_out = out_count // outer_size
    second_block = out_start // outer_size
    last_real, last_imag = phase_table(
        index_range(0, inner_size), index_range(second_block, blocks_out), inner_size, exponent_sign
    )
    done_real, done_imag = complex_einsum("rkq,qj->rjk", mid_real, mid_imag, last_real, last_imag)
    return (
        done_real.reshape(row_count, blocks_out * outer_size),
        done_imag.reshape(row_count, blocks_out * outer_size),
    )


def _allmax_kernel(nr, nc, x_ref, o_ref, buf_c, buf_r, part, ssem_c, rsem_c, ssem_r, rsem_r):
    me_r = lax.axis_index("row")
    me_c = lax.axis_index("col")
    mesh_t = pl.DeviceIdType.MESH
    barrier = pltpu.get_barrier_semaphore()
    for k in range(1, nc):
        pl.semaphore_signal(barrier, inc=1, device_id=(me_r, lax.rem(me_c + k, nc)), device_id_type=mesh_t)
    for k in range(1, nr):
        pl.semaphore_signal(barrier, inc=1, device_id=(lax.rem(me_r + k, nr), me_c), device_id_type=mesh_t)
    pl.semaphore_wait(barrier, (nc - 1) + (nr - 1))

    def col_copy(dst_c, slot):
        return pltpu.make_async_remote_copy(
            src_ref=x_ref, dst_ref=buf_c.at[slot], send_sem=ssem_c.at[dst_c],
            recv_sem=rsem_c.at[slot], device_id=(me_r, dst_c), device_id_type=mesh_t)
    sends = []
    for k in range(1, nc):
        cp = col_copy(lax.rem(me_c + k, nc), me_c)
        cp.start()
        sends.append(cp)
    acc = x_ref[...]
    for k in range(1, nc):
        src = lax.rem(me_c + nc - k, nc)
        col_copy(src, src).wait_recv()
        acc = jnp.maximum(acc, buf_c[src])
    for cp in sends:
        cp.wait_send()
    part[...] = acc

    def row_copy(dst_r, slot):
        return pltpu.make_async_remote_copy(
            src_ref=part, dst_ref=buf_r.at[slot], send_sem=ssem_r.at[dst_r],
            recv_sem=rsem_r.at[slot], device_id=(dst_r, me_c), device_id_type=mesh_t)
    sends = []
    for k in range(1, nr):
        cp = row_copy(lax.rem(me_r + k, nr), me_r)
        cp.start()
        sends.append(cp)
    for k in range(1, nr):
        src = lax.rem(me_r + nr - k, nr)
        row_copy(src, src).wait_recv()
        acc = jnp.maximum(acc, buf_r[src])
    for cp in sends:
        cp.wait_send()
    o_ref[...] = acc


def global_max(tile, nr, nc):
    return pl.pallas_call(
        functools.partial(_allmax_kernel, nr, nc),
        out_shape=jax.ShapeDtypeStruct(tile.shape, tile.dtype),
        in_specs=[pl.BlockSpec(memory_space=pltpu.VMEM)],
        out_specs=pl.BlockSpec(memory_space=pltpu.VMEM),
        scratch_shapes=[
            pltpu.VMEM((nc,) + tile.shape, tile.dtype),
            pltpu.VMEM((nr,) + tile.shape, tile.dtype),
            pltpu.VMEM(tile.shape, tile.dtype),
            pltpu.SemaphoreType.DMA((nc,)),
            pltpu.SemaphoreType.DMA((nc,)),
            pltpu.SemaphoreType.DMA((nr,)),
            pltpu.SemaphoreType.DMA((nr,)),
        ],
        compiler_params=pltpu.CompilerParams(collective_id=0, has_side_effects=True),
    )(tile)


def _col_exchange_kernel(nc, piece, place, re_ref, im_ref, re_out, im_out, send_sem, recv_sem, own_sem):
    me_r = lax.axis_index("row")
    me = lax.axis_index("col")
    mesh_t = pl.DeviceIdType.MESH
    barrier = pltpu.get_barrier_semaphore()
    def greet(k, carry):
        pl.semaphore_signal(barrier, inc=1, device_id=(me_r, lax.rem(me + k, nc)), device_id_type=mesh_t)
        return carry

    lax.fori_loop(1, nc, greet, 0)
    pl.semaphore_wait(barrier, nc - 1)
    srcs = (re_ref, im_ref)
    dsts = (re_out, im_out)

    def remote(peer, slot, part):
        return pltpu.make_async_remote_copy(
            src_ref=piece(srcs[part], peer), dst_ref=place(dsts[part], slot),
            send_sem=send_sem.at[peer, part], recv_sem=recv_sem.at[slot, part],
            device_id=(me_r, peer), device_id_type=mesh_t)

    def send(k, carry):
        for part in range(2):
            remote(lax.rem(me + k, nc), me, part).start()
        return carry

    lax.fori_loop(1, nc, send, 0)
    owns = []
    for part in range(2):
        cp = pltpu.make_async_copy(piece(srcs[part], me), place(dsts[part], me), own_sem.at[part])
        cp.start()
        owns.append(cp)
    for cp in owns:
        cp.wait()

    def recv(k, carry):
        src = lax.rem(me + nc - k, nc)
        for part in range(2):
            remote(src, src, part).wait_recv()
            remote(lax.rem(me + k, nc), me, part).wait_send()
        return carry

    lax.fori_loop(1, nc, recv, 0)


def col_exchange(re, im, out_rows, out_cols, piece, place, nc, cid):
    out = jax.ShapeDtypeStruct((out_rows, out_cols), re.dtype)
    return pl.pallas_call(
        functools.partial(_col_exchange_kernel, nc, piece, place),
        out_shape=(out, out),
        in_specs=[pl.BlockSpec(memory_space=pl.ANY)] * 2,
        out_specs=(pl.BlockSpec(memory_space=pl.ANY),) * 2,
        scratch_shapes=[
            pltpu.SemaphoreType.DMA((nc, 2)),
            pltpu.SemaphoreType.DMA((nc, 2)),
            pltpu.SemaphoreType.DMA((2,)),
        ],
        compiler_params=pltpu.CompilerParams(collective_id=cid, has_side_effects=True),
    )(re, im)


def rows_to_strip(re, im, nc, cid):
    rows, cols = re.shape
    band = rows // nc
    piece = lambda ref, p: ref.at[pl.ds(p * band, band), :]
    place = lambda ref, s: ref.at[:, pl.ds(s * cols, cols)]
    return col_exchange(re, im, band, cols * nc, piece, place, nc, cid)


def strip_to_rows(re, im, nc, cid):
    rows, cols = re.shape
    width = cols // nc
    piece = lambda ref, p: ref.at[:, pl.ds(p * width, width)]
    place = lambda ref, s: ref.at[pl.ds(s * rows, rows), :]
    return col_exchange(re, im, rows * nc, width, piece, place, nc, cid)


def _finish_kernel(nr, nc, re_ref, im_ref, peak_ref, re_out, im_out, top_out,
                   buf_c, buf_r, part, send_sem, recv_sem, own_sem, ssem_c, rsem_c, ssem_r, rsem_r):
    me_r = lax.axis_index("row")
    me = lax.axis_index("col")
    mesh_t = pl.DeviceIdType.MESH
    barrier = pltpu.get_barrier_semaphore()
    for k in range(1, nc):
        pl.semaphore_signal(barrier, inc=1, device_id=(me_r, lax.rem(me + k, nc)), device_id_type=mesh_t)
    for k in range(1, nr):
        pl.semaphore_signal(barrier, inc=1, device_id=(lax.rem(me_r + k, nr), me), device_id_type=mesh_t)
    pl.semaphore_wait(barrier, (nc - 1) + (nr - 1))

    def col_top(peer, slot):
        return pltpu.make_async_remote_copy(
            src_ref=peak_ref, dst_ref=buf_c.at[slot], send_sem=ssem_c.at[peer],
            recv_sem=rsem_c.at[slot], device_id=(me_r, peer), device_id_type=mesh_t)

    def top_send(k, carry):
        col_top(lax.rem(me + k, nc), me).start()
        return carry

    lax.fori_loop(1, nc, top_send, 0)

    rows = re_ref.shape[0]
    width = re_ref.shape[1] // nc
    srcs = (re_ref, im_ref)
    dsts = (re_out, im_out)

    def data(peer, slot, part_id):
        return pltpu.make_async_remote_copy(
            src_ref=srcs[part_id].at[:, pl.ds(peer * width, width)],
            dst_ref=dsts[part_id].at[pl.ds(slot * rows, rows), :],
            send_sem=send_sem.at[peer, part_id], recv_sem=recv_sem.at[slot, part_id],
            device_id=(me_r, peer), device_id_type=mesh_t)

    def data_send(k, carry):
        for part_id in range(2):
            data(lax.rem(me + k, nc), me, part_id).start()
        return carry

    lax.fori_loop(1, nc, data_send, 0)
    owns = []
    for part_id in range(2):
        cp = pltpu.make_async_copy(
            srcs[part_id].at[:, pl.ds(me * width, width)],
            dsts[part_id].at[pl.ds(me * rows, rows), :], own_sem.at[part_id])
        cp.start()
        owns.append(cp)

    acc = peak_ref[...]
    def top_recv(k, acc):
        src = lax.rem(me + nc - k, nc)
        col_top(src, src).wait_recv()
        col_top(lax.rem(me + k, nc), me).wait_send()
        return jnp.maximum(acc, buf_c[src])

    acc = lax.fori_loop(1, nc, top_recv, acc)
    part[...] = acc

    def row_top(peer, slot):
        return pltpu.make_async_remote_copy(
            src_ref=part, dst_ref=buf_r.at[slot], send_sem=ssem_r.at[peer],
            recv_sem=rsem_r.at[slot], device_id=(peer, me), device_id_type=mesh_t)

    for k in range(1, nr):
        row_top(lax.rem(me_r + k, nr), me_r).start()
    for k in range(1, nr):
        src = lax.rem(me_r + nr - k, nr)
        row_top(src, src).wait_recv()
        acc = jnp.maximum(acc, buf_r[src])
    for k in range(1, nr):
        row_top(lax.rem(me_r + k, nr), me_r).wait_send()
    top_out[...] = acc

    for cp in owns:
        cp.wait()
    def data_recv(k, carry):
        src = lax.rem(me + nc - k, nc)
        for part_id in range(2):
            data(src, src, part_id).wait_recv()
            data(lax.rem(me + k, nc), me, part_id).wait_send()
        return carry

    lax.fori_loop(1, nc, data_recv, 0)


def finish_exchange(re, im, peak_tile, nr, nc, cid):
    rows, cols = re.shape
    out = jax.ShapeDtypeStruct((rows * nc, cols // nc), re.dtype)
    top = jax.ShapeDtypeStruct(peak_tile.shape, peak_tile.dtype)
    return pl.pallas_call(
        functools.partial(_finish_kernel, nr, nc),
        out_shape=(out, out, top),
        in_specs=[pl.BlockSpec(memory_space=pl.ANY)] * 2 + [pl.BlockSpec(memory_space=pltpu.VMEM)],
        out_specs=(pl.BlockSpec(memory_space=pl.ANY),) * 2 + (pl.BlockSpec(memory_space=pltpu.VMEM),),
        scratch_shapes=[
            pltpu.VMEM((nc,) + peak_tile.shape, peak_tile.dtype),
            pltpu.VMEM((nr,) + peak_tile.shape, peak_tile.dtype),
            pltpu.VMEM(peak_tile.shape, peak_tile.dtype),
            pltpu.SemaphoreType.DMA((nc, 2)),
            pltpu.SemaphoreType.DMA((nc, 2)),
            pltpu.SemaphoreType.DMA((2,)),
            pltpu.SemaphoreType.DMA((nc,)),
            pltpu.SemaphoreType.DMA((nc,)),
            pltpu.SemaphoreType.DMA((nr,)),
            pltpu.SemaphoreType.DMA((nr,)),
        ],
        compiler_params=pltpu.CompilerParams(collective_id=cid, has_side_effects=True),
    )(re, im, peak_tile)


def _one_exchange_kernel(nr, nc, x_ref, x_out, send_sem, recv_sem, own_sem):
    n = nr * nc
    me = lax.axis_index("row") * nc + lax.axis_index("col")
    mesh_t = pl.DeviceIdType.MESH
    barrier = pltpu.get_barrier_semaphore()

    def where(p):
        return (p // nc, lax.rem(p, nc))

    def greet(k, carry):
        pl.semaphore_signal(barrier, inc=1, device_id=where(lax.rem(me + k, n)), device_id_type=mesh_t)
        return carry

    lax.fori_loop(1, n, greet, 0)
    pl.semaphore_wait(barrier, n - 1)

    def remote(peer, slot):
        return pltpu.make_async_remote_copy(
            src_ref=x_ref.at[peer], dst_ref=x_out.at[slot],
            send_sem=send_sem.at[peer], recv_sem=recv_sem.at[slot],
            device_id=where(peer), device_id_type=mesh_t)

    def send(k, carry):
        remote(lax.rem(me + k, n), me).start()
        return carry

    lax.fori_loop(1, n, send, 0)
    own = pltpu.make_async_copy(x_ref.at[me], x_out.at[me], own_sem.at[0])
    own.start()
    own.wait()

    def recv(k, carry):
        remote(lax.rem(me + n - k, n), lax.rem(me + n - k, n)).wait_recv()
        remote(lax.rem(me + k, n), me).wait_send()
        return carry

    lax.fori_loop(1, n, recv, 0)


def one_exchange(x, nr, nc, cid):
    n = nr * nc
    return pl.pallas_call(
        functools.partial(_one_exchange_kernel, nr, nc),
        out_shape=jax.ShapeDtypeStruct(x.shape, x.dtype),
        in_specs=[pl.BlockSpec(memory_space=pl.ANY)],
        out_specs=pl.BlockSpec(memory_space=pl.ANY),
        scratch_shapes=[
            pltpu.SemaphoreType.DMA((n,)),
            pltpu.SemaphoreType.DMA((n,)),
            pltpu.SemaphoreType.DMA((1,)),
        ],
        compiler_params=pltpu.CompilerParams(collective_id=cid, has_side_effects=True),
    )(x)


def transform_blocks(
    values_real, values_imag, exponent_sign, length, outer_size, in_blocks, out_blocks,
    lead_in=False, lead_out=False,
):
    inner_size = length // outer_size
    if lead_in:
        row_count = values_real.shape[1]
        cube_real = values_real.reshape(len(in_blocks), inner_size, row_count)
        cube_imag = values_imag.reshape(len(in_blocks), inner_size, row_count)
        first_form = "nqr,nk->rkq"
    else:
        row_count = values_real.shape[0]
        cube_real = values_real.reshape(row_count, len(in_blocks), inner_size)
        cube_imag = values_imag.reshape(row_count, len(in_blocks), inner_size)
        first_form = "rnq,nk->rkq"
    step_real, step_imag = phase_table(
        jnp.asarray(in_blocks, jnp.int32), index_range(0, outer_size), outer_size, exponent_sign
    )
    mid_real, mid_imag = complex_einsum(first_form, cube_real, cube_imag, step_real, step_imag)
    twist_real, twist_imag = phase_table(
        index_range(0, outer_size), index_range(0, inner_size), length, exponent_sign
    )
    mid_real, mid_imag = (
        mid_real * twist_real - mid_imag * twist_imag,
        mid_real * twist_imag + mid_imag * twist_real,
    )
    last_real, last_imag = phase_table(
        index_range(0, inner_size), jnp.asarray(out_blocks, jnp.int32), inner_size, exponent_sign
    )
    if lead_out:
        done_real, done_imag = complex_einsum(
            "rkq,qj->jkr", mid_real, mid_imag, last_real, last_imag
        )
        return (
            done_real.reshape(len(out_blocks) * outer_size, row_count),
            done_imag.reshape(len(out_blocks) * outer_size, row_count),
        )
    done_real, done_imag = complex_einsum("rkq,qj->rjk", mid_real, mid_imag, last_real, last_imag)
    return (
        done_real.reshape(row_count, len(out_blocks) * outer_size),
        done_imag.reshape(row_count, len(out_blocks) * outer_size),
    )


def band_blocks(padded, block, band_limit, multiple):
    top = math.ceil(band_limit) - 1
    low = list(range(top // block + 1))
    high = list(range((padded - top) // block, padded // block))
    while (len(low) + len(high)) * block % multiple:
        if len(low) <= len(high):
            low.append(low[-1] + 1)
        else:
            high.insert(0, high[0] - 1)
    return low + high


def pack_chunks(first, second, device_total, lead):
    if lead:
        width = first.shape[0] // device_total
        both = jnp.stack([first, second]).reshape(2, device_total, width, first.shape[1])
        both = both.transpose(1, 0, 2, 3)
    else:
        width = first.shape[1] // device_total
        both = jnp.stack([first, second]).reshape(2, first.shape[0], device_total, width)
        both = both.transpose(2, 0, 1, 3)
    return both.reshape(device_total, -1, 128)


def body(field_real, field_imag):
    padded = 2 * N
    quarter = padded // 4
    col_total = lax.axis_size("col")
    device_total = lax.axis_size("row") * col_total
    device = lax.axis_index("row") * col_total + lax.axis_index("col")
    strip_real, strip_imag = rows_to_strip(field_real, field_imag, col_total, 1)
    ratio_sq, band_limit = optics(padded)
    fwd_outer, fwd_inner = factor_pair(padded)
    inv_outer, inv_inner = fwd_outer, fwd_inner
    band = band_blocks(padded, fwd_outer, band_limit, device_total * 2)
    field_blocks = list(range(quarter // fwd_inner, (quarter + N) // fwd_inner))
    near_blocks = list(range(quarter // inv_outer, (quarter + N) // inv_outer))
    inv_band = band[::2] if all(b % 2 == 0 and band[i * 2 + 1] == b + 1 for i, b in enumerate(band[::2])) else None
    inv_band = [b // 2 for b in inv_band]
    pick_real, pick_imag = transform_blocks(
        strip_real, strip_imag, -1.0, padded, fwd_outer, field_blocks, band
    )
    strip_rows = pick_real.shape[0]
    col_width = pick_real.shape[1] // device_total
    packed = jnp.stack([pick_real, pick_imag]).reshape(2, strip_rows, device_total, col_width)
    packed = packed.transpose(2, 0, 1, 3).reshape(device_total, -1, 128)
    arrived = one_exchange(packed, lax.axis_size("row"), col_total, 4)
    arrived = arrived.reshape(device_total, 2, strip_rows, col_width).transpose(1, 0, 2, 3)
    arrived = arrived.reshape(2, device_total * strip_rows, col_width)
    turned_real, turned_imag = arrived[0], arrived[1]
    spec_real, spec_imag = transform_blocks(
        turned_real, turned_imag, -1.0, padded, fwd_outer, field_blocks, band, lead_in=True
    )
    band_freqs = np.array(band, np.int32)[:, None] * fwd_outer + np.arange(fwd_outer, dtype=np.int32)
    freq_ids = jnp.asarray(band_freqs.reshape(-1))
    freq_signed = signed_index(freq_ids, padded).astype(jnp.float32)
    col_ids = lax.dynamic_slice(freq_ids, (device * col_width,), (col_width,))
    col_signed = signed_index(col_ids, padded).astype(jnp.float32)
    gain_real, gain_imag = transfer(col_signed, freq_signed, ratio_sq, band_limit)
    mixed_real = spec_real * gain_real - spec_imag * gain_imag
    mixed_imag = spec_real * gain_imag + spec_imag * gain_real
    inv_real, inv_imag = transform_blocks(
        mixed_real, mixed_imag, 1.0, padded, inv_outer, inv_band, near_blocks
    )
    returned = one_exchange(
        pack_chunks(inv_real, inv_imag, device_total, False), lax.axis_size("row"), col_total, 5
    )
    returned = returned.reshape(device_total, 2, col_width, strip_rows).transpose(1, 0, 2, 3)
    returned = returned.reshape(2, device_total * col_width, strip_rows)
    line_real, line_imag = returned[0], returned[1]
    near_real, near_imag = transform_blocks(
        line_real, line_imag, 1.0, padded, inv_outer, inv_band, near_blocks, lead_in=True
    )
    local_amp = jnp.sqrt(near_real * near_real + near_imag * near_imag)
    peak_tile = jnp.max(local_amp.reshape(-1, 8, 128), axis=0)
    tile_near_real, tile_near_imag, top = finish_exchange(
        near_real, near_imag, peak_tile, lax.axis_size("row"), col_total, 3
    )
    peak = jnp.max(top)
    amplitude = jnp.sqrt(tile_near_real * tile_near_real + tile_near_imag * tile_near_imag)
    tile_rows, tile_cols = tile_near_real.shape
    row_ids = lax.axis_index("row") * tile_rows + jnp.arange(tile_rows, dtype=jnp.int32)
    col_ids_out = lax.axis_index("col") * tile_cols + jnp.arange(tile_cols, dtype=jnp.int32)
    even_cell = (row_ids[:, None] + col_ids_out[None, :]) % 2 == 0
    tile_real, tile_imag = encode(tile_near_real, tile_near_imag, amplitude, peak, even_cell)
    return (tile_real, tile_imag)


def solution(mesh):
    in_specs = (P("row", "col"), P("row", "col"))
    out_specs = (P("row", "col"), P("row", "col"))
    return jax.shard_map(body, mesh=mesh, in_specs=in_specs, out_specs=out_specs, check_vma=False)
```

```python
from functools import partial
import math

import jax
import jax.numpy as jnp
from jax import lax
from jax.sharding import PartitionSpec as P
from jax.experimental import pallas as pl
from jax.experimental.pallas import tpu as pltpu
import functools

import numpy as np

N = 4096


wavelength = 5.2e-07
distance = 0.2


def optics(padded_side):
    pitch = 2e-06 * math.sqrt(8192.0 / padded_side)
    extent = padded_side * pitch
    ratio_sq = (wavelength / extent) ** 2
    band_limit = extent / (wavelength * math.sqrt((2.0 * distance / extent) ** 2 + 1.0))
    return (ratio_sq, band_limit)


def factor_pair(length):
    bit_count = length.bit_length() - 1
    inner_size = 2 ** ((bit_count + 1) // 2)
    return (length // inner_size, inner_size)


def signed_index(index_ids, modulus):
    return jnp.where(index_ids >= modulus // 2, index_ids - modulus, index_ids)


def transfer(row_signed, col_signed, ratio_sq, band_limit):
    square = row_signed[:, None] * row_signed[:, None] + col_signed[None, :] * col_signed[None, :]
    scaled = ratio_sq * square
    phase_angle = -2.0 * math.pi * distance / wavelength * scaled / (1.0 + jnp.sqrt(1.0 - scaled))
    gauss_gain = jnp.exp(square * (-2.0 / (band_limit * band_limit)))
    inside = (jnp.abs(row_signed)[:, None] < band_limit) & (
        jnp.abs(col_signed)[None, :] < band_limit
    )
    total_gain = jnp.where(inside, gauss_gain, 0.0)
    return (total_gain * jnp.cos(phase_angle), total_gain * jnp.sin(phase_angle))


def encode(near_real, near_imag, amplitude, peak, even_cell):
    amp_level = 0.8 * amplitude / peak
    amp_floor = jnp.maximum(amplitude, 0.05 * peak)
    unit_real = near_real / amp_floor
    unit_imag = near_imag / amp_floor
    lift_part = jnp.sqrt(1.0 - amp_level * amp_level)
    cell_sign = jnp.where(even_cell, 1.0, -1.0)
    out_real = unit_real * amp_level + cell_sign * unit_imag * lift_part
    out_imag = unit_imag * amp_level - cell_sign * unit_real * lift_part
    return (out_real, out_imag)


def index_range(range_start, id_count):
    return jnp.arange(id_count, dtype=jnp.int32) + range_start


def phase_table(first_ids, second_ids, modulus, exponent_sign):
    product = first_ids[:, None] * second_ids[None, :] % modulus
    phase_arg = exponent_sign * 2.0 * math.pi / modulus * product.astype(jnp.float32)
    return (jnp.cos(phase_arg), jnp.sin(phase_arg))


def complex_einsum(form, left_real, left_imag, right_real, right_imag):
    real_dot = partial(jnp.einsum, form, precision=lax.Precision.HIGH)
    out_form = form.split("->")[1]
    axis = out_form.index(form.split("->")[0].split(",")[1][-1])
    width = right_real.shape[-1]
    both = jnp.concatenate([right_real, right_imag], axis=-1)
    from_real = real_dot(left_real, both)
    from_imag = real_dot(left_imag, both)
    real_part = partial(lax.slice_in_dim, start_index=0, limit_index=width, axis=axis)
    imag_part = partial(lax.slice_in_dim, start_index=width, limit_index=2 * width, axis=axis)
    out_real = real_part(from_real) - imag_part(from_imag)
    out_imag = imag_part(from_real) + real_part(from_imag)
    return (out_real, out_imag)


def transform_last(values_real, values_imag, exponent_sign, in_start, out_start, out_count, length):
    outer_size, inner_size = factor_pair(length)
    row_count = values_real.shape[0]
    blocks_in = values_real.shape[1] // inner_size
    first_block = in_start // inner_size
    cube_real = values_real.reshape(row_count, blocks_in, inner_size)
    cube_imag = values_imag.reshape(row_count, blocks_in, inner_size)
    step_real, step_imag = phase_table(
        index_range(first_block, blocks_in), index_range(0, outer_size), outer_size, exponent_sign
    )
    mid_real, mid_imag = complex_einsum("rnq,nk->rkq", cube_real, cube_imag, step_real, step_imag)
    twist_real, twist_imag = phase_table(
        index_range(0, outer_size), index_range(0, inner_size), length, exponent_sign
    )
    mid_real, mid_imag = (
        mid_real * twist_real - mid_imag * twist_imag,
        mid_real * twist_imag + mid_imag * twist_real,
    )
    blocks_out = out_count // outer_size
    second_block = out_start // outer_size
    last_real, last_imag = phase_table(
        index_range(0, inner_size), index_range(second_block, blocks_out), inner_size, exponent_sign
    )
    done_real, done_imag = complex_einsum("rkq,qj->rjk", mid_real, mid_imag, last_real, last_imag)
    return (
        done_real.reshape(row_count, blocks_out * outer_size),
        done_imag.reshape(row_count, blocks_out * outer_size),
    )


def _allmax_kernel(nr, nc, x_ref, o_ref, buf_c, buf_r, part, ssem_c, rsem_c, ssem_r, rsem_r):
    me_r = lax.axis_index("row")
    me_c = lax.axis_index("col")
    mesh_t = pl.DeviceIdType.MESH
    barrier = pltpu.get_barrier_semaphore()
    for k in range(1, nc):
        pl.semaphore_signal(barrier, inc=1, device_id=(me_r, lax.rem(me_c + k, nc)), device_id_type=mesh_t)
    for k in range(1, nr):
        pl.semaphore_signal(barrier, inc=1, device_id=(lax.rem(me_r + k, nr), me_c), device_id_type=mesh_t)
    pl.semaphore_wait(barrier, (nc - 1) + (nr - 1))

    def col_copy(dst_c, slot):
        return pltpu.make_async_remote_copy(
            src_ref=x_ref, dst_ref=buf_c.at[slot], send_sem=ssem_c.at[dst_c],
            recv_sem=rsem_c.at[slot], device_id=(me_r, dst_c), device_id_type=mesh_t)
    sends = []
    for k in range(1, nc):
        cp = col_copy(lax.rem(me_c + k, nc), me_c)
        cp.start()
        sends.append(cp)
    acc = x_ref[...]
    for k in range(1, nc):
        src = lax.rem(me_c + nc - k, nc)
        col_copy(src, src).wait_recv()
        acc = jnp.maximum(acc, buf_c[src])
    for cp in sends:
        cp.wait_send()
    part[...] = acc

    def row_copy(dst_r, slot):
        return pltpu.make_async_remote_copy(
            src_ref=part, dst_ref=buf_r.at[slot], send_sem=ssem_r.at[dst_r],
            recv_sem=rsem_r.at[slot], device_id=(dst_r, me_c), device_id_type=mesh_t)
    sends = []
    for k in range(1, nr):
        cp = row_copy(lax.rem(me_r + k, nr), me_r)
        cp.start()
        sends.append(cp)
    for k in range(1, nr):
        src = lax.rem(me_r + nr - k, nr)
        row_copy(src, src).wait_recv()
        acc = jnp.maximum(acc, buf_r[src])
    for cp in sends:
        cp.wait_send()
    o_ref[...] = acc


def global_max(tile, nr, nc):
    return pl.pallas_call(
        functools.partial(_allmax_kernel, nr, nc),
        out_shape=jax.ShapeDtypeStruct(tile.shape, tile.dtype),
        in_specs=[pl.BlockSpec(memory_space=pltpu.VMEM)],
        out_specs=pl.BlockSpec(memory_space=pltpu.VMEM),
        scratch_shapes=[
            pltpu.VMEM((nc,) + tile.shape, tile.dtype),
            pltpu.VMEM((nr,) + tile.shape, tile.dtype),
            pltpu.VMEM(tile.shape, tile.dtype),
            pltpu.SemaphoreType.DMA((nc,)),
            pltpu.SemaphoreType.DMA((nc,)),
            pltpu.SemaphoreType.DMA((nr,)),
            pltpu.SemaphoreType.DMA((nr,)),
        ],
        compiler_params=pltpu.CompilerParams(collective_id=0, has_side_effects=True),
    )(tile)


def _col_exchange_kernel(nc, piece, place, re_ref, im_ref, re_out, im_out, send_sem, recv_sem, own_sem):
    me_r = lax.axis_index("row")
    me = lax.axis_index("col")
    mesh_t = pl.DeviceIdType.MESH
    barrier = pltpu.get_barrier_semaphore()
    for k in range(1, nc):
        pl.semaphore_signal(barrier, inc=1, device_id=(me_r, lax.rem(me + k, nc)), device_id_type=mesh_t)
    pl.semaphore_wait(barrier, nc - 1)
    srcs = (re_ref, im_ref)
    dsts = (re_out, im_out)

    def remote(peer, slot, part):
        return pltpu.make_async_remote_copy(
            src_ref=piece(srcs[part], peer), dst_ref=place(dsts[part], slot),
            send_sem=send_sem.at[peer, part], recv_sem=recv_sem.at[slot, part],
            device_id=(me_r, peer), device_id_type=mesh_t)

    sends = []
    for k in range(1, nc):
        peer = lax.rem(me + k, nc)
        for part in range(2):
            cp = remote(peer, me, part)
            cp.start()
            sends.append(cp)
    owns = []
    for part in range(2):
        cp = pltpu.make_async_copy(piece(srcs[part], me), place(dsts[part], me), own_sem.at[part])
        cp.start()
        owns.append(cp)
    for cp in owns:
        cp.wait()
    for k in range(1, nc):
        src = lax.rem(me + nc - k, nc)
        for part in range(2):
            remote(src, src, part).wait_recv()
    for cp in sends:
        cp.wait_send()


def col_exchange(re, im, out_rows, out_cols, piece, place, nc, cid):
    out = jax.ShapeDtypeStruct((out_rows, out_cols), re.dtype)
    return pl.pallas_call(
        functools.partial(_col_exchange_kernel, nc, piece, place),
        out_shape=(out, out),
        in_specs=[pl.BlockSpec(memory_space=pl.ANY)] * 2,
        out_specs=(pl.BlockSpec(memory_space=pl.ANY),) * 2,
        scratch_shapes=[
            pltpu.SemaphoreType.DMA((nc, 2)),
            pltpu.SemaphoreType.DMA((nc, 2)),
            pltpu.SemaphoreType.DMA((2,)),
        ],
        compiler_params=pltpu.CompilerParams(collective_id=cid, has_side_effects=True),
    )(re, im)


def rows_to_strip(re, im, nc, cid):
    rows, cols = re.shape
    band = rows // nc
    piece = lambda ref, p: ref.at[pl.ds(p * band, band), :]
    place = lambda ref, s: ref.at[:, pl.ds(s * cols, cols)]
    return col_exchange(re, im, band, cols * nc, piece, place, nc, cid)


def strip_to_rows(re, im, nc, cid):
    rows, cols = re.shape
    width = cols // nc
    piece = lambda ref, p: ref.at[:, pl.ds(p * width, width)]
    place = lambda ref, s: ref.at[pl.ds(s * rows, rows), :]
    return col_exchange(re, im, rows * nc, width, piece, place, nc, cid)


def _finish_kernel(nr, nc, re_ref, im_ref, peak_ref, re_out, im_out, top_out,
                   buf_c, buf_r, part, send_sem, recv_sem, own_sem, ssem_c, rsem_c, ssem_r, rsem_r):
    me_r = lax.axis_index("row")
    me = lax.axis_index("col")
    mesh_t = pl.DeviceIdType.MESH
    barrier = pltpu.get_barrier_semaphore()
    for k in range(1, nc):
        pl.semaphore_signal(barrier, inc=1, device_id=(me_r, lax.rem(me + k, nc)), device_id_type=mesh_t)
    for k in range(1, nr):
        pl.semaphore_signal(barrier, inc=1, device_id=(lax.rem(me_r + k, nr), me), device_id_type=mesh_t)
    pl.semaphore_wait(barrier, (nc - 1) + (nr - 1))

    def col_top(peer, slot):
        return pltpu.make_async_remote_copy(
            src_ref=peak_ref, dst_ref=buf_c.at[slot], send_sem=ssem_c.at[peer],
            recv_sem=rsem_c.at[slot], device_id=(me_r, peer), device_id_type=mesh_t)

    for k in range(1, nc):
        col_top(lax.rem(me + k, nc), me).start()

    rows = re_ref.shape[0]
    width = re_ref.shape[1] // nc
    srcs = (re_ref, im_ref)
    dsts = (re_out, im_out)

    def data(peer, slot, part_id):
        return pltpu.make_async_remote_copy(
            src_ref=srcs[part_id].at[:, pl.ds(peer * width, width)],
            dst_ref=dsts[part_id].at[pl.ds(slot * rows, rows), :],
            send_sem=send_sem.at[peer, part_id], recv_sem=recv_sem.at[slot, part_id],
            device_id=(me_r, peer), device_id_type=mesh_t)

    for k in range(1, nc):
        for part_id in range(2):
            data(lax.rem(me + k, nc), me, part_id).start()
    owns = []
    for part_id in range(2):
        cp = pltpu.make_async_copy(
            srcs[part_id].at[:, pl.ds(me * width, width)],
            dsts[part_id].at[pl.ds(me * rows, rows), :], own_sem.at[part_id])
        cp.start()
        owns.append(cp)

    acc = peak_ref[...]
    for k in range(1, nc):
        src = lax.rem(me + nc - k, nc)
        col_top(src, src).wait_recv()
        acc = jnp.maximum(acc, buf_c[src])
    for k in range(1, nc):
        col_top(lax.rem(me + k, nc), me).wait_send()
    part[...] = acc

    def row_top(peer, slot):
        return pltpu.make_async_remote_copy(
            src_ref=part, dst_ref=buf_r.at[slot], send_sem=ssem_r.at[peer],
            recv_sem=rsem_r.at[slot], device_id=(peer, me), device_id_type=mesh_t)

    for k in range(1, nr):
        row_top(lax.rem(me_r + k, nr), me_r).start()
    for k in range(1, nr):
        src = lax.rem(me_r + nr - k, nr)
        row_top(src, src).wait_recv()
        acc = jnp.maximum(acc, buf_r[src])
    for k in range(1, nr):
        row_top(lax.rem(me_r + k, nr), me_r).wait_send()
    top_out[...] = acc

    for cp in owns:
        cp.wait()
    for k in range(1, nc):
        src = lax.rem(me + nc - k, nc)
        for part_id in range(2):
            data(src, src, part_id).wait_recv()
            data(lax.rem(me + k, nc), me, part_id).wait_send()


def finish_exchange(re, im, peak_tile, nr, nc, cid):
    rows, cols = re.shape
    out = jax.ShapeDtypeStruct((rows * nc, cols // nc), re.dtype)
    top = jax.ShapeDtypeStruct(peak_tile.shape, peak_tile.dtype)
    return pl.pallas_call(
        functools.partial(_finish_kernel, nr, nc),
        out_shape=(out, out, top),
        in_specs=[pl.BlockSpec(memory_space=pl.ANY)] * 2 + [pl.BlockSpec(memory_space=pltpu.VMEM)],
        out_specs=(pl.BlockSpec(memory_space=pl.ANY),) * 2 + (pl.BlockSpec(memory_space=pltpu.VMEM),),
        scratch_shapes=[
            pltpu.VMEM((nc,) + peak_tile.shape, peak_tile.dtype),
            pltpu.VMEM((nr,) + peak_tile.shape, peak_tile.dtype),
            pltpu.VMEM(peak_tile.shape, peak_tile.dtype),
            pltpu.SemaphoreType.DMA((nc, 2)),
            pltpu.SemaphoreType.DMA((nc, 2)),
            pltpu.SemaphoreType.DMA((2,)),
            pltpu.SemaphoreType.DMA((nc,)),
            pltpu.SemaphoreType.DMA((nc,)),
            pltpu.SemaphoreType.DMA((nr,)),
            pltpu.SemaphoreType.DMA((nr,)),
        ],
        compiler_params=pltpu.CompilerParams(collective_id=cid, has_side_effects=True),
    )(re, im, peak_tile)


def _one_exchange_kernel(nr, nc, x_ref, x_out, send_sem, recv_sem, own_sem):
    n = nr * nc
    me = lax.axis_index("row") * nc + lax.axis_index("col")
    mesh_t = pl.DeviceIdType.MESH
    barrier = pltpu.get_barrier_semaphore()

    def where(p):
        return (p // nc, lax.rem(p, nc))

    def greet(k, carry):
        pl.semaphore_signal(barrier, inc=1, device_id=where(lax.rem(me + k, n)), device_id_type=mesh_t)
        return carry

    lax.fori_loop(1, n, greet, 0, unroll=8)
    pl.semaphore_wait(barrier, n - 1)

    def remote(peer, slot):
        return pltpu.make_async_remote_copy(
            src_ref=x_ref.at[peer], dst_ref=x_out.at[slot],
            send_sem=send_sem.at[peer], recv_sem=recv_sem.at[slot],
            device_id=where(peer), device_id_type=mesh_t)

    for k in range(1, n):
        remote(lax.rem(me + k, n), me).start()
    own = pltpu.make_async_copy(x_ref.at[me], x_out.at[me], own_sem.at[0])
    own.start()
    own.wait()

    def recv(k, carry):
        remote(lax.rem(me + n - k, n), lax.rem(me + n - k, n)).wait_recv()
        return carry

    def sent(k, carry):
        remote(lax.rem(me + k, n), me).wait_send()
        return carry

    lax.fori_loop(1, n, recv, 0, unroll=8)
    lax.fori_loop(1, n, sent, 0, unroll=8)


def one_exchange(x, nr, nc, cid):
    n = nr * nc
    return pl.pallas_call(
        functools.partial(_one_exchange_kernel, nr, nc),
        out_shape=jax.ShapeDtypeStruct(x.shape, x.dtype),
        in_specs=[pl.BlockSpec(memory_space=pl.ANY)],
        out_specs=pl.BlockSpec(memory_space=pl.ANY),
        scratch_shapes=[
            pltpu.SemaphoreType.DMA((n,)),
            pltpu.SemaphoreType.DMA((n,)),
            pltpu.SemaphoreType.DMA((1,)),
        ],
        compiler_params=pltpu.CompilerParams(collective_id=cid, has_side_effects=True),
    )(x)


def transform_blocks(
    values_real, values_imag, exponent_sign, length, outer_size, in_blocks, out_blocks,
    lead_in=False, lead_out=False,
):
    inner_size = length // outer_size
    if lead_in:
        row_count = values_real.shape[1]
        cube_real = values_real.reshape(len(in_blocks), inner_size, row_count)
        cube_imag = values_imag.reshape(len(in_blocks), inner_size, row_count)
        first_form = "nqr,nk->rkq"
    else:
        row_count = values_real.shape[0]
        cube_real = values_real.reshape(row_count, len(in_blocks), inner_size)
        cube_imag = values_imag.reshape(row_count, len(in_blocks), inner_size)
        first_form = "rnq,nk->rkq"
    step_real, step_imag = phase_table(
        jnp.asarray(in_blocks, jnp.int32), index_range(0, outer_size), outer_size, exponent_sign
    )
    mid_real, mid_imag = complex_einsum(first_form, cube_real, cube_imag, step_real, step_imag)
    twist_real, twist_imag = phase_table(
        index_range(0, outer_size), index_range(0, inner_size), length, exponent_sign
    )
    mid_real, mid_imag = (
        mid_real * twist_real - mid_imag * twist_imag,
        mid_real * twist_imag + mid_imag * twist_real,
    )
    last_real, last_imag = phase_table(
        index_range(0, inner_size), jnp.asarray(out_blocks, jnp.int32), inner_size, exponent_sign
    )
    if lead_out:
        done_real, done_imag = complex_einsum(
            "rkq,qj->jkr", mid_real, mid_imag, last_real, last_imag
        )
        return (
            done_real.reshape(len(out_blocks) * outer_size, row_count),
            done_imag.reshape(len(out_blocks) * outer_size, row_count),
        )
    done_real, done_imag = complex_einsum("rkq,qj->rjk", mid_real, mid_imag, last_real, last_imag)
    return (
        done_real.reshape(row_count, len(out_blocks) * outer_size),
        done_imag.reshape(row_count, len(out_blocks) * outer_size),
    )


def band_blocks(padded, block, band_limit, multiple):
    top = math.ceil(band_limit) - 1
    low = list(range(top // block + 1))
    high = list(range((padded - top) // block, padded // block))
    while (len(low) + len(high)) * block % multiple:
        if len(low) <= len(high):
            low.append(low[-1] + 1)
        else:
            high.insert(0, high[0] - 1)
    return low + high


def pack_chunks(first, second, device_total, lead):
    if lead:
        width = first.shape[0] // device_total
        both = jnp.stack([first, second]).reshape(2, device_total, width, first.shape[1])
        both = both.transpose(1, 0, 2, 3)
    else:
        width = first.shape[1] // device_total
        both = jnp.stack([first, second]).reshape(2, first.shape[0], device_total, width)
        both = both.transpose(2, 0, 1, 3)
    return both.reshape(device_total, -1, 128)


def body(field_real, field_imag):
    padded = 2 * N
    quarter = padded // 4
    col_total = lax.axis_size("col")
    device_total = lax.axis_size("row") * col_total
    device = lax.axis_index("row") * col_total + lax.axis_index("col")
    strip_real, strip_imag = rows_to_strip(field_real, field_imag, col_total, 1)
    ratio_sq, band_limit = optics(padded)
    fwd_outer, fwd_inner = factor_pair(padded)
    inv_outer, inv_inner = fwd_outer, fwd_inner
    band = band_blocks(padded, fwd_outer, band_limit, device_total * 2)
    field_blocks = list(range(quarter // fwd_inner, (quarter + N) // fwd_inner))
    near_blocks = list(range(quarter // inv_outer, (quarter + N) // inv_outer))
    inv_band = band[::2] if all(b % 2 == 0 and band[i * 2 + 1] == b + 1 for i, b in enumerate(band[::2])) else None
    inv_band = [b // 2 for b in inv_band]
    pick_real, pick_imag = transform_blocks(
        strip_real, strip_imag, -1.0, padded, fwd_outer, field_blocks, band
    )
    strip_rows = pick_real.shape[0]
    col_width = pick_real.shape[1] // device_total
    packed = jnp.stack([pick_real, pick_imag]).reshape(2, strip_rows, device_total, col_width)
    packed = packed.transpose(2, 0, 1, 3).reshape(device_total, -1, 128)
    arrived = one_exchange(packed, lax.axis_size("row"), col_total, 4)
    arrived = arrived.reshape(device_total, 2, strip_rows, col_width).transpose(1, 0, 2, 3)
    arrived = arrived.reshape(2, device_total * strip_rows, col_width)
    turned_real, turned_imag = arrived[0], arrived[1]
    spec_real, spec_imag = transform_blocks(
        turned_real, turned_imag, -1.0, padded, fwd_outer, field_blocks, band, lead_in=True
    )
    band_freqs = np.array(band, np.int32)[:, None] * fwd_outer + np.arange(fwd_outer, dtype=np.int32)
    freq_ids = jnp.asarray(band_freqs.reshape(-1))
    freq_signed = signed_index(freq_ids, padded).astype(jnp.float32)
    col_ids = lax.dynamic_slice(freq_ids, (device * col_width,), (col_width,))
    col_signed = signed_index(col_ids, padded).astype(jnp.float32)
    gain_real, gain_imag = transfer(col_signed, freq_signed, ratio_sq, band_limit)
    mixed_real = spec_real * gain_real - spec_imag * gain_imag
    mixed_imag = spec_real * gain_imag + spec_imag * gain_real
    inv_real, inv_imag = transform_blocks(
        mixed_real, mixed_imag, 1.0, padded, inv_outer, inv_band, near_blocks
    )
    returned = one_exchange(
        pack_chunks(inv_real, inv_imag, device_total, False), lax.axis_size("row"), col_total, 5
    )
    returned = returned.reshape(device_total, 2, col_width, strip_rows).transpose(1, 0, 2, 3)
    returned = returned.reshape(2, device_total * col_width, strip_rows)
    line_real, line_imag = returned[0], returned[1]
    near_real, near_imag = transform_blocks(
        line_real, line_imag, 1.0, padded, inv_outer, inv_band, near_blocks, lead_in=True
    )
    local_amp = jnp.sqrt(near_real * near_real + near_imag * near_imag)
    peak_tile = jnp.max(local_amp.reshape(-1, 8, 128), axis=0)
    tile_near_real, tile_near_imag, top = finish_exchange(
        near_real, near_imag, peak_tile, lax.axis_size("row"), col_total, 3
    )
    peak = jnp.max(top)
    amplitude = jnp.sqrt(tile_near_real * tile_near_real + tile_near_imag * tile_near_imag)
    tile_rows, tile_cols = tile_near_real.shape
    row_ids = lax.axis_index("row") * tile_rows + jnp.arange(tile_rows, dtype=jnp.int32)
    col_ids_out = lax.axis_index("col") * tile_cols + jnp.arange(tile_cols, dtype=jnp.int32)
    even_cell = (row_ids[:, None] + col_ids_out[None, :]) % 2 == 0
    tile_real, tile_imag = encode(tile_near_real, tile_near_imag, amplitude, peak, even_cell)
    return (tile_real, tile_imag)


def solution(mesh):
    in_specs = (P("row", "col"), P("row", "col"))
    out_specs = (P("row", "col"), P("row", "col"))
    return jax.shard_map(body, mesh=mesh, in_specs=in_specs, out_specs=out_specs, check_vma=False)
```

```python
from functools import partial
import math

import jax
import jax.numpy as jnp
from jax import lax
from jax.sharding import PartitionSpec as P
from jax.experimental import pallas as pl
from jax.experimental.pallas import tpu as pltpu
import functools

import numpy as np

N = 4096


wavelength = 5.2e-07
distance = 0.2


def optics(padded_side):
    pitch = 2e-06 * math.sqrt(8192.0 / padded_side)
    extent = padded_side * pitch
    ratio_sq = (wavelength / extent) ** 2
    band_limit = extent / (wavelength * math.sqrt((2.0 * distance / extent) ** 2 + 1.0))
    return (ratio_sq, band_limit)


def factor_pair(length):
    bit_count = length.bit_length() - 1
    inner_size = 2 ** ((bit_count + 1) // 2)
    return (length // inner_size, inner_size)


def signed_index(index_ids, modulus):
    return jnp.where(index_ids >= modulus // 2, index_ids - modulus, index_ids)


def transfer(row_signed, col_signed, ratio_sq, band_limit):
    square = row_signed[:, None] * row_signed[:, None] + col_signed[None, :] * col_signed[None, :]
    scaled = ratio_sq * square
    phase_angle = -2.0 * math.pi * distance / wavelength * scaled / (1.0 + jnp.sqrt(1.0 - scaled))
    gauss_gain = jnp.exp(square * (-2.0 / (band_limit * band_limit)))
    inside = (jnp.abs(row_signed)[:, None] < band_limit) & (
        jnp.abs(col_signed)[None, :] < band_limit
    )
    total_gain = jnp.where(inside, gauss_gain, 0.0)
    return (total_gain * jnp.cos(phase_angle), total_gain * jnp.sin(phase_angle))


def encode(near_real, near_imag, amplitude, peak, even_cell):
    amp_level = 0.8 * amplitude / peak
    amp_floor = jnp.maximum(amplitude, 0.05 * peak)
    unit_real = near_real / amp_floor
    unit_imag = near_imag / amp_floor
    lift_part = jnp.sqrt(1.0 - amp_level * amp_level)
    cell_sign = jnp.where(even_cell, 1.0, -1.0)
    out_real = unit_real * amp_level + cell_sign * unit_imag * lift_part
    out_imag = unit_imag * amp_level - cell_sign * unit_real * lift_part
    return (out_real, out_imag)


def index_range(range_start, id_count):
    return jnp.arange(id_count, dtype=jnp.int32) + range_start


def phase_table(first_ids, second_ids, modulus, exponent_sign):
    product = first_ids[:, None] * second_ids[None, :] % modulus
    phase_arg = exponent_sign * 2.0 * math.pi / modulus * product.astype(jnp.float32)
    return (jnp.cos(phase_arg), jnp.sin(phase_arg))


def complex_einsum(form, left_real, left_imag, right_real, right_imag):
    real_dot = partial(jnp.einsum, form, precision=lax.Precision.HIGH)
    out_form = form.split("->")[1]
    axis = out_form.index(form.split("->")[0].split(",")[1][-1])
    width = right_real.shape[-1]
    both = jnp.concatenate([right_real, right_imag], axis=-1)
    from_real = real_dot(left_real, both)
    from_imag = real_dot(left_imag, both)
    real_part = partial(lax.slice_in_dim, start_index=0, limit_index=width, axis=axis)
    imag_part = partial(lax.slice_in_dim, start_index=width, limit_index=2 * width, axis=axis)
    out_real = real_part(from_real) - imag_part(from_imag)
    out_imag = imag_part(from_real) + real_part(from_imag)
    return (out_real, out_imag)


def transform_last(values_real, values_imag, exponent_sign, in_start, out_start, out_count, length):
    outer_size, inner_size = factor_pair(length)
    row_count = values_real.shape[0]
    blocks_in = values_real.shape[1] // inner_size
    first_block = in_start // inner_size
    cube_real = values_real.reshape(row_count, blocks_in, inner_size)
    cube_imag = values_imag.reshape(row_count, blocks_in, inner_size)
    step_real, step_imag = phase_table(
        index_range(first_block, blocks_in), index_range(0, outer_size), outer_size, exponent_sign
    )
    mid_real, mid_imag = complex_einsum("rnq,nk->rkq", cube_real, cube_imag, step_real, step_imag)
    twist_real, twist_imag = phase_table(
        index_range(0, outer_size), index_range(0, inner_size), length, exponent_sign
    )
    mid_real, mid_imag = (
        mid_real * twist_real - mid_imag * twist_imag,
        mid_real * twist_imag + mid_imag * twist_real,
    )
    blocks_out = out_count // outer_size
    second_block = out_start // outer_size
    last_real, last_imag = phase_table(
        index_range(0, inner_size), index_range(second_block, blocks_out), inner_size, exponent_sign
    )
    done_real, done_imag = complex_einsum("rkq,qj->rjk", mid_real, mid_imag, last_real, last_imag)
    return (
        done_real.reshape(row_count, blocks_out * outer_size),
        done_imag.reshape(row_count, blocks_out * outer_size),
    )


def _allmax_kernel(nr, nc, x_ref, o_ref, buf_c, buf_r, part, ssem_c, rsem_c, ssem_r, rsem_r):
    me_r = lax.axis_index("row")
    me_c = lax.axis_index("col")
    mesh_t = pl.DeviceIdType.MESH
    barrier = pltpu.get_barrier_semaphore()
    for k in range(1, nc):
        pl.semaphore_signal(barrier, inc=1, device_id=(me_r, lax.rem(me_c + k, nc)), device_id_type=mesh_t)
    for k in range(1, nr):
        pl.semaphore_signal(barrier, inc=1, device_id=(lax.rem(me_r + k, nr), me_c), device_id_type=mesh_t)
    pl.semaphore_wait(barrier, (nc - 1) + (nr - 1))

    def col_copy(dst_c, slot):
        return pltpu.make_async_remote_copy(
            src_ref=x_ref, dst_ref=buf_c.at[slot], send_sem=ssem_c.at[dst_c],
            recv_sem=rsem_c.at[slot], device_id=(me_r, dst_c), device_id_type=mesh_t)
    sends = []
    for k in range(1, nc):
        cp = col_copy(lax.rem(me_c + k, nc), me_c)
        cp.start()
        sends.append(cp)
    acc = x_ref[...]
    for k in range(1, nc):
        src = lax.rem(me_c + nc - k, nc)
        col_copy(src, src).wait_recv()
        acc = jnp.maximum(acc, buf_c[src])
    for cp in sends:
        cp.wait_send()
    part[...] = acc

    def row_copy(dst_r, slot):
        return pltpu.make_async_remote_copy(
            src_ref=part, dst_ref=buf_r.at[slot], send_sem=ssem_r.at[dst_r],
            recv_sem=rsem_r.at[slot], device_id=(dst_r, me_c), device_id_type=mesh_t)
    sends = []
    for k in range(1, nr):
        cp = row_copy(lax.rem(me_r + k, nr), me_r)
        cp.start()
        sends.append(cp)
    for k in range(1, nr):
        src = lax.rem(me_r + nr - k, nr)
        row_copy(src, src).wait_recv()
        acc = jnp.maximum(acc, buf_r[src])
    for cp in sends:
        cp.wait_send()
    o_ref[...] = acc


def global_max(tile, nr, nc):
    return pl.pallas_call(
        functools.partial(_allmax_kernel, nr, nc),
        out_shape=jax.ShapeDtypeStruct(tile.shape, tile.dtype),
        in_specs=[pl.BlockSpec(memory_space=pltpu.VMEM)],
        out_specs=pl.BlockSpec(memory_space=pltpu.VMEM),
        scratch_shapes=[
            pltpu.VMEM((nc,) + tile.shape, tile.dtype),
            pltpu.VMEM((nr,) + tile.shape, tile.dtype),
            pltpu.VMEM(tile.shape, tile.dtype),
            pltpu.SemaphoreType.DMA((nc,)),
            pltpu.SemaphoreType.DMA((nc,)),
            pltpu.SemaphoreType.DMA((nr,)),
            pltpu.SemaphoreType.DMA((nr,)),
        ],
        compiler_params=pltpu.CompilerParams(collective_id=0, has_side_effects=True),
    )(tile)


def _col_exchange_kernel(nc, piece, place, re_ref, im_ref, re_out, im_out, send_sem, recv_sem, own_sem):
    me_r = lax.axis_index("row")
    me = lax.axis_index("col")
    mesh_t = pl.DeviceIdType.MESH
    barrier = pltpu.get_barrier_semaphore()
    for k in range(1, nc):
        pl.semaphore_signal(barrier, inc=1, device_id=(me_r, lax.rem(me + k, nc)), device_id_type=mesh_t)
    pl.semaphore_wait(barrier, nc - 1)
    srcs = (re_ref, im_ref)
    dsts = (re_out, im_out)

    def remote(peer, slot, part):
        return pltpu.make_async_remote_copy(
            src_ref=piece(srcs[part], peer), dst_ref=place(dsts[part], slot),
            send_sem=send_sem.at[peer, part], recv_sem=recv_sem.at[slot, part],
            device_id=(me_r, peer), device_id_type=mesh_t)

    sends = []
    for k in range(1, nc):
        peer = lax.rem(me + k, nc)
        for part in range(2):
            cp = remote(peer, me, part)
            cp.start()
            sends.append(cp)
    owns = []
    for part in range(2):
        cp = pltpu.make_async_copy(piece(srcs[part], me), place(dsts[part], me), own_sem.at[part])
        cp.start()
        owns.append(cp)
    for cp in owns:
        cp.wait()
    for k in range(1, nc):
        src = lax.rem(me + nc - k, nc)
        for part in range(2):
            remote(src, src, part).wait_recv()
    for cp in sends:
        cp.wait_send()


def col_exchange(re, im, out_rows, out_cols, piece, place, nc, cid):
    out = jax.ShapeDtypeStruct((out_rows, out_cols), re.dtype)
    return pl.pallas_call(
        functools.partial(_col_exchange_kernel, nc, piece, place),
        out_shape=(out, out),
        in_specs=[pl.BlockSpec(memory_space=pl.ANY)] * 2,
        out_specs=(pl.BlockSpec(memory_space=pl.ANY),) * 2,
        scratch_shapes=[
            pltpu.SemaphoreType.DMA((nc, 2)),
            pltpu.SemaphoreType.DMA((nc, 2)),
            pltpu.SemaphoreType.DMA((2,)),
        ],
        compiler_params=pltpu.CompilerParams(collective_id=cid, has_side_effects=True),
    )(re, im)


def rows_to_strip(re, im, nc, cid):
    rows, cols = re.shape
    band = rows // nc
    piece = lambda ref, p: ref.at[pl.ds(p * band, band), :]
    place = lambda ref, s: ref.at[:, pl.ds(s * cols, cols)]
    return col_exchange(re, im, band, cols * nc, piece, place, nc, cid)


def strip_to_rows(re, im, nc, cid):
    rows, cols = re.shape
    width = cols // nc
    piece = lambda ref, p: ref.at[:, pl.ds(p * width, width)]
    place = lambda ref, s: ref.at[pl.ds(s * rows, rows), :]
    return col_exchange(re, im, rows * nc, width, piece, place, nc, cid)


def _finish_kernel(nr, nc, re_ref, im_ref, peak_ref, re_out, im_out, top_out,
                   buf_c, buf_r, part, send_sem, recv_sem, own_sem, ssem_c, rsem_c, ssem_r, rsem_r):
    me_r = lax.axis_index("row")
    me = lax.axis_index("col")
    mesh_t = pl.DeviceIdType.MESH
    barrier = pltpu.get_barrier_semaphore()
    for k in range(1, nc):
        pl.semaphore_signal(barrier, inc=1, device_id=(me_r, lax.rem(me + k, nc)), device_id_type=mesh_t)
    for k in range(1, nr):
        pl.semaphore_signal(barrier, inc=1, device_id=(lax.rem(me_r + k, nr), me), device_id_type=mesh_t)
    pl.semaphore_wait(barrier, (nc - 1) + (nr - 1))

    def col_top(peer, slot):
        return pltpu.make_async_remote_copy(
            src_ref=peak_ref, dst_ref=buf_c.at[slot], send_sem=ssem_c.at[peer],
            recv_sem=rsem_c.at[slot], device_id=(me_r, peer), device_id_type=mesh_t)

    for k in range(1, nc):
        col_top(lax.rem(me + k, nc), me).start()

    rows = re_ref.shape[0]
    width = re_ref.shape[1] // nc
    srcs = (re_ref, im_ref)
    dsts = (re_out, im_out)

    def data(peer, slot, part_id):
        return pltpu.make_async_remote_copy(
            src_ref=srcs[part_id].at[:, pl.ds(peer * width, width)],
            dst_ref=dsts[part_id].at[pl.ds(slot * rows, rows), :],
            send_sem=send_sem.at[peer, part_id], recv_sem=recv_sem.at[slot, part_id],
            device_id=(me_r, peer), device_id_type=mesh_t)

    for k in range(1, nc):
        for part_id in range(2):
            data(lax.rem(me + k, nc), me, part_id).start()
    owns = []
    for part_id in range(2):
        cp = pltpu.make_async_copy(
            srcs[part_id].at[:, pl.ds(me * width, width)],
            dsts[part_id].at[pl.ds(me * rows, rows), :], own_sem.at[part_id])
        cp.start()
        owns.append(cp)

    acc = peak_ref[...]
    for k in range(1, nc):
        src = lax.rem(me + nc - k, nc)
        col_top(src, src).wait_recv()
        acc = jnp.maximum(acc, buf_c[src])
    for k in range(1, nc):
        col_top(lax.rem(me + k, nc), me).wait_send()
    part[...] = acc

    def row_top(peer, slot):
        return pltpu.make_async_remote_copy(
            src_ref=part, dst_ref=buf_r.at[slot], send_sem=ssem_r.at[peer],
            recv_sem=rsem_r.at[slot], device_id=(peer, me), device_id_type=mesh_t)

    for k in range(1, nr):
        row_top(lax.rem(me_r + k, nr), me_r).start()
    for k in range(1, nr):
        src = lax.rem(me_r + nr - k, nr)
        row_top(src, src).wait_recv()
        acc = jnp.maximum(acc, buf_r[src])
    for k in range(1, nr):
        row_top(lax.rem(me_r + k, nr), me_r).wait_send()
    top_out[...] = acc

    for cp in owns:
        cp.wait()
    for k in range(1, nc):
        src = lax.rem(me + nc - k, nc)
        for part_id in range(2):
            data(src, src, part_id).wait_recv()
            data(lax.rem(me + k, nc), me, part_id).wait_send()


def finish_exchange(re, im, peak_tile, nr, nc, cid):
    rows, cols = re.shape
    out = jax.ShapeDtypeStruct((rows * nc, cols // nc), re.dtype)
    top = jax.ShapeDtypeStruct(peak_tile.shape, peak_tile.dtype)
    return pl.pallas_call(
        functools.partial(_finish_kernel, nr, nc),
        out_shape=(out, out, top),
        in_specs=[pl.BlockSpec(memory_space=pl.ANY)] * 2 + [pl.BlockSpec(memory_space=pltpu.VMEM)],
        out_specs=(pl.BlockSpec(memory_space=pl.ANY),) * 2 + (pl.BlockSpec(memory_space=pltpu.VMEM),),
        scratch_shapes=[
            pltpu.VMEM((nc,) + peak_tile.shape, peak_tile.dtype),
            pltpu.VMEM((nr,) + peak_tile.shape, peak_tile.dtype),
            pltpu.VMEM(peak_tile.shape, peak_tile.dtype),
            pltpu.SemaphoreType.DMA((nc, 2)),
            pltpu.SemaphoreType.DMA((nc, 2)),
            pltpu.SemaphoreType.DMA((2,)),
            pltpu.SemaphoreType.DMA((nc,)),
            pltpu.SemaphoreType.DMA((nc,)),
            pltpu.SemaphoreType.DMA((nr,)),
            pltpu.SemaphoreType.DMA((nr,)),
        ],
        compiler_params=pltpu.CompilerParams(collective_id=cid, has_side_effects=True),
    )(re, im, peak_tile)


def _one_exchange_kernel(nr, nc, x_ref, x_out, send_sem, recv_sem, own_sem):
    n = nr * nc
    me = lax.axis_index("row") * nc + lax.axis_index("col")
    mesh_t = pl.DeviceIdType.MESH
    barrier = pltpu.get_barrier_semaphore()

    def where(p):
        return (p // nc, lax.rem(p, nc))

    for k in range(1, n):
        pl.semaphore_signal(barrier, inc=1, device_id=where(lax.rem(me + k, n)), device_id_type=mesh_t)
    pl.semaphore_wait(barrier, n - 1)

    def remote(peer, slot):
        return pltpu.make_async_remote_copy(
            src_ref=x_ref.at[peer], dst_ref=x_out.at[slot],
            send_sem=send_sem.at[peer], recv_sem=recv_sem.at[slot],
            device_id=where(peer), device_id_type=mesh_t)

    for k in range(1, n):
        remote(lax.rem(me + k, n), me).start()
    own = pltpu.make_async_copy(x_ref.at[me], x_out.at[me], own_sem.at[0])
    own.start()
    own.wait()

    def recv(k, carry):
        remote(lax.rem(me + n - k, n), lax.rem(me + n - k, n)).wait_recv()
        return carry

    def sent(k, carry):
        remote(lax.rem(me + k, n), me).wait_send()
        return carry

    lax.fori_loop(1, n, recv, 0, unroll=8)
    lax.fori_loop(1, n, sent, 0, unroll=8)


def one_exchange(x, nr, nc, cid):
    n = nr * nc
    return pl.pallas_call(
        functools.partial(_one_exchange_kernel, nr, nc),
        out_shape=jax.ShapeDtypeStruct(x.shape, x.dtype),
        in_specs=[pl.BlockSpec(memory_space=pl.ANY)],
        out_specs=pl.BlockSpec(memory_space=pl.ANY),
        scratch_shapes=[
            pltpu.SemaphoreType.DMA((n,)),
            pltpu.SemaphoreType.DMA((n,)),
            pltpu.SemaphoreType.DMA((1,)),
        ],
        compiler_params=pltpu.CompilerParams(collective_id=cid, has_side_effects=True),
    )(x)


def transform_blocks(
    values_real, values_imag, exponent_sign, length, outer_size, in_blocks, out_blocks,
    lead_in=False, lead_out=False,
):
    inner_size = length // outer_size
    if lead_in:
        row_count = values_real.shape[1]
        cube_real = values_real.reshape(len(in_blocks), inner_size, row_count)
        cube_imag = values_imag.reshape(len(in_blocks), inner_size, row_count)
        first_form = "nqr,nk->rkq"
    else:
        row_count = values_real.shape[0]
        cube_real = values_real.reshape(row_count, len(in_blocks), inner_size)
        cube_imag = values_imag.reshape(row_count, len(in_blocks), inner_size)
        first_form = "rnq,nk->rkq"
    step_real, step_imag = phase_table(
        jnp.asarray(in_blocks, jnp.int32), index_range(0, outer_size), outer_size, exponent_sign
    )
    mid_real, mid_imag = complex_einsum(first_form, cube_real, cube_imag, step_real, step_imag)
    twist_real, twist_imag = phase_table(
        index_range(0, outer_size), index_range(0, inner_size), length, exponent_sign
    )
    mid_real, mid_imag = (
        mid_real * twist_real - mid_imag * twist_imag,
        mid_real * twist_imag + mid_imag * twist_real,
    )
    last_real, last_imag = phase_table(
        index_range(0, inner_size), jnp.asarray(out_blocks, jnp.int32), inner_size, exponent_sign
    )
    if lead_out:
        done_real, done_imag = complex_einsum(
            "rkq,qj->jkr", mid_real, mid_imag, last_real, last_imag
        )
        return (
            done_real.reshape(len(out_blocks) * outer_size, row_count),
            done_imag.reshape(len(out_blocks) * outer_size, row_count),
        )
    done_real, done_imag = complex_einsum("rkq,qj->rjk", mid_real, mid_imag, last_real, last_imag)
    return (
        done_real.reshape(row_count, len(out_blocks) * outer_size),
        done_imag.reshape(row_count, len(out_blocks) * outer_size),
    )


def band_blocks(padded, block, band_limit, multiple):
    top = math.ceil(band_limit) - 1
    low = list(range(top // block + 1))
    high = list(range((padded - top) // block, padded // block))
    while (len(low) + len(high)) * block % multiple:
        if len(low) <= len(high):
            low.append(low[-1] + 1)
        else:
            high.insert(0, high[0] - 1)
    return low + high


def pack_chunks(first, second, device_total, lead):
    if lead:
        width = first.shape[0] // device_total
        both = jnp.stack([first, second]).reshape(2, device_total, width, first.shape[1])
        both = both.transpose(1, 0, 2, 3)
    else:
        width = first.shape[1] // device_total
        both = jnp.stack([first, second]).reshape(2, first.shape[0], device_total, width)
        both = both.transpose(2, 0, 1, 3)
    return both.reshape(device_total, -1, 128)


def body(field_real, field_imag):
    padded = 2 * N
    quarter = padded // 4
    col_total = lax.axis_size("col")
    device_total = lax.axis_size("row") * col_total
    device = lax.axis_index("row") * col_total + lax.axis_index("col")
    strip_real, strip_imag = rows_to_strip(field_real, field_imag, col_total, 1)
    ratio_sq, band_limit = optics(padded)
    fwd_outer, fwd_inner = factor_pair(padded)
    inv_outer, inv_inner = fwd_outer, fwd_inner
    band = band_blocks(padded, fwd_outer, band_limit, device_total * 2)
    field_blocks = list(range(quarter // fwd_inner, (quarter + N) // fwd_inner))
    near_blocks = list(range(quarter // inv_outer, (quarter + N) // inv_outer))
    inv_band = band[::2] if all(b % 2 == 0 and band[i * 2 + 1] == b + 1 for i, b in enumerate(band[::2])) else None
    inv_band = [b // 2 for b in inv_band]
    pick_real, pick_imag = transform_blocks(
        strip_real, strip_imag, -1.0, padded, fwd_outer, field_blocks, band
    )
    strip_rows = pick_real.shape[0]
    col_width = pick_real.shape[1] // device_total
    packed = jnp.stack([pick_real, pick_imag]).reshape(2, strip_rows, device_total, col_width)
    packed = packed.transpose(2, 0, 1, 3).reshape(device_total, -1, 128)
    arrived = one_exchange(packed, lax.axis_size("row"), col_total, 4)
    arrived = arrived.reshape(device_total, 2, strip_rows, col_width).transpose(1, 0, 2, 3)
    arrived = arrived.reshape(2, device_total * strip_rows, col_width)
    turned_real, turned_imag = arrived[0], arrived[1]
    spec_real, spec_imag = transform_blocks(
        turned_real, turned_imag, -1.0, padded, fwd_outer, field_blocks, band, lead_in=True
    )
    band_freqs = np.array(band, np.int32)[:, None] * fwd_outer + np.arange(fwd_outer, dtype=np.int32)
    freq_ids = jnp.asarray(band_freqs.reshape(-1))
    freq_signed = signed_index(freq_ids, padded).astype(jnp.float32)
    col_ids = lax.dynamic_slice(freq_ids, (device * col_width,), (col_width,))
    col_signed = signed_index(col_ids, padded).astype(jnp.float32)
    gain_real, gain_imag = transfer(col_signed, freq_signed, ratio_sq, band_limit)
    mixed_real = spec_real * gain_real - spec_imag * gain_imag
    mixed_imag = spec_real * gain_imag + spec_imag * gain_real
    inv_real, inv_imag = transform_blocks(
        mixed_real, mixed_imag, 1.0, padded, inv_outer, inv_band, near_blocks
    )
    returned = one_exchange(
        pack_chunks(inv_real, inv_imag, device_total, False), lax.axis_size("row"), col_total, 5
    )
    returned = returned.reshape(device_total, 2, col_width, strip_rows).transpose(1, 0, 2, 3)
    returned = returned.reshape(2, device_total * col_width, strip_rows)
    line_real, line_imag = returned[0], returned[1]
    near_real, near_imag = transform_blocks(
        line_real, line_imag, 1.0, padded, inv_outer, inv_band, near_blocks, lead_in=True
    )
    local_amp = jnp.sqrt(near_real * near_real + near_imag * near_imag)
    peak_tile = jnp.max(local_amp.reshape(-1, 8, 128), axis=0)
    tile_near_real, tile_near_imag, top = finish_exchange(
        near_real, near_imag, peak_tile, lax.axis_size("row"), col_total, 3
    )
    peak = jnp.max(top)
    amplitude = jnp.sqrt(tile_near_real * tile_near_real + tile_near_imag * tile_near_imag)
    tile_rows, tile_cols = tile_near_real.shape
    row_ids = lax.axis_index("row") * tile_rows + jnp.arange(tile_rows, dtype=jnp.int32)
    col_ids_out = lax.axis_index("col") * tile_cols + jnp.arange(tile_cols, dtype=jnp.int32)
    even_cell = (row_ids[:, None] + col_ids_out[None, :]) % 2 == 0
    tile_real, tile_imag = encode(tile_near_real, tile_near_imag, amplitude, peak, even_cell)
    return (tile_real, tile_imag)


def solution(mesh):
    in_specs = (P("row", "col"), P("row", "col"))
    out_specs = (P("row", "col"), P("row", "col"))
    return jax.shard_map(body, mesh=mesh, in_specs=in_specs, out_specs=out_specs, check_vma=False)
```

```python
from functools import partial
import math

import jax
import jax.numpy as jnp
from jax import lax
from jax.sharding import PartitionSpec as P
from jax.experimental import pallas as pl
from jax.experimental.pallas import tpu as pltpu
import functools

import numpy as np

N = 4096


wavelength = 5.2e-07
distance = 0.2


def optics(padded_side):
    pitch = 2e-06 * math.sqrt(8192.0 / padded_side)
    extent = padded_side * pitch
    ratio_sq = (wavelength / extent) ** 2
    band_limit = extent / (wavelength * math.sqrt((2.0 * distance / extent) ** 2 + 1.0))
    return (ratio_sq, band_limit)


def factor_pair(length):
    bit_count = length.bit_length() - 1
    inner_size = 2 ** ((bit_count + 1) // 2)
    return (length // inner_size, inner_size)


def signed_index(index_ids, modulus):
    return jnp.where(index_ids >= modulus // 2, index_ids - modulus, index_ids)


def transfer(row_signed, col_signed, ratio_sq, band_limit):
    square = row_signed[:, None] * row_signed[:, None] + col_signed[None, :] * col_signed[None, :]
    scaled = ratio_sq * square
    phase_angle = -2.0 * math.pi * distance / wavelength * scaled / (1.0 + jnp.sqrt(1.0 - scaled))
    gauss_gain = jnp.exp(square * (-2.0 / (band_limit * band_limit)))
    inside = (jnp.abs(row_signed)[:, None] < band_limit) & (
        jnp.abs(col_signed)[None, :] < band_limit
    )
    total_gain = jnp.where(inside, gauss_gain, 0.0)
    return (total_gain * jnp.cos(phase_angle), total_gain * jnp.sin(phase_angle))


def encode(near_real, near_imag, amplitude, peak, even_cell):
    amp_level = 0.8 * amplitude / peak
    amp_floor = jnp.maximum(amplitude, 0.05 * peak)
    unit_real = near_real / amp_floor
    unit_imag = near_imag / amp_floor
    lift_part = jnp.sqrt(1.0 - amp_level * amp_level)
    cell_sign = jnp.where(even_cell, 1.0, -1.0)
    out_real = unit_real * amp_level + cell_sign * unit_imag * lift_part
    out_imag = unit_imag * amp_level - cell_sign * unit_real * lift_part
    return (out_real, out_imag)


def index_range(range_start, id_count):
    return jnp.arange(id_count, dtype=jnp.int32) + range_start


def phase_table(first_ids, second_ids, modulus, exponent_sign):
    product = first_ids[:, None] * second_ids[None, :] % modulus
    phase_arg = exponent_sign * 2.0 * math.pi / modulus * product.astype(jnp.float32)
    return (jnp.cos(phase_arg), jnp.sin(phase_arg))


def complex_einsum(form, left_real, left_imag, right_real, right_imag):
    real_dot = partial(jnp.einsum, form, precision=lax.Precision.HIGH)
    out_form = form.split("->")[1]
    axis = out_form.index(form.split("->")[0].split(",")[1][-1])
    width = right_real.shape[-1]
    both = jnp.concatenate([right_real, right_imag], axis=-1)
    from_real = real_dot(left_real, both)
    from_imag = real_dot(left_imag, both)
    real_part = partial(lax.slice_in_dim, start_index=0, limit_index=width, axis=axis)
    imag_part = partial(lax.slice_in_dim, start_index=width, limit_index=2 * width, axis=axis)
    out_real = real_part(from_real) - imag_part(from_imag)
    out_imag = imag_part(from_real) + real_part(from_imag)
    return (out_real, out_imag)


def transform_last(values_real, values_imag, exponent_sign, in_start, out_start, out_count, length):
    outer_size, inner_size = factor_pair(length)
    row_count = values_real.shape[0]
    blocks_in = values_real.shape[1] // inner_size
    first_block = in_start // inner_size
    cube_real = values_real.reshape(row_count, blocks_in, inner_size)
    cube_imag = values_imag.reshape(row_count, blocks_in, inner_size)
    step_real, step_imag = phase_table(
        index_range(first_block, blocks_in), index_range(0, outer_size), outer_size, exponent_sign
    )
    mid_real, mid_imag = complex_einsum("rnq,nk->rkq", cube_real, cube_imag, step_real, step_imag)
    twist_real, twist_imag = phase_table(
        index_range(0, outer_size), index_range(0, inner_size), length, exponent_sign
    )
    mid_real, mid_imag = (
        mid_real * twist_real - mid_imag * twist_imag,
        mid_real * twist_imag + mid_imag * twist_real,
    )
    blocks_out = out_count // outer_size
    second_block = out_start // outer_size
    last_real, last_imag = phase_table(
        index_range(0, inner_size), index_range(second_block, blocks_out), inner_size, exponent_sign
    )
    done_real, done_imag = complex_einsum("rkq,qj->rjk", mid_real, mid_imag, last_real, last_imag)
    return (
        done_real.reshape(row_count, blocks_out * outer_size),
        done_imag.reshape(row_count, blocks_out * outer_size),
    )


def _allmax_kernel(nr, nc, x_ref, o_ref, buf_c, buf_r, part, ssem_c, rsem_c, ssem_r, rsem_r):
    me_r = lax.axis_index("row")
    me_c = lax.axis_index("col")
    mesh_t = pl.DeviceIdType.MESH
    barrier = pltpu.get_barrier_semaphore()
    for k in range(1, nc):
        pl.semaphore_signal(barrier, inc=1, device_id=(me_r, lax.rem(me_c + k, nc)), device_id_type=mesh_t)
    for k in range(1, nr):
        pl.semaphore_signal(barrier, inc=1, device_id=(lax.rem(me_r + k, nr), me_c), device_id_type=mesh_t)
    pl.semaphore_wait(barrier, (nc - 1) + (nr - 1))

    def col_copy(dst_c, slot):
        return pltpu.make_async_remote_copy(
            src_ref=x_ref, dst_ref=buf_c.at[slot], send_sem=ssem_c.at[dst_c],
            recv_sem=rsem_c.at[slot], device_id=(me_r, dst_c), device_id_type=mesh_t)
    sends = []
    for k in range(1, nc):
        cp = col_copy(lax.rem(me_c + k, nc), me_c)
        cp.start()
        sends.append(cp)
    acc = x_ref[...]
    for k in range(1, nc):
        src = lax.rem(me_c + nc - k, nc)
        col_copy(src, src).wait_recv()
        acc = jnp.maximum(acc, buf_c[src])
    for cp in sends:
        cp.wait_send()
    part[...] = acc

    def row_copy(dst_r, slot):
        return pltpu.make_async_remote_copy(
            src_ref=part, dst_ref=buf_r.at[slot], send_sem=ssem_r.at[dst_r],
            recv_sem=rsem_r.at[slot], device_id=(dst_r, me_c), device_id_type=mesh_t)
    sends = []
    for k in range(1, nr):
        cp = row_copy(lax.rem(me_r + k, nr), me_r)
        cp.start()
        sends.append(cp)
    for k in range(1, nr):
        src = lax.rem(me_r + nr - k, nr)
        row_copy(src, src).wait_recv()
        acc = jnp.maximum(acc, buf_r[src])
    for cp in sends:
        cp.wait_send()
    o_ref[...] = acc


def global_max(tile, nr, nc):
    return pl.pallas_call(
        functools.partial(_allmax_kernel, nr, nc),
        out_shape=jax.ShapeDtypeStruct(tile.shape, tile.dtype),
        in_specs=[pl.BlockSpec(memory_space=pltpu.VMEM)],
        out_specs=pl.BlockSpec(memory_space=pltpu.VMEM),
        scratch_shapes=[
            pltpu.VMEM((nc,) + tile.shape, tile.dtype),
            pltpu.VMEM((nr,) + tile.shape, tile.dtype),
            pltpu.VMEM(tile.shape, tile.dtype),
            pltpu.SemaphoreType.DMA((nc,)),
            pltpu.SemaphoreType.DMA((nc,)),
            pltpu.SemaphoreType.DMA((nr,)),
            pltpu.SemaphoreType.DMA((nr,)),
        ],
        compiler_params=pltpu.CompilerParams(collective_id=0, has_side_effects=True),
    )(tile)


def _col_exchange_kernel(nc, piece, place, re_ref, im_ref, re_out, im_out, send_sem, recv_sem, own_sem):
    me_r = lax.axis_index("row")
    me = lax.axis_index("col")
    mesh_t = pl.DeviceIdType.MESH
    barrier = pltpu.get_barrier_semaphore()
    for k in range(1, nc):
        pl.semaphore_signal(barrier, inc=1, device_id=(me_r, lax.rem(me + k, nc)), device_id_type=mesh_t)
    pl.semaphore_wait(barrier, nc - 1)
    srcs = (re_ref, im_ref)
    dsts = (re_out, im_out)

    def remote(peer, slot, part):
        return pltpu.make_async_remote_copy(
            src_ref=piece(srcs[part], peer), dst_ref=place(dsts[part], slot),
            send_sem=send_sem.at[peer, part], recv_sem=recv_sem.at[slot, part],
            device_id=(me_r, peer), device_id_type=mesh_t)

    sends = []
    for k in range(1, nc):
        peer = lax.rem(me + k, nc)
        for part in range(2):
            cp = remote(peer, me, part)
            cp.start()
            sends.append(cp)
    owns = []
    for part in range(2):
        cp = pltpu.make_async_copy(piece(srcs[part], me), place(dsts[part], me), own_sem.at[part])
        cp.start()
        owns.append(cp)
    for cp in owns:
        cp.wait()
    for k in range(1, nc):
        src = lax.rem(me + nc - k, nc)
        for part in range(2):
            remote(src, src, part).wait_recv()
    for cp in sends:
        cp.wait_send()


def col_exchange(re, im, out_rows, out_cols, piece, place, nc, cid):
    out = jax.ShapeDtypeStruct((out_rows, out_cols), re.dtype)
    return pl.pallas_call(
        functools.partial(_col_exchange_kernel, nc, piece, place),
        out_shape=(out, out),
        in_specs=[pl.BlockSpec(memory_space=pl.ANY)] * 2,
        out_specs=(pl.BlockSpec(memory_space=pl.ANY),) * 2,
        scratch_shapes=[
            pltpu.SemaphoreType.DMA((nc, 2)),
            pltpu.SemaphoreType.DMA((nc, 2)),
            pltpu.SemaphoreType.DMA((2,)),
        ],
        compiler_params=pltpu.CompilerParams(collective_id=cid, has_side_effects=True),
    )(re, im)


def rows_to_strip(re, im, nc, cid):
    rows, cols = re.shape
    band = rows // nc
    piece = lambda ref, p: ref.at[pl.ds(p * band, band), :]
    place = lambda ref, s: ref.at[:, pl.ds(s * cols, cols)]
    return col_exchange(re, im, band, cols * nc, piece, place, nc, cid)


def strip_to_rows(re, im, nc, cid):
    rows, cols = re.shape
    width = cols // nc
    piece = lambda ref, p: ref.at[:, pl.ds(p * width, width)]
    place = lambda ref, s: ref.at[pl.ds(s * rows, rows), :]
    return col_exchange(re, im, rows * nc, width, piece, place, nc, cid)


def _finish_kernel(nr, nc, re_ref, im_ref, peak_ref, re_out, im_out, top_out,
                   buf_c, buf_r, part, send_sem, recv_sem, own_sem, ssem_c, rsem_c, ssem_r, rsem_r):
    me_r = lax.axis_index("row")
    me = lax.axis_index("col")
    mesh_t = pl.DeviceIdType.MESH
    barrier = pltpu.get_barrier_semaphore()
    for k in range(1, nc):
        pl.semaphore_signal(barrier, inc=1, device_id=(me_r, lax.rem(me + k, nc)), device_id_type=mesh_t)
    for k in range(1, nr):
        pl.semaphore_signal(barrier, inc=1, device_id=(lax.rem(me_r + k, nr), me), device_id_type=mesh_t)
    pl.semaphore_wait(barrier, (nc - 1) + (nr - 1))

    def col_top(peer, slot):
        return pltpu.make_async_remote_copy(
            src_ref=peak_ref, dst_ref=buf_c.at[slot], send_sem=ssem_c.at[peer],
            recv_sem=rsem_c.at[slot], device_id=(me_r, peer), device_id_type=mesh_t)

    for k in range(1, nc):
        col_top(lax.rem(me + k, nc), me).start()

    rows = re_ref.shape[0]
    width = re_ref.shape[1] // nc
    srcs = (re_ref, im_ref)
    dsts = (re_out, im_out)

    def data(peer, slot, part_id):
        return pltpu.make_async_remote_copy(
            src_ref=srcs[part_id].at[:, pl.ds(peer * width, width)],
            dst_ref=dsts[part_id].at[pl.ds(slot * rows, rows), :],
            send_sem=send_sem.at[peer, part_id], recv_sem=recv_sem.at[slot, part_id],
            device_id=(me_r, peer), device_id_type=mesh_t)

    for k in range(1, nc):
        for part_id in range(2):
            data(lax.rem(me + k, nc), me, part_id).start()
    owns = []
    for part_id in range(2):
        cp = pltpu.make_async_copy(
            srcs[part_id].at[:, pl.ds(me * width, width)],
            dsts[part_id].at[pl.ds(me * rows, rows), :], own_sem.at[part_id])
        cp.start()
        owns.append(cp)

    acc = peak_ref[...]
    for k in range(1, nc):
        src = lax.rem(me + nc - k, nc)
        col_top(src, src).wait_recv()
        acc = jnp.maximum(acc, buf_c[src])
    for k in range(1, nc):
        col_top(lax.rem(me + k, nc), me).wait_send()
    part[...] = acc

    def row_top(peer, slot):
        return pltpu.make_async_remote_copy(
            src_ref=part, dst_ref=buf_r.at[slot], send_sem=ssem_r.at[peer],
            recv_sem=rsem_r.at[slot], device_id=(peer, me), device_id_type=mesh_t)

    for k in range(1, nr):
        row_top(lax.rem(me_r + k, nr), me_r).start()
    for k in range(1, nr):
        src = lax.rem(me_r + nr - k, nr)
        row_top(src, src).wait_recv()
        acc = jnp.maximum(acc, buf_r[src])
    for k in range(1, nr):
        row_top(lax.rem(me_r + k, nr), me_r).wait_send()
    top_out[...] = acc

    for cp in owns:
        cp.wait()
    for k in range(1, nc):
        src = lax.rem(me + nc - k, nc)
        for part_id in range(2):
            data(src, src, part_id).wait_recv()
            data(lax.rem(me + k, nc), me, part_id).wait_send()


def finish_exchange(re, im, peak_tile, nr, nc, cid):
    rows, cols = re.shape
    out = jax.ShapeDtypeStruct((rows * nc, cols // nc), re.dtype)
    top = jax.ShapeDtypeStruct(peak_tile.shape, peak_tile.dtype)
    return pl.pallas_call(
        functools.partial(_finish_kernel, nr, nc),
        out_shape=(out, out, top),
        in_specs=[pl.BlockSpec(memory_space=pl.ANY)] * 2 + [pl.BlockSpec(memory_space=pltpu.VMEM)],
        out_specs=(pl.BlockSpec(memory_space=pl.ANY),) * 2 + (pl.BlockSpec(memory_space=pltpu.VMEM),),
        scratch_shapes=[
            pltpu.VMEM((nc,) + peak_tile.shape, peak_tile.dtype),
            pltpu.VMEM((nr,) + peak_tile.shape, peak_tile.dtype),
            pltpu.VMEM(peak_tile.shape, peak_tile.dtype),
            pltpu.SemaphoreType.DMA((nc, 2)),
            pltpu.SemaphoreType.DMA((nc, 2)),
            pltpu.SemaphoreType.DMA((2,)),
            pltpu.SemaphoreType.DMA((nc,)),
            pltpu.SemaphoreType.DMA((nc,)),
            pltpu.SemaphoreType.DMA((nr,)),
            pltpu.SemaphoreType.DMA((nr,)),
        ],
        compiler_params=pltpu.CompilerParams(collective_id=cid, has_side_effects=True),
    )(re, im, peak_tile)


def _one_exchange_kernel(nr, nc, x_ref, x_out, send_sem, recv_sem, own_sem):
    n = nr * nc
    me = lax.axis_index("row") * nc + lax.axis_index("col")
    mesh_t = pl.DeviceIdType.MESH
    barrier = pltpu.get_barrier_semaphore()

    def where(p):
        return (p // nc, lax.rem(p, nc))

    for k in range(1, n):
        pl.semaphore_signal(barrier, inc=1, device_id=where(lax.rem(me + k, n)), device_id_type=mesh_t)
    pl.semaphore_wait(barrier, n - 1)

    def remote(peer, slot):
        return pltpu.make_async_remote_copy(
            src_ref=x_ref.at[peer], dst_ref=x_out.at[slot],
            send_sem=send_sem.at[peer], recv_sem=recv_sem.at[slot],
            device_id=where(peer), device_id_type=mesh_t)

    for k in range(1, n):
        remote(lax.rem(me + k, n), me).start()
    own = pltpu.make_async_copy(x_ref.at[me], x_out.at[me], own_sem.at[0])
    own.start()
    own.wait()

    for k in range(1, n):
        remote(lax.rem(me + n - k, n), lax.rem(me + n - k, n)).wait_recv()
    for k in range(1, n):
        remote(lax.rem(me + k, n), me).wait_send()


def one_exchange(x, nr, nc, cid):
    n = nr * nc
    return pl.pallas_call(
        functools.partial(_one_exchange_kernel, nr, nc),
        out_shape=jax.ShapeDtypeStruct(x.shape, x.dtype),
        in_specs=[pl.BlockSpec(memory_space=pl.ANY)],
        out_specs=pl.BlockSpec(memory_space=pl.ANY),
        scratch_shapes=[
            pltpu.SemaphoreType.DMA((n,)),
            pltpu.SemaphoreType.DMA((n,)),
            pltpu.SemaphoreType.DMA((1,)),
        ],
        compiler_params=pltpu.CompilerParams(collective_id=cid, has_side_effects=True),
    )(x)


def transform_blocks(
    values_real, values_imag, exponent_sign, length, outer_size, in_blocks, out_blocks,
    lead_in=False, lead_out=False,
):
    inner_size = length // outer_size
    if lead_in:
        row_count = values_real.shape[1]
        cube_real = values_real.reshape(len(in_blocks), inner_size, row_count)
        cube_imag = values_imag.reshape(len(in_blocks), inner_size, row_count)
        first_form = "nqr,nk->rkq"
    else:
        row_count = values_real.shape[0]
        cube_real = values_real.reshape(row_count, len(in_blocks), inner_size)
        cube_imag = values_imag.reshape(row_count, len(in_blocks), inner_size)
        first_form = "rnq,nk->rkq"
    step_real, step_imag = phase_table(
        jnp.asarray(in_blocks, jnp.int32), index_range(0, outer_size), outer_size, exponent_sign
    )
    mid_real, mid_imag = complex_einsum(first_form, cube_real, cube_imag, step_real, step_imag)
    twist_real, twist_imag = phase_table(
        index_range(0, outer_size), index_range(0, inner_size), length, exponent_sign
    )
    mid_real, mid_imag = (
        mid_real * twist_real - mid_imag * twist_imag,
        mid_real * twist_imag + mid_imag * twist_real,
    )
    last_real, last_imag = phase_table(
        index_range(0, inner_size), jnp.asarray(out_blocks, jnp.int32), inner_size, exponent_sign
    )
    if lead_out:
        done_real, done_imag = complex_einsum(
            "rkq,qj->jkr", mid_real, mid_imag, last_real, last_imag
        )
        return (
            done_real.reshape(len(out_blocks) * outer_size, row_count),
            done_imag.reshape(len(out_blocks) * outer_size, row_count),
        )
    done_real, done_imag = complex_einsum("rkq,qj->rjk", mid_real, mid_imag, last_real, last_imag)
    return (
        done_real.reshape(row_count, len(out_blocks) * outer_size),
        done_imag.reshape(row_count, len(out_blocks) * outer_size),
    )


def band_blocks(padded, block, band_limit, multiple):
    top = math.ceil(band_limit) - 1
    low = list(range(top // block + 1))
    high = list(range((padded - top) // block, padded // block))
    while (len(low) + len(high)) * block % multiple:
        if len(low) <= len(high):
            low.append(low[-1] + 1)
        else:
            high.insert(0, high[0] - 1)
    return low + high


def pack_chunks(first, second, device_total, lead):
    if lead:
        width = first.shape[0] // device_total
        both = jnp.stack([first, second]).reshape(2, device_total, width, first.shape[1])
        both = both.transpose(1, 0, 2, 3)
    else:
        width = first.shape[1] // device_total
        both = jnp.stack([first, second]).reshape(2, first.shape[0], device_total, width)
        both = both.transpose(2, 0, 1, 3)
    return both.reshape(device_total, -1, 128)


def body(field_real, field_imag):
    padded = 2 * N
    quarter = padded // 4
    col_total = lax.axis_size("col")
    device_total = lax.axis_size("row") * col_total
    device = lax.axis_index("row") * col_total + lax.axis_index("col")
    strip_real, strip_imag = rows_to_strip(field_real, field_imag, col_total, 1)
    ratio_sq, band_limit = optics(padded)
    fwd_outer, fwd_inner = factor_pair(padded)
    inv_outer, inv_inner = fwd_outer, fwd_inner
    band = band_blocks(padded, fwd_outer, band_limit, device_total * 2)
    field_blocks = list(range(quarter // fwd_inner, (quarter + N) // fwd_inner))
    near_blocks = list(range(quarter // inv_outer, (quarter + N) // inv_outer))
    inv_band = band[::2] if all(b % 2 == 0 and band[i * 2 + 1] == b + 1 for i, b in enumerate(band[::2])) else None
    inv_band = [b // 2 for b in inv_band]
    pick_real, pick_imag = transform_blocks(
        strip_real, strip_imag, -1.0, padded, fwd_outer, field_blocks, band
    )
    strip_rows = pick_real.shape[0]
    col_width = pick_real.shape[1] // device_total
    packed = jnp.stack([pick_real, pick_imag]).reshape(2, strip_rows, device_total, col_width)
    packed = packed.transpose(2, 0, 1, 3).reshape(device_total, -1, 128)
    arrived = one_exchange(packed, lax.axis_size("row"), col_total, 4)
    arrived = arrived.reshape(device_total, 2, strip_rows, col_width).transpose(1, 0, 2, 3)
    arrived = arrived.reshape(2, device_total * strip_rows, col_width)
    turned_real, turned_imag = arrived[0], arrived[1]
    spec_real, spec_imag = transform_blocks(
        turned_real, turned_imag, -1.0, padded, fwd_outer, field_blocks, band, lead_in=True
    )
    band_freqs = np.array(band, np.int32)[:, None] * fwd_outer + np.arange(fwd_outer, dtype=np.int32)
    freq_ids = jnp.asarray(band_freqs.reshape(-1))
    freq_signed = signed_index(freq_ids, padded).astype(jnp.float32)
    col_ids = lax.dynamic_slice(freq_ids, (device * col_width,), (col_width,))
    col_signed = signed_index(col_ids, padded).astype(jnp.float32)
    gain_real, gain_imag = transfer(col_signed, freq_signed, ratio_sq, band_limit)
    mixed_real = spec_real * gain_real - spec_imag * gain_imag
    mixed_imag = spec_real * gain_imag + spec_imag * gain_real
    inv_real, inv_imag = transform_blocks(
        mixed_real, mixed_imag, 1.0, padded, inv_outer, inv_band, near_blocks
    )
    returned = one_exchange(
        pack_chunks(inv_real, inv_imag, device_total, False), lax.axis_size("row"), col_total, 5
    )
    returned = returned.reshape(device_total, 2, col_width, strip_rows).transpose(1, 0, 2, 3)
    returned = returned.reshape(2, device_total * col_width, strip_rows)
    line_real, line_imag = returned[0], returned[1]
    near_real, near_imag = transform_blocks(
        line_real, line_imag, 1.0, padded, inv_outer, inv_band, near_blocks, lead_in=True
    )
    local_amp = jnp.sqrt(near_real * near_real + near_imag * near_imag)
    peak_tile = jnp.max(local_amp.reshape(-1, 8, 128), axis=0)
    tile_near_real, tile_near_imag, top = finish_exchange(
        near_real, near_imag, peak_tile, lax.axis_size("row"), col_total, 3
    )
    peak = jnp.max(top)
    amplitude = jnp.sqrt(tile_near_real * tile_near_real + tile_near_imag * tile_near_imag)
    tile_rows, tile_cols = tile_near_real.shape
    row_ids = lax.axis_index("row") * tile_rows + jnp.arange(tile_rows, dtype=jnp.int32)
    col_ids_out = lax.axis_index("col") * tile_cols + jnp.arange(tile_cols, dtype=jnp.int32)
    even_cell = (row_ids[:, None] + col_ids_out[None, :]) % 2 == 0
    tile_real, tile_imag = encode(tile_near_real, tile_near_imag, amplitude, peak, even_cell)
    return (tile_real, tile_imag)


def solution(mesh):
    in_specs = (P("row", "col"), P("row", "col"))
    out_specs = (P("row", "col"), P("row", "col"))
    return jax.shard_map(body, mesh=mesh, in_specs=in_specs, out_specs=out_specs, check_vma=False)
```
